32 devices in a mesh: section: 2 (over core), ctx: 4 (over y, x), shard: 4 (over z).
Axes of the slice: x: 2, y: 2, z: 4, core: 2. Of those that a mesh axis runs over, the one named last changes fastest.
Arguments:
- inputs: bfloat16 [2, 1024, 2048], P(None, ('ctx', 'shard')), may hold values from -6 to 6
- cotangent: bfloat16 [2, 1024, 2048], P(None, ('ctx', 'shard')), may hold values from -6 to 6
- doc_lengths: int32 [2, 4], replicated, may hold values from 1 to 512, 1024 in all within a row
- norm_in: float32 [2, 2048], P('section'), may hold values from 0.5 to 1.5
- w_query: bfloat16 [2, 2048, 1024], P('section', None, 'shard'), may hold values from -0.125 to 0.125
- w_keyval: bfloat16 [2, 2048, 2, 256], P('section'), may hold values from -0.125 to 0.125
- w_attn_out: bfloat16 [2, 1024, 2048], P('section', 'shard'), may hold values from -0.75 to 0.75
- w_mixer_in: bfloat16 [2, 2048, 2, 3072], P('section', None, None, 'shard'), may hold values from -0.125 to 0.125
- w_state_io: bfloat16 [2, 2048, 512], P('section'), may hold values from -0.125 to 0.125
- w_step: bfloat16 [2, 2048, 48], P('section', None, 'shard'), may hold values from -0.125 to 0.125
- step_bias: float32 [2, 48], P('section', 'shard'), may hold values from -4 to -1
- decay_rate: float32 [2, 48], P('section', 'shard'), may hold values from 0.001 to 2
- skip_gain: float32 [2, 48], P('section', 'shard'), may hold values from 0.5 to 1.5
- w_mixer_out: bfloat16 [2, 3072, 2048], P('section', 'shard'), may hold values from -0.109375 to 0.109375
- norm_ffn: float32 [2, 2048], P('section'), may hold values from 0.5 to 1.5
- w_gate_up: bfloat16 [2, 2048, 2, 4096], P('section', None, None, 'shard'), may hold values from -0.125 to 0.125
- w_down: bfloat16 [2, 4096, 2048], P('section', 'shard'), may hold values from -0.09375 to 0.09375
Outputs:
- section_out: bfloat16 [2, 2, 1024, 2048], P('section', None, ('ctx', 'shard'))
- input_grad: float32 [2, 2, 1024, 2048], P('section', None, ('ctx', 'shard'))
- grad_norm_in: float32 [2, 2048], P('section', ('ctx', 'shard'))
- grad_query: float32 [2, 2048, 1024], P('section', 'ctx', 'shard')
- grad_keyval: float32 [2, 2048, 2, 256], P('section', ('ctx', 'shard'))
- grad_attn_out: float32 [2, 1024, 2048], P('section', 'shard', 'ctx')
- grad_mixer_in: float32 [2, 2048, 2, 3072], P('section', 'ctx', None, 'shard')
- grad_state_io: float32 [2, 2048, 512], P('section', ('ctx', 'shard'))
- grad_step: float32 [2, 2048, 48], P('section', 'ctx', 'shard')
- grad_step_bias: float32 [2, 48], P('section', 'shard')
- grad_decay: float32 [2, 48], P('section', 'shard')
- grad_skip: float32 [2, 48], P('section', 'shard')
- grad_mixer_out: float32 [2, 3072, 2048], P('section', 'shard', 'ctx')
- grad_norm_ffn: float32 [2, 2048], P('section', ('ctx', 'shard'))
- grad_gate_up: float32 [2, 2048, 2, 4096], P('section', 'ctx', None, 'shard')
- grad_down: float32 [2, 4096, 2048], P('section', 'shard', 'ctx')
The draws below stay inside these ranges and needn't reach their ends.
Inputs may be any that keep to these rules, and one draw needn't show every extreme that they name: Each row of doc_lengths sums to 1024.
All inputs are finite; a program needn't handle non-finite values.
Results may differ from the reference program's by a relative error of at most 0.025.
Values may be sent and summed in bfloat16 or wider, within the bound.
A program may use at most 320 MiB of HBM per device.

```python
import math
import jax
import jax.numpy as jnp
import numpy as np
from jax import lax

D = 2048
QH = 8
KVH = 2
HD = 128
HEADS = 48
HP = 64
NS = 256
FF = 4096
DI = 3072
TOK_CTX = 256
MICRO = 2
NDOC = 4
SEQ = 1024
N_SHARD = 4


def shard_levels(rng, dims, shards, smallest, largest):
    level = 1.0
    for dim, shards_of in shards:
        steps = jax.random.uniform(jax.random.fold_in(jax.random.fold_in(rng, 6), dim), (shards_of,), jnp.float32, smallest / len(shards), largest / len(shards))
        level = level * jnp.repeat(jnp.exp(steps), dims[dim] // shards_of).reshape((-1,) + (1,) * (len(dims) - 1 - dim))
    return level


def length_profile(count, total, limit, slope):
    weights = [(1 << 20) // math.isqrt(grade ** slope) + 1 for grade in range(2, count + 1)]
    rest, given = total - limit - (count - 1), [1] * (count - 1)
    while rest > 0:
        movable = [i for i in range(count - 1) if given[i] < limit]
        mass, remaining = sum([weights[i] for i in movable]), rest
        for i in movable:
            more = min(limit - given[i], max(1, remaining * weights[i] // mass), rest)
            given[i] = given[i] + more
            rest = rest - more
    return np.array([limit] + given)


def uneven_parts(key, amount, total, most, skew):
    if amount == 2:
        one = jax.random.randint(key, (), max(1, total - most), min(most, total - 1) + 1)
        return jnp.stack([one, total - one])
    tallies = jnp.asarray(length_profile(amount, total, most, skew), jnp.int32)
    pairs = (amount - 1) // 2
    giver, receiver = tallies[1:1 + 2 * pairs:2], tallies[2:2 + 2 * pairs:2]
    room = jnp.minimum(giver - 1, most - receiver)
    shifted = jax.random.randint(jax.random.fold_in(key, 1), (pairs,), 0, 1 << 20) % (room + 1)
    tallies = tallies.at[1:1 + 2 * pairs:2].set(giver - shifted).at[2:2 + 2 * pairs:2].set(receiver + shifted)
    return tallies[jax.random.permutation(jax.random.fold_in(key, 2), amount)]


def centred(key, dims, deviation, limit, shards=(), held_as=jnp.bfloat16):
    result = deviation * jax.random.normal(key, dims, jnp.float32)
    if shards:
        result = result * shard_levels(key, dims, shards, -0.22, 0.18)
    return jnp.clip(result, -limit, limit).astype(held_as)


def setup_inputs(seed: int = 0) -> dict:
    streams_of = jax.random.split(jax.random.key(seed), 18)
    return {
        "inputs": centred(streams_of[0], (MICRO, SEQ, D), 1.0, 6.0, ((1, 16),)),
        "cotangent": centred(streams_of[1], (MICRO, SEQ, D), 1.0, 6.0, ((1, 16),)),
        "doc_lengths": jax.vmap(lambda own: uneven_parts(own, NDOC, SEQ, SEQ // 2, 2))(jax.random.split(streams_of[2], MICRO)).reshape((MICRO, NDOC)).astype(jnp.int32),
        "norm_in": jnp.clip(1.0 + 0.1 * jax.random.normal(streams_of[3], (2, D), jnp.float32), 0.5, 1.5),
        "w_query": centred(streams_of[4], (2, D, QH * HD), D ** -0.5, 0.125, ((0, 2), (2, 4))),
        "w_keyval": centred(streams_of[5], (2, D, 2, KVH * HD), D ** -0.5, 0.125, ((0, 2),)),
        "w_attn_out": centred(streams_of[6], (2, QH * HD, D), (QH * HD // 16) ** -0.5, 0.75, ((0, 2), (1, 4))),
        "w_mixer_in": centred(streams_of[7], (2, D, 2, DI), D ** -0.5, 0.125, ((0, 2), (3, 4))),
        "w_state_io": centred(streams_of[8], (2, D, 2 * NS), D ** -0.5, 0.125, ((0, 2),)),
        "w_step": centred(streams_of[9], (2, D, HEADS), D ** -0.5, 0.125, ((0, 2), (2, 4))),
        "step_bias": jnp.clip(-4.0 + 3.0 * jax.random.uniform(streams_of[10], (2, HEADS), jnp.float32) ** shard_levels(streams_of[10], (2, HEADS), ((0, 2), (1, 4)), -0.2, 0.2), -4.0, -1.0),
        "decay_rate": jnp.clip(jnp.exp(math.log(2.0) - 7.6009024 * jax.random.uniform(streams_of[11], (2, HEADS), jnp.float32) ** shard_levels(streams_of[11], (2, HEADS), ((0, 2), (1, 4)), -0.2, 0.2)), 0.001, 2.0),
        "skip_gain": jnp.clip(0.5 + 1.0 * jax.random.uniform(streams_of[12], (2, HEADS), jnp.float32) ** shard_levels(streams_of[12], (2, HEADS), ((0, 2), (1, 4)), -0.2, 0.2), 0.5, 1.5),
        "w_mixer_out": centred(streams_of[13], (2, DI, D), DI ** -0.5, 0.109375, ((0, 2), (1, 4))),
        "norm_ffn": jnp.clip(1.0 + 0.1 * jax.random.normal(streams_of[14], (2, D), jnp.float32), 0.5, 1.5),
        "w_gate_up": centred(streams_of[15], (2, D, 2, FF), D ** -0.5, 0.125, ((0, 2), (3, 4))),
        "w_down": centred(streams_of[16], (2, FF, D), FF ** -0.5, 0.09375, ((0, 2), (1, 4))),
    }


@jax.custom_vjp
def low(v):
    return lax.optimization_barrier(v.astype(jnp.bfloat16)).astype(jnp.float32)

@jax.custom_vjp
def low_back(v):
    return v

def low_keep(v):
    return (low(v), None)

def low_pass(kept, grad):
    return (grad,)

def back_keep(v):
    return (v, None)

def back_low(kept, grad):
    return (low(grad),)
low.defvjp(low_keep, low_pass)
low_back.defvjp(back_keep, back_low)
highest = lax.Precision.HIGHEST
eps = 1e-05

def matmul(left, right):
    return jnp.dot(left, right, precision=highest)

def norm_apply(values, gain):
    return values * lax.rsqrt(lax.optimization_barrier(jnp.mean(values * values, axis=-1, keepdims=True)) + eps) * gain

def segment_ids(doc_lengths):
    bounds = jnp.cumsum(doc_lengths).astype(jnp.int32)[:-1]
    positions = jnp.arange(SEQ, dtype=jnp.int32)
    return lax.optimization_barrier(jnp.sum((positions[:, None] >= bounds[None, :]).astype(jnp.int32), axis=1)).astype(jnp.int32)

def attention(queries, keys_rep, values_rep, segments):
    positions = jnp.arange(SEQ, dtype=jnp.int32)
    blocks = SEQ // TOK_CTX
    query_blocks = queries.reshape(blocks, TOK_CTX, QH, HD)

    def one_block(block):
        query_part, position_part, segment_part = block
        raw_scores = jnp.einsum('qhd,khd->hqk', query_part, keys_rep, precision=highest)
        scores = low_back(raw_scores) * HD ** (-0.5)
        key_mask = (position_part[:, None] >= positions[None, :]) & (segment_part[:, None] == segments[None, :])
        scores = jnp.where(key_mask[None], scores, -1e+30)
        row_top = lax.optimization_barrier(jnp.max(scores, axis=-1, keepdims=True))
        expo = jnp.exp(scores - row_top)
        soft = expo / lax.optimization_barrier(jnp.sum(expo, axis=-1, keepdims=True))
        return jnp.einsum('hqk,khd->qhd', low(soft), values_rep, precision=highest)
    attended = lax.map(jax.checkpoint(one_block), (query_blocks, positions.reshape(blocks, TOK_CTX), segments.reshape(blocks, TOK_CTX)))
    return attended.reshape(SEQ, QH * HD)

def mamba(xvalues, b_groups, c_groups, step_raw, step_bias, decay_rate, skip_gain, segments):
    step_size = jax.nn.softplus(step_raw + step_bias)
    log_decay = -step_size * decay_rate
    per_group = HEADS // N_SHARD
    blocks = SEQ // TOK_CTX
    b_heads = jnp.repeat(b_groups, per_group, axis=0).reshape(HEADS, blocks, TOK_CTX, NS).transpose(1, 0, 2, 3)
    c_heads = jnp.repeat(c_groups, per_group, axis=0).reshape(HEADS, blocks, TOK_CTX, NS).transpose(1, 0, 2, 3)
    x_blocks = xvalues.reshape(blocks, TOK_CTX, HEADS, HP)
    step_blocks = step_size.reshape(blocks, TOK_CTX, HEADS)
    log_blocks = log_decay.reshape(blocks, TOK_CTX, HEADS)
    seg_blocks = segments.reshape(blocks, TOK_CTX).astype(jnp.int32)

    def one_block(carry, block):
        state_in, prev_segment = carry
        x_part, b_part, c_part, step_part, log_part, seg_part = block
        cumulated = jnp.cumsum(log_part, axis=0)
        offsets = jnp.arange(TOK_CTX)
        causal = (offsets[:, None] >= offsets[None, :]) & (seg_part[:, None] == seg_part[None, :])
        cum_heads = cumulated.T
        spread = cum_heads[:, :, None] - cum_heads[:, None, :]
        weight = jnp.where(causal[None], jnp.exp(jnp.where(causal[None], spread, 0.0)), 0.0)
        intersection = jnp.einsum('htn,hsn->hts', c_part, b_part, precision=highest) * NS ** (-0.5)
        mixing = weight * intersection * step_part.T[:, None, :]
        output = jnp.einsum('hts,shp->thp', mixing, x_part, precision=highest)
        carried = jnp.einsum('htn,hpn->thp', c_part, state_in, precision=highest)
        carries = (seg_part == prev_segment).astype(cumulated.dtype)
        output = output + carried * (jnp.exp(cumulated) * carries[:, None])[:, :, None] + skip_gain[None, :, None] * x_part
        keeps = seg_part == seg_part[-1]
        coeffs = jnp.where(keeps[:, None], jnp.exp(cumulated[-1][None, :] - cumulated), 0.0) * step_part
        fresh_state = jnp.einsum('th,thp,htn->hpn', coeffs, x_part, b_part, precision=highest)
        block_decay = jnp.exp(cumulated[-1]) * (seg_part[-1] == prev_segment).astype(cumulated.dtype)
        return ((block_decay[:, None, None] * state_in + fresh_state, seg_part[-1].astype(jnp.int32)), output)
    start_carry = (jnp.zeros((HEADS, HP, NS), xvalues.dtype), jnp.array(-1, jnp.int32))
    _, outputs = lax.scan(jax.checkpoint(one_block), start_carry, (x_blocks, b_heads, c_heads, step_blocks, log_blocks, seg_blocks))
    return outputs.reshape(SEQ, HEADS * HP)

def layer(weights, hidden, segments):
    gain_in, w_query, w_keyval, w_attn_out, w_mixer_in, w_state_io, w_step, step_bias, decay_rate, skip_gain, w_mixer_out, gain_ffn, w_gate_up, w_down = weights
    normed = low(norm_apply(hidden, gain_in))
    queries = low_back(low(matmul(normed, w_query))).reshape(SEQ, QH, HD)
    keyval = low(matmul(normed, w_keyval.reshape(D, 2 * KVH * HD))).reshape(SEQ, 2, KVH, HD)
    owners = np.arange(N_SHARD) * (QH // N_SHARD) // (QH // KVH)
    key_groups = low_back(keyval[:, 0][:, owners])
    value_groups = low_back(keyval[:, 1][:, owners])
    keys_rep = jnp.repeat(key_groups, QH // N_SHARD, axis=1)
    values_rep = jnp.repeat(value_groups, QH // N_SHARD, axis=1)
    attended = low_back(low(attention(queries, keys_rep, values_rep, segments)))
    mixer_pre = matmul(normed, w_mixer_in.reshape(D, 2 * DI))
    gate_z = low_back(mixer_pre[:, :DI])
    xvalues = low_back(low(mixer_pre[:, DI:]))
    bc_values = low(matmul(normed, w_state_io))
    b_groups = low_back(jnp.broadcast_to(bc_values[:, :NS], (N_SHARD, SEQ, NS)))
    c_groups = low_back(jnp.broadcast_to(bc_values[:, NS:], (N_SHARD, SEQ, NS)))
    step_raw = low_back(matmul(normed, w_step))
    ssm_y = mamba(xvalues.reshape(SEQ, HEADS, HP), b_groups, c_groups, step_raw, step_bias, decay_rate, skip_gain, segments)
    gated = low(ssm_y * jax.nn.silu(gate_z))
    middle = hidden + low_back(matmul(attended, w_attn_out) + matmul(gated, w_mixer_out))
    ffn_in = low(norm_apply(middle, gain_ffn))
    gate_up = matmul(ffn_in, w_gate_up.reshape(D, 2 * FF))
    gate_pre = low_back(gate_up[:, :FF])
    upward = low_back(gate_up[:, FF:])
    product = low(jax.nn.silu(gate_pre) * upward)
    return middle + low_back(matmul(product, w_down))

def reference(inputs, cotangent, doc_lengths, norm_in, w_query, w_keyval, w_attn_out, w_mixer_in, w_state_io, w_step, step_bias, decay_rate, skip_gain, w_mixer_out, norm_ffn, w_gate_up, w_down):
    params = tuple((array.astype(jnp.float32) for array in (norm_in, w_query, w_keyval, w_attn_out, w_mixer_in, w_state_io, w_step, step_bias, decay_rate, skip_gain, w_mixer_out, norm_ffn, w_gate_up, w_down)))
    first_params = tuple((array[0] for array in params))
    second_params = tuple((array[1] for array in params))

    def one_batch(totals, batch):
        sequence, target, lengths = batch
        segments = segment_ids(lengths)

        def run_layer(weights, hidden):
            return layer(weights, hidden, segments)
        out_first, back_first = jax.vjp(run_layer, first_params, sequence.astype(jnp.float32))
        passed = low(out_first)
        out_second, back_second = jax.vjp(run_layer, second_params, passed)
        grads_second, d_passed = back_second(target.astype(jnp.float32))
        grads_first, d_sequence = back_first(low(d_passed))
        totals_first = tuple((acc + new for acc, new in zip(totals[0], grads_first)))
        totals_second = tuple((acc + new for acc, new in zip(totals[1], grads_second)))
        return ((totals_first, totals_second), (out_first.astype(jnp.bfloat16), out_second.astype(jnp.bfloat16), d_sequence, d_passed))
    zeros = tuple((jnp.zeros_like(array) for array in first_params))
    (grads_first, grads_second), (outs_first, outs_second, din_first, din_second) = lax.scan(one_batch, (zeros, zeros), (inputs, cotangent, doc_lengths))
    stacked = [jnp.stack([left, right]) for left, right in zip(grads_first, grads_second)]
    return (jnp.stack([outs_first, outs_second]), jnp.stack([din_first, din_second]), stacked[0], stacked[1], stacked[2], stacked[3], stacked[4], stacked[5], stacked[6], stacked[7], stacked[8], stacked[9], stacked[10], stacked[11], stacked[12], stacked[13])
```

```python
import functools
import types

import jax
import jax.numpy as jnp
from jax import lax
from jax.experimental import pallas as pl
from jax.experimental.pallas import tpu as pltpu
from jax.sharding import PartitionSpec as P

SECTION, CTX, SHARD = "section", "ctx", "shard"
QH = 8
KVH = 2
HD = 128
HP = 64
CHUNKS = 16
LAG = 3

MESH = pl.DeviceIdType.MESH
eps = 1e-05
bf16 = jnp.bfloat16
f32 = jnp.float32


def line_sum(n, chunks, lag, p_rows, done, sr, sl, rr, rl, srs, sls, rrs, rls, tot, fill=None):
    z = lax.axis_index(SHARD)
    hasr, hasl = z < n - 1, z > 0
    bar = pltpu.get_barrier_semaphore()
    more = 0
    if fill is not None:
        more = fill.greet(bar)

    @pl.when(hasr)
    def _():
        pl.semaphore_signal(bar, inc=1, device_id={SHARD: z + 1}, device_id_type=MESH)

    @pl.when(hasl)
    def _():
        pl.semaphore_signal(bar, inc=1, device_id={SHARD: z - 1}, device_id_type=MESH)

    @pl.when(hasl & hasr)
    def _():
        pl.semaphore_wait(bar, 2 + more)

    @pl.when(jnp.logical_not(hasl & hasr))
    def _():
        pl.semaphore_wait(bar, 1 + more)

    def right(j):
        return pltpu.make_async_remote_copy(
            sr.at[j], rr.at[j], srs.at[j], rrs.at[j], device_id={SHARD: z + 1}, device_id_type=MESH
        )

    def left(j):
        return pltpu.make_async_remote_copy(
            sl.at[j], rl.at[j], sls.at[j], rls.at[j], device_id={SHARD: z - 1}, device_id_type=MESH
        )

    steps = chunks + lag * (n - 1)
    if fill is not None:
        fill.start()

    def one(i, _):
        def go(j, copy, came, goes, inbox, outbox):
            live = (j >= 0) & (j < chunks)

            @pl.when(live & came & goes)
            def _():
                copy(j).wait_recv()
                outbox[j] = (p_rows(j) + inbox[j].astype(f32)).astype(bf16)
                copy(j).start()

            @pl.when(live & jnp.logical_not(came))
            def _():
                outbox[j] = p_rows(j).astype(bf16)
                copy(j).start()

            @pl.when(live & jnp.logical_not(goes))
            def _():
                copy(j).wait_recv()

        go(i - lag * z, right, hasl, hasr, rr, sr)
        go(i - lag * (n - 1 - z), left, hasr, hasl, rl, sl)
        jd = i - lag * jnp.maximum(z, n - 1 - z)

        @pl.when((jd >= 0) & (jd < chunks))
        def _():
            tot[...] = p_rows(jd)

            @pl.when(hasl)
            def _():
                tot[...] += rr[jd].astype(f32)

            @pl.when(hasr)
            def _():
                tot[...] += rl[jd].astype(f32)

            done(jd, tot[...])

        if fill is not None:
            fill.step(i, steps)
        return 0

    lax.fori_loop(0, steps, one, 0)
    if fill is not None:
        fill.finish()

    def drain(j, _):
        @pl.when(hasr)
        def _():
            right(j).wait_send()

        @pl.when(hasl)
        def _():
            left(j).wait_send()

        return 0

    lax.fori_loop(0, chunks, drain, 0)


def row_slice(j, rows):
    return pl.ds(pl.multiple_of(j * rows, rows), rows)


def middle_kernel(n, chunks, lag, p_ref, h_ref, gain_ref, mid_ref, low_ref, *scratch, fill=None):
    rows = p_ref.shape[0] // chunks

    def p_rows(j):
        return p_ref[row_slice(j, rows), :]

    def done(j, total):
        v = h_ref[row_slice(j, rows), :] + total
        r = lax.rsqrt(jnp.mean(v * v, axis=-1, keepdims=True) + eps)
        mid_ref[row_slice(j, rows), :] = v
        low_ref[row_slice(j, rows), :] = (v * r * gain_ref[...]).astype(bf16)

    line_sum(n, chunks, lag, p_rows, done, *scratch, fill=fill)


class Copies:
    parts = 16

    def __init__(self, layers, own, other, out, boxes, came, went):
        self.layers, self.own, self.other, self.out = layers, own, other, out
        self.boxes, self.came, self.went = boxes, came, went

    def greet(self, bar):
        return 0

    def start(self):
        pass

    def rows(self, a, j):
        size = self.boxes[a].shape[1]
        return pl.ds(pl.multiple_of(j * size, size), size)

    def fetch(self, a, j, act):
        section, slot = lax.axis_index(SECTION), lax.rem(j, 2)
        for mine, source in ((True, self.own[a]), (False, self.other[a])):

            @pl.when((section == self.layers[a]) == mine)
            def _():
                part = source.at[self.rows(a, j), :]
                act(
                    pltpu.make_async_copy(
                        part, self.boxes[a].at[slot], self.came.at[2 * a + slot]
                    )
                )

    def store(self, a, j):
        slot = lax.rem(j, 2)
        part = self.out[a].at[self.rows(a, j), :]
        return pltpu.make_async_copy(self.boxes[a].at[slot], part, self.went.at[2 * a + slot])

    def step(self, i, steps):
        @pl.when((i >= 1) & (i <= self.parts))
        def _():
            for a in range(len(self.layers)):
                self.fetch(a, i - 1, lambda copy: copy.wait())
                self.store(a, i - 1).start()

        @pl.when((i >= 2) & (i < self.parts))
        def _():
            for a in range(len(self.layers)):
                self.store(a, i - 2).wait()

        @pl.when(i < self.parts)
        def _():
            for a in range(len(self.layers)):
                self.fetch(a, i, lambda copy: copy.start())

    def finish(self):
        for a in range(len(self.layers)):
            for j in (self.parts - 2, self.parts - 1):
                self.store(a, j).wait()


def copying(kernel, layers, n, chunks, lag, p_ref, h_ref, gain_ref, *refs):
    count = len(layers)
    own, other, refs = refs[:count], refs[count : 2 * count], refs[2 * count :]
    first_ref, low_ref, refs = refs[0], refs[1], refs[2:]
    out, refs = refs[:count], refs[count:]
    copies = Copies(layers, own, other, out, refs[9 : 9 + count], *refs[9 + count :])
    kernel(n, chunks, lag, p_ref, h_ref, gain_ref, first_ref, low_ref, *refs[:9], fill=copies)


def layer_end_kernel(n, chunks, lag, p_ref, h_ref, gain_ref, out_ref, low_ref, *scratch, fill=None):
    rows = p_ref.shape[0] // chunks

    def p_rows(j):
        return p_ref[row_slice(j, rows), :]

    def done(j, total):
        out = (h_ref[row_slice(j, rows), :] + total).astype(bf16)
        out_ref[row_slice(j, rows), :] = out
        v = out.astype(f32)
        r = lax.rsqrt(jnp.mean(v * v, axis=-1, keepdims=True) + eps)
        low_ref[row_slice(j, rows), :] = (v * r * gain_ref[...]).astype(bf16)

    line_sum(n, chunks, lag, p_rows, done, *scratch, fill=fill)


def flipped(place, k, count):
    total, bit = 0, 1
    while bit < count:
        total = total + (place // bit + k // bit) % 2 * bit
        bit *= 2
    return total


def mirrored(k, count):
    total, bit = 0, 1
    while bit < count:
        total = total + k // bit % 2 * (count // (2 * bit))
        bit *= 2
    return total


class Fill:
    first = 6

    def __init__(self, plan, xs, ys, outs, scratch):
        self.plan, self.xs, self.ys, self.outs = plan, xs, ys, outs
        count = len(plan)
        self.other_x, rest = scratch[: len(xs)], scratch[len(xs) :]
        self.own_y, self.other_y = rest[:count], rest[count : 2 * count]
        self.send, self.recv = rest[2 * count :]

    def greet(self, bar):
        other = 1 - lax.axis_index(SECTION)
        pl.semaphore_signal(bar, inc=1, device_id={SECTION: other}, device_id_type=MESH)
        return 1

    def copies(self):
        section = lax.axis_index(SECTION)
        copies = []

        def add(source, target):
            i = len(copies)
            copies.append(
                pltpu.make_async_remote_copy(
                    source,
                    target,
                    self.send.at[i],
                    self.recv.at[i],
                    device_id={SECTION: 1 - section},
                    device_id_type=MESH,
                )
            )

        for x, target in zip(self.xs, self.other_x):
            add(x, target)
        for (_, _, parts), target in zip(self.plan, self.other_y):
            at = 0
            for y, low, high, width in parts:
                start = pl.multiple_of(low + (high - low) * (1 - section), 128)
                add(self.ys[y].at[:, pl.ds(start, width)], target.at[:, at : at + width])
                at += width
        return copies

    def start(self):
        for copy in self.copies():
            copy.start()
        section = lax.axis_index(SECTION)
        for (_, _, parts), own in zip(self.plan, self.own_y):
            at = 0
            for y, low, high, width in parts:
                start = pl.multiple_of(low + (high - low) * section, 128)
                own[:, at : at + width] = self.ys[y][:, pl.ds(start, width)]
                at += width

    def step(self, i, steps):
        place, count = lax.axis_index(CTX), lax.axis_size(CTX)

        @pl.when(i == self.first)
        def _():
            for copy in self.copies():
                copy.wait_recv()

        each = -(-count * len(self.plan) // (steps - self.first))
        begin = (i - self.first) * each

        def piece(t, _):
            at = [0, 0]
            for f, (x, stream, _) in enumerate(self.plan):
                k = t - f * count
                width = self.own_y[f].shape[1]
                where = slice(at[stream], at[stream] + width)
                at[stream] += width
                kept, sent = self.outs[2 * stream : 2 * stream + 2]

                @pl.when((k >= 0) & (k < count))
                def _():
                    block = kept.shape[1]
                    source = flipped(place, mirrored(k, count) if stream else k, count)
                    cols = pl.ds(pl.multiple_of(source * block, block), block)
                    dims = (((0,), (0,)), ((), ()))
                    total = lax.dot_general(
                        self.xs[x][:, cols], self.own_y[f][...], dims, preferred_element_type=f32
                    ) + lax.dot_general(
                        self.other_x[x][:, cols],
                        self.other_y[f][...],
                        dims,
                        preferred_element_type=f32,
                    )
                    low = total.astype(bf16)

                    @pl.when(k < count // 2)
                    def _():
                        kept[k, :, where] = low

                    @pl.when(k >= count // 2)
                    def _():
                        sent[k - count // 2, :, where] = low

            return 0

        @pl.when(i >= self.first)
        def _():
            lax.fori_loop(begin, begin + each, piece, 0)

    def finish(self):
        for copy in self.copies():
            copy.wait_send()


class Scatter:
    def __init__(self, blocks, out, inbox, send, recv):
        self.blocks, self.out, self.inbox, self.send, self.recv = blocks, out, inbox, send, recv
        self.count, self.place = lax.axis_size(CTX), lax.axis_index(CTX)

    def peer(self, k):
        return flipped(self.place, k, self.count)

    def copy(self, k):
        return pltpu.make_async_remote_copy(
            self.blocks.at[k],
            self.inbox.at[k],
            self.send.at[k],
            self.recv.at[k],
            device_id={CTX: self.peer(k)},
            device_id_type=MESH,
        )

    def greet(self, bar):
        for k in range(1, self.count):
            pl.semaphore_signal(bar, inc=1, device_id={CTX: self.peer(k)}, device_id_type=MESH)
        return self.count - 1

    def start(self):
        for k in reversed(range(1, self.count)):
            self.copy(k).start()

    def step(self, i, steps):
        pass

    def finish(self):
        rows = 64

        for k in range(1, self.count):
            self.copy(k).wait_recv()

        def add(j, _):
            part = row_slice(j, rows)
            total = self.blocks[0, part, :].astype(f32)
            for k in range(1, self.count):
                total += self.inbox[k, part, :].astype(f32)
            self.out[part, :] = total.astype(bf16)
            return 0

        lax.fori_loop(0, self.out.shape[0] // rows, add, 0)
        for k in range(1, self.count):
            self.copy(k).wait_send()


class Halving:
    cuts = 2
    turns = (11, 20)

    def __init__(self, streams, outs, scratch):
        self.place, self.count = lax.axis_index(CTX), lax.axis_size(CTX)
        self.streams, self.outs = streams, outs
        self.orders = ctx_orders()
        self.levels = len(self.orders[0])
        self.inbox = [scratch[k * self.levels : (k + 1) * self.levels] for k in range(2)]
        rest = scratch[2 * self.levels :]
        self.sums = [rest[k * (self.levels - 1) : (k + 1) * (self.levels - 1)] for k in range(2)]
        self.send, self.recv = rest[2 * (self.levels - 1) :]

    def greet(self, bar):
        for bit in self.orders[0]:
            peer = flipped(self.place, bit, self.count)
            pl.semaphore_signal(bar, inc=1, device_id={CTX: peer}, device_id_type=MESH)
        return self.levels

    def rows(self, cut):
        size = self.outs[0].shape[0] // self.cuts
        return pl.ds(cut * size, size)

    def copy(self, level, stream, cut):
        rows = self.rows(cut)
        if level == 0:
            source = self.streams[2 * stream + 1].at[:, rows, :]
        else:
            blocks = self.count >> (level + 1)
            source = self.sums[stream][level - 1].at[pl.ds(blocks, blocks), rows, :]
        i = (level * 2 + stream) * self.cuts + cut
        return pltpu.make_async_remote_copy(
            source,
            self.inbox[stream][level].at[:, rows, :],
            self.send.at[i],
            self.recv.at[i],
            device_id={CTX: flipped(self.place, self.orders[stream][level], self.count)},
            device_id_type=MESH,
        )

    def advance(self, level, cut):
        rows, blocks = self.rows(cut), self.count >> (level + 1)
        for stream in range(2):
            self.copy(level, stream, cut).wait_recv()
            kept = self.streams[2 * stream] if level == 0 else self.sums[stream][level - 1]
            for k in range(blocks):
                total = kept[k, rows, :].astype(f32) + self.inbox[stream][level][k, rows, :].astype(
                    f32
                )
                if level + 1 < self.levels:
                    self.sums[stream][level][k, rows, :] = total.astype(bf16)
                else:
                    self.outs[stream][rows, :] = total.astype(bf16)
            if level + 1 < self.levels:
                self.copy(level + 1, stream, cut).start()

    def start(self):
        for cut in range(self.cuts):
            for stream in range(2):
                self.copy(0, stream, cut).start()

    def step(self, i, steps):
        for cut, turn in enumerate(self.turns):

            @pl.when(i == turn)
            def _():
                self.advance(0, cut)

    def finish(self):
        for level in range(1, self.levels):
            for cut in range(self.cuts):
                self.advance(level, cut)
        for level in range(self.levels):
            for stream in range(2):
                for cut in range(self.cuts):
                    self.copy(level, stream, cut).wait_send()


def halving_scratch(streams):
    blocks, rows, width = streams[0].shape
    levels = len(ctx_bits())
    inbox = [pltpu.VMEM((blocks >> k, rows, width), bf16) for k in range(levels)]
    copies = levels * 2 * Halving.cuts
    return [*inbox * 2, *inbox[: levels - 1] * 2, *[pltpu.SemaphoreType.DMA((copies,))] * 2]


class Together:
    def __init__(self, *jobs):
        self.jobs = jobs

    def greet(self, bar):
        return sum(job.greet(bar) for job in self.jobs)

    def start(self):
        for job in self.jobs:
            job.start()

    def step(self, i, steps):
        for job in self.jobs:
            job.step(i, steps)

    def finish(self):
        for job in self.jobs:
            job.finish()


def scatter_kernel(n, chunks, lag, p_ref, q_ref, d_ref, v_ref, gain_ref, blocks, *refs):
    outs, out, scratch = refs[:4], refs[4], refs[5:]
    job = Scatter(blocks, out, *scratch[9:])
    back_rows(n, chunks, lag, p_ref, d_ref, v_ref, gain_ref, *outs[:3], scratch[:9], job, q_ref, outs[3])


def back_kernel(n, chunks, lag, plan, x_count, y_count, beside, ready, p_ref, *refs):
    q_ref = q_out = None
    if beside:
        q_ref, refs = refs[0], refs[1:]
    (d_ref, v_ref, gain_ref), refs = refs[:3], refs[3:]
    xs, refs = refs[:x_count], refs[x_count:]
    ys, refs = refs[:y_count], refs[y_count:]
    streams, refs = refs[:ready], refs[ready:]
    out_ref, low_ref, gg_ref = refs[:3]
    refs = refs[3:]
    if beside:
        q_out, refs = refs[0], refs[1:]
    sums, refs = refs[:4], refs[4:]
    totals, refs = refs[: ready // 2], refs[ready // 2 :]
    cut = len(xs) + 2 * len(plan) + 2
    fill = Fill(plan, xs, ys, sums, refs[9 : 9 + cut])
    if ready:
        fill = Together(fill, Halving(streams, totals, refs[9 + cut :]))
    outs = out_ref, low_ref, gg_ref
    back_rows(n, chunks, lag, p_ref, d_ref, v_ref, gain_ref, *outs, refs[:9], fill, q_ref, q_out)


def back_rows(
    n,
    chunks,
    lag,
    p_ref,
    d_ref,
    v_ref,
    gain_ref,
    out_ref,
    low_ref,
    gg_ref,
    scratch,
    fill,
    q_ref=None,
    q_out=None,
):
    rows, width = p_ref.shape[0] // chunks, p_ref.shape[1]
    gg_ref[...] = jnp.zeros_like(gg_ref)

    def p_rows(j):
        part = row_slice(j, rows)
        if q_ref is None:
            return p_ref[part, :]
        return jnp.concatenate([p_ref[part, :], q_ref[part, :].astype(f32)], axis=1)

    def done(j, total):
        if q_ref is not None:
            q_out[row_slice(j, rows), :] = total[:, width:].astype(bf16)
            total = total[:, :width]
        v = v_ref[row_slice(j, rows), :].astype(f32)
        r = lax.rsqrt(jnp.mean(v * v, axis=-1, keepdims=True) + eps)
        vr = v * r
        dg = total * gain_ref[...]
        inner = jnp.mean(dg * vr, axis=-1, keepdims=True)
        gg_ref[...] += jnp.sum((total * vr).reshape(rows // 8, 8, vr.shape[1]), axis=0)
        out = d_ref[row_slice(j, rows), :].astype(f32) + r * (dg - vr * inner)
        out_ref[row_slice(j, rows), :] = out
        low_ref[row_slice(j, rows), :] = out.astype(bf16)

    line_sum(n, chunks, lag, p_rows, done, *scratch, fill=fill)


def summed(kernel, collective, outs, *operands, extra=(), more=0, far=(0, 0)):
    n = lax.axis_size(SHARD)
    length, width = operands[0].shape[0], operands[0].shape[1] + more
    box = pltpu.VMEM((CHUNKS, length // CHUNKS, width), bf16)
    distant = pl.BlockSpec(memory_space=pl.ANY)
    whole = pl.BlockSpec(memory_space=pltpu.VMEM)
    return pl.pallas_call(
        functools.partial(kernel, n, CHUNKS, LAG),
        out_shape=outs,
        in_specs=[whole] * (len(operands) - far[0]) + [distant] * far[0],
        out_specs=[whole] * (len(outs) - far[1]) + [distant] * far[1],
        scratch_shapes=[box] * 4
        + [pltpu.SemaphoreType.DMA((CHUNKS,))] * 4
        + [pltpu.VMEM((length // CHUNKS, width), f32), *extra],
        compiler_params=pltpu.CompilerParams(
            collective_id=collective, has_side_effects=True, vmem_limit_bytes=58 << 20
        ),
        cost_estimate=pl.CostEstimate(flops=0, bytes_accessed=20 << 20, transcendentals=0),
        name="line_sum"+str(collective),
    )(*operands)


def gather_kernel(n, rows_ref, out_ref, box, send, recv):
    z = lax.axis_index(SHARD)
    part = rows_ref.shape[0]
    bar = pltpu.get_barrier_semaphore()

    def copy(k):
        return pltpu.make_async_remote_copy(
            rows_ref,
            box.at[k],
            send.at[k],
            recv.at[k],
            device_id={SHARD: lax.rem(z + k, n)},
            device_id_type=MESH,
        )

    for k in range(1, n):
        pl.semaphore_signal(bar, inc=1, device_id={SHARD: lax.rem(z + k, n)}, device_id_type=MESH)
    pl.semaphore_wait(bar, n - 1)
    for k in range(1, n):
        copy(k).start()
    out_ref[row_slice(z, part), :] = rows_ref[...]
    for k in range(1, n):
        copy(k).wait_recv()
        out_ref[row_slice(lax.rem(z + n - k, n), part), :] = box[k]
    for k in range(1, n):
        copy(k).wait_send()


def line_gather(rows):
    n = lax.axis_size(SHARD)
    whole = pl.BlockSpec(memory_space=pltpu.VMEM)
    return pl.pallas_call(
        functools.partial(gather_kernel, n),
        out_shape=jax.ShapeDtypeStruct((n * rows.shape[0], rows.shape[1]), rows.dtype),
        in_specs=[whole],
        out_specs=whole,
        scratch_shapes=[pltpu.VMEM((n,) + rows.shape, rows.dtype)]
        + [pltpu.SemaphoreType.DMA((n,))] * 2,
        compiler_params=pltpu.CompilerParams(collective_id=8, has_side_effects=True),
        name="gather",
    )(rows)


def shaped(array, dtype):
    return jax.ShapeDtypeStruct(array.shape, dtype)


def copying_sum(kernel, collective, dtype, p, hidden, gain, wanted):
    layers, own, other = zip(*wanted)
    outs = [shaped(p, dtype), shaped(p, bf16)] + [shaped(a, bf16) for a in own]
    boxes = [pltpu.VMEM((2, a.shape[0] // Copies.parts, a.shape[1]), bf16) for a in own]
    first, low, *chosen = summed(
        functools.partial(copying, kernel, layers),
        collective,
        outs,
        p,
        hidden,
        gain[None],
        *own,
        *other,
        extra=[*boxes, *[pltpu.SemaphoreType.DMA((2 * len(layers),))] * 2],
        far=(2 * len(layers), len(layers)),
    )
    return first, low, chosen


def back_sum(collective, p, d_out, values, gain, plan, xs, ys, beside=(), ready=()):
    count = lax.axis_size(CTX)
    length = p.shape[0]
    outs = [shaped(p, f32), shaped(p, bf16), jax.ShapeDtypeStruct((8, p.shape[1]), f32)]
    outs += [shaped(q, bf16) for q in beside]
    widths = [sum(part[3] for part in parts) for _, _, parts in plan]
    for stream in range(2):
        total = sum(w for (_, at, _), w in zip(plan, widths) if at == stream)
        shape = (count // 2, xs[0].shape[1] // count, total)
        outs += [jax.ShapeDtypeStruct(shape, bf16)] * 2
    extra = [pltpu.VMEM(x.shape, bf16) for x in xs]
    extra += [pltpu.VMEM((length, w), bf16) for w in widths] * 2
    copies = len(xs) + sum(len(parts) for _, _, parts in plan)
    extra += [pltpu.SemaphoreType.DMA((copies,))] * 2
    if ready:
        outs += [jax.ShapeDtypeStruct(a.shape[1:], bf16) for a in ready[::2]]
        extra += halving_scratch(ready)

    def bound(n, chunks, lag, *refs):
        back_kernel(n, chunks, lag, plan, len(xs), len(ys), bool(beside), len(ready), *refs)

    operands = (p, *beside, d_out, values, gain[None], *xs, *ys, *ready)
    more = sum(q.shape[1] for q in beside)
    out, low, gg, *sums = summed(bound, collective, outs, *operands, extra=extra, more=more)
    return out, low, jnp.sum(gg, axis=0), *sums


def back_sum_scatter(collective, p, beside, d_out, values, gain, blocks):
    outs = [shaped(p, f32), shaped(p, bf16), jax.ShapeDtypeStruct((8, p.shape[1]), f32)]
    outs += [shaped(beside, bf16), jax.ShapeDtypeStruct(blocks.shape[1:], bf16)]
    sems = [pltpu.SemaphoreType.DMA((blocks.shape[0],))] * 2
    extra = [pltpu.VMEM(blocks.shape, bf16), *sems]
    operands = (p, beside, d_out, values, gain[None], blocks)
    more = beside.shape[1]
    out, low, gg, whole, total = summed(
        scatter_kernel, collective, outs, *operands, extra=extra, more=more
    )
    return out, low, jnp.sum(gg, axis=0), whole, total


def dot(left, right, dims=((1,), (0,))):
    return lax.dot_general(left, right, (dims, ((), ())), preferred_element_type=f32)


NT = ((1,), (1,))
TN = ((0,), (0,))


def in_three(values):
    high = values.astype(bf16)
    rest = values - high.astype(f32)
    mid = rest.astype(bf16)
    return high, mid, (rest - mid.astype(f32)).astype(bf16)


def running_sum(values, reverse):
    length = values.shape[0]
    row = lax.broadcasted_iota(jnp.int32, (length, length), 0)
    col = lax.broadcasted_iota(jnp.int32, (length, length), 1)
    kept = jnp.where(row <= col if reverse else row >= col, 1.0, 0.0).astype(bf16)
    return sum(dot(kept, part) for part in in_three(values))


def lanes(shape):
    return lax.broadcasted_iota(jnp.int32, shape, 1)


def column(values, head):
    return jnp.sum(jnp.where(lanes(values.shape) == head, values, 0.0), axis=1, keepdims=True)


def in_pair(values, pair):
    low, high = column(values, 2 * pair), column(values, 2 * pair + 1)
    return jnp.where(lanes(values.shape) < HP, low, high)


def from_pair(values, pair):
    lane = lanes(values.shape)
    low = jnp.sum(jnp.where(lane < HP, values, 0.0), axis=1, keepdims=True)
    high = jnp.sum(jnp.where(lane < HP, 0.0, values), axis=1, keepdims=True)
    return jnp.where(lane == 2 * pair, low, 0.0) + jnp.where(lane == 2 * pair + 1, high, 0.0)


def pair_ds(pair, start=0):
    return pl.ds(pl.multiple_of(start + pair * 2 * HP, 2 * HP), 2 * HP)


def steps_of(step_raw, vec_ref, tok_ref, cum, cum_rows, step, enter, fade):
    shifted = step_raw + vec_ref[0:1, :]
    step[...] = jnp.maximum(shifted, 0.0) + jnp.log1p(jnp.exp(-jnp.abs(shifted)))
    cum[...] = running_sum(-step[...] * vec_ref[1:2, :], False)
    total = cum[...]
    cum_rows[...] = total.T
    enter[...] = jnp.exp(total) * tok_ref[:, 1:2]
    fade[...] = jnp.exp(total[-1:, :] - total) * tok_ref[:, 2:3]
    return shifted


def masks_of(tok_ref, key_ref):
    kept = (tok_ref[:, 3:4] >= key_ref[1:2, :]) & (tok_ref[:, 0:1] == key_ref[0:1, :])
    return jnp.where(kept, 0.0, -1e30)


def ctx_barrier(count, place):
    bar = pltpu.get_barrier_semaphore()

    def greet(k, _):
        pl.semaphore_signal(
            bar, inc=1, device_id={CTX: lax.rem(place + k, count)}, device_id_type=MESH
        )
        return 0

    lax.fori_loop(1, count, greet, 0)
    pl.semaphore_wait(bar, count - 1)


def ctx_copy(source, target, send, recv, peer):
    return pltpu.make_async_remote_copy(
        source, target, send, recv, device_id={CTX: peer}, device_id_type=MESH
    )


def mix_forward_kernel(
    count,
    widths,
    heads,
    proj_ref,
    vec_ref,
    skip_ref,
    tok_ref,
    key_ref,
    both_ref,
    mixed_ref,
    state_ref,
    keyval_ref,
    decay_ref,
    cum,
    cum_rows,
    step,
    enter,
    fade,
    mask,
    crossed,
    keyvals,
    fresh,
    decays,
    total_state,
    kv_send,
    kv_recv,
    st_send,
    st_recv,
    dc_send,
    dc_recv,
):
    place = lax.axis_index(CTX)
    length = proj_ref.shape[0]
    inner = (proj_ref.shape[1] - widths[3]) // 2
    pairs = heads // 2
    states = (widths[2] - widths[1]) // 2
    ctx_barrier(count, place)

    keyvals[0] = proj_ref[:, widths[0] : widths[1]].astype(bf16)

    def kv_copy(k):
        peer = lax.rem(place + k, count)
        return ctx_copy(keyvals.at[0], keyvals.at[k], kv_send.at[k], kv_recv.at[k], peer)

    def st_copy(k):
        peer = lax.rem(place + k, count)
        return ctx_copy(fresh.at[0], fresh.at[k], st_send.at[k], st_recv.at[k], peer)

    def dc_copy(k):
        peer = lax.rem(place + k, count)
        return ctx_copy(decays.at[0], decays.at[k], dc_send.at[k], dc_recv.at[k], peer)

    def kv_start(k, _):
        kv_copy(k).start()
        return 0

    lax.fori_loop(1, count, kv_start, 0)
    steps_of(
        proj_ref[:, widths[2] : widths[2] + 128], vec_ref, tok_ref, cum, cum_rows, step, enter, fade
    )
    last = cum_rows[: decays.shape[1], length - 1 :]
    decays[0] = jnp.broadcast_to(jnp.exp(last) * tok_ref[0:1, 4:5], decays.shape[1:])
    b_low = proj_ref[:, widths[1] : widths[1] + states].astype(bf16)
    c_low = proj_ref[:, widths[1] + states : widths[2]].astype(bf16)

    def make_fresh(pair, _):
        x = proj_ref[:, pair_ds(pair, widths[3] + inner)]
        x = x.astype(bf16).astype(f32)
        faded = (x * in_pair(fade[...] * step[...], pair)).astype(bf16)
        fresh[0, pair_ds(pair), :] = dot(faded, b_low, TN).astype(bf16)
        return 0

    lax.fori_loop(0, pairs, make_fresh, 0)

    def st_start(k, _):
        dc_copy(k).start()

        @pl.when(place + k < count)
        def _():
            st_copy(k).start()

        return 0

    lax.fori_loop(1, count, st_start, 0)
    mask[...] = masks_of(tok_ref, key_ref)
    crossed[...] = dot(c_low, b_low, NT) * states ** (-0.5)

    def inside(pair, _):
        x = proj_ref[:, pair_ds(pair, widths[3] + inner)]
        x = x.astype(bf16).astype(f32)
        xdt = (x * in_pair(step[...], pair)).astype(bf16)
        parts = []
        for side in range(2):
            head = 2 * pair + side
            spread = column(cum[...], head) - cum_rows[pl.ds(head, 1), :]
            weight = jnp.exp(spread + mask[:, :length])
            parts.append(dot((weight * crossed[...]).astype(bf16), xdt))
        mixed_ref[:, pair_ds(pair)] = jnp.where(lanes(parts[0].shape) < HP, *parts)
        return 0

    lax.fori_loop(0, pairs, inside, 0)

    def kv_wait(k, _):
        kv_copy(k).wait_recv()
        return 0

    lax.fori_loop(1, count, kv_wait, 0)
    keyval_ref[...] = keyvals[...].reshape(keyval_ref.shape)
    for head in range(widths[0] // HD):
        query = proj_ref[:, head * HD : (head + 1) * HD].astype(bf16)
        scores = dot(query, keyval_ref[:, :HD], NT) * HD ** (-0.5) + mask[...]
        expo = jnp.exp(scores - jnp.max(scores, axis=1, keepdims=True))
        soft = expo * (1.0 / jnp.sum(expo, axis=1, keepdims=True))
        both_ref[:, head * HD : (head + 1) * HD] = dot(
            soft.astype(bf16), keyval_ref[:, HD:]
        ).astype(bf16)

    def dc_wait(k, _):
        dc_copy(k).wait_recv()

        @pl.when(k <= place)
        def _():
            st_copy(k).wait_recv()

        return 0

    lax.fori_loop(1, count, dc_wait, 0)
    total_state[...] = jnp.zeros_like(total_state)
    head_width = inner // heads

    def combine(index, _):
        slot = place - index

        def one_head(head, _):
            rows = pl.ds(pl.multiple_of(head * head_width, head_width), head_width)
            total_state[rows, :] = total_state[rows, :] * decays[slot, pl.ds(head, 1), :] + fresh[
                slot, rows, :
            ].astype(f32)
            return 0

        lax.fori_loop(0, heads, one_head, 0)
        return 0

    lax.fori_loop(0, place, combine, 0)
    state_ref[...] = total_state[...].astype(bf16)
    decay_ref[...] = decays[...]

    def finish(pair, _):
        carried = dot(c_low, state_ref[pair_ds(pair), :], NT)
        mixed = mixed_ref[:, pair_ds(pair)] + carried * in_pair(enter[...], pair)
        mixed_ref[:, pair_ds(pair)] = mixed
        x = proj_ref[:, pair_ds(pair, widths[3] + inner)]
        x = x.astype(bf16).astype(f32)
        gate = proj_ref[:, pair_ds(pair, widths[3])]
        y = mixed + x * skip_ref[0:1, pair_ds(pair)]
        both_ref[:, pair_ds(pair, widths[0])] = (
            y * gate / (1.0 + jnp.exp(-gate))
        ).astype(bf16)
        return 0

    lax.fori_loop(0, pairs, finish, 0)

    def drain(k, _):
        kv_copy(k).wait_send()
        dc_copy(k).wait_send()

        @pl.when(place + k < count)
        def _():
            st_copy(k).wait_send()

        return 0

    lax.fori_loop(1, count, drain, 0)


def mix_backward_kernel(
    count,
    widths,
    heads,
    proj_ref,
    vec_ref,
    skip_ref,
    tok_ref,
    key_ref,
    mixed_ref,
    state_ref,
    keyval_ref,
    decay_ref,
    d_both_ref,
    d_proj_ref,
    d_vec_ref,
    cum,
    cum_rows,
    step,
    enter,
    fade,
    mask,
    crossed,
    d_crossed,
    d_y,
    d_carried,
    d_x,
    d_keyval,
    d_b,
    d_c,
    d_cum,
    d_step,
    d_coeff,
    d_skip,
    d_states,
    total_state,
    kv_out,
    kv_in,
    kv_send,
    kv_recv,
    st_send,
    st_recv,
):
    place = lax.axis_index(CTX)
    length = proj_ref.shape[0]
    inner = (proj_ref.shape[1] - widths[3]) // 2
    pairs = heads // 2
    head_width = inner // heads
    states = (widths[2] - widths[1]) // 2
    ctx_barrier(count, place)

    def back(k):
        return lax.rem(place + count - k, count)

    def kv_copy(k):
        return ctx_copy(kv_out.at[k], kv_in.at[k], kv_send.at[k], kv_recv.at[k], back(k))

    def st_copy(k):
        return ctx_copy(d_states.at[0], d_states.at[k], st_send.at[k], st_recv.at[k], back(k))

    shifted = steps_of(
        proj_ref[:, widths[2] : widths[2] + 128], vec_ref, tok_ref, cum, cum_rows, step, enter, fade
    )
    b_low = proj_ref[:, widths[1] : widths[1] + states].astype(bf16)
    c_low = proj_ref[:, widths[1] + states : widths[2]].astype(bf16)
    d_cum[...] = jnp.zeros_like(d_cum)
    d_step[...] = jnp.zeros_like(d_step)
    d_coeff[...] = jnp.zeros_like(d_coeff)
    d_skip[...] = jnp.zeros_like(d_skip)

    def x_of(pair):
        x = proj_ref[:, pair_ds(pair, widths[3] + inner)]
        return x.astype(bf16).astype(f32)

    def outer(pair, _):
        gate = proj_ref[:, pair_ds(pair, widths[3])]
        d_gated = d_both_ref[:, pair_ds(pair, widths[0])]
        x, mixed, skip = x_of(pair), mixed_ref[:, pair_ds(pair)], skip_ref[0:1, pair_ds(pair)]
        sig = 1.0 / (1.0 + jnp.exp(-gate))
        dy = d_gated * gate * sig
        d_gate = d_gated * (mixed + x * skip) * sig * (1.0 + gate * (1.0 - sig))
        d_proj_ref[:, pair_ds(pair, widths[3])] = d_gate.astype(bf16)
        low = dy.astype(bf16)
        d_y[:, pair_ds(pair)] = low
        d_x[:, pair_ds(pair)] = dy * skip
        d_skip[...] += from_pair(dy * x, pair)
        d_cum[...] += from_pair(low.astype(f32) * mixed, pair)
        carried = (low.astype(f32) * in_pair(enter[...], pair)).astype(bf16)
        d_carried[:, pair_ds(pair)] = carried
        d_states[0, pair_ds(pair), :] = dot(carried, c_low, TN).astype(bf16)
        return 0

    lax.fori_loop(0, pairs, outer, 0)

    def st_start(k, _):
        @pl.when(k <= place)
        def _():
            st_copy(k).start()

        return 0

    lax.fori_loop(1, count, st_start, 0)
    mask[...] = masks_of(tok_ref, key_ref)
    for head in range(widths[0] // HD):
        cols = slice(head * HD, (head + 1) * HD)
        query = proj_ref[:, cols].astype(bf16)
        scores = dot(query, keyval_ref[:, :HD], NT) * HD ** (-0.5) + mask[...]
        expo = jnp.exp(scores - jnp.max(scores, axis=1, keepdims=True))
        soft = expo * (1.0 / jnp.sum(expo, axis=1, keepdims=True))
        grad = d_both_ref[:, cols].astype(bf16)
        d_soft = dot(grad, keyval_ref[:, HD:], NT)
        d_scores = soft * (d_soft - jnp.sum(soft * d_soft, axis=1, keepdims=True))
        d_raw = (d_scores * HD ** (-0.5)).astype(bf16)
        d_proj_ref[:, cols] = dot(d_raw, keyval_ref[:, :HD]).astype(bf16)
        d_keys, d_values = dot(d_raw, query, TN), dot(soft.astype(bf16), grad, TN)
        if head == 0:
            d_keyval[:, :HD] = d_keys
            d_keyval[:, HD:] = d_values
        else:
            d_keyval[:, :HD] += d_keys
            d_keyval[:, HD:] += d_values
    kv_out[...] = d_keyval[...].astype(bf16).reshape(kv_out.shape)

    def kv_start(k, _):
        kv_copy(k).start()
        return 0

    lax.fori_loop(1, count, kv_start, 0)
    crossed[...] = dot(c_low, b_low, NT) * states ** (-0.5)
    d_crossed[...] = jnp.zeros_like(d_crossed)

    def inside(pair, _):
        x = x_of(pair)
        steps = in_pair(step[...], pair)
        xdt = (x * steps).astype(bf16)
        low = d_y[:, pair_ds(pair)]
        lane = lanes(low.shape)
        parts = []
        for side in range(2):
            head = 2 * pair + side
            spread = column(cum[...], head) - cum_rows[pl.ds(head, 1), :]
            weight = jnp.exp(spread + mask[:, :length])
            parts.append(dot((weight * crossed[...]).astype(bf16), low, TN))
            mine = (lane >= HP) if side else (lane < HP)
            alone = jnp.where(mine, low.astype(f32), 0.0).astype(bf16)
            d_crossed[...] += dot(alone, xdt, NT) * weight
        d_xdt = jnp.where(lane < HP, *parts)
        d_x[:, pair_ds(pair)] += d_xdt * steps
        d_step[...] += from_pair(d_xdt * x, pair)
        d_cum[...] -= from_pair(d_xdt * xdt.astype(f32), pair)
        return 0

    lax.fori_loop(0, pairs, inside, 0)
    low_crossed = (d_crossed[...] * states ** (-0.5)).astype(bf16)
    d_c[...] = dot(low_crossed, b_low) + dot(d_carried[...], state_ref[...])
    d_b[...] = dot(low_crossed, c_low, TN)

    def st_wait(k, _):
        @pl.when(place + k < count)
        def _():
            st_copy(k).wait_recv()

        return 0

    lax.fori_loop(1, count, st_wait, 0)
    total_state[...] = jnp.zeros_like(total_state)

    def combine(index, _):
        slot = count - 1 - place - index
        source = lax.rem(count - slot, count)

        def one_head(head, _):
            rows = pl.ds(pl.multiple_of(head * head_width, head_width), head_width)
            total_state[rows, :] = total_state[rows, :] * decay_ref[
                source, pl.ds(head, 1), :
            ] + d_states[slot, rows, :].astype(f32)
            return 0

        lax.fori_loop(0, heads, one_head, 0)
        return 0

    lax.fori_loop(0, count - 1 - place, combine, 0)
    d_vec_ref[...] = jnp.zeros_like(d_vec_ref)

    def from_later(pair, _):
        rows = pair_ds(pair)
        later = total_state[rows, :]
        low = later.astype(bf16)
        x = x_of(pair)
        coeffs = in_pair(fade[...] * step[...], pair)
        back_x = dot(b_low, low, NT)
        d_proj_ref[:, pair_ds(pair, widths[3] + inner)] = (
            d_x[:, rows] + back_x * coeffs
        ).astype(bf16)
        d_coeff[...] += from_pair(back_x * x, pair)
        d_b[...] += dot((x * coeffs).astype(bf16), low)
        product = later * state_ref[rows, :].astype(f32)
        row = lax.broadcasted_iota(jnp.int32, product.shape, 0)
        lane = lanes((1, 128))
        for side in range(2):
            mine = (row >= HP) if side else (row < HP)
            part = jnp.sum(jnp.where(mine, product, 0.0), axis=0, keepdims=True)
            part = jnp.sum(part, axis=1, keepdims=True)
            d_vec_ref[3:4, :] += jnp.where(lane == 2 * pair + side, part, 0.0)
        return 0

    lax.fori_loop(0, pairs, from_later, 0)
    fading = fade[...]
    d_keep = d_coeff[...] * fading * step[...]
    block_decay = jnp.exp(cum[length - 1 :, :]) * tok_ref[0:1, 4:5]
    d_last = jnp.sum(d_keep, axis=0, keepdims=True) + block_decay * d_vec_ref[3:4, :]
    d_log = running_sum(d_cum[...] - d_keep, True) + d_last
    d_size = d_step[...] + d_coeff[...] * fading - vec_ref[1:2, :] * d_log
    d_raw_step = d_size / (1.0 + jnp.exp(-shifted))
    d_proj_ref[:, widths[2] : widths[3]] = jnp.where(
        lanes(d_raw_step.shape) < heads, d_raw_step, 0.0
    ).astype(bf16)
    d_vec_ref[0:1, :] = jnp.sum(d_raw_step, axis=0, keepdims=True)
    d_vec_ref[1:2, :] = -jnp.sum(step[...] * d_log, axis=0, keepdims=True)
    d_vec_ref[2:3, :] = jnp.sum(d_skip[...], axis=0, keepdims=True)
    d_proj_ref[:, widths[1] : widths[1] + states] = d_b[...].astype(bf16)
    d_proj_ref[:, widths[1] + states : widths[2]] = d_c[...].astype(bf16)

    def kv_wait(k, _):
        kv_copy(k).wait_recv()
        d_keyval[:length, :] += kv_in[k].astype(f32)
        return 0

    lax.fori_loop(1, count, kv_wait, 0)
    d_proj_ref[:, widths[0] : widths[1]] = d_keyval[:length, :].astype(bf16)

    def drain(k, _):
        kv_copy(k).wait_send()

        @pl.when(k <= place)
        def _():
            st_copy(k).wait_send()

        return 0

    lax.fori_loop(1, count, drain, 0)


def mixer_call(kernel, collective, outs, scratch, sems, widths, heads, operands):
    count = lax.axis_size(CTX)
    whole = pl.BlockSpec(memory_space=pltpu.VMEM)
    return pl.pallas_call(
        functools.partial(kernel, count, widths, heads),
        out_shape=outs,
        in_specs=[whole] * len(operands),
        out_specs=[whole] * len(outs),
        scratch_shapes=[pltpu.VMEM(*s) for s in scratch]
        + [pltpu.SemaphoreType.DMA((count,))] * sems,
        compiler_params=pltpu.CompilerParams(
            collective_id=collective, has_side_effects=True, vmem_limit_bytes=56 << 20
        ),
        cost_estimate=pl.CostEstimate(flops=0, bytes_accessed=20 << 20, transcendentals=0),
        name="mixer"+str(collective),
    )(*operands)


def mix_forward(weights, proj, layout):
    count = lax.axis_size(CTX)
    widths, heads = weights.widths, weights.heads
    length, inner = proj.shape[0], (proj.shape[1] - widths[3]) // 2
    states = (widths[2] - widths[1]) // 2
    kv = widths[1] - widths[0]
    shape = jax.ShapeDtypeStruct
    head_rows = -(-heads // 8) * 8
    outs = [
        shape((length, widths[0] + inner), bf16),
        shape((length, inner), f32),
        shape((inner, states), bf16),
        shape((count * length, kv), bf16),
        shape((count, head_rows, states), f32),
    ]
    per_head = ((length, 128), f32)
    scratch = [
        per_head,
        ((128, length), f32),
        per_head,
        per_head,
        per_head,
        ((length, count * length), f32),
        ((length, length), f32),
        ((count, length, kv), bf16),
        ((count, inner, states), bf16),
        ((count, head_rows, states), f32),
        ((inner, states), f32),
    ]
    operands = (proj, weights.head_rows, weights.skip_row, *layout)
    return mixer_call(mix_forward_kernel, 5, outs, scratch, 6, widths, heads, operands)


def mix_backward(weights, saved, d_both, layout):
    count = lax.axis_size(CTX)
    widths, heads = weights.widths, weights.heads
    proj = saved.proj
    length, inner = proj.shape[0], (proj.shape[1] - widths[3]) // 2
    states = (widths[2] - widths[1]) // 2
    kv = widths[1] - widths[0]
    shape = jax.ShapeDtypeStruct
    outs = [shape(proj.shape, bf16), shape((8, 128), f32)]
    per_head = ((length, 128), f32)
    square = ((length, length), f32)
    scratch = [
        per_head,
        ((128, length), f32),
        per_head,
        per_head,
        per_head,
        ((length, count * length), f32),
        square,
        square,
        ((length, inner), bf16),
        ((length, inner), bf16),
        ((length, inner), f32),
        ((count * length, kv), f32),
        ((length, states), f32),
        ((length, states), f32),
        per_head,
        per_head,
        per_head,
        per_head,
        ((count, inner, states), bf16),
        ((inner, states), f32),
        ((count, length, kv), bf16),
        ((count, length, kv), bf16),
    ]
    operands = (
        proj,
        weights.head_rows,
        weights.skip_row,
        *layout,
        saved.mixed,
        saved.state_in,
        saved.keyval_all,
        saved.decays,
        d_both,
    )
    return mixer_call(mix_backward_kernel, 6, outs, scratch, 4, widths, heads, operands)


def norm_apply(values, gain):
    return values * lax.rsqrt(jnp.mean(values * values, axis=-1, keepdims=True) + eps) * gain


def matmul(left, right):
    return jnp.dot(left, right, preferred_element_type=f32)


def matmul_nt(left, right):
    return lax.dot_general(left, right, (((1,), (1,)), ((), ())), preferred_element_type=f32)


def matmul_tn(left, right):
    return lax.dot_general(left, right, (((0,), (0,)), ((), ())), preferred_element_type=f32)


def swap(values):
    return lax.ppermute(values, SECTION, [(0, 1), (1, 0)])


def block_layout(doc_lengths, length):
    count, place = lax.axis_size(CTX), lax.axis_index(CTX)
    start = place * length
    bounds = jnp.cumsum(doc_lengths)[:-1]

    def segment_of(positions):
        return jnp.sum((positions[:, None] >= bounds[None, :]).astype(jnp.int32), axis=1)

    order = lax.rem(place + count - jnp.arange(count, dtype=jnp.int32), count)
    inside = jnp.arange(length, dtype=jnp.int32)
    keys = (order[:, None] * length + inside[None, :]).reshape(-1)
    positions = start + inside
    segments = segment_of(positions)
    before = jnp.where(place > 0, segment_of(start[None] - 1)[0], -1)
    goes_on = jnp.broadcast_to(segments[-1] == before, segments.shape)
    columns = [segments, segments == before, segments == segments[-1], positions, goes_on]
    tokens = jnp.stack([c.astype(f32) for c in columns], axis=1)
    return jnp.pad(tokens, ((0, 0), (0, 3))), jnp.stack(
        [segment_of(keys).astype(f32), keys.astype(f32)]
    )


def layer_forward(weights, normed, layout):
    proj = matmul(normed, weights.proj)
    both, mixed, state_in, keyval_all, decays = mix_forward(weights, proj, layout)
    saved = types.SimpleNamespace(
        normed=normed,
        proj=proj,
        both=both,
        mixed=mixed,
        state_in=state_in,
        keyval_all=keyval_all,
        decays=decays,
    )
    return matmul(both, weights.out), saved


def ffn_forward(weights, ffn_in):
    gate_up = matmul(ffn_in, weights.gate_up)
    width = gate_up.shape[1] // 2
    gate_pre, upward = gate_up[:, :width], gate_up[:, width:]
    product = (jax.nn.silu(gate_pre) * upward).astype(bf16)
    return matmul(product, weights.down), gate_pre, upward, product


def ctx_bits():
    return [1 << i for i in reversed(range((lax.axis_size(CTX) - 1).bit_length()))]


def flip(values, bit):
    return lax.ppermute(values, CTX, [(i, i ^ bit) for i in range(lax.axis_size(CTX))])


def own_half(values):
    half = values.shape[1] // 2
    section = lax.axis_index(SECTION)
    return (
        lax.dynamic_slice_in_dim(values, section * half, half, 1),
        lax.dynamic_slice_in_dim(values, (1 - section) * half, half, 1),
    )


def both_batches(kept, sent):
    return jnp.concatenate([kept, swap(sent)], axis=0)


def ctx_orders():
    bits = ctx_bits()
    return bits, bits[::-1]


def relative_order(bits):
    order = [0]
    for bit in reversed(bits):
        order = order + [k ^ bit for k in order]
    return order


def weight_sums(columns, *rows):
    kept, sent = zip(*(own_half(r) for r in rows))
    halves = both_batches(jnp.concatenate(kept, axis=1), jnp.concatenate(sent, axis=1))
    return matmul_tn(both_batches(columns, columns), halves).astype(bf16)


def shared_sums(normed, d_shared):
    place, count = lax.axis_index(CTX), lax.axis_size(CTX)
    shards = lax.axis_size(SHARD)
    block = normed.shape[1] // (count * shards)
    columns = jnp.concatenate(
        [
            lax.dynamic_slice_in_dim(
                normed, ((place ^ k) * shards + lax.axis_index(SHARD)) * block, block, 1
            )
            for k in range(count)
        ],
        axis=1,
    )
    total = weight_sums(columns, d_shared)
    rows = total[:block].astype(f32)
    for k in range(1, count):
        rows = rows + flip(total[k * block : (k + 1) * block], k).astype(f32)
    return rows.astype(bf16)


def blocks_of(total):
    place, count = lax.axis_index(CTX), lax.axis_size(CTX)
    block = total.shape[0] // count
    return jnp.stack(
        [lax.dynamic_slice_in_dim(total, (place ^ k) * block, block, 0) for k in range(count)]
    )


def streams_of(total):
    place, count = lax.axis_index(CTX), lax.axis_size(CTX)
    block, half = total.shape[0] // count, total.shape[1] // 2
    streams = []
    for stream, bits in enumerate(ctx_orders()):
        parts = [
            lax.dynamic_slice(total, ((place ^ k) * block, stream * half), (block, half))
            for k in relative_order(bits)
        ]
        streams += [jnp.stack(parts[: count // 2]), jnp.stack(parts[count // 2 :])]
    return streams


def weight_scatter(streams):
    totals = []
    for i, bits in enumerate(ctx_orders()):
        kept, sent = (a.reshape(-1, a.shape[-1]) for a in streams[2 * i : 2 * i + 2])
        totals.append(scatter_relative(kept, sent, bits))
    return totals


def scatter_relative(kept, sent, bits):
    for i, bit in enumerate(bits):
        got = flip(sent, bit)
        if i + 1 < len(bits):
            rows = kept.shape[0] // 2
            sent = (kept[rows:].astype(f32) + got[rows:].astype(f32)).astype(bf16)
            kept = (kept[:rows].astype(f32) + got[:rows].astype(f32)).astype(bf16)
        else:
            kept = (kept.astype(f32) + got.astype(f32)).astype(bf16)
    return kept


def after(first, *later):
    first, later = lax.optimization_barrier((first, later))
    return first, later


def layer_backward(weights, saved, d_out, d_low, values_in, layout, last, before):
    grads = types.SimpleNamespace()
    d_product = matmul_nt(d_low, weights.down)
    gate_pre, upward = saved.gate_pre, saved.upward
    gate_sig = jax.nn.sigmoid(gate_pre)
    d_gate = d_product * upward * gate_sig * (1.0 + gate_pre * (1.0 - gate_sig))
    d_upward = d_product * gate_pre * gate_sig
    d_gate_up = jnp.concatenate([d_gate, d_upward], axis=1).astype(bf16)
    d_ffn_in = matmul_nt(d_gate_up, weights.gate_up)
    width = d_product.shape[1]
    up, down = width // 2, width // 4
    plan = tuple(
        (x, stream, ((x, stream * part, 2 * part + stream * part, part),))
        for stream in range(2)
        for x, part in ((0, up), (1, down))
    )
    d_middle, d_mixed, grads.gain_ffn, *sums = back_sum(
        10 if last else 3,
        d_ffn_in,
        d_out,
        saved.middle,
        weights.gain_ffn,
        plan,
        (saved.ffn_in, d_low),
        (d_gate_up, saved.product),
        (),
        before.sums_mix if last else (),
    )
    if last:
        sums, before.mix = sums[:4], sums[4:]
        grads.ffn = weight_scatter(sums)
    else:
        sums_ffn = sums
    d_both = matmul_nt(d_mixed, weights.out)
    if not last:
        (d_both,), (before.tail,) = after((d_both,), before.tail)
    if last:
        sums_out = weight_sums(d_mixed, saved.both)
        (sums_out,), (d_both,) = after((streams_of(sums_out),), d_both)
        grads.out = weight_scatter(sums_out)
    d_proj, d_vec = mix_backward(weights, saved, d_both, layout)
    if last:
        (grads.out,), (d_proj,) = after((grads.out,), d_proj)
    heads, widths = weights.heads, weights.widths
    grads.step_bias, grads.decay, grads.skip = (d_vec[i, :heads] for i in range(3))
    d_normed = matmul_nt(d_proj, weights.proj)
    placed = [
        jnp.where(weights.kv_owner == owner, d_proj[:, start : start + HD], 0)
        for start in (widths[0], widths[0] + HD)
        for owner in range(KVH)
    ]
    d_shared = jnp.concatenate([d_proj[:, widths[1] : widths[2]], *placed], axis=1)
    normed = saved.normed
    if last:
        d_step, d_zx = d_proj[:, widths[2] : widths[3]], d_proj[:, widths[3] :]
        sums_proj = weight_sums(
            normed, d_proj[:, : widths[0]], d_zx, jnp.concatenate([d_step, d_step], axis=1)
        )
        blocks = blocks_of(sums_proj)
        (blocks,), (d_normed,) = after((blocks,), d_normed)
        d_hidden, d_hidden_low, grads.gain_in, d_shared, grads.proj = back_sum_scatter(
            7, d_normed, d_shared, d_middle, values_in, weights.gain_in, blocks
        )
    else:
        query, inner = widths[0] // 2, (d_proj.shape[1] - widths[3]) // 2
        step, zx = widths[3] - widths[2], widths[3]
        both, most = saved.both.shape[1] // 4, inner // 2
        plan = (
            (0, 0, ((0, 0, query, query), (0, zx, zx + inner, most))),
            (1, 0, ((1, 0, 2 * both, both),)),
            (0, 1, ((0, zx + most, zx + inner + most, most), (0, widths[2], widths[2], step))),
            (1, 1, ((1, both, 3 * both, both),)),
        )
        d_hidden, d_hidden_low, grads.gain_in, d_shared, *sums = back_sum(
            4,
            d_normed,
            d_middle,
            values_in,
            weights.gain_in,
            plan,
            (normed, d_mixed),
            (d_proj, saved.both),
            (d_shared,),
            sums_ffn,
        )
        sums, grads.ffn = sums[:4], sums[4:]
        grads.sums_mix = sums
    grads.shared = shared_sums(normed, d_shared)
    return d_hidden, d_hidden_low, grads


def body(
    inputs,
    cotangent,
    doc_lengths,
    norm_in,
    w_query,
    w_keyval,
    w_attn_out,
    w_mixer_in,
    w_state_io,
    w_step,
    step_bias,
    decay_rate,
    skip_gain,
    w_mixer_out,
    norm_ffn,
    w_gate_up,
    w_down,
):
    section = lax.axis_index(SECTION)
    leading = section == 0
    shard = lax.axis_index(SHARD)
    width = w_query.shape[1]
    query_width = w_query.shape[2]
    head_count = w_step.shape[2]
    kv_owner = shard * (query_width // HD) // (QH // KVH)
    rows_in = lax.dynamic_index_in_dim(inputs, section, 0, False)
    own_keyval = lax.dynamic_slice_in_dim(w_keyval[0], kv_owner * HD, HD, 2).reshape(width, 2 * HD)
    io_end = query_width + 2 * HD + w_state_io.shape[2]
    widths = (query_width, query_width + 2 * HD, io_end, io_end - (-head_count // 128) * 128)
    proj = jnp.concatenate(
        [
            w_query[0],
            own_keyval,
            w_state_io[0],
            jnp.pad(w_step[0], ((0, 0), (0, -head_count % 128))),
            w_mixer_in[0].reshape(width, -1),
        ],
        axis=1,
    )
    vectors = jnp.concatenate([norm_in[0], norm_ffn[0], step_bias[0], decay_rate[0], skip_gain[0]])
    (proj, vectors), (rows_in,) = after((proj, vectors), rows_in)
    block_in = line_gather(rows_in)
    (block_in,), (w_gate_up, w_attn_out) = after((block_in,), w_gate_up, w_attn_out)
    own = (
        proj,
        jnp.concatenate([w_attn_out[0], w_mixer_out[0]], axis=0),
        w_gate_up[0].reshape(width, -1),
        w_down[0],
        vectors,
    )
    other = tuple(swap(array) for array in own)

    def layer_weights(layer):
        weights = types.SimpleNamespace()
        chosen = [jnp.where(section == layer, a, b) for a, b in zip(own, other)]
        weights.proj, weights.out, weights.gate_up, weights.down, vectors = chosen
        heads = vectors[2 * width :]
        weights.gain_in = vectors[:width]
        weights.gain_ffn = vectors[width : 2 * width]
        skip = heads[2 * head_count :]
        rows = heads[: 2 * head_count].reshape(2, head_count)
        weights.head_rows = jnp.pad(rows, ((0, 6), (0, -head_count % 128)))
        weights.skip_row = jnp.repeat(skip, HP)[None]
        weights.heads = head_count
        weights.widths = widths
        weights.kv_owner = kv_owner
        return weights

    layers = [layer_weights(0), layer_weights(1)]
    rows_cot = lax.dynamic_index_in_dim(cotangent, section, 0, False)
    length = block_in.shape[0]
    part = rows_in.shape[0]
    layout = block_layout(lax.dynamic_index_in_dim(doc_lengths, section, 0, False), length)

    def own_rows(values):
        return lax.dynamic_slice_in_dim(values, shard * part, part, 0)

    hidden = block_in.astype(f32)
    normed = norm_apply(hidden, layers[0].gain_in).astype(bf16)
    hiddens, outs, saves = [], [], []
    for layer in range(2):
        weights = layers[layer]
        hiddens.append(hidden)
        if layer == 1:
            (normed,), (rows_cot,) = after((normed,), rows_cot)
            block_cot = lax.all_gather(rows_cot, SHARD, axis=0, tiled=True)
        partial, saved = layer_forward(weights, normed, layout)
        first, second = layers
        wanted = (2, 3) if layer == 0 else (0, 1)
        wanted = [(0, own[i], other[i]) for i in wanted]
        if layer == 0:
            wanted.append((1, own[0], other[0]))
        saved.middle, saved.ffn_in, chosen = copying_sum(
            middle_kernel, 1 + 8 * layer, f32, partial, hidden, weights.gain_ffn, wanted
        )
        if layer == 0:
            first.gate_up, first.down, second.proj = chosen
        else:
            first.proj, first.out = chosen
        partial, saved.gate_pre, saved.upward, saved.product = ffn_forward(
            weights, saved.ffn_in
        )
        saves.append(saved)
        if layer == 0:
            wanted = [(1, own[i], other[i]) for i in (1, 2, 3)]
            out_low, normed, chosen = copying_sum(
                layer_end_kernel, 2, bf16, partial, saved.middle, second.gain_in, wanted
            )
            second.out, second.gate_up, second.down = chosen
            outs.append(own_rows(out_low))
            hidden = out_low.astype(f32)
        else:
            held = types.SimpleNamespace(tail=partial.astype(bf16))

    d_out = d_low = block_cot
    d_hiddens, grads = [None, None], [None, None]
    for layer in (1, 0):
        d_hidden, d_low, grads[layer] = layer_backward(
            layers[layer], saves[layer], d_out, d_low, hiddens[layer], layout, layer == 0, grads[1] if layer == 0 else held
        )
        d_hiddens[layer] = d_hidden
        d_out = d_low

    def by_layer(first, second):
        kept = jnp.where(leading, first, second)
        came = swap(jnp.where(leading, second, first))
        return jnp.where(leading, kept, came), jnp.where(leading, came, kept)

    total = lax.psum_scatter(held.tail, SHARD, scatter_dimension=0, tiled=True)
    outs.append((own_rows(saves[1].middle) + total.astype(f32)).astype(bf16))
    section_out = jnp.stack(by_layer(*outs))[None]
    input_grad = jnp.stack(by_layer(own_rows(d_hiddens[0]), own_rows(d_hiddens[1])))[None]

    def columns_of(first, second):
        return jnp.concatenate(by_layer(first, second), axis=1).astype(f32)

    def rows_of(first, second):
        return jnp.concatenate([first.T, second.T], axis=0).astype(f32)

    first, second = grads
    tiny = [
        jnp.concatenate([g.gain_in, g.gain_ffn, g.step_bias, g.decay, g.skip]) for g in grads
    ]
    tiny = sum(by_layer(*tiny))
    for bit in ctx_bits():
        tiny = tiny + flip(tiny, bit)
    place = lax.axis_index(CTX) * lax.axis_size(SHARD) + shard
    slot = width // (lax.axis_size(CTX) * lax.axis_size(SHARD))
    grad_in = lax.dynamic_slice_in_dim(tiny, place * slot, slot, 0)
    grad_ffn = lax.dynamic_slice_in_dim(tiny, width + place * slot, slot, 0)
    heads = tiny[2 * width :]

    inner = w_mixer_in.shape[3]
    query, most, both = query_width // 2, inner // 2, (query_width + inner) // 4
    left, right = second.mix
    parts = [
        (left[:, :query], left[:, query : query + most], left[:, query + most :]),
        (right[:, :most], right[:, most : most + head_count], right[:, right.shape[1] - both :]),
    ]
    proj = jnp.concatenate([*parts[0][:2], *parts[1][:2]], axis=1)
    proj_low, proj_high = by_layer(first.proj[:, : proj.shape[1]], proj)
    out_low, out_high = by_layer(
        jnp.concatenate(first.out, axis=1), jnp.concatenate([p[2] for p in parts], axis=1)
    )
    ffn_low, ffn_high = by_layer(
        jnp.concatenate(first.ffn, axis=1), jnp.concatenate(second.ffn, axis=1)
    )
    step_at = query + inner
    shared = columns_of(first.shared, second.shared)
    io_width = w_state_io.shape[2]
    out = rows_of(out_low, out_high)
    ff = w_gate_up.shape[3] // 2

    def ffn_parts(total):
        edge = total.shape[1] // 2
        up = jnp.concatenate([total[:, :ff], total[:, edge : edge + ff]], axis=1)
        return up, jnp.concatenate([total[:, ff:edge], total[:, edge + ff :]], axis=1)

    (up_low, down_low), (up_high, down_high) = ffn_parts(ffn_low), ffn_parts(ffn_high)
    gate_up = jnp.stack([up_low, up_high], axis=1)
    return (
        section_out,
        input_grad,
        grad_in[None],
        jnp.concatenate([proj_low[:, :query], proj_high[:, :query]], axis=1).astype(f32)[None],
        shared[:, io_width:].reshape(-1, 2, KVH * HD)[None],
        out[:query_width][None],
        jnp.stack([p[:, query:step_at] for p in (proj_low, proj_high)], axis=1).astype(f32)[None],
        shared[:, :io_width][None],
        proj_low[:, step_at : step_at + head_count].astype(f32)[None],
        heads[:head_count][None],
        heads[head_count : 2 * head_count][None],
        heads[2 * head_count :][None],
        out[query_width:][None],
        grad_ffn[None],
        gate_up.astype(f32)[None],
        rows_of(down_low, down_high)[None],
    )


def solution(mesh):
    return jax.shard_map(
        body,
        mesh=mesh,
        in_specs=(
            P(None, (CTX, SHARD), None),
            P(None, (CTX, SHARD), None),
            P(),
            P(SECTION, None),
            P(SECTION, None, SHARD),
            P(SECTION, None, None, None),
            P(SECTION, SHARD, None),
            P(SECTION, None, None, SHARD),
            P(SECTION, None, None),
            P(SECTION, None, SHARD),
            P(SECTION, SHARD),
            P(SECTION, SHARD),
            P(SECTION, SHARD),
            P(SECTION, SHARD, None),
            P(SECTION, None),
            P(SECTION, None, None, SHARD),
            P(SECTION, SHARD, None),
        ),
        out_specs=(
            P(SECTION, None, (CTX, SHARD), None),
            P(SECTION, None, (CTX, SHARD), None),
            P(SECTION, (CTX, SHARD)),
            P(SECTION, CTX, SHARD),
            P(SECTION, (CTX, SHARD), None, None),
            P(SECTION, SHARD, CTX),
            P(SECTION, CTX, None, SHARD),
            P(SECTION, (CTX, SHARD), None),
            P(SECTION, CTX, SHARD),
            P(SECTION, SHARD),
            P(SECTION, SHARD),
            P(SECTION, SHARD),
            P(SECTION, SHARD, CTX),
            P(SECTION, (CTX, SHARD)),
            P(SECTION, CTX, None, SHARD),
            P(SECTION, SHARD, CTX),
        ),
        check_vma=False,
    )
```

```python
import functools
import types

import jax
import jax.numpy as jnp
from jax import lax
from jax.experimental import pallas as pl
from jax.experimental.pallas import tpu as pltpu
from jax.sharding import PartitionSpec as P

SECTION, CTX, SHARD = "section", "ctx", "shard"
QH = 8
KVH = 2
HD = 128
HP = 64
CHUNKS = 16
LAG = 3

MESH = pl.DeviceIdType.MESH
eps = 1e-05
bf16 = jnp.bfloat16
f32 = jnp.float32


def line_sum(n, chunks, lag, p_rows, done, sr, sl, rr, rl, srs, sls, rrs, rls, tot, fill=None):
    z = lax.axis_index(SHARD)
    hasr, hasl = z < n - 1, z > 0
    bar = pltpu.get_barrier_semaphore()
    more = 0
    if fill is not None:
        more = fill.greet(bar)

    @pl.when(hasr)
    def _():
        pl.semaphore_signal(bar, inc=1, device_id={SHARD: z + 1}, device_id_type=MESH)

    @pl.when(hasl)
    def _():
        pl.semaphore_signal(bar, inc=1, device_id={SHARD: z - 1}, device_id_type=MESH)

    @pl.when(hasl & hasr)
    def _():
        pl.semaphore_wait(bar, 2 + more)

    @pl.when(jnp.logical_not(hasl & hasr))
    def _():
        pl.semaphore_wait(bar, 1 + more)

    def right(j):
        return pltpu.make_async_remote_copy(
            sr.at[j], rr.at[j], srs.at[j], rrs.at[j], device_id={SHARD: z + 1}, device_id_type=MESH
        )

    def left(j):
        return pltpu.make_async_remote_copy(
            sl.at[j], rl.at[j], sls.at[j], rls.at[j], device_id={SHARD: z - 1}, device_id_type=MESH
        )

    steps = chunks + lag * (n - 1)
    if fill is not None:
        fill.start()

    def one(i, _):
        def go(j, copy, came, goes, inbox, outbox):
            live = (j >= 0) & (j < chunks)

            @pl.when(live & came & goes)
            def _():
                copy(j).wait_recv()
                outbox[j] = (p_rows(j) + inbox[j].astype(f32)).astype(bf16)
                copy(j).start()

            @pl.when(live & jnp.logical_not(came))
            def _():
                outbox[j] = p_rows(j).astype(bf16)
                copy(j).start()

            @pl.when(live & jnp.logical_not(goes))
            def _():
                copy(j).wait_recv()

        go(i - lag * z, right, hasl, hasr, rr, sr)
        go(i - lag * (n - 1 - z), left, hasr, hasl, rl, sl)
        jd = i - lag * jnp.maximum(z, n - 1 - z)

        @pl.when((jd >= 0) & (jd < chunks))
        def _():
            tot[...] = p_rows(jd)

            @pl.when(hasl)
            def _():
                tot[...] += rr[jd].astype(f32)

            @pl.when(hasr)
            def _():
                tot[...] += rl[jd].astype(f32)

            done(jd, tot[...])

        if fill is not None:
            fill.step(i, steps)
        return 0

    lax.fori_loop(0, steps, one, 0)
    if fill is not None:
        fill.finish()

    def drain(j, _):
        @pl.when(hasr)
        def _():
            right(j).wait_send()

        @pl.when(hasl)
        def _():
            left(j).wait_send()

        return 0

    lax.fori_loop(0, chunks, drain, 0)


def row_slice(j, rows):
    return pl.ds(pl.multiple_of(j * rows, rows), rows)


def middle_kernel(n, chunks, lag, p_ref, h_ref, gain_ref, mid_ref, low_ref, *scratch, fill=None):
    rows = p_ref.shape[0] // chunks

    def p_rows(j):
        return p_ref[row_slice(j, rows), :]

    def done(j, total):
        v = h_ref[row_slice(j, rows), :] + total
        r = lax.rsqrt(jnp.mean(v * v, axis=-1, keepdims=True) + eps)
        mid_ref[row_slice(j, rows), :] = v
        low_ref[row_slice(j, rows), :] = (v * r * gain_ref[...]).astype(bf16)

    line_sum(n, chunks, lag, p_rows, done, *scratch, fill=fill)


class Copies:
    parts = 16

    def __init__(self, layers, own, other, out, boxes, came, went):
        self.layers, self.own, self.other, self.out = layers, own, other, out
        self.boxes, self.came, self.went = boxes, came, went

    def greet(self, bar):
        return 0

    def start(self):
        pass

    def rows(self, a, j):
        size = self.boxes[a].shape[1]
        return pl.ds(pl.multiple_of(j * size, size), size)

    def fetch(self, a, j, act):
        section, slot = lax.axis_index(SECTION), lax.rem(j, 2)
        for mine, source in ((True, self.own[a]), (False, self.other[a])):

            @pl.when((section == self.layers[a]) == mine)
            def _():
                part = source.at[self.rows(a, j), :]
                act(
                    pltpu.make_async_copy(
                        part, self.boxes[a].at[slot], self.came.at[2 * a + slot]
                    )
                )

    def store(self, a, j):
        slot = lax.rem(j, 2)
        part = self.out[a].at[self.rows(a, j), :]
        return pltpu.make_async_copy(self.boxes[a].at[slot], part, self.went.at[2 * a + slot])

    def step(self, i, steps):
        @pl.when((i >= 1) & (i <= self.parts))
        def _():
            for a in range(len(self.layers)):
                self.fetch(a, i - 1, lambda copy: copy.wait())
                self.store(a, i - 1).start()

        @pl.when((i >= 2) & (i < self.parts))
        def _():
            for a in range(len(self.layers)):
                self.store(a, i - 2).wait()

        @pl.when(i < self.parts)
        def _():
            for a in range(len(self.layers)):
                self.fetch(a, i, lambda copy: copy.start())

    def finish(self):
        for a in range(len(self.layers)):
            for j in (self.parts - 2, self.parts - 1):
                self.store(a, j).wait()


def copying(kernel, layers, n, chunks, lag, p_ref, h_ref, gain_ref, *refs):
    count = len(layers)
    own, other, refs = refs[:count], refs[count : 2 * count], refs[2 * count :]
    first_ref, low_ref, refs = refs[0], refs[1], refs[2:]
    out, refs = refs[:count], refs[count:]
    copies = Copies(layers, own, other, out, refs[9 : 9 + count], *refs[9 + count :])
    kernel(n, chunks, lag, p_ref, h_ref, gain_ref, first_ref, low_ref, *refs[:9], fill=copies)


def layer_end_kernel(n, chunks, lag, p_ref, h_ref, gain_ref, out_ref, low_ref, *scratch, fill=None):
    rows = p_ref.shape[0] // chunks

    def p_rows(j):
        return p_ref[row_slice(j, rows), :]

    def done(j, total):
        out = (h_ref[row_slice(j, rows), :] + total).astype(bf16)
        out_ref[row_slice(j, rows), :] = out
        v = out.astype(f32)
        r = lax.rsqrt(jnp.mean(v * v, axis=-1, keepdims=True) + eps)
        low_ref[row_slice(j, rows), :] = (v * r * gain_ref[...]).astype(bf16)

    line_sum(n, chunks, lag, p_rows, done, *scratch, fill=fill)


def flipped(place, k, count):
    total, bit = 0, 1
    while bit < count:
        total = total + (place // bit + k // bit) % 2 * bit
        bit *= 2
    return total


def mirrored(k, count):
    total, bit = 0, 1
    while bit < count:
        total = total + k // bit % 2 * (count // (2 * bit))
        bit *= 2
    return total


class Fill:
    first = 6

    def __init__(self, plan, xs, ys, outs, scratch):
        self.plan, self.xs, self.ys, self.outs = plan, xs, ys, outs
        count = len(plan)
        self.other_x, rest = scratch[: len(xs)], scratch[len(xs) :]
        self.own_y, self.other_y = rest[:count], rest[count : 2 * count]
        self.send, self.recv = rest[2 * count :]

    def greet(self, bar):
        other = 1 - lax.axis_index(SECTION)
        pl.semaphore_signal(bar, inc=1, device_id={SECTION: other}, device_id_type=MESH)
        return 1

    def copies(self):
        section = lax.axis_index(SECTION)
        copies = []

        def add(source, target):
            i = len(copies)
            copies.append(
                pltpu.make_async_remote_copy(
                    source,
                    target,
                    self.send.at[i],
                    self.recv.at[i],
                    device_id={SECTION: 1 - section},
                    device_id_type=MESH,
                )
            )

        for x, target in zip(self.xs, self.other_x):
            add(x, target)
        for (_, _, parts), target in zip(self.plan, self.other_y):
            at = 0
            for y, low, high, width in parts:
                start = pl.multiple_of(low + (high - low) * (1 - section), 128)
                add(self.ys[y].at[:, pl.ds(start, width)], target.at[:, at : at + width])
                at += width
        return copies

    def start(self):
        for copy in self.copies():
            copy.start()
        section = lax.axis_index(SECTION)
        for (_, _, parts), own in zip(self.plan, self.own_y):
            at = 0
            for y, low, high, width in parts:
                start = pl.multiple_of(low + (high - low) * section, 128)
                own[:, at : at + width] = self.ys[y][:, pl.ds(start, width)]
                at += width

    def step(self, i, steps):
        place, count = lax.axis_index(CTX), lax.axis_size(CTX)

        @pl.when(i == self.first)
        def _():
            for copy in self.copies():
                copy.wait_recv()

        each = -(-count * len(self.plan) // (steps - self.first))
        begin = (i - self.first) * each

        def piece(t, _):
            at = [0, 0]
            for f, (x, stream, _) in enumerate(self.plan):
                k = t - f * count
                width = self.own_y[f].shape[1]
                where = slice(at[stream], at[stream] + width)
                at[stream] += width
                kept, sent = self.outs[2 * stream : 2 * stream + 2]

                @pl.when((k >= 0) & (k < count))
                def _():
                    block = kept.shape[1]
                    source = flipped(place, mirrored(k, count) if stream else k, count)
                    cols = pl.ds(pl.multiple_of(source * block, block), block)
                    dims = (((0,), (0,)), ((), ()))
                    total = lax.dot_general(
                        self.xs[x][:, cols], self.own_y[f][...], dims, preferred_element_type=f32
                    ) + lax.dot_general(
                        self.other_x[x][:, cols],
                        self.other_y[f][...],
                        dims,
                        preferred_element_type=f32,
                    )
                    low = total.astype(bf16)

                    @pl.when(k < count // 2)
                    def _():
                        kept[k, :, where] = low

                    @pl.when(k >= count // 2)
                    def _():
                        sent[k - count // 2, :, where] = low

            return 0

        @pl.when(i >= self.first)
        def _():
            lax.fori_loop(begin, begin + each, piece, 0)

    def finish(self):
        for copy in self.copies():
            copy.wait_send()


class Scatter:
    def __init__(self, blocks, out, inbox, send, recv):
        self.blocks, self.out, self.inbox, self.send, self.recv = blocks, out, inbox, send, recv
        self.count, self.place = lax.axis_size(CTX), lax.axis_index(CTX)

    def peer(self, k):
        return flipped(self.place, k, self.count)

    def copy(self, k):
        return pltpu.make_async_remote_copy(
            self.blocks.at[k],
            self.inbox.at[k],
            self.send.at[k],
            self.recv.at[k],
            device_id={CTX: self.peer(k)},
            device_id_type=MESH,
        )

    def greet(self, bar):
        for k in range(1, self.count):
            pl.semaphore_signal(bar, inc=1, device_id={CTX: self.peer(k)}, device_id_type=MESH)
        return self.count - 1

    def start(self):
        for k in reversed(range(1, self.count)):
            self.copy(k).start()

    def step(self, i, steps):
        pass

    def finish(self):
        rows = 64

        for k in range(1, self.count):
            self.copy(k).wait_recv()

        def add(j, _):
            part = row_slice(j, rows)
            total = self.blocks[0, part, :].astype(f32)
            for k in range(1, self.count):
                total += self.inbox[k, part, :].astype(f32)
            self.out[part, :] = total.astype(bf16)
            return 0

        lax.fori_loop(0, self.out.shape[0] // rows, add, 0)
        for k in range(1, self.count):
            self.copy(k).wait_send()


class Halving:
    cuts = 2
    turns = (11, 20)

    def __init__(self, streams, outs, scratch):
        self.place, self.count = lax.axis_index(CTX), lax.axis_size(CTX)
        self.streams, self.outs = streams, outs
        self.orders = ctx_orders()
        self.levels = len(self.orders[0])
        self.inbox = [scratch[k * self.levels : (k + 1) * self.levels] for k in range(2)]
        rest = scratch[2 * self.levels :]
        self.sums = [rest[k * (self.levels - 1) : (k + 1) * (self.levels - 1)] for k in range(2)]
        self.send, self.recv = rest[2 * (self.levels - 1) :]

    def greet(self, bar):
        for bit in self.orders[0]:
            peer = flipped(self.place, bit, self.count)
            pl.semaphore_signal(bar, inc=1, device_id={CTX: peer}, device_id_type=MESH)
        return self.levels

    def rows(self, cut):
        size = self.outs[0].shape[0] // self.cuts
        return pl.ds(cut * size, size)

    def copy(self, level, stream, cut):
        rows = self.rows(cut)
        if level == 0:
            source = self.streams[2 * stream + 1].at[:, rows, :]
        else:
            blocks = self.count >> (level + 1)
            source = self.sums[stream][level - 1].at[pl.ds(blocks, blocks), rows, :]
        i = (level * 2 + stream) * self.cuts + cut
        return pltpu.make_async_remote_copy(
            source,
            self.inbox[stream][level].at[:, rows, :],
            self.send.at[i],
            self.recv.at[i],
            device_id={CTX: flipped(self.place, self.orders[stream][level], self.count)},
            device_id_type=MESH,
        )

    def advance(self, level, cut):
        rows, blocks = self.rows(cut), self.count >> (level + 1)
        for stream in range(2):
            self.copy(level, stream, cut).wait_recv()
            kept = self.streams[2 * stream] if level == 0 else self.sums[stream][level - 1]
            for k in range(blocks):
                total = kept[k, rows, :].astype(f32) + self.inbox[stream][level][k, rows, :].astype(
                    f32
                )
                if level + 1 < self.levels:
                    self.sums[stream][level][k, rows, :] = total.astype(bf16)
                else:
                    self.outs[stream][rows, :] = total.astype(bf16)
            if level + 1 < self.levels:
                self.copy(level + 1, stream, cut).start()

    def start(self):
        for cut in range(self.cuts):
            for stream in range(2):
                self.copy(0, stream, cut).start()

    def step(self, i, steps):
        for cut, turn in enumerate(self.turns):

            @pl.when(i == turn)
            def _():
                self.advance(0, cut)

    def finish(self):
        for level in range(1, self.levels):
            for cut in range(self.cuts):
                self.advance(level, cut)
        for level in range(self.levels):
            for stream in range(2):
                for cut in range(self.cuts):
                    self.copy(level, stream, cut).wait_send()


def halving_scratch(streams):
    blocks, rows, width = streams[0].shape
    levels = len(ctx_bits())
    inbox = [pltpu.VMEM((blocks >> k, rows, width), bf16) for k in range(levels)]
    copies = levels * 2 * Halving.cuts
    return [*inbox * 2, *inbox[: levels - 1] * 2, *[pltpu.SemaphoreType.DMA((copies,))] * 2]


class Together:
    def __init__(self, *jobs):
        self.jobs = jobs

    def greet(self, bar):
        return sum(job.greet(bar) for job in self.jobs)

    def start(self):
        for job in self.jobs:
            job.start()

    def step(self, i, steps):
        for job in self.jobs:
            job.step(i, steps)

    def finish(self):
        for job in self.jobs:
            job.finish()


def scatter_kernel(n, chunks, lag, p_ref, q_ref, d_ref, v_ref, gain_ref, blocks, *refs):
    outs, out, scratch = refs[:4], refs[4], refs[5:]
    job = Scatter(blocks, out, *scratch[9:])
    back_rows(n, chunks, lag, p_ref, d_ref, v_ref, gain_ref, *outs[:3], scratch[:9], job, q_ref, outs[3])


def back_kernel(n, chunks, lag, plan, x_count, y_count, beside, ready, p_ref, *refs):
    q_ref = q_out = None
    if beside:
        q_ref, refs = refs[0], refs[1:]
    (d_ref, v_ref, gain_ref), refs = refs[:3], refs[3:]
    xs, refs = refs[:x_count], refs[x_count:]
    ys, refs = refs[:y_count], refs[y_count:]
    streams, refs = refs[:ready], refs[ready:]
    out_ref, low_ref, gg_ref = refs[:3]
    refs = refs[3:]
    if beside:
        q_out, refs = refs[0], refs[1:]
    sums, refs = refs[:4], refs[4:]
    totals, refs = refs[: ready // 2], refs[ready // 2 :]
    cut = len(xs) + 2 * len(plan) + 2
    fill = Fill(plan, xs, ys, sums, refs[9 : 9 + cut])
    if ready:
        fill = Together(fill, Halving(streams, totals, refs[9 + cut :]))
    outs = out_ref, low_ref, gg_ref
    back_rows(n, chunks, lag, p_ref, d_ref, v_ref, gain_ref, *outs, refs[:9], fill, q_ref, q_out)


def back_rows(
    n,
    chunks,
    lag,
    p_ref,
    d_ref,
    v_ref,
    gain_ref,
    out_ref,
    low_ref,
    gg_ref,
    scratch,
    fill,
    q_ref=None,
    q_out=None,
):
    rows, width = p_ref.shape[0] // chunks, p_ref.shape[1]
    gg_ref[...] = jnp.zeros_like(gg_ref)

    def p_rows(j):
        part = row_slice(j, rows)
        if q_ref is None:
            return p_ref[part, :]
        return jnp.concatenate([p_ref[part, :], q_ref[part, :].astype(f32)], axis=1)

    def done(j, total):
        if q_ref is not None:
            q_out[row_slice(j, rows), :] = total[:, width:].astype(bf16)
            total = total[:, :width]
        v = v_ref[row_slice(j, rows), :].astype(f32)
        r = lax.rsqrt(jnp.mean(v * v, axis=-1, keepdims=True) + eps)
        vr = v * r
        dg = total * gain_ref[...]
        inner = jnp.mean(dg * vr, axis=-1, keepdims=True)
        gg_ref[...] += jnp.sum((total * vr).reshape(rows // 8, 8, vr.shape[1]), axis=0)
        out = d_ref[row_slice(j, rows), :].astype(f32) + r * (dg - vr * inner)
        out_ref[row_slice(j, rows), :] = out
        low_ref[row_slice(j, rows), :] = out.astype(bf16)

    line_sum(n, chunks, lag, p_rows, done, *scratch, fill=fill)


def summed(kernel, collective, outs, *operands, extra=(), more=0, far=(0, 0)):
    n = lax.axis_size(SHARD)
    length, width = operands[0].shape[0], operands[0].shape[1] + more
    box = pltpu.VMEM((CHUNKS, length // CHUNKS, width), bf16)
    distant = pl.BlockSpec(memory_space=pl.ANY)
    whole = pl.BlockSpec(memory_space=pltpu.VMEM)
    return pl.pallas_call(
        functools.partial(kernel, n, CHUNKS, LAG),
        out_shape=outs,
        in_specs=[whole] * (len(operands) - far[0]) + [distant] * far[0],
        out_specs=[whole] * (len(outs) - far[1]) + [distant] * far[1],
        scratch_shapes=[box] * 4
        + [pltpu.SemaphoreType.DMA((CHUNKS,))] * 4
        + [pltpu.VMEM((length // CHUNKS, width), f32), *extra],
        compiler_params=pltpu.CompilerParams(
            collective_id=collective, has_side_effects=True, vmem_limit_bytes=58 << 20
        ),
        cost_estimate=pl.CostEstimate(flops=0, bytes_accessed=20 << 20, transcendentals=0),
        name="line_sum"+str(collective),
    )(*operands)


def line_gather(rows):
    count, place = lax.axis_size(SHARD), lax.axis_index(SHARD)
    part = rows.shape[0]
    block = jnp.zeros((count * part, rows.shape[1]), rows.dtype)
    block = lax.dynamic_update_slice_in_dim(block, rows, place * part, 0)
    for k in reversed(range(1, count)):
        got = lax.ppermute(rows, SHARD, [(i, i ^ k) for i in range(count)])
        block = lax.dynamic_update_slice_in_dim(block, got, (place ^ k) * part, 0)
    return block


def shaped(array, dtype):
    return jax.ShapeDtypeStruct(array.shape, dtype)


def copying_sum(kernel, collective, dtype, p, hidden, gain, wanted):
    layers, own, other = zip(*wanted)
    outs = [shaped(p, dtype), shaped(p, bf16)] + [shaped(a, bf16) for a in own]
    boxes = [pltpu.VMEM((2, a.shape[0] // Copies.parts, a.shape[1]), bf16) for a in own]
    first, low, *chosen = summed(
        functools.partial(copying, kernel, layers),
        collective,
        outs,
        p,
        hidden,
        gain[None],
        *own,
        *other,
        extra=[*boxes, *[pltpu.SemaphoreType.DMA((2 * len(layers),))] * 2],
        far=(2 * len(layers), len(layers)),
    )
    return first, low, chosen


def back_sum(collective, p, d_out, values, gain, plan, xs, ys, beside=(), ready=()):
    count = lax.axis_size(CTX)
    length = p.shape[0]
    outs = [shaped(p, f32), shaped(p, bf16), jax.ShapeDtypeStruct((8, p.shape[1]), f32)]
    outs += [shaped(q, bf16) for q in beside]
    widths = [sum(part[3] for part in parts) for _, _, parts in plan]
    for stream in range(2):
        total = sum(w for (_, at, _), w in zip(plan, widths) if at == stream)
        shape = (count // 2, xs[0].shape[1] // count, total)
        outs += [jax.ShapeDtypeStruct(shape, bf16)] * 2
    extra = [pltpu.VMEM(x.shape, bf16) for x in xs]
    extra += [pltpu.VMEM((length, w), bf16) for w in widths] * 2
    copies = len(xs) + sum(len(parts) for _, _, parts in plan)
    extra += [pltpu.SemaphoreType.DMA((copies,))] * 2
    if ready:
        outs += [jax.ShapeDtypeStruct(a.shape[1:], bf16) for a in ready[::2]]
        extra += halving_scratch(ready)

    def bound(n, chunks, lag, *refs):
        back_kernel(n, chunks, lag, plan, len(xs), len(ys), bool(beside), len(ready), *refs)

    operands = (p, *beside, d_out, values, gain[None], *xs, *ys, *ready)
    more = sum(q.shape[1] for q in beside)
    out, low, gg, *sums = summed(bound, collective, outs, *operands, extra=extra, more=more)
    return out, low, jnp.sum(gg, axis=0), *sums


def back_sum_scatter(collective, p, beside, d_out, values, gain, blocks):
    outs = [shaped(p, f32), shaped(p, bf16), jax.ShapeDtypeStruct((8, p.shape[1]), f32)]
    outs += [shaped(beside, bf16), jax.ShapeDtypeStruct(blocks.shape[1:], bf16)]
    sems = [pltpu.SemaphoreType.DMA((blocks.shape[0],))] * 2
    extra = [pltpu.VMEM(blocks.shape, bf16), *sems]
    operands = (p, beside, d_out, values, gain[None], blocks)
    more = beside.shape[1]
    out, low, gg, whole, total = summed(
        scatter_kernel, collective, outs, *operands, extra=extra, more=more
    )
    return out, low, jnp.sum(gg, axis=0), whole, total


def dot(left, right, dims=((1,), (0,))):
    return lax.dot_general(left, right, (dims, ((), ())), preferred_element_type=f32)


NT = ((1,), (1,))
TN = ((0,), (0,))


def in_three(values):
    high = values.astype(bf16)
    rest = values - high.astype(f32)
    mid = rest.astype(bf16)
    return high, mid, (rest - mid.astype(f32)).astype(bf16)


def running_sum(values, reverse):
    length = values.shape[0]
    row = lax.broadcasted_iota(jnp.int32, (length, length), 0)
    col = lax.broadcasted_iota(jnp.int32, (length, length), 1)
    kept = jnp.where(row <= col if reverse else row >= col, 1.0, 0.0).astype(bf16)
    return sum(dot(kept, part) for part in in_three(values))


def lanes(shape):
    return lax.broadcasted_iota(jnp.int32, shape, 1)


def column(values, head):
    return jnp.sum(jnp.where(lanes(values.shape) == head, values, 0.0), axis=1, keepdims=True)


def in_pair(values, pair):
    low, high = column(values, 2 * pair), column(values, 2 * pair + 1)
    return jnp.where(lanes(values.shape) < HP, low, high)


def from_pair(values, pair):
    lane = lanes(values.shape)
    low = jnp.sum(jnp.where(lane < HP, values, 0.0), axis=1, keepdims=True)
    high = jnp.sum(jnp.where(lane < HP, 0.0, values), axis=1, keepdims=True)
    return jnp.where(lane == 2 * pair, low, 0.0) + jnp.where(lane == 2 * pair + 1, high, 0.0)


def pair_ds(pair, start=0):
    return pl.ds(pl.multiple_of(start + pair * 2 * HP, 2 * HP), 2 * HP)


def steps_of(step_raw, vec_ref, tok_ref, cum, cum_rows, step, enter, fade):
    shifted = step_raw + vec_ref[0:1, :]
    step[...] = jnp.maximum(shifted, 0.0) + jnp.log1p(jnp.exp(-jnp.abs(shifted)))
    cum[...] = running_sum(-step[...] * vec_ref[1:2, :], False)
    total = cum[...]
    cum_rows[...] = total.T
    enter[...] = jnp.exp(total) * tok_ref[:, 1:2]
    fade[...] = jnp.exp(total[-1:, :] - total) * tok_ref[:, 2:3]
    return shifted


def masks_of(tok_ref, key_ref):
    kept = (tok_ref[:, 3:4] >= key_ref[1:2, :]) & (tok_ref[:, 0:1] == key_ref[0:1, :])
    return jnp.where(kept, 0.0, -1e30)


def ctx_barrier(count, place):
    bar = pltpu.get_barrier_semaphore()

    def greet(k, _):
        pl.semaphore_signal(
            bar, inc=1, device_id={CTX: lax.rem(place + k, count)}, device_id_type=MESH
        )
        return 0

    lax.fori_loop(1, count, greet, 0)
    pl.semaphore_wait(bar, count - 1)


def ctx_copy(source, target, send, recv, peer):
    return pltpu.make_async_remote_copy(
        source, target, send, recv, device_id={CTX: peer}, device_id_type=MESH
    )


def mix_forward_kernel(
    count,
    widths,
    heads,
    proj_ref,
    vec_ref,
    skip_ref,
    tok_ref,
    key_ref,
    both_ref,
    mixed_ref,
    state_ref,
    keyval_ref,
    decay_ref,
    cum,
    cum_rows,
    step,
    enter,
    fade,
    mask,
    crossed,
    keyvals,
    fresh,
    decays,
    total_state,
    kv_send,
    kv_recv,
    st_send,
    st_recv,
    dc_send,
    dc_recv,
):
    place = lax.axis_index(CTX)
    length = proj_ref.shape[0]
    inner = (proj_ref.shape[1] - widths[3]) // 2
    pairs = heads // 2
    states = (widths[2] - widths[1]) // 2
    ctx_barrier(count, place)

    keyvals[0] = proj_ref[:, widths[0] : widths[1]].astype(bf16)

    def kv_copy(k):
        peer = lax.rem(place + k, count)
        return ctx_copy(keyvals.at[0], keyvals.at[k], kv_send.at[k], kv_recv.at[k], peer)

    def st_copy(k):
        peer = lax.rem(place + k, count)
        return ctx_copy(fresh.at[0], fresh.at[k], st_send.at[k], st_recv.at[k], peer)

    def dc_copy(k):
        peer = lax.rem(place + k, count)
        return ctx_copy(decays.at[0], decays.at[k], dc_send.at[k], dc_recv.at[k], peer)

    def kv_start(k, _):
        kv_copy(k).start()
        return 0

    lax.fori_loop(1, count, kv_start, 0)
    steps_of(
        proj_ref[:, widths[2] : widths[2] + 128], vec_ref, tok_ref, cum, cum_rows, step, enter, fade
    )
    last = cum_rows[: decays.shape[1], length - 1 :]
    decays[0] = jnp.broadcast_to(jnp.exp(last) * tok_ref[0:1, 4:5], decays.shape[1:])
    b_low = proj_ref[:, widths[1] : widths[1] + states].astype(bf16)
    c_low = proj_ref[:, widths[1] + states : widths[2]].astype(bf16)

    def make_fresh(pair, _):
        x = proj_ref[:, pair_ds(pair, widths[3] + inner)]
        x = x.astype(bf16).astype(f32)
        faded = (x * in_pair(fade[...] * step[...], pair)).astype(bf16)
        fresh[0, pair_ds(pair), :] = dot(faded, b_low, TN).astype(bf16)
        return 0

    lax.fori_loop(0, pairs, make_fresh, 0)

    def st_start(k, _):
        dc_copy(k).start()

        @pl.when(place + k < count)
        def _():
            st_copy(k).start()

        return 0

    lax.fori_loop(1, count, st_start, 0)
    mask[...] = masks_of(tok_ref, key_ref)
    crossed[...] = dot(c_low, b_low, NT) * states ** (-0.5)

    def inside(pair, _):
        x = proj_ref[:, pair_ds(pair, widths[3] + inner)]
        x = x.astype(bf16).astype(f32)
        xdt = (x * in_pair(step[...], pair)).astype(bf16)
        parts = []
        for side in range(2):
            head = 2 * pair + side
            spread = column(cum[...], head) - cum_rows[pl.ds(head, 1), :]
            weight = jnp.exp(spread + mask[:, :length])
            parts.append(dot((weight * crossed[...]).astype(bf16), xdt))
        mixed_ref[:, pair_ds(pair)] = jnp.where(lanes(parts[0].shape) < HP, *parts)
        return 0

    lax.fori_loop(0, pairs, inside, 0)

    def kv_wait(k, _):
        kv_copy(k).wait_recv()
        return 0

    lax.fori_loop(1, count, kv_wait, 0)
    keyval_ref[...] = keyvals[...].reshape(keyval_ref.shape)
    for head in range(widths[0] // HD):
        query = proj_ref[:, head * HD : (head + 1) * HD].astype(bf16)
        scores = dot(query, keyval_ref[:, :HD], NT) * HD ** (-0.5) + mask[...]
        expo = jnp.exp(scores - jnp.max(scores, axis=1, keepdims=True))
        soft = expo * (1.0 / jnp.sum(expo, axis=1, keepdims=True))
        both_ref[:, head * HD : (head + 1) * HD] = dot(
            soft.astype(bf16), keyval_ref[:, HD:]
        ).astype(bf16)

    def dc_wait(k, _):
        dc_copy(k).wait_recv()

        @pl.when(k <= place)
        def _():
            st_copy(k).wait_recv()

        return 0

    lax.fori_loop(1, count, dc_wait, 0)
    total_state[...] = jnp.zeros_like(total_state)
    head_width = inner // heads

    def combine(index, _):
        slot = place - index

        def one_head(head, _):
            rows = pl.ds(pl.multiple_of(head * head_width, head_width), head_width)
            total_state[rows, :] = total_state[rows, :] * decays[slot, pl.ds(head, 1), :] + fresh[
                slot, rows, :
            ].astype(f32)
            return 0

        lax.fori_loop(0, heads, one_head, 0)
        return 0

    lax.fori_loop(0, place, combine, 0)
    state_ref[...] = total_state[...].astype(bf16)
    decay_ref[...] = decays[...]

    def finish(pair, _):
        carried = dot(c_low, state_ref[pair_ds(pair), :], NT)
        mixed = mixed_ref[:, pair_ds(pair)] + carried * in_pair(enter[...], pair)
        mixed_ref[:, pair_ds(pair)] = mixed
        x = proj_ref[:, pair_ds(pair, widths[3] + inner)]
        x = x.astype(bf16).astype(f32)
        gate = proj_ref[:, pair_ds(pair, widths[3])]
        y = mixed + x * skip_ref[0:1, pair_ds(pair)]
        both_ref[:, pair_ds(pair, widths[0])] = (
            y * gate / (1.0 + jnp.exp(-gate))
        ).astype(bf16)
        return 0

    lax.fori_loop(0, pairs, finish, 0)

    def drain(k, _):
        kv_copy(k).wait_send()
        dc_copy(k).wait_send()

        @pl.when(place + k < count)
        def _():
            st_copy(k).wait_send()

        return 0

    lax.fori_loop(1, count, drain, 0)


def mix_backward_kernel(
    count,
    widths,
    heads,
    proj_ref,
    vec_ref,
    skip_ref,
    tok_ref,
    key_ref,
    mixed_ref,
    state_ref,
    keyval_ref,
    decay_ref,
    d_both_ref,
    d_proj_ref,
    d_vec_ref,
    cum,
    cum_rows,
    step,
    enter,
    fade,
    mask,
    crossed,
    d_crossed,
    d_y,
    d_carried,
    d_x,
    d_keyval,
    d_b,
    d_c,
    d_cum,
    d_step,
    d_coeff,
    d_skip,
    d_states,
    total_state,
    kv_out,
    kv_in,
    kv_send,
    kv_recv,
    st_send,
    st_recv,
):
    place = lax.axis_index(CTX)
    length = proj_ref.shape[0]
    inner = (proj_ref.shape[1] - widths[3]) // 2
    pairs = heads // 2
    head_width = inner // heads
    states = (widths[2] - widths[1]) // 2
    ctx_barrier(count, place)

    def back(k):
        return lax.rem(place + count - k, count)

    def kv_copy(k):
        return ctx_copy(kv_out.at[k], kv_in.at[k], kv_send.at[k], kv_recv.at[k], back(k))

    def st_copy(k):
        return ctx_copy(d_states.at[0], d_states.at[k], st_send.at[k], st_recv.at[k], back(k))

    shifted = steps_of(
        proj_ref[:, widths[2] : widths[2] + 128], vec_ref, tok_ref, cum, cum_rows, step, enter, fade
    )
    b_low = proj_ref[:, widths[1] : widths[1] + states].astype(bf16)
    c_low = proj_ref[:, widths[1] + states : widths[2]].astype(bf16)
    d_cum[...] = jnp.zeros_like(d_cum)
    d_step[...] = jnp.zeros_like(d_step)
    d_coeff[...] = jnp.zeros_like(d_coeff)
    d_skip[...] = jnp.zeros_like(d_skip)

    def x_of(pair):
        x = proj_ref[:, pair_ds(pair, widths[3] + inner)]
        return x.astype(bf16).astype(f32)

    def outer(pair, _):
        gate = proj_ref[:, pair_ds(pair, widths[3])]
        d_gated = d_both_ref[:, pair_ds(pair, widths[0])]
        x, mixed, skip = x_of(pair), mixed_ref[:, pair_ds(pair)], skip_ref[0:1, pair_ds(pair)]
        sig = 1.0 / (1.0 + jnp.exp(-gate))
        dy = d_gated * gate * sig
        d_gate = d_gated * (mixed + x * skip) * sig * (1.0 + gate * (1.0 - sig))
        d_proj_ref[:, pair_ds(pair, widths[3])] = d_gate.astype(bf16)
        low = dy.astype(bf16)
        d_y[:, pair_ds(pair)] = low
        d_x[:, pair_ds(pair)] = dy * skip
        d_skip[...] += from_pair(dy * x, pair)
        d_cum[...] += from_pair(low.astype(f32) * mixed, pair)
        carried = (low.astype(f32) * in_pair(enter[...], pair)).astype(bf16)
        d_carried[:, pair_ds(pair)] = carried
        d_states[0, pair_ds(pair), :] = dot(carried, c_low, TN).astype(bf16)
        return 0

    lax.fori_loop(0, pairs, outer, 0)

    def st_start(k, _):
        @pl.when(k <= place)
        def _():
            st_copy(k).start()

        return 0

    lax.fori_loop(1, count, st_start, 0)
    mask[...] = masks_of(tok_ref, key_ref)
    for head in range(widths[0] // HD):
        cols = slice(head * HD, (head + 1) * HD)
        query = proj_ref[:, cols].astype(bf16)
        scores = dot(query, keyval_ref[:, :HD], NT) * HD ** (-0.5) + mask[...]
        expo = jnp.exp(scores - jnp.max(scores, axis=1, keepdims=True))
        soft = expo * (1.0 / jnp.sum(expo, axis=1, keepdims=True))
        grad = d_both_ref[:, cols].astype(bf16)
        d_soft = dot(grad, keyval_ref[:, HD:], NT)
        d_scores = soft * (d_soft - jnp.sum(soft * d_soft, axis=1, keepdims=True))
        d_raw = (d_scores * HD ** (-0.5)).astype(bf16)
        d_proj_ref[:, cols] = dot(d_raw, keyval_ref[:, :HD]).astype(bf16)
        d_keys, d_values = dot(d_raw, query, TN), dot(soft.astype(bf16), grad, TN)
        if head == 0:
            d_keyval[:, :HD] = d_keys
            d_keyval[:, HD:] = d_values
        else:
            d_keyval[:, :HD] += d_keys
            d_keyval[:, HD:] += d_values
    kv_out[...] = d_keyval[...].astype(bf16).reshape(kv_out.shape)

    def kv_start(k, _):
        kv_copy(k).start()
        return 0

    lax.fori_loop(1, count, kv_start, 0)
    crossed[...] = dot(c_low, b_low, NT) * states ** (-0.5)
    d_crossed[...] = jnp.zeros_like(d_crossed)

    def inside(pair, _):
        x = x_of(pair)
        steps = in_pair(step[...], pair)
        xdt = (x * steps).astype(bf16)
        low = d_y[:, pair_ds(pair)]
        lane = lanes(low.shape)
        parts = []
        for side in range(2):
            head = 2 * pair + side
            spread = column(cum[...], head) - cum_rows[pl.ds(head, 1), :]
            weight = jnp.exp(spread + mask[:, :length])
            parts.append(dot((weight * crossed[...]).astype(bf16), low, TN))
            mine = (lane >= HP) if side else (lane < HP)
            alone = jnp.where(mine, low.astype(f32), 0.0).astype(bf16)
            d_crossed[...] += dot(alone, xdt, NT) * weight
        d_xdt = jnp.where(lane < HP, *parts)
        d_x[:, pair_ds(pair)] += d_xdt * steps
        d_step[...] += from_pair(d_xdt * x, pair)
        d_cum[...] -= from_pair(d_xdt * xdt.astype(f32), pair)
        return 0

    lax.fori_loop(0, pairs, inside, 0)
    low_crossed = (d_crossed[...] * states ** (-0.5)).astype(bf16)
    d_c[...] = dot(low_crossed, b_low) + dot(d_carried[...], state_ref[...])
    d_b[...] = dot(low_crossed, c_low, TN)

    def st_wait(k, _):
        @pl.when(place + k < count)
        def _():
            st_copy(k).wait_recv()

        return 0

    lax.fori_loop(1, count, st_wait, 0)
    total_state[...] = jnp.zeros_like(total_state)

    def combine(index, _):
        slot = count - 1 - place - index
        source = lax.rem(count - slot, count)

        def one_head(head, _):
            rows = pl.ds(pl.multiple_of(head * head_width, head_width), head_width)
            total_state[rows, :] = total_state[rows, :] * decay_ref[
                source, pl.ds(head, 1), :
            ] + d_states[slot, rows, :].astype(f32)
            return 0

        lax.fori_loop(0, heads, one_head, 0)
        return 0

    lax.fori_loop(0, count - 1 - place, combine, 0)
    d_vec_ref[...] = jnp.zeros_like(d_vec_ref)

    def from_later(pair, _):
        rows = pair_ds(pair)
        later = total_state[rows, :]
        low = later.astype(bf16)
        x = x_of(pair)
        coeffs = in_pair(fade[...] * step[...], pair)
        back_x = dot(b_low, low, NT)
        d_proj_ref[:, pair_ds(pair, widths[3] + inner)] = (
            d_x[:, rows] + back_x * coeffs
        ).astype(bf16)
        d_coeff[...] += from_pair(back_x * x, pair)
        d_b[...] += dot((x * coeffs).astype(bf16), low)
        product = later * state_ref[rows, :].astype(f32)
        row = lax.broadcasted_iota(jnp.int32, product.shape, 0)
        lane = lanes((1, 128))
        for side in range(2):
            mine = (row >= HP) if side else (row < HP)
            part = jnp.sum(jnp.where(mine, product, 0.0), axis=0, keepdims=True)
            part = jnp.sum(part, axis=1, keepdims=True)
            d_vec_ref[3:4, :] += jnp.where(lane == 2 * pair + side, part, 0.0)
        return 0

    lax.fori_loop(0, pairs, from_later, 0)
    fading = fade[...]
    d_keep = d_coeff[...] * fading * step[...]
    block_decay = jnp.exp(cum[length - 1 :, :]) * tok_ref[0:1, 4:5]
    d_last = jnp.sum(d_keep, axis=0, keepdims=True) + block_decay * d_vec_ref[3:4, :]
    d_log = running_sum(d_cum[...] - d_keep, True) + d_last
    d_size = d_step[...] + d_coeff[...] * fading - vec_ref[1:2, :] * d_log
    d_raw_step = d_size / (1.0 + jnp.exp(-shifted))
    d_proj_ref[:, widths[2] : widths[3]] = jnp.where(
        lanes(d_raw_step.shape) < heads, d_raw_step, 0.0
    ).astype(bf16)
    d_vec_ref[0:1, :] = jnp.sum(d_raw_step, axis=0, keepdims=True)
    d_vec_ref[1:2, :] = -jnp.sum(step[...] * d_log, axis=0, keepdims=True)
    d_vec_ref[2:3, :] = jnp.sum(d_skip[...], axis=0, keepdims=True)
    d_proj_ref[:, widths[1] : widths[1] + states] = d_b[...].astype(bf16)
    d_proj_ref[:, widths[1] + states : widths[2]] = d_c[...].astype(bf16)

    def kv_wait(k, _):
        kv_copy(k).wait_recv()
        d_keyval[:length, :] += kv_in[k].astype(f32)
        return 0

    lax.fori_loop(1, count, kv_wait, 0)
    d_proj_ref[:, widths[0] : widths[1]] = d_keyval[:length, :].astype(bf16)

    def drain(k, _):
        kv_copy(k).wait_send()

        @pl.when(k <= place)
        def _():
            st_copy(k).wait_send()

        return 0

    lax.fori_loop(1, count, drain, 0)


def mixer_call(kernel, collective, outs, scratch, sems, widths, heads, operands):
    count = lax.axis_size(CTX)
    whole = pl.BlockSpec(memory_space=pltpu.VMEM)
    return pl.pallas_call(
        functools.partial(kernel, count, widths, heads),
        out_shape=outs,
        in_specs=[whole] * len(operands),
        out_specs=[whole] * len(outs),
        scratch_shapes=[pltpu.VMEM(*s) for s in scratch]
        + [pltpu.SemaphoreType.DMA((count,))] * sems,
        compiler_params=pltpu.CompilerParams(
            collective_id=collective, has_side_effects=True, vmem_limit_bytes=56 << 20
        ),
        cost_estimate=pl.CostEstimate(flops=0, bytes_accessed=20 << 20, transcendentals=0),
        name="mixer"+str(collective),
    )(*operands)


def mix_forward(weights, proj, layout):
    count = lax.axis_size(CTX)
    widths, heads = weights.widths, weights.heads
    length, inner = proj.shape[0], (proj.shape[1] - widths[3]) // 2
    states = (widths[2] - widths[1]) // 2
    kv = widths[1] - widths[0]
    shape = jax.ShapeDtypeStruct
    head_rows = -(-heads // 8) * 8
    outs = [
        shape((length, widths[0] + inner), bf16),
        shape((length, inner), f32),
        shape((inner, states), bf16),
        shape((count * length, kv), bf16),
        shape((count, head_rows, states), f32),
    ]
    per_head = ((length, 128), f32)
    scratch = [
        per_head,
        ((128, length), f32),
        per_head,
        per_head,
        per_head,
        ((length, count * length), f32),
        ((length, length), f32),
        ((count, length, kv), bf16),
        ((count, inner, states), bf16),
        ((count, head_rows, states), f32),
        ((inner, states), f32),
    ]
    operands = (proj, weights.head_rows, weights.skip_row, *layout)
    return mixer_call(mix_forward_kernel, 5, outs, scratch, 6, widths, heads, operands)


def mix_backward(weights, saved, d_both, layout):
    count = lax.axis_size(CTX)
    widths, heads = weights.widths, weights.heads
    proj = saved.proj
    length, inner = proj.shape[0], (proj.shape[1] - widths[3]) // 2
    states = (widths[2] - widths[1]) // 2
    kv = widths[1] - widths[0]
    shape = jax.ShapeDtypeStruct
    outs = [shape(proj.shape, bf16), shape((8, 128), f32)]
    per_head = ((length, 128), f32)
    square = ((length, length), f32)
    scratch = [
        per_head,
        ((128, length), f32),
        per_head,
        per_head,
        per_head,
        ((length, count * length), f32),
        square,
        square,
        ((length, inner), bf16),
        ((length, inner), bf16),
        ((length, inner), f32),
        ((count * length, kv), f32),
        ((length, states), f32),
        ((length, states), f32),
        per_head,
        per_head,
        per_head,
        per_head,
        ((count, inner, states), bf16),
        ((inner, states), f32),
        ((count, length, kv), bf16),
        ((count, length, kv), bf16),
    ]
    operands = (
        proj,
        weights.head_rows,
        weights.skip_row,
        *layout,
        saved.mixed,
        saved.state_in,
        saved.keyval_all,
        saved.decays,
        d_both,
    )
    return mixer_call(mix_backward_kernel, 6, outs, scratch, 4, widths, heads, operands)


def finish_kernel(
    count,
    places,
    widths,
    *refs,
):
    arrays, refs = refs[: len(places[2])], refs[len(places[2]) :]
    (
        rows0,
        rows1,
        grad0,
        grad1,
        tiny0,
        tiny1,
        wide0,
        wide1,
        columns0,
        columns1,
        *refs,
    ) = refs
    (
        query_out,
        zx_out,
        up_out,
        down_out,
        out_out,
        rows_out,
        grad_out,
        shared_out,
        tiny_out,
        *refs,
    ) = refs
    boxes, refs = refs[: len(widths)], refs[len(widths) :]
    (
        rows_box,
        grad_box,
        tiny_box,
        tiny_sum,
        tiny_all,
        wide_boxes,
        columns_boxes,
        blocks,
        blocks_box,
        shared,
        shared_box,
        send,
        recv,
        ctx_send,
        ctx_recv,
    ) = refs
    section, place = lax.axis_index(SECTION), lax.axis_index(CTX)
    bar = pltpu.get_barrier_semaphore()
    pl.semaphore_signal(bar, inc=1, device_id={SECTION: 1 - section}, device_id_type=MESH)
    for k in range(1, count):
        peer = flipped(place, k, count)
        pl.semaphore_signal(bar, inc=1, device_id={CTX: peer}, device_id_type=MESH)
    pl.semaphore_wait(bar, count)
    half = wide0.shape[1] // 2
    own_half = pl.ds(pl.multiple_of(section * half, half), half)
    other_half = pl.ds(pl.multiple_of((1 - section) * half, half), half)

    def over(i, source, target):
        return pltpu.make_async_remote_copy(
            source,
            target,
            send.at[i],
            recv.at[i],
            device_id={SECTION: 1 - section},
            device_id_type=MESH,
        )

    def across(i, k, source, target):
        return pltpu.make_async_remote_copy(
            source,
            target,
            ctx_send.at[i],
            ctx_recv.at[i],
            device_id={CTX: flipped(place, k, count)},
            device_id_type=MESH,
        )

    def part(layer, i):
        array, start, width = places[layer][i]
        return arrays[array].at[:, start : start + width]

    def by_section(act, first, second):
        @pl.when(section == 1)
        def _():
            act(first)

        @pl.when(section == 0)
        def _():
            act(second)

    block = blocks.shape[2]
    wides, columns = (wide0, wide1), (columns0, columns1)
    early = [over(l, wides[l].at[:, other_half], wide_boxes.at[l]) for l in range(2)]
    early += [over(2 + l, columns[l], columns_boxes.at[l]) for l in range(2)]
    for copy in early:
        copy.start()
    pairs = [(tiny0, tiny1, tiny_box)]
    pairs += [(part(0, i), part(1, i), box) for i, box in enumerate(boxes)]
    pairs += [(rows0, rows1, rows_box), (grad0, grad1, grad_box)]
    copies = [
        (over(4 + i, first, box), over(4 + i, second, box))
        for i, (first, second, box) in enumerate(pairs)
    ]

    def each(act, which):
        for first, second in which:
            by_section(act, first, second)

    each(lambda copy: copy.start(), copies)
    for copy in early:
        copy.wait_recv()
    dims = (((0,), (0,)), ((), ()))

    def block_copy(l, k):
        return across(2 * k + l, k, blocks.at[l, k], blocks_box.at[l, k])

    for l in range(2):
        total = lax.dot_general(
            columns[l][...], wides[l][:, own_half], dims, preferred_element_type=f32
        ) + lax.dot_general(columns_boxes[l], wide_boxes[l], dims, preferred_element_type=f32)
        for k in range(count):
            blocks[l, k] = total[k * block : (k + 1) * block, :].astype(bf16)
        for k in range(1, count):
            block_copy(l, k).start()
    each(lambda copy: copy.wait_recv(), copies[:1])

    def first_tiny(mine):
        tiny_sum[...] = mine[...] + tiny_box[...]

    by_section(first_tiny, tiny1, tiny0)
    for k in range(1, count):
        across(2 * count + k, k, tiny_sum, tiny_all.at[k]).start()

    def place_pieces(low_core, take):
        query, zx_a, zx_b, up_a, up_b, down_a, down_b, out_a, out_b = (
            functools.partial(take, i) for i in range(9)
        )
        width = query_out.shape[1] // 2
        query_out[:, pl.ds(pl.multiple_of(low_core * width, width), width)] = query()
        edge = zx_out.shape[2] // 2
        zx_out[low_core, :, :edge] = zx_a().astype(f32)
        zx_out[low_core, :, edge:] = zx_b().astype(f32)
        edge = up_out.shape[2] // 2
        up_out[low_core, :, :edge] = up_a().astype(f32)
        up_out[low_core, :, edge:] = up_b().astype(f32)
        for target, pieces in ((down_out, (down_a, down_b)), (out_out, (out_a, out_b))):
            for i, piece in enumerate(pieces):
                height = target.shape[0] // 4
                start = low_core * 2 * height + i * height
                target[pl.ds(pl.multiple_of(start, height), height), :] = piece().T

    def own(layer):
        def take(i):
            return part(layer, i)[...]

        place_pieces(section, take)

    by_section(own, 1, 0)
    each(lambda copy: copy.wait_recv(), copies[1:])
    place_pieces(1 - section, lambda i: boxes[i][...])

    def rows_done(mine):
        rows_out[section] = mine[0][...]
        grad_out[section] = mine[1][...]

    by_section(rows_done, (rows1, grad1), (rows0, grad0))
    rows_out[1 - section] = rows_box[...]
    grad_out[1 - section] = grad_box[...]
    for l in range(2):
        rows = blocks[l, 0].astype(f32)
        for k in range(1, count):
            block_copy(l, k).wait_recv()
            rows += blocks_box[l, k].astype(f32)
        shared[l] = rows.astype(bf16)
    shared_copy = over(len(pairs) + 4, shared.at[1 - section], shared_box)
    shared_copy.start()
    everything = tiny_sum[...]
    for k in range(1, count):
        across(2 * count + k, k, tiny_sum, tiny_all.at[k]).wait_recv()
        everything += tiny_all[k]
    tiny_out[...] = everything

    shared_out[:, own_half] = shared[section]
    shared_copy.wait_recv()
    shared_out[:, other_half] = shared_box[...]
    for copy in early:
        copy.wait_send()
    each(lambda copy: copy.wait_send(), copies)
    shared_copy.wait_send()
    for k in range(1, count):
        for l in range(2):
            block_copy(l, k).wait_send()
        across(2 * count + k, k, tiny_sum, tiny_all.at[k]).wait_send()


def finish(first, second, rows, d_rows, tinies, wides, columns):
    count = lax.axis_size(CTX)
    arrays = (*first.ffn, first.proj, *first.out, *second.ffn, *second.mix)
    up, down = first.ffn[0].shape[1] // 3 * 2, first.ffn[0].shape[1] // 3
    out = first.out[0].shape[1]
    step = 128
    query = (first.proj.shape[1] - step) - 2 * (second.mix[1].shape[1] - step - out)
    most = second.mix[1].shape[1] - step - out

    def ffn(a):
        return (a, 0, up), (a + 1, 0, up), (a, up, down), (a + 1, up, down)

    places = (
        (
            (2, 0, query),
            (2, query, most),
            (2, query + most, most),
            *ffn(0),
            (3, 0, out),
            (4, 0, out),
        ),
        (
            (7, 0, query),
            (7, query, most),
            (8, 0, most),
            *ffn(5),
            (7, query + most, out),
            (8, most + step, out),
        ),
        arrays,
    )
    length, part = first.proj.shape[0], rows[0].shape[0]
    widths = [piece[2] for piece in places[0]]
    half, block = wides[0].shape[1] // 2, columns[0].shape[1] // count
    shape = jax.ShapeDtypeStruct
    outs = [
        shape((length, 2 * query), bf16),
        shape((2, length, 2 * most), f32),
        shape((2, length, 2 * up), f32),
        shape((4 * down, length), bf16),
        shape((4 * out, length), bf16),
        shape((2,) + rows[0].shape, bf16),
        shape((2,) + d_rows[0].shape, f32),
        shape((block, 2 * half), bf16),
        shape(tinies[0].shape, f32),
    ]
    tokens = columns[0].shape[0]
    scratch = [pltpu.VMEM((length, w), bf16) for w in widths]
    scratch += [
        pltpu.VMEM(rows[0].shape, bf16),
        pltpu.VMEM(d_rows[0].shape, f32),
        pltpu.VMEM(tinies[0].shape, f32),
        pltpu.VMEM(tinies[0].shape, f32),
        pltpu.VMEM((count,) + tinies[0].shape, f32),
        pltpu.VMEM((2, tokens, half), bf16),
        pltpu.VMEM((2, tokens, count * block), bf16),
        pltpu.VMEM((2, count, block, half), bf16),
        pltpu.VMEM((2, count, block, half), bf16),
        pltpu.VMEM((2, block, half), bf16),
        pltpu.VMEM((block, half), bf16),
    ]
    over = len(widths) + 8
    scratch += [pltpu.SemaphoreType.DMA((n,)) for n in (over, over, 3 * count, 3 * count)]
    whole = pl.BlockSpec(memory_space=pltpu.VMEM)
    operands = (*arrays, *rows, *d_rows, *tinies, *wides, *columns)
    return pl.pallas_call(
        functools.partial(finish_kernel, count, places, widths),
        out_shape=outs,
        in_specs=[whole] * len(operands),
        out_specs=[whole] * len(outs),
        scratch_shapes=scratch,
        compiler_params=pltpu.CompilerParams(
            collective_id=11, has_side_effects=True, vmem_limit_bytes=56 << 20
        ),
        cost_estimate=pl.CostEstimate(flops=0, bytes_accessed=20 << 20, transcendentals=0),
        name="finish",
    )(*operands)


def norm_apply(values, gain):
    return values * lax.rsqrt(jnp.mean(values * values, axis=-1, keepdims=True) + eps) * gain


def matmul(left, right):
    return jnp.dot(left, right, preferred_element_type=f32)


def matmul_nt(left, right):
    return lax.dot_general(left, right, (((1,), (1,)), ((), ())), preferred_element_type=f32)


def matmul_tn(left, right):
    return lax.dot_general(left, right, (((0,), (0,)), ((), ())), preferred_element_type=f32)


def swap(values):
    return lax.ppermute(values, SECTION, [(0, 1), (1, 0)])


def block_layout(doc_lengths, length):
    count, place = lax.axis_size(CTX), lax.axis_index(CTX)
    start = place * length
    bounds = jnp.cumsum(doc_lengths)[:-1]

    def segment_of(positions):
        return jnp.sum((positions[:, None] >= bounds[None, :]).astype(jnp.int32), axis=1)

    order = lax.rem(place + count - jnp.arange(count, dtype=jnp.int32), count)
    inside = jnp.arange(length, dtype=jnp.int32)
    keys = (order[:, None] * length + inside[None, :]).reshape(-1)
    positions = start + inside
    segments = segment_of(positions)
    before = jnp.where(place > 0, segment_of(start[None] - 1)[0], -1)
    goes_on = jnp.broadcast_to(segments[-1] == before, segments.shape)
    columns = [segments, segments == before, segments == segments[-1], positions, goes_on]
    tokens = jnp.stack([c.astype(f32) for c in columns], axis=1)
    return jnp.pad(tokens, ((0, 0), (0, 3))), jnp.stack(
        [segment_of(keys).astype(f32), keys.astype(f32)]
    )


def layer_forward(weights, normed, layout):
    proj = matmul(normed, weights.proj)
    both, mixed, state_in, keyval_all, decays = mix_forward(weights, proj, layout)
    saved = types.SimpleNamespace(
        normed=normed,
        proj=proj,
        both=both,
        mixed=mixed,
        state_in=state_in,
        keyval_all=keyval_all,
        decays=decays,
    )
    return matmul(both, weights.out), saved


def ffn_forward(weights, ffn_in):
    gate_up = matmul(ffn_in, weights.gate_up)
    width = gate_up.shape[1] // 2
    gate_pre, upward = gate_up[:, :width], gate_up[:, width:]
    product = (jax.nn.silu(gate_pre) * upward).astype(bf16)
    return matmul(product, weights.down), gate_pre, upward, product


def ctx_bits():
    return [1 << i for i in reversed(range((lax.axis_size(CTX) - 1).bit_length()))]


def flip(values, bit):
    return lax.ppermute(values, CTX, [(i, i ^ bit) for i in range(lax.axis_size(CTX))])


def own_half(values):
    half = values.shape[1] // 2
    section = lax.axis_index(SECTION)
    return (
        lax.dynamic_slice_in_dim(values, section * half, half, 1),
        lax.dynamic_slice_in_dim(values, (1 - section) * half, half, 1),
    )


def both_batches(kept, sent):
    return jnp.concatenate([kept, swap(sent)], axis=0)


def ctx_orders():
    bits = ctx_bits()
    return bits, bits[::-1]


def relative_order(bits):
    order = [0]
    for bit in reversed(bits):
        order = order + [k ^ bit for k in order]
    return order


def weight_sums(columns, *rows):
    kept, sent = zip(*(own_half(r) for r in rows))
    halves = both_batches(jnp.concatenate(kept, axis=1), jnp.concatenate(sent, axis=1))
    return matmul_tn(both_batches(columns, columns), halves).astype(bf16)


def shared_columns(normed):
    place, count = lax.axis_index(CTX), lax.axis_size(CTX)
    shards = lax.axis_size(SHARD)
    block = normed.shape[1] // (count * shards)
    return jnp.concatenate(
        [
            lax.dynamic_slice_in_dim(
                normed, ((place ^ k) * shards + lax.axis_index(SHARD)) * block, block, 1
            )
            for k in range(count)
        ],
        axis=1,
    )


def blocks_of(total):
    place, count = lax.axis_index(CTX), lax.axis_size(CTX)
    block = total.shape[0] // count
    return jnp.stack(
        [lax.dynamic_slice_in_dim(total, (place ^ k) * block, block, 0) for k in range(count)]
    )


def streams_of(total):
    place, count = lax.axis_index(CTX), lax.axis_size(CTX)
    block, half = total.shape[0] // count, total.shape[1] // 2
    streams = []
    for stream, bits in enumerate(ctx_orders()):
        parts = [
            lax.dynamic_slice(total, ((place ^ k) * block, stream * half), (block, half))
            for k in relative_order(bits)
        ]
        streams += [jnp.stack(parts[: count // 2]), jnp.stack(parts[count // 2 :])]
    return streams


def weight_scatter(streams):
    totals = []
    for i, bits in enumerate(ctx_orders()):
        kept, sent = (a.reshape(-1, a.shape[-1]) for a in streams[2 * i : 2 * i + 2])
        totals.append(scatter_relative(kept, sent, bits))
    return totals


def scatter_relative(kept, sent, bits):
    for i, bit in enumerate(bits):
        got = flip(sent, bit)
        if i + 1 < len(bits):
            rows = kept.shape[0] // 2
            sent = (kept[rows:].astype(f32) + got[rows:].astype(f32)).astype(bf16)
            kept = (kept[:rows].astype(f32) + got[:rows].astype(f32)).astype(bf16)
        else:
            kept = (kept.astype(f32) + got.astype(f32)).astype(bf16)
    return kept


def after(first, *later):
    first, later = lax.optimization_barrier((first, later))
    return first, later


def layer_backward(weights, saved, d_out, d_low, values_in, layout, last, before):
    grads = types.SimpleNamespace()
    d_product = matmul_nt(d_low, weights.down)
    gate_pre, upward = saved.gate_pre, saved.upward
    gate_sig = jax.nn.sigmoid(gate_pre)
    d_gate = d_product * upward * gate_sig * (1.0 + gate_pre * (1.0 - gate_sig))
    d_upward = d_product * gate_pre * gate_sig
    d_gate_up = jnp.concatenate([d_gate, d_upward], axis=1).astype(bf16)
    d_ffn_in = matmul_nt(d_gate_up, weights.gate_up)
    width = d_product.shape[1]
    up, down = width // 2, width // 4
    plan = tuple(
        (x, stream, ((x, stream * part, 2 * part + stream * part, part),))
        for stream in range(2)
        for x, part in ((0, up), (1, down))
    )
    d_middle, d_mixed, grads.gain_ffn, *sums = back_sum(
        10 if last else 3,
        d_ffn_in,
        d_out,
        saved.middle,
        weights.gain_ffn,
        plan,
        (saved.ffn_in, d_low),
        (d_gate_up, saved.product),
        (),
        before.sums_mix if last else (),
    )
    if last:
        sums, before.mix = sums[:4], sums[4:]
        grads.ffn = weight_scatter(sums)
    else:
        sums_ffn = sums
    d_both = matmul_nt(d_mixed, weights.out)
    if not last:
        (d_both,), (before.tail,) = after((d_both,), before.tail)
    if last:
        sums_out = weight_sums(d_mixed, saved.both)
        (sums_out,), (d_both,) = after((streams_of(sums_out),), d_both)
        grads.out = weight_scatter(sums_out)
    d_proj, d_vec = mix_backward(weights, saved, d_both, layout)
    heads, widths = weights.heads, weights.widths
    grads.step_bias, grads.decay, grads.skip = (d_vec[i, :heads] for i in range(3))
    d_normed = matmul_nt(d_proj, weights.proj)
    placed = [
        jnp.where(weights.kv_owner == owner, d_proj[:, start : start + HD], 0)
        for start in (widths[0], widths[0] + HD)
        for owner in range(KVH)
    ]
    d_shared = jnp.concatenate([d_proj[:, widths[1] : widths[2]], *placed], axis=1)
    normed = saved.normed
    if last:
        d_step, d_zx = d_proj[:, widths[2] : widths[3]], d_proj[:, widths[3] :]
        sums_proj = weight_sums(
            normed, d_proj[:, : widths[0]], d_zx, jnp.concatenate([d_step, d_step], axis=1)
        )
        blocks = blocks_of(sums_proj)
        (blocks,), (d_normed,) = after((blocks,), d_normed)
        d_hidden, d_hidden_low, grads.gain_in, d_shared, grads.proj = back_sum_scatter(
            7, d_normed, d_shared, d_middle, values_in, weights.gain_in, blocks
        )
    else:
        query, inner = widths[0] // 2, (d_proj.shape[1] - widths[3]) // 2
        step, zx = widths[3] - widths[2], widths[3]
        both, most = saved.both.shape[1] // 4, inner // 2
        plan = (
            (0, 0, ((0, 0, query, query), (0, zx, zx + inner, most))),
            (1, 0, ((1, 0, 2 * both, both),)),
            (0, 1, ((0, zx + most, zx + inner + most, most), (0, widths[2], widths[2], step))),
            (1, 1, ((1, both, 3 * both, both),)),
        )
        d_hidden, d_hidden_low, grads.gain_in, d_shared, *sums = back_sum(
            4,
            d_normed,
            d_middle,
            values_in,
            weights.gain_in,
            plan,
            (normed, d_mixed),
            (d_proj, saved.both),
            (d_shared,),
            sums_ffn,
        )
        sums, grads.ffn = sums[:4], sums[4:]
        grads.sums_mix = sums
    grads.wide = d_shared
    return d_hidden, d_hidden_low, grads


def body(
    inputs,
    cotangent,
    doc_lengths,
    norm_in,
    w_query,
    w_keyval,
    w_attn_out,
    w_mixer_in,
    w_state_io,
    w_step,
    step_bias,
    decay_rate,
    skip_gain,
    w_mixer_out,
    norm_ffn,
    w_gate_up,
    w_down,
):
    section = lax.axis_index(SECTION)
    leading = section == 0
    shard = lax.axis_index(SHARD)
    width = w_query.shape[1]
    query_width = w_query.shape[2]
    head_count = w_step.shape[2]
    kv_owner = shard * (query_width // HD) // (QH // KVH)
    rows_in = lax.dynamic_index_in_dim(inputs, section, 0, False)
    own_keyval = lax.dynamic_slice_in_dim(w_keyval[0], kv_owner * HD, HD, 2).reshape(width, 2 * HD)
    io_end = query_width + 2 * HD + w_state_io.shape[2]
    widths = (query_width, query_width + 2 * HD, io_end, io_end - (-head_count // 128) * 128)
    proj = jnp.concatenate(
        [
            w_query[0],
            own_keyval,
            w_state_io[0],
            jnp.pad(w_step[0], ((0, 0), (0, -head_count % 128))),
            w_mixer_in[0].reshape(width, -1),
        ],
        axis=1,
    )
    vectors = jnp.concatenate([norm_in[0], norm_ffn[0], step_bias[0], decay_rate[0], skip_gain[0]])
    block_in = line_gather(rows_in)
    (block_in,), (proj,) = after((block_in,), proj)
    own = (
        proj,
        jnp.concatenate([w_attn_out[0], w_mixer_out[0]], axis=0),
        w_gate_up[0].reshape(width, -1),
        w_down[0],
        vectors,
    )
    other = tuple(swap(array) for array in own)

    def layer_weights(layer):
        weights = types.SimpleNamespace()
        chosen = [jnp.where(section == layer, a, b) for a, b in zip(own, other)]
        weights.proj, weights.out, weights.gate_up, weights.down, vectors = chosen
        heads = vectors[2 * width :]
        weights.gain_in = vectors[:width]
        weights.gain_ffn = vectors[width : 2 * width]
        skip = heads[2 * head_count :]
        rows = heads[: 2 * head_count].reshape(2, head_count)
        weights.head_rows = jnp.pad(rows, ((0, 6), (0, -head_count % 128)))
        weights.skip_row = jnp.repeat(skip, HP)[None]
        weights.heads = head_count
        weights.widths = widths
        weights.kv_owner = kv_owner
        return weights

    layers = [layer_weights(0), layer_weights(1)]
    rows_cot = lax.dynamic_index_in_dim(cotangent, section, 0, False)
    length = block_in.shape[0]
    part = rows_in.shape[0]
    layout = block_layout(lax.dynamic_index_in_dim(doc_lengths, section, 0, False), length)

    def own_rows(values):
        return lax.dynamic_slice_in_dim(values, shard * part, part, 0)

    hidden = block_in.astype(f32)
    normed = norm_apply(hidden, layers[0].gain_in).astype(bf16)
    hiddens, outs, saves = [], [], []
    for layer in range(2):
        weights = layers[layer]
        hiddens.append(hidden)
        if layer == 1:
            (normed,), (rows_cot,) = after((normed,), rows_cot)
            block_cot = lax.all_gather(rows_cot, SHARD, axis=0, tiled=True)
        partial, saved = layer_forward(weights, normed, layout)
        first, second = layers
        wanted = [(layer, own[i], other[i]) for i in (2, 3)]
        saved.middle, saved.ffn_in, chosen = copying_sum(
            middle_kernel, 1 + 8 * layer, f32, partial, hidden, weights.gain_ffn, wanted
        )
        weights.gate_up, weights.down = chosen
        partial, saved.gate_pre, saved.upward, saved.product = ffn_forward(
            weights, saved.ffn_in
        )
        saves.append(saved)
        if layer == 0:
            wanted = [(1, own[i], other[i]) for i in (0, 1)]
            out_low, normed, chosen = copying_sum(
                layer_end_kernel, 2, bf16, partial, saved.middle, second.gain_in, wanted
            )
            second.proj, second.out = chosen
            outs.append(own_rows(out_low))
            hidden = out_low.astype(f32)
        else:
            held = types.SimpleNamespace(tail=partial.astype(bf16))

    d_out = d_low = block_cot
    d_hiddens, grads = [None, None], [None, None]
    for layer in (1, 0):
        d_hidden, d_low, grads[layer] = layer_backward(
            layers[layer], saves[layer], d_out, d_low, hiddens[layer], layout, layer == 0, grads[1] if layer == 0 else held
        )
        d_hiddens[layer] = d_hidden
        d_out = d_low

    total = lax.psum_scatter(held.tail, SHARD, scatter_dimension=0, tiled=True)
    outs.append((own_rows(saves[1].middle) + total.astype(f32)).astype(bf16))
    first, second = grads
    tinies = []
    for g in grads:
        vector = jnp.concatenate([g.gain_in, g.gain_ffn, g.step_bias, g.decay, g.skip])
        size = -(-vector.shape[0] // 1024) * 8
        tinies.append(jnp.pad(vector, (0, size * 128 - vector.shape[0])).reshape(size, 128))
    query, zx, up, down, out, out_rows, grad_rows, shared, tiny = finish(
        first,
        second,
        outs,
        [own_rows(d) for d in d_hiddens],
        tinies,
        [first.wide, second.wide],
        [shared_columns(saved.normed) for saved in saves],
    )
    tiny = tiny.reshape(-1)
    place = lax.axis_index(CTX) * lax.axis_size(SHARD) + shard
    slot = width // (lax.axis_size(CTX) * lax.axis_size(SHARD))
    grad_in = lax.dynamic_slice_in_dim(tiny, place * slot, slot, 0)
    grad_ffn = lax.dynamic_slice_in_dim(tiny, width + place * slot, slot, 0)
    heads = tiny[2 * width :]
    step = jnp.where(
        leading,
        first.proj[:, first.proj.shape[1] - 128 :],
        second.mix[1][:, zx.shape[2] // 2 : zx.shape[2] // 2 + 128],
    )
    io_width = w_state_io.shape[2]
    return (
        out_rows[None],
        grad_rows[None],
        grad_in[None],
        query.astype(f32)[None],
        shared[:, io_width:].astype(f32).reshape(-1, 2, KVH * HD)[None],
        out[:query_width].astype(f32)[None],
        jnp.swapaxes(zx, 0, 1)[None],
        shared[:, :io_width].astype(f32)[None],
        step[:, :head_count].astype(f32)[None],
        heads[:head_count][None],
        heads[head_count : 2 * head_count][None],
        heads[2 * head_count : 3 * head_count][None],
        out[query_width:].astype(f32)[None],
        grad_ffn[None],
        jnp.swapaxes(up, 0, 1)[None],
        down.astype(f32)[None],
    )


def solution(mesh):
    return jax.shard_map(
        body,
        mesh=mesh,
        in_specs=(
            P(None, (CTX, SHARD), None),
            P(None, (CTX, SHARD), None),
            P(),
            P(SECTION, None),
            P(SECTION, None, SHARD),
            P(SECTION, None, None, None),
            P(SECTION, SHARD, None),
            P(SECTION, None, None, SHARD),
            P(SECTION, None, None),
            P(SECTION, None, SHARD),
            P(SECTION, SHARD),
            P(SECTION, SHARD),
            P(SECTION, SHARD),
            P(SECTION, SHARD, None),
            P(SECTION, None),
            P(SECTION, None, None, SHARD),
            P(SECTION, SHARD, None),
        ),
        out_specs=(
            P(SECTION, None, (CTX, SHARD), None),
            P(SECTION, None, (CTX, SHARD), None),
            P(SECTION, (CTX, SHARD)),
            P(SECTION, CTX, SHARD),
            P(SECTION, (CTX, SHARD), None, None),
            P(SECTION, SHARD, CTX),
            P(SECTION, CTX, None, SHARD),
            P(SECTION, (CTX, SHARD), None),
            P(SECTION, CTX, SHARD),
            P(SECTION, SHARD),
            P(SECTION, SHARD),
            P(SECTION, SHARD),
            P(SECTION, SHARD, CTX),
            P(SECTION, (CTX, SHARD)),
            P(SECTION, CTX, None, SHARD),
            P(SECTION, SHARD, CTX),
        ),
        check_vma=False,
    )
```

```python
import functools
import types

import jax
import jax.numpy as jnp
from jax import lax
from jax.experimental import pallas as pl
from jax.experimental.pallas import tpu as pltpu
from jax.sharding import PartitionSpec as P

SECTION, CTX, SHARD = "section", "ctx", "shard"
QH = 8
KVH = 2
HD = 128
HP = 64
CHUNKS = 16
LAG = 3

MESH = pl.DeviceIdType.MESH
eps = 1e-05
bf16 = jnp.bfloat16
f32 = jnp.float32


def line_sum(n, chunks, lag, p_rows, done, sr, sl, rr, rl, srs, sls, rrs, rls, tot, fill=None):
    z = lax.axis_index(SHARD)
    hasr, hasl = z < n - 1, z > 0
    bar = pltpu.get_barrier_semaphore()
    more = 0
    if fill is not None:
        more = fill.greet(bar)

    @pl.when(hasr)
    def _():
        pl.semaphore_signal(bar, inc=1, device_id={SHARD: z + 1}, device_id_type=MESH)

    @pl.when(hasl)
    def _():
        pl.semaphore_signal(bar, inc=1, device_id={SHARD: z - 1}, device_id_type=MESH)

    @pl.when(hasl & hasr)
    def _():
        pl.semaphore_wait(bar, 2 + more)

    @pl.when(jnp.logical_not(hasl & hasr))
    def _():
        pl.semaphore_wait(bar, 1 + more)

    def right(j):
        return pltpu.make_async_remote_copy(
            sr.at[j], rr.at[j], srs.at[j], rrs.at[j], device_id={SHARD: z + 1}, device_id_type=MESH
        )

    def left(j):
        return pltpu.make_async_remote_copy(
            sl.at[j], rl.at[j], sls.at[j], rls.at[j], device_id={SHARD: z - 1}, device_id_type=MESH
        )

    steps = chunks + lag * (n - 1)
    if fill is not None:
        fill.start()

    def one(i, _):
        def go(j, copy, came, goes, inbox, outbox):
            live = (j >= 0) & (j < chunks)

            @pl.when(live & came & goes)
            def _():
                copy(j).wait_recv()
                outbox[j] = (p_rows(j) + inbox[j].astype(f32)).astype(bf16)
                copy(j).start()

            @pl.when(live & jnp.logical_not(came))
            def _():
                outbox[j] = p_rows(j).astype(bf16)
                copy(j).start()

            @pl.when(live & jnp.logical_not(goes))
            def _():
                copy(j).wait_recv()

        go(i - lag * z, right, hasl, hasr, rr, sr)
        go(i - lag * (n - 1 - z), left, hasr, hasl, rl, sl)
        jd = i - lag * jnp.maximum(z, n - 1 - z)

        @pl.when((jd >= 0) & (jd < chunks))
        def _():
            tot[...] = p_rows(jd)

            @pl.when(hasl)
            def _():
                tot[...] += rr[jd].astype(f32)

            @pl.when(hasr)
            def _():
                tot[...] += rl[jd].astype(f32)

            done(jd, tot[...])

        if fill is not None:
            fill.step(i, steps)
        return 0

    lax.fori_loop(0, steps, one, 0)
    if fill is not None:
        fill.finish()

    def drain(j, _):
        @pl.when(hasr)
        def _():
            right(j).wait_send()

        @pl.when(hasl)
        def _():
            left(j).wait_send()

        return 0

    lax.fori_loop(0, chunks, drain, 0)


def row_slice(j, rows):
    return pl.ds(pl.multiple_of(j * rows, rows), rows)


def middle_kernel(n, chunks, lag, p_ref, h_ref, gain_ref, mid_ref, low_ref, *scratch, fill=None):
    rows = p_ref.shape[0] // chunks

    def p_rows(j):
        return p_ref[row_slice(j, rows), :]

    def done(j, total):
        v = h_ref[row_slice(j, rows), :] + total
        r = lax.rsqrt(jnp.mean(v * v, axis=-1, keepdims=True) + eps)
        mid_ref[row_slice(j, rows), :] = v
        low_ref[row_slice(j, rows), :] = (v * r * gain_ref[...]).astype(bf16)

    line_sum(n, chunks, lag, p_rows, done, *scratch, fill=fill)


class Copies:
    parts = 16

    def __init__(self, layers, own, other, out, boxes, came, went):
        self.layers, self.own, self.other, self.out = layers, own, other, out
        self.boxes, self.came, self.went = boxes, came, went

    def greet(self, bar):
        return 0

    def start(self):
        pass

    def rows(self, a, j):
        size = self.boxes[a].shape[1]
        return pl.ds(pl.multiple_of(j * size, size), size)

    def fetch(self, a, j, act):
        section, slot = lax.axis_index(SECTION), lax.rem(j, 2)
        for mine, source in ((True, self.own[a]), (False, self.other[a])):

            @pl.when((section == self.layers[a]) == mine)
            def _():
                part = source.at[self.rows(a, j), :]
                act(
                    pltpu.make_async_copy(
                        part, self.boxes[a].at[slot], self.came.at[2 * a + slot]
                    )
                )

    def store(self, a, j):
        slot = lax.rem(j, 2)
        part = self.out[a].at[self.rows(a, j), :]
        return pltpu.make_async_copy(self.boxes[a].at[slot], part, self.went.at[2 * a + slot])

    def step(self, i, steps):
        @pl.when((i >= 1) & (i <= self.parts))
        def _():
            for a in range(len(self.layers)):
                self.fetch(a, i - 1, lambda copy: copy.wait())
                self.store(a, i - 1).start()

        @pl.when((i >= 2) & (i < self.parts))
        def _():
            for a in range(len(self.layers)):
                self.store(a, i - 2).wait()

        @pl.when(i < self.parts)
        def _():
            for a in range(len(self.layers)):
                self.fetch(a, i, lambda copy: copy.start())

    def finish(self):
        for a in range(len(self.layers)):
            for j in (self.parts - 2, self.parts - 1):
                self.store(a, j).wait()


def copying(kernel, layers, n, chunks, lag, p_ref, h_ref, gain_ref, *refs):
    count = len(layers)
    own, other, refs = refs[:count], refs[count : 2 * count], refs[2 * count :]
    first_ref, low_ref, refs = refs[0], refs[1], refs[2:]
    out, refs = refs[:count], refs[count:]
    copies = Copies(layers, own, other, out, refs[9 : 9 + count], *refs[9 + count :])
    kernel(n, chunks, lag, p_ref, h_ref, gain_ref, first_ref, low_ref, *refs[:9], fill=copies)


def layer_end_kernel(n, chunks, lag, p_ref, h_ref, gain_ref, out_ref, low_ref, *scratch, fill=None):
    rows = p_ref.shape[0] // chunks

    def p_rows(j):
        return p_ref[row_slice(j, rows), :]

    def done(j, total):
        out = (h_ref[row_slice(j, rows), :] + total).astype(bf16)
        out_ref[row_slice(j, rows), :] = out
        v = out.astype(f32)
        r = lax.rsqrt(jnp.mean(v * v, axis=-1, keepdims=True) + eps)
        low_ref[row_slice(j, rows), :] = (v * r * gain_ref[...]).astype(bf16)

    line_sum(n, chunks, lag, p_rows, done, *scratch, fill=fill)


def flipped(place, k, count):
    total, bit = 0, 1
    while bit < count:
        total = total + (place // bit + k // bit) % 2 * bit
        bit *= 2
    return total


def mirrored(k, count):
    total, bit = 0, 1
    while bit < count:
        total = total + k // bit % 2 * (count // (2 * bit))
        bit *= 2
    return total


class Fill:
    first = 6

    def __init__(self, plan, xs, ys, outs, scratch):
        self.plan, self.xs, self.ys, self.outs = plan, xs, ys, outs
        count = len(plan)
        self.other_x, rest = scratch[: len(xs)], scratch[len(xs) :]
        self.own_y, self.other_y = rest[:count], rest[count : 2 * count]
        self.send, self.recv = rest[2 * count :]

    def greet(self, bar):
        other = 1 - lax.axis_index(SECTION)
        pl.semaphore_signal(bar, inc=1, device_id={SECTION: other}, device_id_type=MESH)
        return 1

    def copies(self):
        section = lax.axis_index(SECTION)
        copies = []

        def add(source, target):
            i = len(copies)
            copies.append(
                pltpu.make_async_remote_copy(
                    source,
                    target,
                    self.send.at[i],
                    self.recv.at[i],
                    device_id={SECTION: 1 - section},
                    device_id_type=MESH,
                )
            )

        for x, target in zip(self.xs, self.other_x):
            add(x, target)
        for (_, _, parts), target in zip(self.plan, self.other_y):
            at = 0
            for y, low, high, width in parts:
                start = pl.multiple_of(low + (high - low) * (1 - section), 128)
                add(self.ys[y].at[:, pl.ds(start, width)], target.at[:, at : at + width])
                at += width
        return copies

    def start(self):
        for copy in self.copies():
            copy.start()
        section = lax.axis_index(SECTION)
        for (_, _, parts), own in zip(self.plan, self.own_y):
            at = 0
            for y, low, high, width in parts:
                start = pl.multiple_of(low + (high - low) * section, 128)
                own[:, at : at + width] = self.ys[y][:, pl.ds(start, width)]
                at += width

    def step(self, i, steps):
        place, count = lax.axis_index(CTX), lax.axis_size(CTX)

        @pl.when(i == self.first)
        def _():
            for copy in self.copies():
                copy.wait_recv()

        each = -(-count * len(self.plan) // (steps - self.first))
        begin = (i - self.first) * each

        def piece(t, _):
            at = [0, 0]
            for f, (x, stream, _) in enumerate(self.plan):
                k = t - f * count
                width = self.own_y[f].shape[1]
                where = slice(at[stream], at[stream] + width)
                at[stream] += width
                kept, sent = self.outs[2 * stream : 2 * stream + 2]

                @pl.when((k >= 0) & (k < count))
                def _():
                    block = kept.shape[1]
                    source = flipped(place, mirrored(k, count) if stream else k, count)
                    cols = pl.ds(pl.multiple_of(source * block, block), block)
                    dims = (((0,), (0,)), ((), ()))
                    total = lax.dot_general(
                        self.xs[x][:, cols], self.own_y[f][...], dims, preferred_element_type=f32
                    ) + lax.dot_general(
                        self.other_x[x][:, cols],
                        self.other_y[f][...],
                        dims,
                        preferred_element_type=f32,
                    )
                    low = total.astype(bf16)

                    @pl.when(k < count // 2)
                    def _():
                        kept[k, :, where] = low

                    @pl.when(k >= count // 2)
                    def _():
                        sent[k - count // 2, :, where] = low

            return 0

        @pl.when(i >= self.first)
        def _():
            lax.fori_loop(begin, begin + each, piece, 0)

    def finish(self):
        for copy in self.copies():
            copy.wait_send()


class Halving:
    cuts = 2

    def __init__(self, streams, outs, scratch, turns):
        self.turns = turns
        self.place, self.count = lax.axis_index(CTX), lax.axis_size(CTX)
        self.streams, self.outs = streams, outs
        self.orders = ctx_orders()
        self.levels = len(self.orders[0])
        self.inbox = [scratch[k * self.levels : (k + 1) * self.levels] for k in range(2)]
        rest = scratch[2 * self.levels :]
        self.sums = [rest[k * (self.levels - 1) : (k + 1) * (self.levels - 1)] for k in range(2)]
        self.send, self.recv = rest[2 * (self.levels - 1) :]

    def greet(self, bar):
        for bit in self.orders[0]:
            peer = flipped(self.place, bit, self.count)
            pl.semaphore_signal(bar, inc=1, device_id={CTX: peer}, device_id_type=MESH)
        return self.levels

    def rows(self, cut):
        size = self.outs[0].shape[0] // self.cuts
        return pl.ds(cut * size, size)

    def copy(self, level, stream, cut):
        rows = self.rows(cut)
        if level == 0:
            source = self.streams[2 * stream + 1].at[:, rows, :]
        else:
            blocks = self.count >> (level + 1)
            source = self.sums[stream][level - 1].at[pl.ds(blocks, blocks), rows, :]
        i = (level * 2 + stream) * self.cuts + cut
        return pltpu.make_async_remote_copy(
            source,
            self.inbox[stream][level].at[:, rows, :],
            self.send.at[i],
            self.recv.at[i],
            device_id={CTX: flipped(self.place, self.orders[stream][level], self.count)},
            device_id_type=MESH,
        )

    def advance(self, level, cut):
        rows, blocks = self.rows(cut), self.count >> (level + 1)
        for stream in range(2):
            self.copy(level, stream, cut).wait_recv()
            kept = self.streams[2 * stream] if level == 0 else self.sums[stream][level - 1]
            for k in range(blocks):
                total = kept[k, rows, :].astype(f32) + self.inbox[stream][level][k, rows, :].astype(
                    f32
                )
                if level + 1 < self.levels:
                    self.sums[stream][level][k, rows, :] = total.astype(bf16)
                else:
                    self.outs[stream][rows, :] = total.astype(bf16)
            if level + 1 < self.levels:
                self.copy(level + 1, stream, cut).start()

    def start(self):
        for cut in range(self.cuts):
            for stream in range(2):
                self.copy(0, stream, cut).start()

    def step(self, i, steps):
        for cut, turn in enumerate(self.turns):

            @pl.when(i == turn)
            def _():
                self.advance(0, cut)

    def finish(self):
        for cut in range(len(self.turns), self.cuts):
            self.advance(0, cut)
        for level in range(1, self.levels):
            for cut in range(self.cuts):
                self.advance(level, cut)
        for level in range(self.levels):
            for stream in range(2):
                for cut in range(self.cuts):
                    self.copy(level, stream, cut).wait_send()


def halving_scratch(streams):
    blocks, rows, width = streams[0].shape
    levels = len(ctx_bits())
    inbox = [pltpu.VMEM((blocks >> k, rows, width), bf16) for k in range(levels)]
    copies = levels * 2 * Halving.cuts
    return [*inbox * 2, *inbox[: levels - 1] * 2, *[pltpu.SemaphoreType.DMA((copies,))] * 2]


class Together:
    def __init__(self, *jobs):
        self.jobs = jobs

    def greet(self, bar):
        return sum(job.greet(bar) for job in self.jobs)

    def start(self):
        for job in self.jobs:
            job.start()

    def step(self, i, steps):
        for job in self.jobs:
            job.step(i, steps)

    def finish(self):
        for job in self.jobs:
            job.finish()


def scatter_kernel(n, chunks, lag, p_ref, q_ref, d_ref, v_ref, gain_ref, *refs):
    streams, outs, totals, scratch = refs[:4], refs[4:8], refs[8:10], refs[10:]
    job = Halving(streams, totals, scratch[9:], (7, 14))
    back_rows(n, chunks, lag, p_ref, d_ref, v_ref, gain_ref, *outs[:3], scratch[:9], job, q_ref, outs[3])


def back_kernel(n, chunks, lag, plan, x_count, y_count, beside, ready, p_ref, *refs):
    q_ref = q_out = None
    if beside:
        q_ref, refs = refs[0], refs[1:]
    (d_ref, v_ref, gain_ref), refs = refs[:3], refs[3:]
    xs, refs = refs[:x_count], refs[x_count:]
    ys, refs = refs[:y_count], refs[y_count:]
    streams, refs = refs[:ready], refs[ready:]
    out_ref, low_ref, gg_ref = refs[:3]
    refs = refs[3:]
    if beside:
        q_out, refs = refs[0], refs[1:]
    sums, refs = refs[:4], refs[4:]
    totals, refs = refs[: ready // 2], refs[ready // 2 :]
    cut = len(xs) + 2 * len(plan) + 2
    fill = Fill(plan, xs, ys, sums, refs[9 : 9 + cut])
    if ready:
        turns = (11, 20) if beside else (14,)
        fill = Together(fill, Halving(streams, totals, refs[9 + cut :], turns))
    outs = out_ref, low_ref, gg_ref
    back_rows(n, chunks, lag, p_ref, d_ref, v_ref, gain_ref, *outs, refs[:9], fill, q_ref, q_out)


def back_rows(
    n,
    chunks,
    lag,
    p_ref,
    d_ref,
    v_ref,
    gain_ref,
    out_ref,
    low_ref,
    gg_ref,
    scratch,
    fill,
    q_ref=None,
    q_out=None,
):
    rows, width = p_ref.shape[0] // chunks, p_ref.shape[1]
    gg_ref[...] = jnp.zeros_like(gg_ref)

    def p_rows(j):
        part = row_slice(j, rows)
        if q_ref is None:
            return p_ref[part, :]
        return jnp.concatenate([p_ref[part, :], q_ref[part, :].astype(f32)], axis=1)

    def done(j, total):
        if q_ref is not None:
            q_out[row_slice(j, rows), :] = total[:, width:].astype(bf16)
            total = total[:, :width]
        v = v_ref[row_slice(j, rows), :].astype(f32)
        r = lax.rsqrt(jnp.mean(v * v, axis=-1, keepdims=True) + eps)
        vr = v * r
        dg = total * gain_ref[...]
        inner = jnp.mean(dg * vr, axis=-1, keepdims=True)
        gg_ref[...] += jnp.sum((total * vr).reshape(rows // 8, 8, vr.shape[1]), axis=0)
        out = d_ref[row_slice(j, rows), :].astype(f32) + r * (dg - vr * inner)
        out_ref[row_slice(j, rows), :] = out
        low_ref[row_slice(j, rows), :] = out.astype(bf16)

    line_sum(n, chunks, lag, p_rows, done, *scratch, fill=fill)


def summed(kernel, collective, outs, *operands, extra=(), more=0, far=(0, 0), room=58):
    n = lax.axis_size(SHARD)
    length, width = operands[0].shape[0], operands[0].shape[1] + more
    box = pltpu.VMEM((CHUNKS, length // CHUNKS, width), bf16)
    distant = pl.BlockSpec(memory_space=pl.ANY)
    whole = pl.BlockSpec(memory_space=pltpu.VMEM)
    return pl.pallas_call(
        functools.partial(kernel, n, CHUNKS, LAG),
        out_shape=outs,
        in_specs=[whole] * (len(operands) - far[0]) + [distant] * far[0],
        out_specs=[whole] * (len(outs) - far[1]) + [distant] * far[1],
        scratch_shapes=[box] * 4
        + [pltpu.SemaphoreType.DMA((CHUNKS,))] * 4
        + [pltpu.VMEM((length // CHUNKS, width), f32), *extra],
        compiler_params=pltpu.CompilerParams(
            collective_id=collective, has_side_effects=True, vmem_limit_bytes=room << 20
        ),
        cost_estimate=pl.CostEstimate(flops=0, bytes_accessed=20 << 20, transcendentals=0),
        name="line_sum"+str(collective),
    )(*operands)


def line_gather(rows):
    count, place = lax.axis_size(SHARD), lax.axis_index(SHARD)
    part = rows.shape[0]
    block = jnp.zeros((count * part, rows.shape[1]), rows.dtype)
    block = lax.dynamic_update_slice_in_dim(block, rows, place * part, 0)
    for k in reversed(range(1, count)):
        got = lax.ppermute(rows, SHARD, [(i, i ^ k) for i in range(count)])
        block = lax.dynamic_update_slice_in_dim(block, got, (place ^ k) * part, 0)
    return block


def shaped(array, dtype):
    return jax.ShapeDtypeStruct(array.shape, dtype)


def copying_sum(kernel, collective, dtype, p, hidden, gain, wanted):
    layers, own, other = zip(*wanted)
    outs = [shaped(p, dtype), shaped(p, bf16)] + [shaped(a, bf16) for a in own]
    boxes = [pltpu.VMEM((2, a.shape[0] // Copies.parts, a.shape[1]), bf16) for a in own]
    first, low, *chosen = summed(
        functools.partial(copying, kernel, layers),
        collective,
        outs,
        p,
        hidden,
        gain[None],
        *own,
        *other,
        extra=[*boxes, *[pltpu.SemaphoreType.DMA((2 * len(layers),))] * 2],
        far=(2 * len(layers), len(layers)),
        room=26,
    )
    return first, low, chosen


def back_sum(collective, p, d_out, values, gain, plan, xs, ys, beside=(), ready=()):
    count = lax.axis_size(CTX)
    length = p.shape[0]
    outs = [shaped(p, f32), shaped(p, bf16), jax.ShapeDtypeStruct((8, p.shape[1]), f32)]
    outs += [shaped(q, bf16) for q in beside]
    widths = [sum(part[3] for part in parts) for _, _, parts in plan]
    for stream in range(2):
        total = sum(w for (_, at, _), w in zip(plan, widths) if at == stream)
        shape = (count // 2, xs[0].shape[1] // count, total)
        outs += [jax.ShapeDtypeStruct(shape, bf16)] * 2
    extra = [pltpu.VMEM(x.shape, bf16) for x in xs]
    extra += [pltpu.VMEM((length, w), bf16) for w in widths] * 2
    copies = len(xs) + sum(len(parts) for _, _, parts in plan)
    extra += [pltpu.SemaphoreType.DMA((copies,))] * 2
    if ready:
        outs += [jax.ShapeDtypeStruct(a.shape[1:], bf16) for a in ready[::2]]
        extra += halving_scratch(ready)

    def bound(n, chunks, lag, *refs):
        back_kernel(n, chunks, lag, plan, len(xs), len(ys), bool(beside), len(ready), *refs)

    operands = (p, *beside, d_out, values, gain[None], *xs, *ys, *ready)
    more = sum(q.shape[1] for q in beside)
    out, low, gg, *sums = summed(bound, collective, outs, *operands, extra=extra, more=more)
    return out, low, jnp.sum(gg, axis=0), *sums


def back_sum_scatter(collective, p, beside, d_out, values, gain, streams):
    outs = [shaped(p, f32), shaped(p, bf16), jax.ShapeDtypeStruct((8, p.shape[1]), f32)]
    outs += [shaped(beside, bf16)]
    outs += [jax.ShapeDtypeStruct(a.shape[1:], bf16) for a in streams[::2]]
    operands = (p, beside, d_out, values, gain[None], *streams)
    more = beside.shape[1]
    out, low, gg, whole, *totals = summed(
        scatter_kernel, collective, outs, *operands, extra=halving_scratch(streams), more=more, room=36
    )
    return out, low, jnp.sum(gg, axis=0), whole, totals


def dot(left, right, dims=((1,), (0,))):
    return lax.dot_general(left, right, (dims, ((), ())), preferred_element_type=f32)


NT = ((1,), (1,))
TN = ((0,), (0,))


def in_three(values):
    high = values.astype(bf16)
    rest = values - high.astype(f32)
    mid = rest.astype(bf16)
    return high, mid, (rest - mid.astype(f32)).astype(bf16)


def running_sum(values, reverse):
    length = values.shape[0]
    row = lax.broadcasted_iota(jnp.int32, (length, length), 0)
    col = lax.broadcasted_iota(jnp.int32, (length, length), 1)
    kept = jnp.where(row <= col if reverse else row >= col, 1.0, 0.0).astype(bf16)
    return sum(dot(kept, part) for part in in_three(values))


def lanes(shape):
    return lax.broadcasted_iota(jnp.int32, shape, 1)


def column(values, head):
    return jnp.sum(jnp.where(lanes(values.shape) == head, values, 0.0), axis=1, keepdims=True)


def in_pair(values, pair):
    low, high = column(values, 2 * pair), column(values, 2 * pair + 1)
    return jnp.where(lanes(values.shape) < HP, low, high)


def from_pair(values, pair):
    lane = lanes(values.shape)
    low = jnp.sum(jnp.where(lane < HP, values, 0.0), axis=1, keepdims=True)
    high = jnp.sum(jnp.where(lane < HP, 0.0, values), axis=1, keepdims=True)
    return jnp.where(lane == 2 * pair, low, 0.0) + jnp.where(lane == 2 * pair + 1, high, 0.0)


def pair_ds(pair, start=0):
    return pl.ds(pl.multiple_of(start + pair * 2 * HP, 2 * HP), 2 * HP)


def steps_of(step_raw, vec_ref, tok_ref, cum, cum_rows, step, enter, fade):
    shifted = step_raw + vec_ref[0:1, :]
    step[...] = jnp.maximum(shifted, 0.0) + jnp.log1p(jnp.exp(-jnp.abs(shifted)))
    cum[...] = running_sum(-step[...] * vec_ref[1:2, :], False)
    total = cum[...]
    cum_rows[...] = total.T
    enter[...] = jnp.exp(total) * tok_ref[:, 1:2]
    fade[...] = jnp.exp(total[-1:, :] - total) * tok_ref[:, 2:3]
    return shifted


def masks_of(tok_ref, key_ref):
    kept = (tok_ref[:, 3:4] >= key_ref[1:2, :]) & (tok_ref[:, 0:1] == key_ref[0:1, :])
    return jnp.where(kept, 0.0, -1e30)


def ctx_barrier(count, place):
    bar = pltpu.get_barrier_semaphore()

    def greet(k, _):
        pl.semaphore_signal(
            bar, inc=1, device_id={CTX: lax.rem(place + k, count)}, device_id_type=MESH
        )
        return 0

    lax.fori_loop(1, count, greet, 0)
    pl.semaphore_wait(bar, count - 1)


def ctx_copy(source, target, send, recv, peer):
    return pltpu.make_async_remote_copy(
        source, target, send, recv, device_id={CTX: peer}, device_id_type=MESH
    )


def mix_forward_kernel(
    count,
    widths,
    heads,
    proj_ref,
    vec_ref,
    skip_ref,
    tok_ref,
    key_ref,
    both_ref,
    mixed_ref,
    state_ref,
    keyval_ref,
    decay_ref,
    cum,
    cum_rows,
    step,
    enter,
    fade,
    mask,
    crossed,
    keyvals,
    fresh,
    decays,
    total_state,
    kv_send,
    kv_recv,
    st_send,
    st_recv,
    dc_send,
    dc_recv,
):
    place = lax.axis_index(CTX)
    length = proj_ref.shape[0]
    inner = (proj_ref.shape[1] - widths[3]) // 2
    pairs = heads // 2
    states = (widths[2] - widths[1]) // 2
    ctx_barrier(count, place)

    keyvals[0] = proj_ref[:, widths[0] : widths[1]].astype(bf16)

    def kv_copy(k):
        peer = lax.rem(place + k, count)
        return ctx_copy(keyvals.at[0], keyvals.at[k], kv_send.at[k], kv_recv.at[k], peer)

    def st_copy(k):
        peer = lax.rem(place + k, count)
        return ctx_copy(fresh.at[0], fresh.at[k], st_send.at[k], st_recv.at[k], peer)

    def dc_copy(k):
        peer = lax.rem(place + k, count)
        return ctx_copy(decays.at[0], decays.at[k], dc_send.at[k], dc_recv.at[k], peer)

    def kv_start(k, _):
        kv_copy(k).start()
        return 0

    lax.fori_loop(1, count, kv_start, 0)
    steps_of(
        proj_ref[:, widths[2] : widths[2] + 128], vec_ref, tok_ref, cum, cum_rows, step, enter, fade
    )
    last = cum_rows[: decays.shape[1], length - 1 :]
    decays[0] = jnp.broadcast_to(jnp.exp(last) * tok_ref[0:1, 4:5], decays.shape[1:])
    b_low = proj_ref[:, widths[1] : widths[1] + states].astype(bf16)
    c_low = proj_ref[:, widths[1] + states : widths[2]].astype(bf16)

    def make_fresh(pair, _):
        x = proj_ref[:, pair_ds(pair, widths[3] + inner)]
        x = x.astype(bf16).astype(f32)
        faded = (x * in_pair(fade[...] * step[...], pair)).astype(bf16)
        fresh[0, pair_ds(pair), :] = dot(faded, b_low, TN).astype(bf16)
        return 0

    lax.fori_loop(0, pairs, make_fresh, 0)

    def st_start(k, _):
        dc_copy(k).start()

        @pl.when(place + k < count)
        def _():
            st_copy(k).start()

        return 0

    lax.fori_loop(1, count, st_start, 0)
    mask[...] = masks_of(tok_ref, key_ref)
    crossed[...] = dot(c_low, b_low, NT) * states ** (-0.5)

    def inside(pair, _):
        x = proj_ref[:, pair_ds(pair, widths[3] + inner)]
        x = x.astype(bf16).astype(f32)
        xdt = (x * in_pair(step[...], pair)).astype(bf16)
        parts = []
        for side in range(2):
            head = 2 * pair + side
            spread = column(cum[...], head) - cum_rows[pl.ds(head, 1), :]
            weight = jnp.exp(spread + mask[:, :length])
            parts.append(dot((weight * crossed[...]).astype(bf16), xdt))
        mixed_ref[:, pair_ds(pair)] = jnp.where(lanes(parts[0].shape) < HP, *parts)
        return 0

    lax.fori_loop(0, pairs, inside, 0)

    def kv_wait(k, _):
        kv_copy(k).wait_recv()
        return 0

    lax.fori_loop(1, count, kv_wait, 0)
    keyval_ref[...] = keyvals[...].reshape(keyval_ref.shape)
    for head in range(widths[0] // HD):
        query = proj_ref[:, head * HD : (head + 1) * HD].astype(bf16)
        scores = dot(query, keyval_ref[:, :HD], NT) * HD ** (-0.5) + mask[...]
        expo = jnp.exp(scores - jnp.max(scores, axis=1, keepdims=True))
        soft = expo * (1.0 / jnp.sum(expo, axis=1, keepdims=True))
        both_ref[:, head * HD : (head + 1) * HD] = dot(
            soft.astype(bf16), keyval_ref[:, HD:]
        ).astype(bf16)

    def dc_wait(k, _):
        dc_copy(k).wait_recv()

        @pl.when(k <= place)
        def _():
            st_copy(k).wait_recv()

        return 0

    lax.fori_loop(1, count, dc_wait, 0)
    total_state[...] = jnp.zeros_like(total_state)
    head_width = inner // heads

    def combine(index, _):
        slot = place - index

        def one_head(head, _):
            rows = pl.ds(pl.multiple_of(head * head_width, head_width), head_width)
            total_state[rows, :] = total_state[rows, :] * decays[slot, pl.ds(head, 1), :] + fresh[
                slot, rows, :
            ].astype(f32)
            return 0

        lax.fori_loop(0, heads, one_head, 0)
        return 0

    lax.fori_loop(0, place, combine, 0)
    state_ref[...] = total_state[...].astype(bf16)
    decay_ref[...] = decays[...]

    def finish(pair, _):
        carried = dot(c_low, state_ref[pair_ds(pair), :], NT)
        mixed = mixed_ref[:, pair_ds(pair)] + carried * in_pair(enter[...], pair)
        mixed_ref[:, pair_ds(pair)] = mixed
        x = proj_ref[:, pair_ds(pair, widths[3] + inner)]
        x = x.astype(bf16).astype(f32)
        gate = proj_ref[:, pair_ds(pair, widths[3])]
        y = mixed + x * skip_ref[0:1, pair_ds(pair)]
        both_ref[:, pair_ds(pair, widths[0])] = (
            y * gate / (1.0 + jnp.exp(-gate))
        ).astype(bf16)
        return 0

    lax.fori_loop(0, pairs, finish, 0)

    def drain(k, _):
        kv_copy(k).wait_send()
        dc_copy(k).wait_send()

        @pl.when(place + k < count)
        def _():
            st_copy(k).wait_send()

        return 0

    lax.fori_loop(1, count, drain, 0)


def mix_backward_kernel(
    count,
    widths,
    heads,
    proj_ref,
    vec_ref,
    skip_ref,
    tok_ref,
    key_ref,
    mixed_ref,
    state_ref,
    keyval_ref,
    decay_ref,
    d_both_ref,
    d_proj_ref,
    d_vec_ref,
    cum,
    cum_rows,
    step,
    enter,
    fade,
    mask,
    crossed,
    d_crossed,
    d_y,
    d_carried,
    d_x,
    d_keyval,
    d_b,
    d_c,
    d_cum,
    d_step,
    d_coeff,
    d_skip,
    d_states,
    total_state,
    kv_out,
    kv_in,
    kv_send,
    kv_recv,
    st_send,
    st_recv,
):
    place = lax.axis_index(CTX)
    length = proj_ref.shape[0]
    inner = (proj_ref.shape[1] - widths[3]) // 2
    pairs = heads // 2
    head_width = inner // heads
    states = (widths[2] - widths[1]) // 2
    ctx_barrier(count, place)

    def back(k):
        return lax.rem(place + count - k, count)

    def kv_copy(k):
        return ctx_copy(kv_out.at[k], kv_in.at[k], kv_send.at[k], kv_recv.at[k], back(k))

    def st_copy(k):
        return ctx_copy(d_states.at[0], d_states.at[k], st_send.at[k], st_recv.at[k], back(k))

    shifted = steps_of(
        proj_ref[:, widths[2] : widths[2] + 128], vec_ref, tok_ref, cum, cum_rows, step, enter, fade
    )
    b_low = proj_ref[:, widths[1] : widths[1] + states].astype(bf16)
    c_low = proj_ref[:, widths[1] + states : widths[2]].astype(bf16)
    d_cum[...] = jnp.zeros_like(d_cum)
    d_step[...] = jnp.zeros_like(d_step)
    d_coeff[...] = jnp.zeros_like(d_coeff)
    d_skip[...] = jnp.zeros_like(d_skip)

    def x_of(pair):
        x = proj_ref[:, pair_ds(pair, widths[3] + inner)]
        return x.astype(bf16).astype(f32)

    def outer(pair, _):
        gate = proj_ref[:, pair_ds(pair, widths[3])]
        d_gated = d_both_ref[:, pair_ds(pair, widths[0])]
        x, mixed, skip = x_of(pair), mixed_ref[:, pair_ds(pair)], skip_ref[0:1, pair_ds(pair)]
        sig = 1.0 / (1.0 + jnp.exp(-gate))
        dy = d_gated * gate * sig
        d_gate = d_gated * (mixed + x * skip) * sig * (1.0 + gate * (1.0 - sig))
        d_proj_ref[:, pair_ds(pair, widths[3])] = d_gate.astype(bf16)
        low = dy.astype(bf16)
        d_y[:, pair_ds(pair)] = low
        d_x[:, pair_ds(pair)] = dy * skip
        d_skip[...] += from_pair(dy * x, pair)
        d_cum[...] += from_pair(low.astype(f32) * mixed, pair)
        carried = (low.astype(f32) * in_pair(enter[...], pair)).astype(bf16)
        d_carried[:, pair_ds(pair)] = carried
        d_states[0, pair_ds(pair), :] = dot(carried, c_low, TN).astype(bf16)
        return 0

    lax.fori_loop(0, pairs, outer, 0)

    def st_start(k, _):
        @pl.when(k <= place)
        def _():
            st_copy(k).start()

        return 0

    lax.fori_loop(1, count, st_start, 0)
    mask[...] = masks_of(tok_ref, key_ref)
    for head in range(widths[0] // HD):
        cols = slice(head * HD, (head + 1) * HD)
        query = proj_ref[:, cols].astype(bf16)
        scores = dot(query, keyval_ref[:, :HD], NT) * HD ** (-0.5) + mask[...]
        expo = jnp.exp(scores - jnp.max(scores, axis=1, keepdims=True))
        soft = expo * (1.0 / jnp.sum(expo, axis=1, keepdims=True))
        grad = d_both_ref[:, cols].astype(bf16)
        d_soft = dot(grad, keyval_ref[:, HD:], NT)
        d_scores = soft * (d_soft - jnp.sum(soft * d_soft, axis=1, keepdims=True))
        d_raw = (d_scores * HD ** (-0.5)).astype(bf16)
        d_proj_ref[:, cols] = dot(d_raw, keyval_ref[:, :HD]).astype(bf16)
        d_keys, d_values = dot(d_raw, query, TN), dot(soft.astype(bf16), grad, TN)
        if head == 0:
            d_keyval[:, :HD] = d_keys
            d_keyval[:, HD:] = d_values
        else:
            d_keyval[:, :HD] += d_keys
            d_keyval[:, HD:] += d_values
    kv_out[...] = d_keyval[...].astype(bf16).reshape(kv_out.shape)

    def kv_start(k, _):
        kv_copy(k).start()
        return 0

    lax.fori_loop(1, count, kv_start, 0)
    crossed[...] = dot(c_low, b_low, NT) * states ** (-0.5)
    d_crossed[...] = jnp.zeros_like(d_crossed)

    def inside(pair, _):
        x = x_of(pair)
        steps = in_pair(step[...], pair)
        xdt = (x * steps).astype(bf16)
        low = d_y[:, pair_ds(pair)]
        lane = lanes(low.shape)
        parts = []
        for side in range(2):
            head = 2 * pair + side
            spread = column(cum[...], head) - cum_rows[pl.ds(head, 1), :]
            weight = jnp.exp(spread + mask[:, :length])
            parts.append(dot((weight * crossed[...]).astype(bf16), low, TN))
            mine = (lane >= HP) if side else (lane < HP)
            alone = jnp.where(mine, low.astype(f32), 0.0).astype(bf16)
            d_crossed[...] += dot(alone, xdt, NT) * weight
        d_xdt = jnp.where(lane < HP, *parts)
        d_x[:, pair_ds(pair)] += d_xdt * steps
        d_step[...] += from_pair(d_xdt * x, pair)
        d_cum[...] -= from_pair(d_xdt * xdt.astype(f32), pair)
        return 0

    lax.fori_loop(0, pairs, inside, 0)
    low_crossed = (d_crossed[...] * states ** (-0.5)).astype(bf16)
    d_c[...] = dot(low_crossed, b_low) + dot(d_carried[...], state_ref[...])
    d_b[...] = dot(low_crossed, c_low, TN)

    def st_wait(k, _):
        @pl.when(place + k < count)
        def _():
            st_copy(k).wait_recv()

        return 0

    lax.fori_loop(1, count, st_wait, 0)
    total_state[...] = jnp.zeros_like(total_state)

    def combine(index, _):
        slot = count - 1 - place - index
        source = lax.rem(count - slot, count)

        def one_head(head, _):
            rows = pl.ds(pl.multiple_of(head * head_width, head_width), head_width)
            total_state[rows, :] = total_state[rows, :] * decay_ref[
                source, pl.ds(head, 1), :
            ] + d_states[slot, rows, :].astype(f32)
            return 0

        lax.fori_loop(0, heads, one_head, 0)
        return 0

    lax.fori_loop(0, count - 1 - place, combine, 0)
    d_vec_ref[...] = jnp.zeros_like(d_vec_ref)

    def from_later(pair, _):
        rows = pair_ds(pair)
        later = total_state[rows, :]
        low = later.astype(bf16)
        x = x_of(pair)
        coeffs = in_pair(fade[...] * step[...], pair)
        back_x = dot(b_low, low, NT)
        d_proj_ref[:, pair_ds(pair, widths[3] + inner)] = (
            d_x[:, rows] + back_x * coeffs
        ).astype(bf16)
        d_coeff[...] += from_pair(back_x * x, pair)
        d_b[...] += dot((x * coeffs).astype(bf16), low)
        product = later * state_ref[rows, :].astype(f32)
        row = lax.broadcasted_iota(jnp.int32, product.shape, 0)
        lane = lanes((1, 128))
        for side in range(2):
            mine = (row >= HP) if side else (row < HP)
            part = jnp.sum(jnp.where(mine, product, 0.0), axis=0, keepdims=True)
            part = jnp.sum(part, axis=1, keepdims=True)
            d_vec_ref[3:4, :] += jnp.where(lane == 2 * pair + side, part, 0.0)
        return 0

    lax.fori_loop(0, pairs, from_later, 0)
    fading = fade[...]
    d_keep = d_coeff[...] * fading * step[...]
    block_decay = jnp.exp(cum[length - 1 :, :]) * tok_ref[0:1, 4:5]
    d_last = jnp.sum(d_keep, axis=0, keepdims=True) + block_decay * d_vec_ref[3:4, :]
    d_log = running_sum(d_cum[...] - d_keep, True) + d_last
    d_size = d_step[...] + d_coeff[...] * fading - vec_ref[1:2, :] * d_log
    d_raw_step = d_size / (1.0 + jnp.exp(-shifted))
    d_proj_ref[:, widths[2] : widths[3]] = jnp.where(
        lanes(d_raw_step.shape) < heads, d_raw_step, 0.0
    ).astype(bf16)
    d_vec_ref[0:1, :] = jnp.sum(d_raw_step, axis=0, keepdims=True)
    d_vec_ref[1:2, :] = -jnp.sum(step[...] * d_log, axis=0, keepdims=True)
    d_vec_ref[2:3, :] = jnp.sum(d_skip[...], axis=0, keepdims=True)
    d_proj_ref[:, widths[1] : widths[1] + states] = d_b[...].astype(bf16)
    d_proj_ref[:, widths[1] + states : widths[2]] = d_c[...].astype(bf16)

    def kv_wait(k, _):
        kv_copy(k).wait_recv()
        d_keyval[:length, :] += kv_in[k].astype(f32)
        return 0

    lax.fori_loop(1, count, kv_wait, 0)
    d_proj_ref[:, widths[0] : widths[1]] = d_keyval[:length, :].astype(bf16)

    def drain(k, _):
        kv_copy(k).wait_send()

        @pl.when(k <= place)
        def _():
            st_copy(k).wait_send()

        return 0

    lax.fori_loop(1, count, drain, 0)


def mixer_call(kernel, collective, outs, scratch, sems, widths, heads, operands, room):
    count = lax.axis_size(CTX)
    whole = pl.BlockSpec(memory_space=pltpu.VMEM)
    return pl.pallas_call(
        functools.partial(kernel, count, widths, heads),
        out_shape=outs,
        in_specs=[whole] * len(operands),
        out_specs=[whole] * len(outs),
        scratch_shapes=[pltpu.VMEM(*s) for s in scratch]
        + [pltpu.SemaphoreType.DMA((count,))] * sems,
        compiler_params=pltpu.CompilerParams(
            collective_id=collective,
            has_side_effects=True,
            vmem_limit_bytes=(room + 2 * count) << 20,
        ),
        cost_estimate=pl.CostEstimate(flops=0, bytes_accessed=20 << 20, transcendentals=0),
        name="mixer"+str(collective),
    )(*operands)


def mix_forward(weights, proj, layout):
    count = lax.axis_size(CTX)
    widths, heads = weights.widths, weights.heads
    length, inner = proj.shape[0], (proj.shape[1] - widths[3]) // 2
    states = (widths[2] - widths[1]) // 2
    kv = widths[1] - widths[0]
    shape = jax.ShapeDtypeStruct
    head_rows = -(-heads // 8) * 8
    outs = [
        shape((length, widths[0] + inner), bf16),
        shape((length, inner), f32),
        shape((inner, states), bf16),
        shape((count * length, kv), bf16),
        shape((count, head_rows, states), f32),
    ]
    per_head = ((length, 128), f32)
    scratch = [
        per_head,
        ((128, length), f32),
        per_head,
        per_head,
        per_head,
        ((length, count * length), f32),
        ((length, length), f32),
        ((count, length, kv), bf16),
        ((count, inner, states), bf16),
        ((count, head_rows, states), f32),
        ((inner, states), f32),
    ]
    operands = (proj, weights.head_rows, weights.skip_row, *layout)
    return mixer_call(mix_forward_kernel, 5, outs, scratch, 6, widths, heads, operands, 18)


def mix_backward(weights, saved, d_both, layout):
    count = lax.axis_size(CTX)
    widths, heads = weights.widths, weights.heads
    proj = saved.proj
    length, inner = proj.shape[0], (proj.shape[1] - widths[3]) // 2
    states = (widths[2] - widths[1]) // 2
    kv = widths[1] - widths[0]
    shape = jax.ShapeDtypeStruct
    outs = [shape(proj.shape, bf16), shape((8, 128), f32)]
    per_head = ((length, 128), f32)
    square = ((length, length), f32)
    scratch = [
        per_head,
        ((128, length), f32),
        per_head,
        per_head,
        per_head,
        ((length, count * length), f32),
        square,
        square,
        ((length, inner), bf16),
        ((length, inner), bf16),
        ((length, inner), f32),
        ((count * length, kv), f32),
        ((length, states), f32),
        ((length, states), f32),
        per_head,
        per_head,
        per_head,
        per_head,
        ((count, inner, states), bf16),
        ((inner, states), f32),
        ((count, length, kv), bf16),
        ((count, length, kv), bf16),
    ]
    operands = (
        proj,
        weights.head_rows,
        weights.skip_row,
        *layout,
        saved.mixed,
        saved.state_in,
        saved.keyval_all,
        saved.decays,
        d_both,
    )
    return mixer_call(mix_backward_kernel, 6, outs, scratch, 4, widths, heads, operands, 24)


def finish_kernel(
    count,
    places,
    widths,
    *refs,
):
    unsummed, arrays, refs = refs[:8], refs[8:14], refs[14:]
    (
        rows0,
        rows1,
        grad0,
        grad1,
        tiny0,
        tiny1,
        wide0,
        wide1,
        columns0,
        columns1,
        *refs,
    ) = refs
    (
        query_out,
        zx_out,
        up_out,
        down_out,
        out_out,
        rows_out,
        grad_out,
        shared_out,
        tiny_out,
        *refs,
    ) = refs
    arrays, refs = (*refs[:4], *arrays), refs[4:]
    boxes, refs = refs[: len(widths)], refs[len(widths) :]
    (
        rows_box,
        grad_box,
        tiny_box,
        tiny_sum,
        tiny_all,
        wide_boxes,
        columns_boxes,
        blocks,
        blocks_box,
        shared,
        shared_box,
        send,
        recv,
        ctx_send,
        ctx_recv,
    ) = refs
    section, place = lax.axis_index(SECTION), lax.axis_index(CTX)
    bar = pltpu.get_barrier_semaphore()
    pl.semaphore_signal(bar, inc=1, device_id={SECTION: 1 - section}, device_id_type=MESH)
    for k in range(1, count):
        peer = flipped(place, k, count)
        pl.semaphore_signal(bar, inc=1, device_id={CTX: peer}, device_id_type=MESH)
    pl.semaphore_wait(bar, count)
    half = wide0.shape[1] // 2
    own_half = pl.ds(pl.multiple_of(section * half, half), half)
    other_half = pl.ds(pl.multiple_of((1 - section) * half, half), half)

    def over(i, source, target):
        return pltpu.make_async_remote_copy(
            source,
            target,
            send.at[i],
            recv.at[i],
            device_id={SECTION: 1 - section},
            device_id_type=MESH,
        )

    def across(i, k, source, target):
        return pltpu.make_async_remote_copy(
            source,
            target,
            ctx_send.at[i],
            ctx_recv.at[i],
            device_id={CTX: flipped(place, k, count)},
            device_id_type=MESH,
        )

    def part(layer, i):
        array, start, width = places[layer][i]
        return arrays[array].at[:, start : start + width]

    def by_section(act, first, second):
        @pl.when(section == 1)
        def _():
            act(first)

        @pl.when(section == 0)
        def _():
            act(second)

    block = blocks.shape[2]
    wides, columns = (wide0, wide1), (columns0, columns1)
    early = [over(l, wides[l].at[:, other_half], wide_boxes.at[l]) for l in range(2)]
    early += [over(2 + l, columns[l], columns_boxes.at[l]) for l in range(2)]
    for copy in early:
        copy.start()
    for i in range(4):
        arrays[i][...] = (unsummed[2 * i][...].astype(f32) + unsummed[2 * i + 1][...].astype(f32)).astype(bf16)
    pairs = [(tiny0, tiny1, tiny_box)]
    pairs += [(part(0, i), part(1, i), box) for i, box in enumerate(boxes)]
    pairs += [(rows0, rows1, rows_box), (grad0, grad1, grad_box)]
    copies = [
        (over(4 + i, first, box), over(4 + i, second, box))
        for i, (first, second, box) in enumerate(pairs)
    ]

    def each(act, which):
        for first, second in which:
            by_section(act, first, second)

    each(lambda copy: copy.start(), copies)
    for copy in early:
        copy.wait_recv()
    dims = (((0,), (0,)), ((), ()))

    def block_copy(l, k):
        return across(2 * k + l, k, blocks.at[l, k], blocks_box.at[l, k])

    for l in range(2):
        total = lax.dot_general(
            columns[l][...], wides[l][:, own_half], dims, preferred_element_type=f32
        ) + lax.dot_general(columns_boxes[l], wide_boxes[l], dims, preferred_element_type=f32)
        for k in range(count):
            blocks[l, k] = total[k * block : (k + 1) * block, :].astype(bf16)
        for k in range(1, count):
            block_copy(l, k).start()
    each(lambda copy: copy.wait_recv(), copies[:1])

    def first_tiny(mine):
        tiny_sum[...] = mine[...] + tiny_box[...]

    by_section(first_tiny, tiny1, tiny0)
    for k in range(1, count):
        across(2 * count + k, k, tiny_sum, tiny_all.at[k]).start()

    def place_pieces(low_core, take):
        query, zx_a, zx_b, up_a, up_b, down_a, down_b, out_a, out_b = (
            functools.partial(take, i) for i in range(9)
        )
        width = query_out.shape[1] // 2
        query_out[:, pl.ds(pl.multiple_of(low_core * width, width), width)] = query()
        edge = zx_out.shape[2] // 2
        zx_out[low_core, :, :edge] = zx_a().astype(f32)
        zx_out[low_core, :, edge:] = zx_b().astype(f32)
        edge = up_out.shape[2] // 2
        up_out[low_core, :, :edge] = up_a().astype(f32)
        up_out[low_core, :, edge:] = up_b().astype(f32)
        for target, pieces in ((down_out, (down_a, down_b)), (out_out, (out_a, out_b))):
            for i, piece in enumerate(pieces):
                height = target.shape[0] // 4
                start = low_core * 2 * height + i * height
                target[pl.ds(pl.multiple_of(start, height), height), :] = piece().T

    def own(layer):
        def take(i):
            return part(layer, i)[...]

        place_pieces(section, take)

    by_section(own, 1, 0)
    each(lambda copy: copy.wait_recv(), copies[1:])
    place_pieces(1 - section, lambda i: boxes[i][...])

    def rows_done(mine):
        rows_out[section] = mine[0][...]
        grad_out[section] = mine[1][...]

    by_section(rows_done, (rows1, grad1), (rows0, grad0))
    rows_out[1 - section] = rows_box[...]
    grad_out[1 - section] = grad_box[...]
    for l in range(2):
        rows = blocks[l, 0].astype(f32)
        for k in range(1, count):
            block_copy(l, k).wait_recv()
            rows += blocks_box[l, k].astype(f32)
        shared[l] = rows.astype(bf16)
    shared_copy = over(len(pairs) + 4, shared.at[1 - section], shared_box)
    shared_copy.start()
    everything = tiny_sum[...]
    for k in range(1, count):
        across(2 * count + k, k, tiny_sum, tiny_all.at[k]).wait_recv()
        everything += tiny_all[k]
    tiny_out[...] = everything

    shared_out[:, own_half] = shared[section]
    shared_copy.wait_recv()
    shared_out[:, other_half] = shared_box[...]
    for copy in early:
        copy.wait_send()
    each(lambda copy: copy.wait_send(), copies)
    shared_copy.wait_send()
    for k in range(1, count):
        for l in range(2):
            block_copy(l, k).wait_send()
        across(2 * count + k, k, tiny_sum, tiny_all.at[k]).wait_send()


def finish(first, second, rows, d_rows, tinies, wides, columns):
    count = lax.axis_size(CTX)
    pairs = [*first.ffn, *first.out]
    arrays = (*first.proj, *second.ffn, *second.mix)
    up, down = second.ffn[0].shape[1] // 3 * 2, second.ffn[0].shape[1] // 3
    out = first.out[0][0].shape[1]
    step = 128
    most = second.mix[1].shape[1] - step - out
    query = first.proj[0].shape[1] - most

    def ffn(a):
        return (a, 0, up), (a + 1, 0, up), (a, up, down), (a + 1, up, down)

    places = (
        (
            (4, 0, query),
            (4, query, most),
            (5, 0, most),
            *ffn(0),
            (2, 0, out),
            (3, 0, out),
        ),
        (
            (8, 0, query),
            (8, query, most),
            (9, 0, most),
            *ffn(6),
            (8, query + most, out),
            (9, most + step, out),
        ),
    )
    length = first.proj[0].shape[0]
    widths = [piece[2] for piece in places[0]]
    half, block = wides[0].shape[1] // 2, columns[0].shape[1] // count
    shape = jax.ShapeDtypeStruct
    outs = [
        shape((length, 2 * query), bf16),
        shape((2, length, 2 * most), f32),
        shape((2, length, 2 * up), f32),
        shape((4 * down, length), bf16),
        shape((4 * out, length), bf16),
        shape((2,) + rows[0].shape, bf16),
        shape((2,) + d_rows[0].shape, f32),
        shape((block, 2 * half), bf16),
        shape(tinies[0].shape, f32),
    ]
    tokens = columns[0].shape[0]
    scratch = [pltpu.VMEM(kept.shape, bf16) for kept, _ in pairs]
    scratch += [pltpu.VMEM((length, w), bf16) for w in widths]
    scratch += [
        pltpu.VMEM(rows[0].shape, bf16),
        pltpu.VMEM(d_rows[0].shape, f32),
        pltpu.VMEM(tinies[0].shape, f32),
        pltpu.VMEM(tinies[0].shape, f32),
        pltpu.VMEM((count,) + tinies[0].shape, f32),
        pltpu.VMEM((2, tokens, half), bf16),
        pltpu.VMEM((2, tokens, count * block), bf16),
        pltpu.VMEM((2, count, block, half), bf16),
        pltpu.VMEM((2, count, block, half), bf16),
        pltpu.VMEM((2, block, half), bf16),
        pltpu.VMEM((block, half), bf16),
    ]
    over = len(widths) + 8
    scratch += [pltpu.SemaphoreType.DMA((n,)) for n in (over, over, 3 * count, 3 * count)]
    whole = pl.BlockSpec(memory_space=pltpu.VMEM)
    operands = (*sum(pairs, ()), *arrays, *rows, *d_rows, *tinies, *wides, *columns)
    return pl.pallas_call(
        functools.partial(finish_kernel, count, places, widths),
        out_shape=outs,
        in_specs=[whole] * len(operands),
        out_specs=[whole] * len(outs),
        scratch_shapes=scratch,
        compiler_params=pltpu.CompilerParams(
            collective_id=11, has_side_effects=True, vmem_limit_bytes=56 << 20
        ),
        cost_estimate=pl.CostEstimate(flops=0, bytes_accessed=20 << 20, transcendentals=0),
        name="finish",
    )(*operands)


def norm_apply(values, gain):
    return values * lax.rsqrt(jnp.mean(values * values, axis=-1, keepdims=True) + eps) * gain


def matmul(left, right):
    return jnp.dot(left, right, preferred_element_type=f32)


def matmul_nt(left, right):
    return lax.dot_general(left, right, (((1,), (1,)), ((), ())), preferred_element_type=f32)


def matmul_tn(left, right):
    return lax.dot_general(left, right, (((0,), (0,)), ((), ())), preferred_element_type=f32)


def swap(values):
    return lax.ppermute(values, SECTION, [(0, 1), (1, 0)])


def block_layout(doc_lengths, length):
    count, place = lax.axis_size(CTX), lax.axis_index(CTX)
    start = place * length
    bounds = jnp.cumsum(doc_lengths)[:-1]

    def segment_of(positions):
        return jnp.sum((positions[:, None] >= bounds[None, :]).astype(jnp.int32), axis=1)

    order = lax.rem(place + count - jnp.arange(count, dtype=jnp.int32), count)
    inside = jnp.arange(length, dtype=jnp.int32)
    keys = (order[:, None] * length + inside[None, :]).reshape(-1)
    positions = start + inside
    segments = segment_of(positions)
    before = jnp.where(place > 0, segment_of(start[None] - 1)[0], -1)
    goes_on = jnp.broadcast_to(segments[-1] == before, segments.shape)
    columns = [segments, segments == before, segments == segments[-1], positions, goes_on]
    tokens = jnp.stack([c.astype(f32) for c in columns], axis=1)
    return jnp.pad(tokens, ((0, 0), (0, 3))), jnp.stack(
        [segment_of(keys).astype(f32), keys.astype(f32)]
    )


def layer_forward(weights, normed, layout):
    proj = matmul(normed, weights.proj)
    both, mixed, state_in, keyval_all, decays = mix_forward(weights, proj, layout)
    saved = types.SimpleNamespace(
        normed=normed,
        proj=proj,
        both=both,
        mixed=mixed,
        state_in=state_in,
        keyval_all=keyval_all,
        decays=decays,
    )
    return matmul(both, weights.out), saved


def ffn_forward(weights, ffn_in):
    gate_up = matmul(ffn_in, weights.gate_up)
    width = gate_up.shape[1] // 2
    gate_pre, upward = gate_up[:, :width], gate_up[:, width:]
    product = (jax.nn.silu(gate_pre) * upward).astype(bf16)
    return matmul(product, weights.down), gate_pre, upward, product


def ctx_bits():
    return [1 << i for i in reversed(range((lax.axis_size(CTX) - 1).bit_length()))]


def flip(values, bit):
    return lax.ppermute(values, CTX, [(i, i ^ bit) for i in range(lax.axis_size(CTX))])


def own_half(values):
    half = values.shape[1] // 2
    section = lax.axis_index(SECTION)
    return (
        lax.dynamic_slice_in_dim(values, section * half, half, 1),
        lax.dynamic_slice_in_dim(values, (1 - section) * half, half, 1),
    )


def both_batches(kept, sent):
    return jnp.concatenate([kept, swap(sent)], axis=0)


def ctx_orders():
    bits = ctx_bits()
    return bits, bits[::-1]


def relative_order(bits):
    order = [0]
    for bit in reversed(bits):
        order = order + [k ^ bit for k in order]
    return order


def weight_sums(columns, *rows):
    kept, sent = zip(*(own_half(r) for r in rows))
    halves = both_batches(jnp.concatenate(kept, axis=1), jnp.concatenate(sent, axis=1))
    return matmul_tn(both_batches(columns, columns), halves).astype(bf16)


def shared_columns(normed):
    place, count = lax.axis_index(CTX), lax.axis_size(CTX)
    shards = lax.axis_size(SHARD)
    block = normed.shape[1] // (count * shards)
    return jnp.concatenate(
        [
            lax.dynamic_slice_in_dim(
                normed, ((place ^ k) * shards + lax.axis_index(SHARD)) * block, block, 1
            )
            for k in range(count)
        ],
        axis=1,
    )


def streams_of(total):
    place, count = lax.axis_index(CTX), lax.axis_size(CTX)
    block, half = total.shape[0] // count, total.shape[1] // 2
    streams = []
    for stream, bits in enumerate(ctx_orders()):
        parts = [
            lax.dynamic_slice(total, ((place ^ k) * block, stream * half), (block, half))
            for k in relative_order(bits)
        ]
        streams += [jnp.stack(parts[: count // 2]), jnp.stack(parts[count // 2 :])]
    return streams


def weight_scatter(streams):
    totals = []
    for i, bits in enumerate(ctx_orders()):
        kept, sent = (a.reshape(-1, a.shape[-1]) for a in streams[2 * i : 2 * i + 2])
        totals.append(scatter_relative(kept, sent, bits))
    return totals


def scatter_relative(kept, sent, bits):
    for i, bit in enumerate(bits):
        got = flip(sent, bit)
        if i + 1 < len(bits):
            rows = kept.shape[0] // 2
            sent = (kept[rows:].astype(f32) + got[rows:].astype(f32)).astype(bf16)
            kept = (kept[:rows].astype(f32) + got[:rows].astype(f32)).astype(bf16)
    return kept, got


def after(first, *later):
    first, later = lax.optimization_barrier((first, later))
    return first, later


def layer_backward(weights, saved, d_out, d_low, values_in, layout, last, before):
    grads = types.SimpleNamespace()
    d_product = matmul_nt(d_low, weights.down)
    gate_pre, upward = saved.gate_pre, saved.upward
    gate_sig = jax.nn.sigmoid(gate_pre)
    d_gate = d_product * upward * gate_sig * (1.0 + gate_pre * (1.0 - gate_sig))
    d_upward = d_product * gate_pre * gate_sig
    d_gate_up = jnp.concatenate([d_gate, d_upward], axis=1).astype(bf16)
    d_ffn_in = matmul_nt(d_gate_up, weights.gate_up)
    width = d_product.shape[1]
    up, down = width // 2, width // 4
    plan = tuple(
        (x, stream, ((x, stream * part, 2 * part + stream * part, part),))
        for stream in range(2)
        for x, part in ((0, up), (1, down))
    )
    d_middle, d_mixed, grads.gain_ffn, *sums = back_sum(
        10 if last else 3,
        d_ffn_in,
        d_out,
        saved.middle,
        weights.gain_ffn,
        plan,
        (saved.ffn_in, d_low),
        (d_gate_up, saved.product),
        (),
        before.sums_mix if last else (),
    )
    if last:
        sums, before.mix = sums[:4], sums[4:]
        grads.ffn = weight_scatter(sums)
    else:
        sums_ffn = sums
    d_both = matmul_nt(d_mixed, weights.out)
    if not last:
        (d_both,), (before.tail,) = after((d_both,), before.tail)
    if last:
        sums_out = weight_sums(d_mixed, saved.both)
        (sums_out,), (d_both,) = after((streams_of(sums_out),), d_both)
        grads.out = weight_scatter(sums_out)
    d_proj, d_vec = mix_backward(weights, saved, d_both, layout)
    heads, widths = weights.heads, weights.widths
    grads.step_bias, grads.decay, grads.skip = (d_vec[i, :heads] for i in range(3))
    d_normed = matmul_nt(d_proj, weights.proj)
    placed = [
        jnp.where(weights.kv_owner == owner, d_proj[:, start : start + HD], 0)
        for start in (widths[0], widths[0] + HD)
        for owner in range(KVH)
    ]
    d_shared = jnp.concatenate([d_proj[:, widths[1] : widths[2]], *placed], axis=1)
    normed = saved.normed
    if last:
        d_step, d_zx = d_proj[:, widths[2] : widths[3]], d_proj[:, widths[3] :]
        sums_proj = weight_sums(
            normed, d_proj[:, : widths[0]], d_zx, jnp.concatenate([d_step, d_step], axis=1)
        )
        streams = streams_of(sums_proj)
        (streams,), (d_normed,) = after((streams,), d_normed)
        d_hidden, d_hidden_low, grads.gain_in, d_shared, grads.proj = back_sum_scatter(
            7, d_normed, d_shared, d_middle, values_in, weights.gain_in, streams
        )
    else:
        query, inner = widths[0] // 2, (d_proj.shape[1] - widths[3]) // 2
        step, zx = widths[3] - widths[2], widths[3]
        both, most = saved.both.shape[1] // 4, inner // 2
        plan = (
            (0, 0, ((0, 0, query, query), (0, zx, zx + inner, most))),
            (1, 0, ((1, 0, 2 * both, both),)),
            (0, 1, ((0, zx + most, zx + inner + most, most), (0, widths[2], widths[2], step))),
            (1, 1, ((1, both, 3 * both, both),)),
        )
        d_hidden, d_hidden_low, grads.gain_in, d_shared, *sums = back_sum(
            4,
            d_normed,
            d_middle,
            values_in,
            weights.gain_in,
            plan,
            (normed, d_mixed),
            (d_proj, saved.both),
            (d_shared,),
            sums_ffn,
        )
        sums, grads.ffn = sums[:4], sums[4:]
        grads.sums_mix = sums
    grads.wide = d_shared
    return d_hidden, d_hidden_low, grads


def body(
    inputs,
    cotangent,
    doc_lengths,
    norm_in,
    w_query,
    w_keyval,
    w_attn_out,
    w_mixer_in,
    w_state_io,
    w_step,
    step_bias,
    decay_rate,
    skip_gain,
    w_mixer_out,
    norm_ffn,
    w_gate_up,
    w_down,
):
    section = lax.axis_index(SECTION)
    leading = section == 0
    shard = lax.axis_index(SHARD)
    width = w_query.shape[1]
    query_width = w_query.shape[2]
    head_count = w_step.shape[2]
    kv_owner = shard * (query_width // HD) // (QH // KVH)
    rows_in = lax.dynamic_index_in_dim(inputs, section, 0, False)
    own_keyval = lax.dynamic_slice_in_dim(w_keyval[0], kv_owner * HD, HD, 2).reshape(width, 2 * HD)
    io_end = query_width + 2 * HD + w_state_io.shape[2]
    widths = (query_width, query_width + 2 * HD, io_end, io_end - (-head_count // 128) * 128)
    proj = jnp.concatenate(
        [
            w_query[0],
            own_keyval,
            w_state_io[0],
            jnp.pad(w_step[0], ((0, 0), (0, -head_count % 128))),
            w_mixer_in[0].reshape(width, -1),
        ],
        axis=1,
    )
    vectors = jnp.concatenate([norm_in[0], norm_ffn[0], step_bias[0], decay_rate[0], skip_gain[0]])
    block_in = line_gather(rows_in)
    (block_in,), (proj,) = after((block_in,), proj)
    own = (
        proj,
        jnp.concatenate([w_attn_out[0], w_mixer_out[0]], axis=0),
        w_gate_up[0].reshape(width, -1),
        w_down[0],
        vectors,
    )
    other = tuple(swap(array) for array in own)

    def layer_weights(layer):
        weights = types.SimpleNamespace()
        chosen = [jnp.where(section == layer, a, b) for a, b in zip(own, other)]
        weights.proj, weights.out, weights.gate_up, weights.down, vectors = chosen
        heads = vectors[2 * width :]
        weights.gain_in = vectors[:width]
        weights.gain_ffn = vectors[width : 2 * width]
        skip = heads[2 * head_count :]
        rows = heads[: 2 * head_count].reshape(2, head_count)
        weights.head_rows = jnp.pad(rows, ((0, 6), (0, -head_count % 128)))
        weights.skip_row = jnp.repeat(skip, HP)[None]
        weights.heads = head_count
        weights.widths = widths
        weights.kv_owner = kv_owner
        return weights

    layers = [layer_weights(0), layer_weights(1)]
    rows_cot = lax.dynamic_index_in_dim(cotangent, section, 0, False)
    length = block_in.shape[0]
    part = rows_in.shape[0]
    layout = block_layout(lax.dynamic_index_in_dim(doc_lengths, section, 0, False), length)

    def own_rows(values):
        return lax.dynamic_slice_in_dim(values, shard * part, part, 0)

    hidden = block_in.astype(f32)
    normed = norm_apply(hidden, layers[0].gain_in).astype(bf16)
    hiddens, outs, saves = [], [], []
    for layer in range(2):
        weights = layers[layer]
        hiddens.append(hidden)
        if layer == 1:
            (normed,), (rows_cot,) = after((normed,), rows_cot)
            block_cot = lax.all_gather(rows_cot, SHARD, axis=0, tiled=True)
        partial, saved = layer_forward(weights, normed, layout)
        first, second = layers
        wanted = [(1, own[i], other[i]) for i in (0, 1)]
        if layer == 1:
            wanted = [(0, own[i], other[i]) for i in (2, 3)]
        saved.middle, saved.ffn_in, chosen = copying_sum(
            middle_kernel, 1 + 8 * layer, f32, partial, hidden, weights.gain_ffn, wanted
        )
        if layer == 0:
            second.proj, second.out = chosen
        else:
            first.gate_up, first.down = chosen
        partial, saved.gate_pre, saved.upward, saved.product = ffn_forward(
            weights, saved.ffn_in
        )
        saves.append(saved)
        if layer == 0:
            wanted = [(1, own[i], other[i]) for i in (2, 3)]
            out_low, normed, chosen = copying_sum(
                layer_end_kernel, 2, bf16, partial, saved.middle, second.gain_in, wanted
            )
            second.gate_up, second.down = chosen
            outs.append(own_rows(out_low))
            hidden = out_low.astype(f32)
        else:
            held = types.SimpleNamespace(tail=partial.astype(bf16))

    d_out = d_low = block_cot
    d_hiddens, grads = [None, None], [None, None]
    for layer in (1, 0):
        d_hidden, d_low, grads[layer] = layer_backward(
            layers[layer], saves[layer], d_out, d_low, hiddens[layer], layout, layer == 0, grads[1] if layer == 0 else held
        )
        d_hiddens[layer] = d_hidden
        d_out = d_low

    total = lax.psum_scatter(held.tail, SHARD, scatter_dimension=0, tiled=True)
    outs.append((own_rows(saves[1].middle) + total.astype(f32)).astype(bf16))
    first, second = grads
    tinies = []
    for g in grads:
        vector = jnp.concatenate([g.gain_in, g.gain_ffn, g.step_bias, g.decay, g.skip])
        size = -(-vector.shape[0] // 1024) * 8
        tinies.append(jnp.pad(vector, (0, size * 128 - vector.shape[0])).reshape(size, 128))
    query, zx, up, down, out, out_rows, grad_rows, shared, tiny = finish(
        first,
        second,
        outs,
        [own_rows(d) for d in d_hiddens],
        tinies,
        [first.wide, second.wide],
        [shared_columns(saved.normed) for saved in saves],
    )
    tiny = tiny.reshape(-1)
    place = lax.axis_index(CTX) * lax.axis_size(SHARD) + shard
    slot = width // (lax.axis_size(CTX) * lax.axis_size(SHARD))
    grad_in = lax.dynamic_slice_in_dim(tiny, place * slot, slot, 0)
    grad_ffn = lax.dynamic_slice_in_dim(tiny, width + place * slot, slot, 0)
    heads = tiny[2 * width :]
    step = jnp.where(
        leading,
        first.proj[1][:, zx.shape[2] // 2 :],
        second.mix[1][:, zx.shape[2] // 2 : zx.shape[2] // 2 + 128],
    )
    io_width = w_state_io.shape[2]
    return (
        out_rows[None],
        grad_rows[None],
        grad_in[None],
        query.astype(f32)[None],
        shared[:, io_width:].astype(f32).reshape(-1, 2, KVH * HD)[None],
        out[:query_width].astype(f32)[None],
        jnp.swapaxes(zx, 0, 1)[None],
        shared[:, :io_width].astype(f32)[None],
        step[:, :head_count].astype(f32)[None],
        heads[:head_count][None],
        heads[head_count : 2 * head_count][None],
        heads[2 * head_count : 3 * head_count][None],
        out[query_width:].astype(f32)[None],
        grad_ffn[None],
        jnp.swapaxes(up, 0, 1)[None],
        down.astype(f32)[None],
    )


def solution(mesh):
    return jax.shard_map(
        body,
        mesh=mesh,
        in_specs=(
            P(None, (CTX, SHARD), None),
            P(None, (CTX, SHARD), None),
            P(),
            P(SECTION, None),
            P(SECTION, None, SHARD),
            P(SECTION, None, None, None),
            P(SECTION, SHARD, None),
            P(SECTION, None, None, SHARD),
            P(SECTION, None, None),
            P(SECTION, None, SHARD),
            P(SECTION, SHARD),
            P(SECTION, SHARD),
            P(SECTION, SHARD),
            P(SECTION, SHARD, None),
            P(SECTION, None),
            P(SECTION, None, None, SHARD),
            P(SECTION, SHARD, None),
        ),
        out_specs=(
            P(SECTION, None, (CTX, SHARD), None),
            P(SECTION, None, (CTX, SHARD), None),
            P(SECTION, (CTX, SHARD)),
            P(SECTION, CTX, SHARD),
            P(SECTION, (CTX, SHARD), None, None),
            P(SECTION, SHARD, CTX),
            P(SECTION, CTX, None, SHARD),
            P(SECTION, (CTX, SHARD), None),
            P(SECTION, CTX, SHARD),
            P(SECTION, SHARD),
            P(SECTION, SHARD),
            P(SECTION, SHARD),
            P(SECTION, SHARD, CTX),
            P(SECTION, (CTX, SHARD)),
            P(SECTION, CTX, None, SHARD),
            P(SECTION, SHARD, CTX),
        ),
        check_vma=False,
    )
```

```python
import functools
import types

import jax
import jax.numpy as jnp
from jax import lax
from jax.experimental import pallas as pl
from jax.experimental.pallas import tpu as pltpu
from jax.sharding import PartitionSpec as P

SECTION, CTX, SHARD = "section", "ctx", "shard"
QH = 8
KVH = 2
HD = 128
HP = 64
CHUNKS = 16
LAG = 3

MESH = pl.DeviceIdType.MESH
eps = 1e-05
bf16 = jnp.bfloat16
f32 = jnp.float32


def line_sum(n, chunks, lag, p_rows, done, sr, sl, rr, rl, srs, sls, rrs, rls, tot, fill=None):
    z = lax.axis_index(SHARD)
    hasr, hasl = z < n - 1, z > 0
    bar = pltpu.get_barrier_semaphore()
    more = 0
    if fill is not None:
        more = fill.greet(bar)

    @pl.when(hasr)
    def _():
        pl.semaphore_signal(bar, inc=1, device_id={SHARD: z + 1}, device_id_type=MESH)

    @pl.when(hasl)
    def _():
        pl.semaphore_signal(bar, inc=1, device_id={SHARD: z - 1}, device_id_type=MESH)

    @pl.when(hasl & hasr)
    def _():
        pl.semaphore_wait(bar, 2 + more)

    @pl.when(jnp.logical_not(hasl & hasr))
    def _():
        pl.semaphore_wait(bar, 1 + more)

    def right(j):
        return pltpu.make_async_remote_copy(
            sr.at[j], rr.at[j], srs.at[j], rrs.at[j], device_id={SHARD: z + 1}, device_id_type=MESH
        )

    def left(j):
        return pltpu.make_async_remote_copy(
            sl.at[j], rl.at[j], sls.at[j], rls.at[j], device_id={SHARD: z - 1}, device_id_type=MESH
        )

    steps = chunks + lag * (n - 1)
    if fill is not None:
        fill.start()

    def one(i, _):
        def go(j, copy, came, goes, inbox, outbox):
            live = (j >= 0) & (j < chunks)

            @pl.when(live & came & goes)
            def _():
                copy(j).wait_recv()
                outbox[j] = (p_rows(j) + inbox[j].astype(f32)).astype(bf16)
                copy(j).start()

            @pl.when(live & jnp.logical_not(came))
            def _():
                outbox[j] = p_rows(j).astype(bf16)
                copy(j).start()

            @pl.when(live & jnp.logical_not(goes))
            def _():
                copy(j).wait_recv()

        go(i - lag * z, right, hasl, hasr, rr, sr)
        go(i - lag * (n - 1 - z), left, hasr, hasl, rl, sl)
        jd = i - lag * jnp.maximum(z, n - 1 - z)

        @pl.when((jd >= 0) & (jd < chunks))
        def _():
            tot[...] = p_rows(jd)

            @pl.when(hasl)
            def _():
                tot[...] += rr[jd].astype(f32)

            @pl.when(hasr)
            def _():
                tot[...] += rl[jd].astype(f32)

            done(jd, tot[...])

        if fill is not None:
            fill.step(i, steps)
        return 0

    lax.fori_loop(0, steps, one, 0)
    if fill is not None:
        fill.finish()

    def drain(j, _):
        @pl.when(hasr)
        def _():
            right(j).wait_send()

        @pl.when(hasl)
        def _():
            left(j).wait_send()

        return 0

    lax.fori_loop(0, chunks, drain, 0)


def row_slice(j, rows):
    return pl.ds(pl.multiple_of(j * rows, rows), rows)


def middle_kernel(n, chunks, lag, p_ref, h_ref, gain_ref, mid_ref, low_ref, *scratch, fill=None):
    rows = p_ref.shape[0] // chunks

    def p_rows(j):
        return p_ref[row_slice(j, rows), :]

    def done(j, total):
        v = h_ref[row_slice(j, rows), :] + total
        r = lax.rsqrt(jnp.mean(v * v, axis=-1, keepdims=True) + eps)
        mid_ref[row_slice(j, rows), :] = v
        low_ref[row_slice(j, rows), :] = (v * r * gain_ref[...]).astype(bf16)

    line_sum(n, chunks, lag, p_rows, done, *scratch, fill=fill)


class Copies:
    parts = 16

    def __init__(self, layers, own, other, out, boxes, came, went):
        self.layers, self.own, self.other, self.out = layers, own, other, out
        self.boxes, self.came, self.went = boxes, came, went

    def greet(self, bar):
        return 0

    def start(self):
        pass

    def rows(self, a, j):
        size = self.boxes[a].shape[1]
        return pl.ds(pl.multiple_of(j * size, size), size)

    def fetch(self, a, j, act):
        section, slot = lax.axis_index(SECTION), lax.rem(j, 2)
        for mine, source in ((True, self.own[a]), (False, self.other[a])):

            @pl.when((section == self.layers[a]) == mine)
            def _():
                part = source.at[self.rows(a, j), :]
                act(
                    pltpu.make_async_copy(
                        part, self.boxes[a].at[slot], self.came.at[2 * a + slot]
                    )
                )

    def store(self, a, j):
        slot = lax.rem(j, 2)
        part = self.out[a].at[self.rows(a, j), :]
        return pltpu.make_async_copy(self.boxes[a].at[slot], part, self.went.at[2 * a + slot])

    def step(self, i, steps):
        @pl.when((i >= 1) & (i <= self.parts))
        def _():
            for a in range(len(self.layers)):
                self.fetch(a, i - 1, lambda copy: copy.wait())
                self.store(a, i - 1).start()

        @pl.when((i >= 2) & (i < self.parts))
        def _():
            for a in range(len(self.layers)):
                self.store(a, i - 2).wait()

        @pl.when(i < self.parts)
        def _():
            for a in range(len(self.layers)):
                self.fetch(a, i, lambda copy: copy.start())

    def finish(self):
        for a in range(len(self.layers)):
            for j in (self.parts - 2, self.parts - 1):
                self.store(a, j).wait()


def copying(kernel, layers, n, chunks, lag, p_ref, h_ref, gain_ref, *refs):
    count = len(layers)
    own, other, refs = refs[:count], refs[count : 2 * count], refs[2 * count :]
    first_ref, low_ref, refs = refs[0], refs[1], refs[2:]
    out, refs = refs[:count], refs[count:]
    copies = Copies(layers, own, other, out, refs[9 : 9 + count], *refs[9 + count :])
    kernel(n, chunks, lag, p_ref, h_ref, gain_ref, first_ref, low_ref, *refs[:9], fill=copies)


def layer_end_kernel(n, chunks, lag, p_ref, h_ref, gain_ref, out_ref, low_ref, *scratch, fill=None):
    rows = p_ref.shape[0] // chunks

    def p_rows(j):
        return p_ref[row_slice(j, rows), :]

    def done(j, total):
        out = (h_ref[row_slice(j, rows), :] + total).astype(bf16)
        out_ref[row_slice(j, rows), :] = out
        v = out.astype(f32)
        r = lax.rsqrt(jnp.mean(v * v, axis=-1, keepdims=True) + eps)
        low_ref[row_slice(j, rows), :] = (v * r * gain_ref[...]).astype(bf16)

    line_sum(n, chunks, lag, p_rows, done, *scratch, fill=fill)


def flipped(place, k, count):
    total, bit = 0, 1
    while bit < count:
        total = total + (place // bit + k // bit) % 2 * bit
        bit *= 2
    return total


def mirrored(k, count):
    total, bit = 0, 1
    while bit < count:
        total = total + k // bit % 2 * (count // (2 * bit))
        bit *= 2
    return total


class Fill:
    first = 6

    def __init__(self, plan, xs, ys, outs, scratch):
        self.plan, self.xs, self.ys, self.outs = plan, xs, ys, outs
        count = len(plan)
        self.other_x, rest = scratch[: len(xs)], scratch[len(xs) :]
        self.own_y, self.other_y = rest[:count], rest[count : 2 * count]
        self.send, self.recv = rest[2 * count :]

    def greet(self, bar):
        other = 1 - lax.axis_index(SECTION)
        pl.semaphore_signal(bar, inc=1, device_id={SECTION: other}, device_id_type=MESH)
        return 1

    def copies(self):
        section = lax.axis_index(SECTION)
        copies = []

        def add(source, target):
            i = len(copies)
            copies.append(
                pltpu.make_async_remote_copy(
                    source,
                    target,
                    self.send.at[i],
                    self.recv.at[i],
                    device_id={SECTION: 1 - section},
                    device_id_type=MESH,
                )
            )

        for x, target in zip(self.xs, self.other_x):
            add(x, target)
        for (_, _, parts), target in zip(self.plan, self.other_y):
            at = 0
            for y, low, high, width in parts:
                start = pl.multiple_of(low + (high - low) * (1 - section), 128)
                add(self.ys[y].at[:, pl.ds(start, width)], target.at[:, at : at + width])
                at += width
        return copies

    def start(self):
        for copy in self.copies():
            copy.start()
        section = lax.axis_index(SECTION)
        for (_, _, parts), own in zip(self.plan, self.own_y):
            at = 0
            for y, low, high, width in parts:
                start = pl.multiple_of(low + (high - low) * section, 128)
                own[:, at : at + width] = self.ys[y][:, pl.ds(start, width)]
                at += width

    def each(self, steps):
        return -(-lax.axis_size(CTX) * len(self.plan) // (steps - self.first))

    def step(self, i, steps):
        place, count = lax.axis_index(CTX), lax.axis_size(CTX)

        @pl.when(i == self.first)
        def _():
            for copy in self.copies():
                copy.wait_recv()

        each = self.each(steps)
        begin = (i - self.first) * each

        def piece(t, _):
            at = [0] * 4
            for f, (x, stream, _) in enumerate(self.plan):
                k = t - f * count
                width = self.own_y[f].shape[1]
                where = slice(at[stream], at[stream] + width)
                at[stream] += width
                kept, sent = self.outs[2 * stream : 2 * stream + 2]
                turned = stream % 2

                @pl.when((k >= 0) & (k < count))
                def _():
                    block = kept.shape[1]
                    source = flipped(place, mirrored(k, count) if turned else k, count)
                    cols = pl.ds(pl.multiple_of(source * block, block), block)
                    dims = (((0,), (0,)), ((), ()))
                    total = lax.dot_general(
                        self.xs[x][:, cols], self.own_y[f][...], dims, preferred_element_type=f32
                    ) + lax.dot_general(
                        self.other_x[x][:, cols],
                        self.other_y[f][...],
                        dims,
                        preferred_element_type=f32,
                    )
                    low = total.astype(bf16)

                    @pl.when(k < count // 2)
                    def _():
                        kept[k, :, where] = low

                    @pl.when(k >= count // 2)
                    def _():
                        sent[k - count // 2, :, where] = low

            return 0

        @pl.when(i >= self.first)
        def _():
            lax.fori_loop(begin, begin + each, piece, 0)

    def finish(self):
        for copy in self.copies():
            copy.wait_send()


class Halving:
    cuts = 2

    def __init__(self, streams, outs, scratch, turns, begin=None, greets=True):
        self.turns, self.begin, self.greets = turns, begin, greets
        self.place, self.count = lax.axis_index(CTX), lax.axis_size(CTX)
        self.streams, self.outs = streams, outs
        self.orders = ctx_orders()
        self.levels = len(self.orders[0])
        self.inbox = [scratch[k * self.levels : (k + 1) * self.levels] for k in range(2)]
        rest = scratch[2 * self.levels :]
        self.sums = [rest[k * (self.levels - 1) : (k + 1) * (self.levels - 1)] for k in range(2)]
        self.send, self.recv = rest[2 * (self.levels - 1) :]

    def greet(self, bar):
        if not self.greets:
            return 0
        for bit in self.orders[0]:
            peer = flipped(self.place, bit, self.count)
            pl.semaphore_signal(bar, inc=1, device_id={CTX: peer}, device_id_type=MESH)
        return self.levels

    def rows(self, cut):
        size = self.outs[0].shape[0] // self.cuts
        return pl.ds(cut * size, size)

    def copy(self, level, stream, cut):
        rows = self.rows(cut)
        if level == 0:
            source = self.streams[2 * stream + 1].at[:, rows, :]
        else:
            blocks = self.count >> (level + 1)
            source = self.sums[stream][level - 1].at[pl.ds(blocks, blocks), rows, :]
        i = (level * 2 + stream) * self.cuts + cut
        return pltpu.make_async_remote_copy(
            source,
            self.inbox[stream][level].at[:, rows, :],
            self.send.at[i],
            self.recv.at[i],
            device_id={CTX: flipped(self.place, self.orders[stream][level], self.count)},
            device_id_type=MESH,
        )

    def advance(self, level, cut):
        rows, blocks = self.rows(cut), self.count >> (level + 1)
        for stream in range(2):
            self.copy(level, stream, cut).wait_recv()
            kept = self.streams[2 * stream] if level == 0 else self.sums[stream][level - 1]
            for k in range(blocks):
                total = kept[k, rows, :].astype(f32) + self.inbox[stream][level][k, rows, :].astype(
                    f32
                )
                if level + 1 < self.levels:
                    self.sums[stream][level][k, rows, :] = total.astype(bf16)
                else:
                    self.outs[stream][rows, :] = total.astype(bf16)
            if level + 1 < self.levels:
                self.copy(level + 1, stream, cut).start()

    def start(self):
        if self.begin is None:
            self.first_copies()

    def first_copies(self):
        for cut in range(self.cuts):
            for stream in range(2):
                self.copy(0, stream, cut).start()

    def step(self, i, steps):
        if self.begin is not None:

            @pl.when(i == self.begin)
            def _():
                self.first_copies()

        for cut, turn in enumerate(self.turns):

            @pl.when(i == turn)
            def _():
                self.advance(0, cut)

    def finish(self):
        for cut in range(len(self.turns), self.cuts):
            self.advance(0, cut)
        for level in range(1, self.levels):
            for cut in range(self.cuts):
                self.advance(level, cut)
        for level in range(self.levels):
            for stream in range(2):
                for cut in range(self.cuts):
                    self.copy(level, stream, cut).wait_send()


def halving_scratch(streams):
    blocks, rows, width = streams[0].shape
    levels = len(ctx_bits())
    inbox = [pltpu.VMEM((blocks >> k, rows, width), bf16) for k in range(levels)]
    copies = levels * 2 * Halving.cuts
    return [*inbox * 2, *inbox[: levels - 1] * 2, *[pltpu.SemaphoreType.DMA((copies,))] * 2]


class Together:
    def __init__(self, *jobs):
        self.jobs = jobs

    def greet(self, bar):
        return sum(job.greet(bar) for job in self.jobs)

    def start(self):
        for job in self.jobs:
            job.start()

    def step(self, i, steps):
        for job in self.jobs:
            job.step(i, steps)

    def finish(self):
        for job in self.jobs:
            job.finish()


def scatter_kernel(n, chunks, lag, p_ref, q_ref, d_ref, v_ref, gain_ref, *refs):
    streams, outs, totals, scratch = refs[:4], refs[4:8], refs[8:10], refs[10:]
    job = Halving(streams, totals, scratch[9:], (7, 14))
    back_rows(n, chunks, lag, p_ref, d_ref, v_ref, gain_ref, *outs[:3], scratch[:9], job, q_ref, outs[3])


def back_kernel(n, chunks, lag, plan, x_count, y_count, beside, ready, soon, p_ref, *refs):
    q_ref = q_out = None
    if beside:
        q_ref, refs = refs[0], refs[1:]
    (d_ref, v_ref, gain_ref), refs = refs[:3], refs[3:]
    xs, refs = refs[:x_count], refs[x_count:]
    ys, refs = refs[:y_count], refs[y_count:]
    streams, refs = refs[:ready], refs[ready:]
    out_ref, low_ref, gg_ref = refs[:3]
    refs = refs[3:]
    if beside:
        q_out, refs = refs[0], refs[1:]
    sums, refs = refs[:4], refs[4:]
    totals, refs = refs[: ready // 2], refs[ready // 2 :]
    soon_totals, refs = refs[: 2 * soon], refs[2 * soon :]
    scratch, rest = refs[:9], refs[9:]
    cut = len(xs) + 2 * len(plan) + 2
    own, rest = rest[:cut], rest[cut:]
    here, rest = rest[: 4 * soon], rest[4 * soon :]
    fill = Fill(plan, xs, ys, (*sums, *here), own)
    jobs = [fill]
    boxes = 4 * len(ctx_bits())
    if ready:
        turns = (8, 14) if beside else (9,)
        jobs.append(Halving(streams, totals, rest[:boxes], turns))
        rest = rest[boxes:]
    if soon:
        begin = Fill.first + -(-2 * lax.axis_size(CTX) // fill.each(chunks + lag * (n - 1)))
        jobs.append(Halving(here, soon_totals, rest, (), begin, not ready))
    fill = Together(*jobs)
    outs = out_ref, low_ref, gg_ref
    back_rows(n, chunks, lag, p_ref, d_ref, v_ref, gain_ref, *outs, scratch, fill, q_ref, q_out)


def back_rows(
    n,
    chunks,
    lag,
    p_ref,
    d_ref,
    v_ref,
    gain_ref,
    out_ref,
    low_ref,
    gg_ref,
    scratch,
    fill,
    q_ref=None,
    q_out=None,
):
    rows, width = p_ref.shape[0] // chunks, p_ref.shape[1]
    gg_ref[...] = jnp.zeros_like(gg_ref)

    def p_rows(j):
        part = row_slice(j, rows)
        if q_ref is None:
            return p_ref[part, :]
        return jnp.concatenate([p_ref[part, :], q_ref[part, :].astype(f32)], axis=1)

    def done(j, total):
        if q_ref is not None:
            q_out[row_slice(j, rows), :] = total[:, width:].astype(bf16)
            total = total[:, :width]
        v = v_ref[row_slice(j, rows), :].astype(f32)
        r = lax.rsqrt(jnp.mean(v * v, axis=-1, keepdims=True) + eps)
        vr = v * r
        dg = total * gain_ref[...]
        inner = jnp.mean(dg * vr, axis=-1, keepdims=True)
        gg_ref[...] += jnp.sum((total * vr).reshape(rows // 8, 8, vr.shape[1]), axis=0)
        out = d_ref[row_slice(j, rows), :].astype(f32) + r * (dg - vr * inner)
        out_ref[row_slice(j, rows), :] = out
        low_ref[row_slice(j, rows), :] = out.astype(bf16)

    line_sum(n, chunks, lag, p_rows, done, *scratch, fill=fill)


def summed(kernel, collective, outs, *operands, extra=(), more=0, far=(0, 0), room=50):
    n = lax.axis_size(SHARD)
    length, width = operands[0].shape[0], operands[0].shape[1] + more
    box = pltpu.VMEM((CHUNKS, length // CHUNKS, width), bf16)
    distant = pl.BlockSpec(memory_space=pl.ANY)
    whole = pl.BlockSpec(memory_space=pltpu.VMEM)
    return pl.pallas_call(
        functools.partial(kernel, n, CHUNKS, LAG),
        out_shape=outs,
        in_specs=[whole] * (len(operands) - far[0]) + [distant] * far[0],
        out_specs=[whole] * (len(outs) - far[1]) + [distant] * far[1],
        scratch_shapes=[box] * 4
        + [pltpu.SemaphoreType.DMA((CHUNKS,))] * 4
        + [pltpu.VMEM((length // CHUNKS, width), f32), *extra],
        compiler_params=pltpu.CompilerParams(
            collective_id=collective, has_side_effects=True, vmem_limit_bytes=room << 20
        ),
        cost_estimate=pl.CostEstimate(flops=0, bytes_accessed=20 << 20, transcendentals=0),
        name="line_sum"+str(collective),
    )(*operands)


def line_gather(rows):
    count, place = lax.axis_size(SHARD), lax.axis_index(SHARD)
    part = rows.shape[0]
    block = jnp.zeros((count * part, rows.shape[1]), rows.dtype)
    block = lax.dynamic_update_slice_in_dim(block, rows, place * part, 0)
    for k in reversed(range(1, count)):
        got = lax.ppermute(rows, SHARD, [(i, i ^ k) for i in range(count)])
        block = lax.dynamic_update_slice_in_dim(block, got, (place ^ k) * part, 0)
    return block


def shaped(array, dtype):
    return jax.ShapeDtypeStruct(array.shape, dtype)


def copying_sum(kernel, collective, dtype, p, hidden, gain, wanted):
    layers, own, other = zip(*wanted)
    outs = [shaped(p, dtype), shaped(p, bf16)] + [shaped(a, bf16) for a in own]
    boxes = [pltpu.VMEM((2, a.shape[0] // Copies.parts, a.shape[1]), bf16) for a in own]
    first, low, *chosen = summed(
        functools.partial(copying, kernel, layers),
        collective,
        outs,
        p,
        hidden,
        gain[None],
        *own,
        *other,
        extra=[*boxes, *[pltpu.SemaphoreType.DMA((2 * len(layers),))] * 2],
        far=(2 * len(layers), len(layers)),
        room=26,
    )
    return first, low, chosen


def back_sum(collective, p, d_out, values, gain, plan, xs, ys, beside=(), ready=(), soon=False):
    count = lax.axis_size(CTX)
    length = p.shape[0]
    outs = [shaped(p, f32), shaped(p, bf16), jax.ShapeDtypeStruct((8, p.shape[1]), f32)]
    outs += [shaped(q, bf16) for q in beside]
    widths = [sum(part[3] for part in parts) for _, _, parts in plan]
    sums = []
    for stream in range(4 if soon else 2):
        total = sum(w for (_, at, _), w in zip(plan, widths) if at == stream)
        shape = (count // 2, xs[0].shape[1] // count, total)
        sums += [jax.ShapeDtypeStruct(shape, bf16)] * 2
    outs += sums[:4]
    extra = [pltpu.VMEM(x.shape, bf16) for x in xs]
    extra += [pltpu.VMEM((length, w), bf16) for w in widths] * 2
    copies = len(xs) + sum(len(parts) for _, _, parts in plan)
    extra += [pltpu.SemaphoreType.DMA((copies,))] * 2
    outs += [jax.ShapeDtypeStruct(a.shape[1:], bf16) for a in ready[::2]]
    if soon:
        outs += [jax.ShapeDtypeStruct(sums[4].shape[1:], bf16)] * 2
        extra += [pltpu.VMEM(a.shape, bf16) for a in sums[4:]]
    if ready:
        extra += halving_scratch(ready)
    if soon:
        extra += halving_scratch(sums[4:])

    def bound(n, chunks, lag, *refs):
        back_kernel(n, chunks, lag, plan, len(xs), len(ys), bool(beside), len(ready), soon, *refs)

    operands = (p, *beside, d_out, values, gain[None], *xs, *ys, *ready)
    more = sum(q.shape[1] for q in beside)
    room = 50 if ready else 38
    out, low, gg, *sums = summed(
        bound, collective, outs, *operands, extra=extra, more=more, room=room
    )
    return out, low, jnp.sum(gg, axis=0), *sums


def back_sum_scatter(collective, p, beside, d_out, values, gain, streams):
    outs = [shaped(p, f32), shaped(p, bf16), jax.ShapeDtypeStruct((8, p.shape[1]), f32)]
    outs += [shaped(beside, bf16)]
    outs += [jax.ShapeDtypeStruct(a.shape[1:], bf16) for a in streams[::2]]
    operands = (p, beside, d_out, values, gain[None], *streams)
    more = beside.shape[1]
    out, low, gg, whole, *totals = summed(
        scatter_kernel, collective, outs, *operands, extra=halving_scratch(streams), more=more, room=36
    )
    return out, low, jnp.sum(gg, axis=0), whole, totals


def dot(left, right, dims=((1,), (0,))):
    return lax.dot_general(left, right, (dims, ((), ())), preferred_element_type=f32)


NT = ((1,), (1,))
TN = ((0,), (0,))


def in_three(values):
    high = values.astype(bf16)
    rest = values - high.astype(f32)
    mid = rest.astype(bf16)
    return high, mid, (rest - mid.astype(f32)).astype(bf16)


def running_sum(values, reverse):
    length = values.shape[0]
    row = lax.broadcasted_iota(jnp.int32, (length, length), 0)
    col = lax.broadcasted_iota(jnp.int32, (length, length), 1)
    kept = jnp.where(row <= col if reverse else row >= col, 1.0, 0.0).astype(bf16)
    return sum(dot(kept, part) for part in in_three(values))


def lanes(shape):
    return lax.broadcasted_iota(jnp.int32, shape, 1)


def column(values, head):
    return jnp.sum(jnp.where(lanes(values.shape) == head, values, 0.0), axis=1, keepdims=True)


def in_pair(values, pair):
    low, high = column(values, 2 * pair), column(values, 2 * pair + 1)
    return jnp.where(lanes(values.shape) < HP, low, high)


def from_pair(values, pair):
    lane = lanes(values.shape)
    low = jnp.sum(jnp.where(lane < HP, values, 0.0), axis=1, keepdims=True)
    high = jnp.sum(jnp.where(lane < HP, 0.0, values), axis=1, keepdims=True)
    return jnp.where(lane == 2 * pair, low, 0.0) + jnp.where(lane == 2 * pair + 1, high, 0.0)


def pair_ds(pair, start=0):
    return pl.ds(pl.multiple_of(start + pair * 2 * HP, 2 * HP), 2 * HP)


def steps_of(step_raw, vec_ref, tok_ref, cum, cum_rows, step, enter, fade):
    shifted = step_raw + vec_ref[0:1, :]
    step[...] = jnp.maximum(shifted, 0.0) + jnp.log1p(jnp.exp(-jnp.abs(shifted)))
    cum[...] = running_sum(-step[...] * vec_ref[1:2, :], False)
    total = cum[...]
    cum_rows[...] = total.T
    enter[...] = jnp.exp(total) * tok_ref[:, 1:2]
    fade[...] = jnp.exp(total[-1:, :] - total) * tok_ref[:, 2:3]
    return shifted


def masks_of(tok_ref, key_ref):
    kept = (tok_ref[:, 3:4] >= key_ref[1:2, :]) & (tok_ref[:, 0:1] == key_ref[0:1, :])
    return jnp.where(kept, 0.0, -1e30)


def ctx_barrier(count, place):
    bar = pltpu.get_barrier_semaphore()

    def greet(k, _):
        pl.semaphore_signal(
            bar, inc=1, device_id={CTX: lax.rem(place + k, count)}, device_id_type=MESH
        )
        return 0

    lax.fori_loop(1, count, greet, 0)
    pl.semaphore_wait(bar, count - 1)


def ctx_copy(source, target, send, recv, peer):
    return pltpu.make_async_remote_copy(
        source, target, send, recv, device_id={CTX: peer}, device_id_type=MESH
    )


def mix_forward_kernel(
    count,
    widths,
    heads,
    proj_ref,
    vec_ref,
    skip_ref,
    tok_ref,
    key_ref,
    both_ref,
    mixed_ref,
    state_ref,
    keyval_ref,
    decay_ref,
    cum,
    cum_rows,
    step,
    enter,
    fade,
    mask,
    crossed,
    keyvals,
    fresh,
    decays,
    total_state,
    kv_send,
    kv_recv,
    st_send,
    st_recv,
    dc_send,
    dc_recv,
):
    place = lax.axis_index(CTX)
    length = proj_ref.shape[0]
    inner = (proj_ref.shape[1] - widths[3]) // 2
    pairs = heads // 2
    states = (widths[2] - widths[1]) // 2
    ctx_barrier(count, place)

    keyvals[0] = proj_ref[:, widths[0] : widths[1]].astype(bf16)

    def kv_copy(k):
        peer = lax.rem(place + k, count)
        return ctx_copy(keyvals.at[0], keyvals.at[k], kv_send.at[k], kv_recv.at[k], peer)

    def st_copy(k):
        peer = lax.rem(place + k, count)
        return ctx_copy(fresh.at[0], fresh.at[k], st_send.at[k], st_recv.at[k], peer)

    def dc_copy(k):
        peer = lax.rem(place + k, count)
        return ctx_copy(decays.at[0], decays.at[k], dc_send.at[k], dc_recv.at[k], peer)

    def kv_start(k, _):
        kv_copy(k).start()
        return 0

    lax.fori_loop(1, count, kv_start, 0)
    steps_of(
        proj_ref[:, widths[2] : widths[2] + 128], vec_ref, tok_ref, cum, cum_rows, step, enter, fade
    )
    last = cum_rows[: decays.shape[1], length - 1 :]
    decays[0] = jnp.broadcast_to(jnp.exp(last) * tok_ref[0:1, 4:5], decays.shape[1:])
    b_low = proj_ref[:, widths[1] : widths[1] + states].astype(bf16)
    c_low = proj_ref[:, widths[1] + states : widths[2]].astype(bf16)

    def make_fresh(pair, _):
        x = proj_ref[:, pair_ds(pair, widths[3] + inner)]
        x = x.astype(bf16).astype(f32)
        faded = (x * in_pair(fade[...] * step[...], pair)).astype(bf16)
        fresh[0, pair_ds(pair), :] = dot(faded, b_low, TN).astype(bf16)
        return 0

    lax.fori_loop(0, pairs, make_fresh, 0)

    def st_start(k, _):
        dc_copy(k).start()

        @pl.when(place + k < count)
        def _():
            st_copy(k).start()

        return 0

    lax.fori_loop(1, count, st_start, 0)
    mask[...] = masks_of(tok_ref, key_ref)
    crossed[...] = dot(c_low, b_low, NT) * states ** (-0.5)

    def inside(pair, _):
        x = proj_ref[:, pair_ds(pair, widths[3] + inner)]
        x = x.astype(bf16).astype(f32)
        xdt = (x * in_pair(step[...], pair)).astype(bf16)
        parts = []
        for side in range(2):
            head = 2 * pair + side
            spread = column(cum[...], head) - cum_rows[pl.ds(head, 1), :]
            weight = jnp.exp(spread + mask[:, :length])
            parts.append(dot((weight * crossed[...]).astype(bf16), xdt))
        mixed_ref[:, pair_ds(pair)] = jnp.where(lanes(parts[0].shape) < HP, *parts)
        return 0

    lax.fori_loop(0, pairs, inside, 0)

    def kv_wait(k, _):
        kv_copy(k).wait_recv()
        return 0

    lax.fori_loop(1, count, kv_wait, 0)
    keyval_ref[...] = keyvals[...].reshape(keyval_ref.shape)
    for head in range(widths[0] // HD):
        query = proj_ref[:, head * HD : (head + 1) * HD].astype(bf16)
        scores = dot(query, keyval_ref[:, :HD], NT) * HD ** (-0.5) + mask[...]
        expo = jnp.exp(scores - jnp.max(scores, axis=1, keepdims=True))
        soft = expo * (1.0 / jnp.sum(expo, axis=1, keepdims=True))
        both_ref[:, head * HD : (head + 1) * HD] = dot(
            soft.astype(bf16), keyval_ref[:, HD:]
        ).astype(bf16)

    def dc_wait(k, _):
        dc_copy(k).wait_recv()

        @pl.when(k <= place)
        def _():
            st_copy(k).wait_recv()

        return 0

    lax.fori_loop(1, count, dc_wait, 0)
    total_state[...] = jnp.zeros_like(total_state)
    head_width = inner // heads

    def combine(index, _):
        slot = place - index

        def one_head(head, _):
            rows = pl.ds(pl.multiple_of(head * head_width, head_width), head_width)
            total_state[rows, :] = total_state[rows, :] * decays[slot, pl.ds(head, 1), :] + fresh[
                slot, rows, :
            ].astype(f32)
            return 0

        lax.fori_loop(0, heads, one_head, 0)
        return 0

    lax.fori_loop(0, place, combine, 0)
    state_ref[...] = total_state[...].astype(bf16)
    decay_ref[...] = decays[...]

    def finish(pair, _):
        carried = dot(c_low, state_ref[pair_ds(pair), :], NT)
        mixed = mixed_ref[:, pair_ds(pair)] + carried * in_pair(enter[...], pair)
        mixed_ref[:, pair_ds(pair)] = mixed
        x = proj_ref[:, pair_ds(pair, widths[3] + inner)]
        x = x.astype(bf16).astype(f32)
        gate = proj_ref[:, pair_ds(pair, widths[3])]
        y = mixed + x * skip_ref[0:1, pair_ds(pair)]
        both_ref[:, pair_ds(pair, widths[0])] = (
            y * gate / (1.0 + jnp.exp(-gate))
        ).astype(bf16)
        return 0

    lax.fori_loop(0, pairs, finish, 0)

    def drain(k, _):
        kv_copy(k).wait_send()
        dc_copy(k).wait_send()

        @pl.when(place + k < count)
        def _():
            st_copy(k).wait_send()

        return 0

    lax.fori_loop(1, count, drain, 0)


def mix_backward_kernel(
    count,
    widths,
    heads,
    proj_ref,
    vec_ref,
    skip_ref,
    tok_ref,
    key_ref,
    mixed_ref,
    state_ref,
    keyval_ref,
    decay_ref,
    d_both_ref,
    d_proj_ref,
    d_vec_ref,
    cum,
    cum_rows,
    step,
    enter,
    fade,
    mask,
    crossed,
    d_crossed,
    d_y,
    d_carried,
    d_x,
    d_keyval,
    d_b,
    d_c,
    d_cum,
    d_step,
    d_coeff,
    d_skip,
    d_states,
    total_state,
    kv_out,
    kv_in,
    kv_send,
    kv_recv,
    st_send,
    st_recv,
):
    place = lax.axis_index(CTX)
    length = proj_ref.shape[0]
    inner = (proj_ref.shape[1] - widths[3]) // 2
    pairs = heads // 2
    head_width = inner // heads
    states = (widths[2] - widths[1]) // 2
    ctx_barrier(count, place)

    def back(k):
        return lax.rem(place + count - k, count)

    def kv_copy(k):
        return ctx_copy(kv_out.at[k], kv_in.at[k], kv_send.at[k], kv_recv.at[k], back(k))

    def st_copy(k):
        return ctx_copy(d_states.at[0], d_states.at[k], st_send.at[k], st_recv.at[k], back(k))

    shifted = steps_of(
        proj_ref[:, widths[2] : widths[2] + 128], vec_ref, tok_ref, cum, cum_rows, step, enter, fade
    )
    b_low = proj_ref[:, widths[1] : widths[1] + states].astype(bf16)
    c_low = proj_ref[:, widths[1] + states : widths[2]].astype(bf16)
    d_cum[...] = jnp.zeros_like(d_cum)
    d_step[...] = jnp.zeros_like(d_step)
    d_coeff[...] = jnp.zeros_like(d_coeff)
    d_skip[...] = jnp.zeros_like(d_skip)

    def x_of(pair):
        x = proj_ref[:, pair_ds(pair, widths[3] + inner)]
        return x.astype(bf16).astype(f32)

    def outer(pair, _):
        gate = proj_ref[:, pair_ds(pair, widths[3])]
        d_gated = d_both_ref[:, pair_ds(pair, widths[0])]
        x, mixed, skip = x_of(pair), mixed_ref[:, pair_ds(pair)], skip_ref[0:1, pair_ds(pair)]
        sig = 1.0 / (1.0 + jnp.exp(-gate))
        dy = d_gated * gate * sig
        d_gate = d_gated * (mixed + x * skip) * sig * (1.0 + gate * (1.0 - sig))
        d_proj_ref[:, pair_ds(pair, widths[3])] = d_gate.astype(bf16)
        low = dy.astype(bf16)
        d_y[:, pair_ds(pair)] = low
        d_x[:, pair_ds(pair)] = dy * skip
        d_skip[...] += from_pair(dy * x, pair)
        d_cum[...] += from_pair(low.astype(f32) * mixed, pair)
        carried = (low.astype(f32) * in_pair(enter[...], pair)).astype(bf16)
        d_carried[:, pair_ds(pair)] = carried
        d_states[0, pair_ds(pair), :] = dot(carried, c_low, TN).astype(bf16)
        return 0

    lax.fori_loop(0, pairs, outer, 0)

    def st_start(k, _):
        @pl.when(k <= place)
        def _():
            st_copy(k).start()

        return 0

    lax.fori_loop(1, count, st_start, 0)
    mask[...] = masks_of(tok_ref, key_ref)
    for head in range(widths[0] // HD):
        cols = slice(head * HD, (head + 1) * HD)
        query = proj_ref[:, cols].astype(bf16)
        scores = dot(query, keyval_ref[:, :HD], NT) * HD ** (-0.5) + mask[...]
        expo = jnp.exp(scores - jnp.max(scores, axis=1, keepdims=True))
        soft = expo * (1.0 / jnp.sum(expo, axis=1, keepdims=True))
        grad = d_both_ref[:, cols].astype(bf16)
        d_soft = dot(grad, keyval_ref[:, HD:], NT)
        d_scores = soft * (d_soft - jnp.sum(soft * d_soft, axis=1, keepdims=True))
        d_raw = (d_scores * HD ** (-0.5)).astype(bf16)
        d_proj_ref[:, cols] = dot(d_raw, keyval_ref[:, :HD]).astype(bf16)
        d_keys, d_values = dot(d_raw, query, TN), dot(soft.astype(bf16), grad, TN)
        if head == 0:
            d_keyval[:, :HD] = d_keys
            d_keyval[:, HD:] = d_values
        else:
            d_keyval[:, :HD] += d_keys
            d_keyval[:, HD:] += d_values
    kv_out[...] = d_keyval[...].astype(bf16).reshape(kv_out.shape)

    def kv_start(k, _):
        kv_copy(k).start()
        return 0

    lax.fori_loop(1, count, kv_start, 0)
    crossed[...] = dot(c_low, b_low, NT) * states ** (-0.5)
    d_crossed[...] = jnp.zeros_like(d_crossed)

    def inside(pair, _):
        x = x_of(pair)
        steps = in_pair(step[...], pair)
        xdt = (x * steps).astype(bf16)
        low = d_y[:, pair_ds(pair)]
        lane = lanes(low.shape)
        parts = []
        for side in range(2):
            head = 2 * pair + side
            spread = column(cum[...], head) - cum_rows[pl.ds(head, 1), :]
            weight = jnp.exp(spread + mask[:, :length])
            parts.append(dot((weight * crossed[...]).astype(bf16), low, TN))
            mine = (lane >= HP) if side else (lane < HP)
            alone = jnp.where(mine, low.astype(f32), 0.0).astype(bf16)
            d_crossed[...] += dot(alone, xdt, NT) * weight
        d_xdt = jnp.where(lane < HP, *parts)
        d_x[:, pair_ds(pair)] += d_xdt * steps
        d_step[...] += from_pair(d_xdt * x, pair)
        d_cum[...] -= from_pair(d_xdt * xdt.astype(f32), pair)
        return 0

    lax.fori_loop(0, pairs, inside, 0)
    low_crossed = (d_crossed[...] * states ** (-0.5)).astype(bf16)
    d_c[...] = dot(low_crossed, b_low) + dot(d_carried[...], state_ref[...])
    d_b[...] = dot(low_crossed, c_low, TN)

    def st_wait(k, _):
        @pl.when(place + k < count)
        def _():
            st_copy(k).wait_recv()

        return 0

    lax.fori_loop(1, count, st_wait, 0)
    total_state[...] = jnp.zeros_like(total_state)

    def combine(index, _):
        slot = count - 1 - place - index
        source = lax.rem(count - slot, count)

        def one_head(head, _):
            rows = pl.ds(pl.multiple_of(head * head_width, head_width), head_width)
            total_state[rows, :] = total_state[rows, :] * decay_ref[
                source, pl.ds(head, 1), :
            ] + d_states[slot, rows, :].astype(f32)
            return 0

        lax.fori_loop(0, heads, one_head, 0)
        return 0

    lax.fori_loop(0, count - 1 - place, combine, 0)
    d_vec_ref[...] = jnp.zeros_like(d_vec_ref)

    def from_later(pair, _):
        rows = pair_ds(pair)
        later = total_state[rows, :]
        low = later.astype(bf16)
        x = x_of(pair)
        coeffs = in_pair(fade[...] * step[...], pair)
        back_x = dot(b_low, low, NT)
        d_proj_ref[:, pair_ds(pair, widths[3] + inner)] = (
            d_x[:, rows] + back_x * coeffs
        ).astype(bf16)
        d_coeff[...] += from_pair(back_x * x, pair)
        d_b[...] += dot((x * coeffs).astype(bf16), low)
        product = later * state_ref[rows, :].astype(f32)
        row = lax.broadcasted_iota(jnp.int32, product.shape, 0)
        lane = lanes((1, 128))
        for side in range(2):
            mine = (row >= HP) if side else (row < HP)
            part = jnp.sum(jnp.where(mine, product, 0.0), axis=0, keepdims=True)
            part = jnp.sum(part, axis=1, keepdims=True)
            d_vec_ref[3:4, :] += jnp.where(lane == 2 * pair + side, part, 0.0)
        return 0

    lax.fori_loop(0, pairs, from_later, 0)
    fading = fade[...]
    d_keep = d_coeff[...] * fading * step[...]
    block_decay = jnp.exp(cum[length - 1 :, :]) * tok_ref[0:1, 4:5]
    d_last = jnp.sum(d_keep, axis=0, keepdims=True) + block_decay * d_vec_ref[3:4, :]
    d_log = running_sum(d_cum[...] - d_keep, True) + d_last
    d_size = d_step[...] + d_coeff[...] * fading - vec_ref[1:2, :] * d_log
    d_raw_step = d_size / (1.0 + jnp.exp(-shifted))
    d_proj_ref[:, widths[2] : widths[3]] = jnp.where(
        lanes(d_raw_step.shape) < heads, d_raw_step, 0.0
    ).astype(bf16)
    d_vec_ref[0:1, :] = jnp.sum(d_raw_step, axis=0, keepdims=True)
    d_vec_ref[1:2, :] = -jnp.sum(step[...] * d_log, axis=0, keepdims=True)
    d_vec_ref[2:3, :] = jnp.sum(d_skip[...], axis=0, keepdims=True)
    d_proj_ref[:, widths[1] : widths[1] + states] = d_b[...].astype(bf16)
    d_proj_ref[:, widths[1] + states : widths[2]] = d_c[...].astype(bf16)

    def kv_wait(k, _):
        kv_copy(k).wait_recv()
        d_keyval[:length, :] += kv_in[k].astype(f32)
        return 0

    lax.fori_loop(1, count, kv_wait, 0)
    d_proj_ref[:, widths[0] : widths[1]] = d_keyval[:length, :].astype(bf16)

    def drain(k, _):
        kv_copy(k).wait_send()

        @pl.when(k <= place)
        def _():
            st_copy(k).wait_send()

        return 0

    lax.fori_loop(1, count, drain, 0)


def mixer_call(kernel, collective, outs, scratch, sems, widths, heads, operands, room):
    count = lax.axis_size(CTX)
    whole = pl.BlockSpec(memory_space=pltpu.VMEM)
    return pl.pallas_call(
        functools.partial(kernel, count, widths, heads),
        out_shape=outs,
        in_specs=[whole] * len(operands),
        out_specs=[whole] * len(outs),
        scratch_shapes=[pltpu.VMEM(*s) for s in scratch]
        + [pltpu.SemaphoreType.DMA((count,))] * sems,
        compiler_params=pltpu.CompilerParams(
            collective_id=collective,
            has_side_effects=True,
            vmem_limit_bytes=(room + 2 * count) << 20,
        ),
        cost_estimate=pl.CostEstimate(flops=0, bytes_accessed=20 << 20, transcendentals=0),
        name="mixer"+str(collective),
    )(*operands)


def mix_forward(weights, proj, layout):
    count = lax.axis_size(CTX)
    widths, heads = weights.widths, weights.heads
    length, inner = proj.shape[0], (proj.shape[1] - widths[3]) // 2
    states = (widths[2] - widths[1]) // 2
    kv = widths[1] - widths[0]
    shape = jax.ShapeDtypeStruct
    head_rows = -(-heads // 8) * 8
    outs = [
        shape((length, widths[0] + inner), bf16),
        shape((length, inner), f32),
        shape((inner, states), bf16),
        shape((count * length, kv), bf16),
        shape((count, head_rows, states), f32),
    ]
    per_head = ((length, 128), f32)
    scratch = [
        per_head,
        ((128, length), f32),
        per_head,
        per_head,
        per_head,
        ((length, count * length), f32),
        ((length, length), f32),
        ((count, length, kv), bf16),
        ((count, inner, states), bf16),
        ((count, head_rows, states), f32),
        ((inner, states), f32),
    ]
    operands = (proj, weights.head_rows, weights.skip_row, *layout)
    return mixer_call(mix_forward_kernel, 5, outs, scratch, 6, widths, heads, operands, 18)


def mix_backward(weights, saved, d_both, layout):
    count = lax.axis_size(CTX)
    widths, heads = weights.widths, weights.heads
    proj = saved.proj
    length, inner = proj.shape[0], (proj.shape[1] - widths[3]) // 2
    states = (widths[2] - widths[1]) // 2
    kv = widths[1] - widths[0]
    shape = jax.ShapeDtypeStruct
    outs = [shape(proj.shape, bf16), shape((8, 128), f32)]
    per_head = ((length, 128), f32)
    square = ((length, length), f32)
    scratch = [
        per_head,
        ((128, length), f32),
        per_head,
        per_head,
        per_head,
        ((length, count * length), f32),
        square,
        square,
        ((length, inner), bf16),
        ((length, inner), bf16),
        ((length, inner), f32),
        ((count * length, kv), f32),
        ((length, states), f32),
        ((length, states), f32),
        per_head,
        per_head,
        per_head,
        per_head,
        ((count, inner, states), bf16),
        ((inner, states), f32),
        ((count, length, kv), bf16),
        ((count, length, kv), bf16),
    ]
    operands = (
        proj,
        weights.head_rows,
        weights.skip_row,
        *layout,
        saved.mixed,
        saved.state_in,
        saved.keyval_all,
        saved.decays,
        d_both,
    )
    return mixer_call(mix_backward_kernel, 6, outs, scratch, 4, widths, heads, operands, 24)


def finish_kernel(
    count,
    places,
    widths,
    *refs,
):
    unsummed, arrays, refs = refs[:8], refs[8:18], refs[18:]
    (
        rows0,
        rows1,
        grad0,
        grad1,
        tiny0,
        tiny1,
        wide0,
        wide1,
        columns0,
        columns1,
        *refs,
    ) = refs
    (
        query_out,
        zx_out,
        up_out,
        down_out,
        out_out,
        rows_out,
        grad_out,
        shared_out,
        tiny_out,
        *refs,
    ) = refs
    arrays, refs = (*refs[:4], *arrays), refs[4:]
    boxes, refs = refs[: len(widths)], refs[len(widths) :]
    (
        rows_box,
        grad_box,
        tiny_box,
        tiny_sum,
        tiny_all,
        wide_boxes,
        columns_boxes,
        blocks,
        blocks_box,
        shared,
        shared_box,
        send,
        recv,
        ctx_send,
        ctx_recv,
    ) = refs
    section, place = lax.axis_index(SECTION), lax.axis_index(CTX)
    bar = pltpu.get_barrier_semaphore()
    pl.semaphore_signal(bar, inc=1, device_id={SECTION: 1 - section}, device_id_type=MESH)
    for k in range(1, count):
        peer = flipped(place, k, count)
        pl.semaphore_signal(bar, inc=1, device_id={CTX: peer}, device_id_type=MESH)
    pl.semaphore_wait(bar, count)
    half = wide0.shape[1] // 2
    own_half = pl.ds(pl.multiple_of(section * half, half), half)
    other_half = pl.ds(pl.multiple_of((1 - section) * half, half), half)

    def over(i, source, target):
        return pltpu.make_async_remote_copy(
            source,
            target,
            send.at[i],
            recv.at[i],
            device_id={SECTION: 1 - section},
            device_id_type=MESH,
        )

    def across(i, k, source, target):
        return pltpu.make_async_remote_copy(
            source,
            target,
            ctx_send.at[i],
            ctx_recv.at[i],
            device_id={CTX: flipped(place, k, count)},
            device_id_type=MESH,
        )

    def part(layer, i):
        array, start, width = places[layer][i]
        return arrays[array].at[:, start : start + width]

    def by_section(act, first, second):
        @pl.when(section == 1)
        def _():
            act(first)

        @pl.when(section == 0)
        def _():
            act(second)

    block = blocks.shape[2]
    wides, columns = (wide0, wide1), (columns0, columns1)
    early = [over(l, wides[l].at[:, other_half], wide_boxes.at[l]) for l in range(2)]
    early += [over(2 + l, columns[l], columns_boxes.at[l]) for l in range(2)]
    for copy in early:
        copy.start()
    for i in range(4):
        arrays[i][...] = (unsummed[2 * i][...].astype(f32) + unsummed[2 * i + 1][...].astype(f32)).astype(bf16)
    pairs = [(tiny0, tiny1, tiny_box)]
    pairs += [(part(0, i), part(1, i), box) for i, box in enumerate(boxes)]
    pairs += [(rows0, rows1, rows_box), (grad0, grad1, grad_box)]
    copies = [
        (over(4 + i, first, box), over(4 + i, second, box))
        for i, (first, second, box) in enumerate(pairs)
    ]

    def each(act, which):
        for first, second in which:
            by_section(act, first, second)

    each(lambda copy: copy.start(), copies)
    for copy in early:
        copy.wait_recv()
    dims = (((0,), (0,)), ((), ()))

    def block_copy(l, k):
        return across(2 * k + l, k, blocks.at[l, k], blocks_box.at[l, k])

    for l in range(2):
        total = lax.dot_general(
            columns[l][...], wides[l][:, own_half], dims, preferred_element_type=f32
        ) + lax.dot_general(columns_boxes[l], wide_boxes[l], dims, preferred_element_type=f32)
        for k in range(count):
            blocks[l, k] = total[k * block : (k + 1) * block, :].astype(bf16)
        for k in range(1, count):
            block_copy(l, k).start()
    each(lambda copy: copy.wait_recv(), copies[:1])

    def first_tiny(mine):
        tiny_sum[...] = mine[...] + tiny_box[...]

    by_section(first_tiny, tiny1, tiny0)
    for k in range(1, count):
        across(2 * count + k, k, tiny_sum, tiny_all.at[k]).start()

    def place_pieces(low_core, take):
        query, zx_a, zx_b, up_a, up_b, down_a, down_b, out_a, out_b = (
            functools.partial(take, i) for i in range(9)
        )
        width = query_out.shape[1] // 2
        query_out[:, pl.ds(pl.multiple_of(low_core * width, width), width)] = query()
        edge = zx_out.shape[2] // 2
        zx_out[low_core, :, :edge] = zx_a().astype(f32)
        zx_out[low_core, :, edge:] = zx_b().astype(f32)
        edge = up_out.shape[2] // 2
        up_out[low_core, :, :edge] = up_a().astype(f32)
        up_out[low_core, :, edge:] = up_b().astype(f32)
        for target, pieces in ((down_out, (down_a, down_b)), (out_out, (out_a, out_b))):
            for i, piece in enumerate(pieces):
                height = target.shape[0] // 4
                start = low_core * 2 * height + i * height
                target[pl.ds(pl.multiple_of(start, height), height), :] = piece().T

    def own(layer):
        def take(i):
            return part(layer, i)[...]

        place_pieces(section, take)

    by_section(own, 1, 0)
    each(lambda copy: copy.wait_recv(), copies[1:])
    place_pieces(1 - section, lambda i: boxes[i][...])

    def rows_done(mine):
        rows_out[section] = mine[0][...]
        grad_out[section] = mine[1][...]

    by_section(rows_done, (rows1, grad1), (rows0, grad0))
    rows_out[1 - section] = rows_box[...]
    grad_out[1 - section] = grad_box[...]
    for l in range(2):
        rows = blocks[l, 0].astype(f32)
        for k in range(1, count):
            block_copy(l, k).wait_recv()
            rows += blocks_box[l, k].astype(f32)
        shared[l] = rows.astype(bf16)
    shared_copy = over(len(pairs) + 4, shared.at[1 - section], shared_box)
    shared_copy.start()
    everything = tiny_sum[...]
    for k in range(1, count):
        across(2 * count + k, k, tiny_sum, tiny_all.at[k]).wait_recv()
        everything += tiny_all[k]
    tiny_out[...] = everything

    shared_out[:, own_half] = shared[section]
    shared_copy.wait_recv()
    shared_out[:, other_half] = shared_box[...]
    for copy in early:
        copy.wait_send()
    each(lambda copy: copy.wait_send(), copies)
    shared_copy.wait_send()
    for k in range(1, count):
        for l in range(2):
            block_copy(l, k).wait_send()
        across(2 * count + k, k, tiny_sum, tiny_all.at[k]).wait_send()


def finish(first, second, rows, d_rows, tinies, wides, columns):
    count = lax.axis_size(CTX)
    pairs = [*first.ffn, *first.out]
    arrays = (*first.proj, *second.ffn, *second.down, *second.mix, *second.out)
    up, down = second.ffn[0].shape[1], second.down[0].shape[1]
    out = first.out[0][0].shape[1]
    step = 128
    most = second.mix[1].shape[1] - step
    query = first.proj[0].shape[1] - most

    places = (
        (
            (4, 0, query),
            (4, query, most),
            (5, 0, most),
            (0, 0, up),
            (1, 0, up),
            (0, up, down),
            (1, up, down),
            (2, 0, out),
            (3, 0, out),
        ),
        (
            (10, 0, query),
            (10, query, most),
            (11, 0, most),
            (6, 0, up),
            (7, 0, up),
            (8, 0, down),
            (9, 0, down),
            (12, 0, out),
            (13, 0, out),
        ),
    )
    length = first.proj[0].shape[0]
    widths = [piece[2] for piece in places[0]]
    half, block = wides[0].shape[1] // 2, columns[0].shape[1] // count
    shape = jax.ShapeDtypeStruct
    outs = [
        shape((length, 2 * query), bf16),
        shape((2, length, 2 * most), f32),
        shape((2, length, 2 * up), f32),
        shape((4 * down, length), bf16),
        shape((4 * out, length), bf16),
        shape((2,) + rows[0].shape, bf16),
        shape((2,) + d_rows[0].shape, f32),
        shape((block, 2 * half), bf16),
        shape(tinies[0].shape, f32),
    ]
    tokens = columns[0].shape[0]
    scratch = [pltpu.VMEM(kept.shape, bf16) for kept, _ in pairs]
    scratch += [pltpu.VMEM((length, w), bf16) for w in widths]
    scratch += [
        pltpu.VMEM(rows[0].shape, bf16),
        pltpu.VMEM(d_rows[0].shape, f32),
        pltpu.VMEM(tinies[0].shape, f32),
        pltpu.VMEM(tinies[0].shape, f32),
        pltpu.VMEM((count,) + tinies[0].shape, f32),
        pltpu.VMEM((2, tokens, half), bf16),
        pltpu.VMEM((2, tokens, count * block), bf16),
        pltpu.VMEM((2, count, block, half), bf16),
        pltpu.VMEM((2, count, block, half), bf16),
        pltpu.VMEM((2, block, half), bf16),
        pltpu.VMEM((block, half), bf16),
    ]
    over = len(widths) + 8
    scratch += [pltpu.SemaphoreType.DMA((n,)) for n in (over, over, 3 * count, 3 * count)]
    whole = pl.BlockSpec(memory_space=pltpu.VMEM)
    operands = (*sum(pairs, ()), *arrays, *rows, *d_rows, *tinies, *wides, *columns)
    return pl.pallas_call(
        functools.partial(finish_kernel, count, places, widths),
        out_shape=outs,
        in_specs=[whole] * len(operands),
        out_specs=[whole] * len(outs),
        scratch_shapes=scratch,
        compiler_params=pltpu.CompilerParams(
            collective_id=11, has_side_effects=True, vmem_limit_bytes=56 << 20
        ),
        cost_estimate=pl.CostEstimate(flops=0, bytes_accessed=20 << 20, transcendentals=0),
        name="finish",
    )(*operands)


def norm_apply(values, gain):
    return values * lax.rsqrt(jnp.mean(values * values, axis=-1, keepdims=True) + eps) * gain


def matmul(left, right):
    return jnp.dot(left, right, preferred_element_type=f32)


def matmul_nt(left, right):
    return lax.dot_general(left, right, (((1,), (1,)), ((), ())), preferred_element_type=f32)


def matmul_tn(left, right):
    return lax.dot_general(left, right, (((0,), (0,)), ((), ())), preferred_element_type=f32)


def swap(values):
    return lax.ppermute(values, SECTION, [(0, 1), (1, 0)])


def block_layout(doc_lengths, length):
    count, place = lax.axis_size(CTX), lax.axis_index(CTX)
    start = place * length
    bounds = jnp.cumsum(doc_lengths)[:-1]

    def segment_of(positions):
        return jnp.sum((positions[:, None] >= bounds[None, :]).astype(jnp.int32), axis=1)

    order = lax.rem(place + count - jnp.arange(count, dtype=jnp.int32), count)
    inside = jnp.arange(length, dtype=jnp.int32)
    keys = (order[:, None] * length + inside[None, :]).reshape(-1)
    positions = start + inside
    segments = segment_of(positions)
    before = jnp.where(place > 0, segment_of(start[None] - 1)[0], -1)
    goes_on = jnp.broadcast_to(segments[-1] == before, segments.shape)
    columns = [segments, segments == before, segments == segments[-1], positions, goes_on]
    tokens = jnp.stack([c.astype(f32) for c in columns], axis=1)
    return jnp.pad(tokens, ((0, 0), (0, 3))), jnp.stack(
        [segment_of(keys).astype(f32), keys.astype(f32)]
    )


def layer_forward(weights, normed, layout):
    proj = matmul(normed, weights.proj)
    both, mixed, state_in, keyval_all, decays = mix_forward(weights, proj, layout)
    saved = types.SimpleNamespace(
        normed=normed,
        proj=proj,
        both=both,
        mixed=mixed,
        state_in=state_in,
        keyval_all=keyval_all,
        decays=decays,
    )
    return matmul(both, weights.out), saved


def ffn_forward(weights, ffn_in):
    gate_up = matmul(ffn_in, weights.gate_up)
    width = gate_up.shape[1] // 2
    gate_pre, upward = gate_up[:, :width], gate_up[:, width:]
    product = (jax.nn.silu(gate_pre) * upward).astype(bf16)
    return matmul(product, weights.down), gate_pre, upward, product


def ctx_bits():
    return [1 << i for i in reversed(range((lax.axis_size(CTX) - 1).bit_length()))]


def flip(values, bit):
    return lax.ppermute(values, CTX, [(i, i ^ bit) for i in range(lax.axis_size(CTX))])


def own_half(values):
    half = values.shape[1] // 2
    section = lax.axis_index(SECTION)
    return (
        lax.dynamic_slice_in_dim(values, section * half, half, 1),
        lax.dynamic_slice_in_dim(values, (1 - section) * half, half, 1),
    )


def both_batches(kept, sent):
    return jnp.concatenate([kept, swap(sent)], axis=0)


def ctx_orders():
    bits = ctx_bits()
    return bits, bits[::-1]


def relative_order(bits):
    order = [0]
    for bit in reversed(bits):
        order = order + [k ^ bit for k in order]
    return order


def weight_sums(columns, *rows):
    kept, sent = zip(*(own_half(r) for r in rows))
    halves = both_batches(jnp.concatenate(kept, axis=1), jnp.concatenate(sent, axis=1))
    return matmul_tn(both_batches(columns, columns), halves).astype(bf16)


def shared_columns(normed):
    place, count = lax.axis_index(CTX), lax.axis_size(CTX)
    shards = lax.axis_size(SHARD)
    block = normed.shape[1] // (count * shards)
    return jnp.concatenate(
        [
            lax.dynamic_slice_in_dim(
                normed, ((place ^ k) * shards + lax.axis_index(SHARD)) * block, block, 1
            )
            for k in range(count)
        ],
        axis=1,
    )


def streams_of(total):
    place, count = lax.axis_index(CTX), lax.axis_size(CTX)
    block, half = total.shape[0] // count, total.shape[1] // 2
    streams = []
    for stream, bits in enumerate(ctx_orders()):
        parts = [
            lax.dynamic_slice(total, ((place ^ k) * block, stream * half), (block, half))
            for k in relative_order(bits)
        ]
        streams += [jnp.stack(parts[: count // 2]), jnp.stack(parts[count // 2 :])]
    return streams


def weight_scatter(streams):
    totals = []
    for i, bits in enumerate(ctx_orders()):
        kept, sent = (a.reshape(-1, a.shape[-1]) for a in streams[2 * i : 2 * i + 2])
        totals.append(scatter_relative(kept, sent, bits))
    return totals


def scatter_relative(kept, sent, bits):
    for i, bit in enumerate(bits):
        got = flip(sent, bit)
        if i + 1 < len(bits):
            rows = kept.shape[0] // 2
            sent = (kept[rows:].astype(f32) + got[rows:].astype(f32)).astype(bf16)
            kept = (kept[:rows].astype(f32) + got[:rows].astype(f32)).astype(bf16)
    return kept, got


def after(first, *later):
    first, later = lax.optimization_barrier((first, later))
    return first, later


def layer_backward(weights, saved, d_out, d_low, values_in, layout, last, before):
    grads = types.SimpleNamespace()
    d_product = matmul_nt(d_low, weights.down)
    gate_pre, upward = saved.gate_pre, saved.upward
    gate_sig = jax.nn.sigmoid(gate_pre)
    d_gate = d_product * upward * gate_sig * (1.0 + gate_pre * (1.0 - gate_sig))
    d_upward = d_product * gate_pre * gate_sig
    d_gate_up = jnp.concatenate([d_gate, d_upward], axis=1).astype(bf16)
    d_ffn_in = matmul_nt(d_gate_up, weights.gate_up)
    width = d_product.shape[1]
    up, down = width // 2, width // 4
    plan = tuple(
        (x, stream, ((x, stream * part, 2 * part + stream * part, part),))
        for stream in range(2)
        for x, part in ((0, up), (1, down))
    )
    if not last:
        plan = tuple(
            (x, 2 * x + stream, parts)
            for x, stream, parts in sorted(plan, key=lambda entry: -entry[0])
        )
    d_middle, d_mixed, grads.gain_ffn, *sums = back_sum(
        10 if last else 3,
        d_ffn_in,
        d_out,
        saved.middle,
        weights.gain_ffn,
        plan,
        (saved.ffn_in, d_low),
        (d_gate_up, saved.product),
        (),
        before.sums_mix if last else (),
        not last,
    )
    if last:
        sums, before.mix = sums[:4], sums[4:]
        grads.ffn = weight_scatter(sums)
    else:
        sums_ffn, grads.down = sums[:4], sums[4:]
    d_both = matmul_nt(d_mixed, weights.out)
    if not last:
        (d_both,), (before.tail,) = after((d_both,), before.tail)
    if last:
        sums_out = weight_sums(d_mixed, saved.both)
        (sums_out,), (d_both,) = after((streams_of(sums_out),), d_both)
        grads.out = weight_scatter(sums_out)
    d_proj, d_vec = mix_backward(weights, saved, d_both, layout)
    heads, widths = weights.heads, weights.widths
    grads.step_bias, grads.decay, grads.skip = (d_vec[i, :heads] for i in range(3))
    d_normed = matmul_nt(d_proj, weights.proj)
    placed = [
        jnp.where(weights.kv_owner == owner, d_proj[:, start : start + HD], 0)
        for start in (widths[0], widths[0] + HD)
        for owner in range(KVH)
    ]
    d_shared = jnp.concatenate([d_proj[:, widths[1] : widths[2]], *placed], axis=1)
    normed = saved.normed
    if last:
        d_step, d_zx = d_proj[:, widths[2] : widths[3]], d_proj[:, widths[3] :]
        sums_proj = weight_sums(
            normed, d_proj[:, : widths[0]], d_zx, jnp.concatenate([d_step, d_step], axis=1)
        )
        streams = streams_of(sums_proj)
        (streams,), (d_normed,) = after((streams,), d_normed)
        d_hidden, d_hidden_low, grads.gain_in, d_shared, grads.proj = back_sum_scatter(
            7, d_normed, d_shared, d_middle, values_in, weights.gain_in, streams
        )
    else:
        query, inner = widths[0] // 2, (d_proj.shape[1] - widths[3]) // 2
        step, zx = widths[3] - widths[2], widths[3]
        both, most = saved.both.shape[1] // 4, inner // 2
        plan = (
            (1, 2, ((1, 0, 2 * both, both),)),
            (1, 3, ((1, both, 3 * both, both),)),
            (0, 0, ((0, 0, query, query), (0, zx, zx + inner, most))),
            (0, 1, ((0, zx + most, zx + inner + most, most), (0, widths[2], widths[2], step))),
        )
        d_hidden, d_hidden_low, grads.gain_in, d_shared, *sums = back_sum(
            4,
            d_normed,
            d_middle,
            values_in,
            weights.gain_in,
            plan,
            (normed, d_mixed),
            (d_proj, saved.both),
            (d_shared,),
            sums_ffn,
            True,
        )
        sums, grads.ffn, grads.out = sums[:4], sums[4:6], sums[6:]
        grads.sums_mix = sums
    grads.wide = d_shared
    return d_hidden, d_hidden_low, grads


def body(
    inputs,
    cotangent,
    doc_lengths,
    norm_in,
    w_query,
    w_keyval,
    w_attn_out,
    w_mixer_in,
    w_state_io,
    w_step,
    step_bias,
    decay_rate,
    skip_gain,
    w_mixer_out,
    norm_ffn,
    w_gate_up,
    w_down,
):
    section = lax.axis_index(SECTION)
    leading = section == 0
    shard = lax.axis_index(SHARD)
    width = w_query.shape[1]
    query_width = w_query.shape[2]
    head_count = w_step.shape[2]
    kv_owner = shard * (query_width // HD) // (QH // KVH)
    rows_in = lax.dynamic_index_in_dim(inputs, section, 0, False)
    own_keyval = lax.dynamic_slice_in_dim(w_keyval[0], kv_owner * HD, HD, 2).reshape(width, 2 * HD)
    io_end = query_width + 2 * HD + w_state_io.shape[2]
    widths = (query_width, query_width + 2 * HD, io_end, io_end - (-head_count // 128) * 128)
    proj = jnp.concatenate(
        [
            w_query[0],
            own_keyval,
            w_state_io[0],
            jnp.pad(w_step[0], ((0, 0), (0, -head_count % 128))),
            w_mixer_in[0].reshape(width, -1),
        ],
        axis=1,
    )
    vectors = jnp.concatenate([norm_in[0], norm_ffn[0], step_bias[0], decay_rate[0], skip_gain[0]])
    block_in = line_gather(rows_in)
    (block_in,), (proj,) = after((block_in,), proj)
    own = (
        proj,
        jnp.concatenate([w_attn_out[0], w_mixer_out[0]], axis=0),
        w_gate_up[0].reshape(width, -1),
        w_down[0],
        vectors,
    )
    other = tuple(swap(array) for array in own)

    def layer_weights(layer):
        weights = types.SimpleNamespace()
        chosen = [jnp.where(section == layer, a, b) for a, b in zip(own, other)]
        weights.proj, weights.out, weights.gate_up, weights.down, vectors = chosen
        heads = vectors[2 * width :]
        weights.gain_in = vectors[:width]
        weights.gain_ffn = vectors[width : 2 * width]
        skip = heads[2 * head_count :]
        rows = heads[: 2 * head_count].reshape(2, head_count)
        weights.head_rows = jnp.pad(rows, ((0, 6), (0, -head_count % 128)))
        weights.skip_row = jnp.repeat(skip, HP)[None]
        weights.heads = head_count
        weights.widths = widths
        weights.kv_owner = kv_owner
        return weights

    layers = [layer_weights(0), layer_weights(1)]
    rows_cot = lax.dynamic_index_in_dim(cotangent, section, 0, False)
    length = block_in.shape[0]
    part = rows_in.shape[0]
    layout = block_layout(lax.dynamic_index_in_dim(doc_lengths, section, 0, False), length)

    def own_rows(values):
        return lax.dynamic_slice_in_dim(values, shard * part, part, 0)

    hidden = block_in.astype(f32)
    normed = norm_apply(hidden, layers[0].gain_in).astype(bf16)
    hiddens, outs, saves = [], [], []
    for layer in range(2):
        weights = layers[layer]
        hiddens.append(hidden)
        if layer == 1:
            (normed,), (rows_cot,) = after((normed,), rows_cot)
            block_cot = lax.all_gather(rows_cot, SHARD, axis=0, tiled=True)
        partial, saved = layer_forward(weights, normed, layout)
        first, second = layers
        wanted = [(1, own[i], other[i]) for i in (0, 1)]
        if layer == 1:
            wanted = [(0, own[i], other[i]) for i in (2, 3)]
        saved.middle, saved.ffn_in, chosen = copying_sum(
            middle_kernel, 1 + 8 * layer, f32, partial, hidden, weights.gain_ffn, wanted
        )
        if layer == 0:
            second.proj, second.out = chosen
        else:
            first.gate_up, first.down = chosen
        partial, saved.gate_pre, saved.upward, saved.product = ffn_forward(
            weights, saved.ffn_in
        )
        saves.append(saved)
        if layer == 0:
            wanted = [(1, own[i], other[i]) for i in (2, 3)]
            out_low, normed, chosen = copying_sum(
                layer_end_kernel, 2, bf16, partial, saved.middle, second.gain_in, wanted
            )
            second.gate_up, second.down = chosen
            outs.append(own_rows(out_low))
            hidden = out_low.astype(f32)
        else:
            held = types.SimpleNamespace(tail=partial.astype(bf16))

    d_out = d_low = block_cot
    d_hiddens, grads = [None, None], [None, None]
    for layer in (1, 0):
        d_hidden, d_low, grads[layer] = layer_backward(
            layers[layer], saves[layer], d_out, d_low, hiddens[layer], layout, layer == 0, grads[1] if layer == 0 else held
        )
        d_hiddens[layer] = d_hidden
        d_out = d_low

    total = lax.psum_scatter(held.tail, SHARD, scatter_dimension=0, tiled=True)
    outs.append((own_rows(saves[1].middle) + total.astype(f32)).astype(bf16))
    first, second = grads
    tinies = []
    for g in grads:
        vector = jnp.concatenate([g.gain_in, g.gain_ffn, g.step_bias, g.decay, g.skip])
        size = -(-vector.shape[0] // 1024) * 8
        tinies.append(jnp.pad(vector, (0, size * 128 - vector.shape[0])).reshape(size, 128))
    query, zx, up, down, out, out_rows, grad_rows, shared, tiny = finish(
        first,
        second,
        outs,
        [own_rows(d) for d in d_hiddens],
        tinies,
        [first.wide, second.wide],
        [shared_columns(saved.normed) for saved in saves],
    )
    tiny = tiny.reshape(-1)
    place = lax.axis_index(CTX) * lax.axis_size(SHARD) + shard
    slot = width // (lax.axis_size(CTX) * lax.axis_size(SHARD))
    grad_in = lax.dynamic_slice_in_dim(tiny, place * slot, slot, 0)
    grad_ffn = lax.dynamic_slice_in_dim(tiny, width + place * slot, slot, 0)
    heads = tiny[2 * width :]
    step = jnp.where(
        leading,
        first.proj[1][:, zx.shape[2] // 2 :],
        second.mix[1][:, zx.shape[2] // 2 : zx.shape[2] // 2 + 128],
    )
    io_width = w_state_io.shape[2]
    return (
        out_rows[None],
        grad_rows[None],
        grad_in[None],
        query.astype(f32)[None],
        shared[:, io_width:].astype(f32).reshape(-1, 2, KVH * HD)[None],
        out[:query_width].astype(f32)[None],
        jnp.swapaxes(zx, 0, 1)[None],
        shared[:, :io_width].astype(f32)[None],
        step[:, :head_count].astype(f32)[None],
        heads[:head_count][None],
        heads[head_count : 2 * head_count][None],
        heads[2 * head_count : 3 * head_count][None],
        out[query_width:].astype(f32)[None],
        grad_ffn[None],
        jnp.swapaxes(up, 0, 1)[None],
        down.astype(f32)[None],
    )


def solution(mesh):
    return jax.shard_map(
        body,
        mesh=mesh,
        in_specs=(
            P(None, (CTX, SHARD), None),
            P(None, (CTX, SHARD), None),
            P(),
            P(SECTION, None),
            P(SECTION, None, SHARD),
            P(SECTION, None, None, None),
            P(SECTION, SHARD, None),
            P(SECTION, None, None, SHARD),
            P(SECTION, None, None),
            P(SECTION, None, SHARD),
            P(SECTION, SHARD),
            P(SECTION, SHARD),
            P(SECTION, SHARD),
            P(SECTION, SHARD, None),
            P(SECTION, None),
            P(SECTION, None, None, SHARD),
            P(SECTION, SHARD, None),
        ),
        out_specs=(
            P(SECTION, None, (CTX, SHARD), None),
            P(SECTION, None, (CTX, SHARD), None),
            P(SECTION, (CTX, SHARD)),
            P(SECTION, CTX, SHARD),
            P(SECTION, (CTX, SHARD), None, None),
            P(SECTION, SHARD, CTX),
            P(SECTION, CTX, None, SHARD),
            P(SECTION, (CTX, SHARD), None),
            P(SECTION, CTX, SHARD),
            P(SECTION, SHARD),
            P(SECTION, SHARD),
            P(SECTION, SHARD),
            P(SECTION, SHARD, CTX),
            P(SECTION, (CTX, SHARD)),
            P(SECTION, CTX, None, SHARD),
            P(SECTION, SHARD, CTX),
        ),
        check_vma=False,
    )
```

```python
import functools
import types

import jax
import jax.numpy as jnp
from jax import lax
from jax.experimental import pallas as pl
from jax.experimental.pallas import tpu as pltpu
from jax.sharding import PartitionSpec as P

SECTION, CTX, SHARD = "section", "ctx", "shard"
QH = 8
KVH = 2
HD = 128
HP = 64
CHUNKS = 16
LAG = 3

MESH = pl.DeviceIdType.MESH
eps = 1e-05
bf16 = jnp.bfloat16
f32 = jnp.float32


def line_sum(n, chunks, lag, p_rows, done, sr, sl, rr, rl, srs, sls, rrs, rls, tot, fill=None):
    z = lax.axis_index(SHARD)
    hasr, hasl = z < n - 1, z > 0
    bar = pltpu.get_barrier_semaphore()
    more = 0
    if fill is not None:
        more = fill.greet(bar)

    @pl.when(hasr)
    def _():
        pl.semaphore_signal(bar, inc=1, device_id={SHARD: z + 1}, device_id_type=MESH)

    @pl.when(hasl)
    def _():
        pl.semaphore_signal(bar, inc=1, device_id={SHARD: z - 1}, device_id_type=MESH)

    @pl.when(hasl & hasr)
    def _():
        pl.semaphore_wait(bar, 2 + more)

    @pl.when(jnp.logical_not(hasl & hasr))
    def _():
        pl.semaphore_wait(bar, 1 + more)

    def right(j):
        return pltpu.make_async_remote_copy(
            sr.at[j], rr.at[j], srs.at[j], rrs.at[j], device_id={SHARD: z + 1}, device_id_type=MESH
        )

    def left(j):
        return pltpu.make_async_remote_copy(
            sl.at[j], rl.at[j], sls.at[j], rls.at[j], device_id={SHARD: z - 1}, device_id_type=MESH
        )

    steps = chunks + lag * (n - 1)
    if fill is not None:
        fill.start()

    def one(i, _):
        def go(j, copy, came, goes, inbox, outbox):
            live = (j >= 0) & (j < chunks)

            @pl.when(live & came & goes)
            def _():
                copy(j).wait_recv()
                outbox[j] = (p_rows(j) + inbox[j].astype(f32)).astype(bf16)
                copy(j).start()

            @pl.when(live & jnp.logical_not(came))
            def _():
                outbox[j] = p_rows(j).astype(bf16)
                copy(j).start()

            @pl.when(live & jnp.logical_not(goes))
            def _():
                copy(j).wait_recv()

        go(i - lag * z, right, hasl, hasr, rr, sr)
        go(i - lag * (n - 1 - z), left, hasr, hasl, rl, sl)
        jd = i - lag * jnp.maximum(z, n - 1 - z)

        @pl.when((jd >= 0) & (jd < chunks))
        def _():
            tot[...] = p_rows(jd)

            @pl.when(hasl)
            def _():
                tot[...] += rr[jd].astype(f32)

            @pl.when(hasr)
            def _():
                tot[...] += rl[jd].astype(f32)

            done(jd, tot[...])

        if fill is not None:
            fill.step(i, steps)
        return 0

    lax.fori_loop(0, steps, one, 0)
    if fill is not None:
        fill.finish()

    def drain(j, _):
        @pl.when(hasr)
        def _():
            right(j).wait_send()

        @pl.when(hasl)
        def _():
            left(j).wait_send()

        return 0

    lax.fori_loop(0, chunks, drain, 0)


def row_slice(j, rows):
    return pl.ds(pl.multiple_of(j * rows, rows), rows)


def middle_kernel(n, chunks, lag, p_ref, h_ref, gain_ref, mid_ref, low_ref, *scratch, fill=None):
    rows = p_ref.shape[0] // chunks

    def p_rows(j):
        return p_ref[row_slice(j, rows), :]

    def done(j, total):
        v = h_ref[row_slice(j, rows), :].astype(f32) + total
        r = lax.rsqrt(jnp.mean(v * v, axis=-1, keepdims=True) + eps)
        mid_ref[row_slice(j, rows), :] = v
        low_ref[row_slice(j, rows), :] = (v * r * gain_ref[...]).astype(bf16)

    line_sum(n, chunks, lag, p_rows, done, *scratch, fill=fill)


class Copies:
    parts = 16

    def __init__(self, layers, own, other, out, boxes, came, went):
        self.layers, self.own, self.other, self.out = layers, own, other, out
        self.boxes, self.came, self.went = boxes, came, went

    def greet(self, bar):
        return 0

    def start(self):
        pass

    def rows(self, a, j):
        size = self.boxes[a].shape[1]
        return pl.ds(pl.multiple_of(j * size, size), size)

    def fetch(self, a, j, act):
        section, slot = lax.axis_index(SECTION), lax.rem(j, 2)
        for mine, source in ((True, self.own[a]), (False, self.other[a])):

            @pl.when((section == self.layers[a]) == mine)
            def _():
                part = source.at[self.rows(a, j), :]
                act(
                    pltpu.make_async_copy(
                        part, self.boxes[a].at[slot], self.came.at[2 * a + slot]
                    )
                )

    def store(self, a, j):
        slot = lax.rem(j, 2)
        part = self.out[a].at[self.rows(a, j), :]
        return pltpu.make_async_copy(self.boxes[a].at[slot], part, self.went.at[2 * a + slot])

    def step(self, i, steps):
        @pl.when((i >= 1) & (i <= self.parts))
        def _():
            for a in range(len(self.layers)):
                self.fetch(a, i - 1, lambda copy: copy.wait())
                self.store(a, i - 1).start()

        @pl.when((i >= 2) & (i < self.parts))
        def _():
            for a in range(len(self.layers)):
                self.store(a, i - 2).wait()

        @pl.when(i < self.parts)
        def _():
            for a in range(len(self.layers)):
                self.fetch(a, i, lambda copy: copy.start())

    def finish(self):
        for a in range(len(self.layers)):
            for j in (self.parts - 2, self.parts - 1):
                self.store(a, j).wait()


def copying(kernel, layers, n, chunks, lag, p_ref, h_ref, gain_ref, *refs):
    count = len(layers)
    own, other, refs = refs[:count], refs[count : 2 * count], refs[2 * count :]
    first_ref, low_ref, refs = refs[0], refs[1], refs[2:]
    out, refs = refs[:count], refs[count:]
    copies = Copies(layers, own, other, out, refs[9 : 9 + count], *refs[9 + count :])
    kernel(n, chunks, lag, p_ref, h_ref, gain_ref, first_ref, low_ref, *refs[:9], fill=copies)


def layer_end_kernel(n, chunks, lag, p_ref, h_ref, gain_ref, out_ref, low_ref, *scratch, fill=None):
    rows = p_ref.shape[0] // chunks

    def p_rows(j):
        return p_ref[row_slice(j, rows), :]

    def done(j, total):
        out = (h_ref[row_slice(j, rows), :] + total).astype(bf16)
        out_ref[row_slice(j, rows), :] = out
        v = out.astype(f32)
        r = lax.rsqrt(jnp.mean(v * v, axis=-1, keepdims=True) + eps)
        low_ref[row_slice(j, rows), :] = (v * r * gain_ref[...]).astype(bf16)

    line_sum(n, chunks, lag, p_rows, done, *scratch, fill=fill)


def flipped(place, k, count):
    total, bit = 0, 1
    while bit < count:
        total = total + (place // bit + k // bit) % 2 * bit
        bit *= 2
    return total


def mirrored(k, count):
    total, bit = 0, 1
    while bit < count:
        total = total + k // bit % 2 * (count // (2 * bit))
        bit *= 2
    return total


class Fill:
    first = 6

    def __init__(self, plan, xs, ys, outs, scratch):
        self.plan, self.xs, self.ys, self.outs = plan, xs, ys, outs
        count = len(plan)
        self.other_x, rest = scratch[: len(xs)], scratch[len(xs) :]
        self.own_y, self.other_y = rest[:count], rest[count : 2 * count]
        self.send, self.recv = rest[2 * count :]

    def greet(self, bar):
        other = 1 - lax.axis_index(SECTION)
        pl.semaphore_signal(bar, inc=1, device_id={SECTION: other}, device_id_type=MESH)
        return 1

    def copies(self):
        section = lax.axis_index(SECTION)
        copies = []

        def add(source, target):
            i = len(copies)
            copies.append(
                pltpu.make_async_remote_copy(
                    source,
                    target,
                    self.send.at[i],
                    self.recv.at[i],
                    device_id={SECTION: 1 - section},
                    device_id_type=MESH,
                )
            )

        for x, target in zip(self.xs, self.other_x):
            add(x, target)
        for (_, _, parts), target in zip(self.plan, self.other_y):
            at = 0
            for y, low, high, width in parts:
                start = pl.multiple_of(low + (high - low) * (1 - section), 128)
                add(self.ys[y].at[:, pl.ds(start, width)], target.at[:, at : at + width])
                at += width
        return copies

    def start(self):
        for copy in self.copies():
            copy.start()
        section = lax.axis_index(SECTION)
        for (_, _, parts), own in zip(self.plan, self.own_y):
            at = 0
            for y, low, high, width in parts:
                start = pl.multiple_of(low + (high - low) * section, 128)
                own[:, at : at + width] = self.ys[y][:, pl.ds(start, width)]
                at += width

    def each(self, steps):
        return -(-lax.axis_size(CTX) * len(self.plan) // (steps - self.first))

    def step(self, i, steps):
        place, count = lax.axis_index(CTX), lax.axis_size(CTX)

        @pl.when(i == self.first)
        def _():
            for copy in self.copies():
                copy.wait_recv()

        each = self.each(steps)
        begin = (i - self.first) * each

        def piece(t, _):
            at = [0] * 4
            for f, (x, stream, _) in enumerate(self.plan):
                k = t - f * count
                width = self.own_y[f].shape[1]
                where = slice(at[stream], at[stream] + width)
                at[stream] += width
                kept, sent = self.outs[2 * stream : 2 * stream + 2]
                turned = stream % 2

                @pl.when((k >= 0) & (k < count))
                def _():
                    block = kept.shape[1]
                    source = flipped(place, mirrored(k, count) if turned else k, count)
                    cols = pl.ds(pl.multiple_of(source * block, block), block)
                    dims = (((0,), (0,)), ((), ()))
                    total = lax.dot_general(
                        self.xs[x][:, cols], self.own_y[f][...], dims, preferred_element_type=f32
                    ) + lax.dot_general(
                        self.other_x[x][:, cols],
                        self.other_y[f][...],
                        dims,
                        preferred_element_type=f32,
                    )
                    low = total.astype(bf16)

                    @pl.when(k < count // 2)
                    def _():
                        kept[k, :, where] = low

                    @pl.when(k >= count // 2)
                    def _():
                        sent[k - count // 2, :, where] = low

            return 0

        @pl.when(i >= self.first)
        def _():
            lax.fori_loop(begin, begin + each, piece, 0)

    def finish(self):
        for copy in self.copies():
            copy.wait_send()


class Halving:
    cuts = 2

    def __init__(self, streams, outs, scratch, turns, begin=None, greets=True):
        self.turns, self.begin, self.greets = turns, begin, greets
        self.place, self.count = lax.axis_index(CTX), lax.axis_size(CTX)
        self.streams, self.outs = streams, outs
        self.orders = ctx_orders()
        self.levels = len(self.orders[0])
        self.inbox = [scratch[k * self.levels : (k + 1) * self.levels] for k in range(2)]
        rest = scratch[2 * self.levels :]
        self.sums = [rest[k * (self.levels - 1) : (k + 1) * (self.levels - 1)] for k in range(2)]
        self.send, self.recv = rest[2 * (self.levels - 1) :]

    def greet(self, bar):
        if not self.greets:
            return 0
        for bit in self.orders[0]:
            peer = flipped(self.place, bit, self.count)
            pl.semaphore_signal(bar, inc=1, device_id={CTX: peer}, device_id_type=MESH)
        return self.levels

    def rows(self, cut):
        size = self.outs[0].shape[0] // self.cuts
        return pl.ds(cut * size, size)

    def copy(self, level, stream, cut):
        rows = self.rows(cut)
        if level == 0:
            source = self.streams[2 * stream + 1].at[:, rows, :]
        else:
            blocks = self.count >> (level + 1)
            source = self.sums[stream][level - 1].at[pl.ds(blocks, blocks), rows, :]
        i = (level * 2 + stream) * self.cuts + cut
        return pltpu.make_async_remote_copy(
            source,
            self.inbox[stream][level].at[:, rows, :],
            self.send.at[i],
            self.recv.at[i],
            device_id={CTX: flipped(self.place, self.orders[stream][level], self.count)},
            device_id_type=MESH,
        )

    def advance(self, level, cut):
        rows, blocks = self.rows(cut), self.count >> (level + 1)
        for stream in range(2):
            self.copy(level, stream, cut).wait_recv()
            kept = self.streams[2 * stream] if level == 0 else self.sums[stream][level - 1]
            for k in range(blocks):
                total = kept[k, rows, :].astype(f32) + self.inbox[stream][level][k, rows, :].astype(
                    f32
                )
                if level + 1 < self.levels:
                    self.sums[stream][level][k, rows, :] = total.astype(bf16)
                else:
                    self.outs[stream][rows, :] = total.astype(bf16)
            if level + 1 < self.levels:
                self.copy(level + 1, stream, cut).start()

    def start(self):
        if self.begin is None:
            self.first_copies()

    def first_copies(self):
        for cut in range(self.cuts):
            for stream in range(2):
                self.copy(0, stream, cut).start()

    def step(self, i, steps):
        if self.begin is not None:

            @pl.when(i == self.begin)
            def _():
                self.first_copies()

        for cut, turn in enumerate(self.turns):

            @pl.when(i == turn)
            def _():
                self.advance(0, cut)

    def finish(self):
        for cut in range(len(self.turns), self.cuts):
            self.advance(0, cut)
        for level in range(1, self.levels):
            for cut in range(self.cuts):
                self.advance(level, cut)
        for level in range(self.levels):
            for stream in range(2):
                for cut in range(self.cuts):
                    self.copy(level, stream, cut).wait_send()


def halving_scratch(streams):
    blocks, rows, width = streams[0].shape
    levels = len(ctx_bits())
    inbox = [pltpu.VMEM((blocks >> k, rows, width), bf16) for k in range(levels)]
    copies = levels * 2 * Halving.cuts
    return [*inbox * 2, *inbox[: levels - 1] * 2, *[pltpu.SemaphoreType.DMA((copies,))] * 2]


class Together:
    def __init__(self, *jobs):
        self.jobs = jobs

    def greet(self, bar):
        return sum(job.greet(bar) for job in self.jobs)

    def start(self):
        for job in self.jobs:
            job.start()

    def step(self, i, steps):
        for job in self.jobs:
            job.step(i, steps)

    def finish(self):
        for job in self.jobs:
            job.finish()


def scatter_kernel(n, chunks, lag, p_ref, q_ref, d_ref, v_ref, gain_ref, *refs):
    streams, outs, totals, scratch = refs[:4], refs[4:8], refs[8:10], refs[10:]
    job = Halving(streams, totals, scratch[9:], (7, 14))
    back_rows(n, chunks, lag, p_ref, d_ref, v_ref, gain_ref, *outs[:3], scratch[:9], job, q_ref, outs[3])


def back_kernel(n, chunks, lag, plan, x_count, y_count, beside, ready, soon, p_ref, *refs):
    q_ref = q_out = None
    if beside:
        q_ref, refs = refs[0], refs[1:]
    (d_ref, v_ref, gain_ref), refs = refs[:3], refs[3:]
    xs, refs = refs[:x_count], refs[x_count:]
    ys, refs = refs[:y_count], refs[y_count:]
    streams, refs = refs[:ready], refs[ready:]
    out_ref, low_ref, gg_ref = refs[:3]
    refs = refs[3:]
    if beside:
        q_out, refs = refs[0], refs[1:]
    sums, refs = refs[:4], refs[4:]
    totals, refs = refs[: ready // 2], refs[ready // 2 :]
    soon_totals, refs = refs[: 2 * soon], refs[2 * soon :]
    scratch, rest = refs[:9], refs[9:]
    cut = len(xs) + 2 * len(plan) + 2
    own, rest = rest[:cut], rest[cut:]
    here, rest = rest[: 4 * soon], rest[4 * soon :]
    fill = Fill(plan, xs, ys, (*sums, *here), own)
    jobs = [fill]
    boxes = 4 * len(ctx_bits())
    if ready:
        turns = (9, 17) if beside else (9,)
        jobs.append(Halving(streams, totals, rest[:boxes], turns))
        rest = rest[boxes:]
    if soon:
        begin = Fill.first + -(-2 * lax.axis_size(CTX) // fill.each(chunks + lag * (n - 1)))
        jobs.append(Halving(here, soon_totals, rest, (), begin, not ready))
    fill = Together(*jobs)
    outs = out_ref, low_ref, gg_ref
    back_rows(n, chunks, lag, p_ref, d_ref, v_ref, gain_ref, *outs, scratch, fill, q_ref, q_out)


def back_rows(
    n,
    chunks,
    lag,
    p_ref,
    d_ref,
    v_ref,
    gain_ref,
    out_ref,
    low_ref,
    gg_ref,
    scratch,
    fill,
    q_ref=None,
    q_out=None,
):
    rows, width = p_ref.shape[0] // chunks, p_ref.shape[1]
    gg_ref[...] = jnp.zeros_like(gg_ref)

    def p_rows(j):
        part = row_slice(j, rows)
        if q_ref is None:
            return p_ref[part, :]
        return jnp.concatenate([p_ref[part, :], q_ref[part, :].astype(f32)], axis=1)

    def done(j, total):
        if q_ref is not None:
            q_out[row_slice(j, rows), :] = total[:, width:].astype(bf16)
            total = total[:, :width]
        v = v_ref[row_slice(j, rows), :].astype(f32)
        r = lax.rsqrt(jnp.mean(v * v, axis=-1, keepdims=True) + eps)
        vr = v * r
        dg = total * gain_ref[...]
        inner = jnp.mean(dg * vr, axis=-1, keepdims=True)
        gg_ref[...] += jnp.sum((total * vr).reshape(rows // 8, 8, vr.shape[1]), axis=0)
        out = d_ref[row_slice(j, rows), :].astype(f32) + r * (dg - vr * inner)
        out_ref[row_slice(j, rows), :] = out
        low_ref[row_slice(j, rows), :] = out.astype(bf16)

    line_sum(n, chunks, lag, p_rows, done, *scratch, fill=fill)


def summed(kernel, collective, outs, *operands, extra=(), more=0, far=(0, 0), room=50):
    n = lax.axis_size(SHARD)
    length, width = operands[0].shape[0], operands[0].shape[1] + more
    box = pltpu.VMEM((CHUNKS, length // CHUNKS, width), bf16)
    distant = pl.BlockSpec(memory_space=pl.ANY)
    whole = pl.BlockSpec(memory_space=pltpu.VMEM)
    return pl.pallas_call(
        functools.partial(kernel, n, CHUNKS, LAG),
        out_shape=outs,
        in_specs=[whole] * (len(operands) - far[0]) + [distant] * far[0],
        out_specs=[whole] * (len(outs) - far[1]) + [distant] * far[1],
        scratch_shapes=[box] * 4
        + [pltpu.SemaphoreType.DMA((CHUNKS,))] * 4
        + [pltpu.VMEM((length // CHUNKS, width), f32), *extra],
        compiler_params=pltpu.CompilerParams(
            collective_id=collective, has_side_effects=True, vmem_limit_bytes=room << 20
        ),
        cost_estimate=pl.CostEstimate(flops=0, bytes_accessed=20 << 20, transcendentals=0),
        name="line_sum"+str(collective),
    )(*operands)


def line_gather(rows):
    count, place = lax.axis_size(SHARD), lax.axis_index(SHARD)
    part = rows.shape[0]
    block = jnp.zeros((count * part, rows.shape[1]), rows.dtype)
    block = lax.dynamic_update_slice_in_dim(block, rows, place * part, 0)
    for k in reversed(range(1, count)):
        got = lax.ppermute(rows, SHARD, [(i, i ^ k) for i in range(count)])
        block = lax.dynamic_update_slice_in_dim(block, got, (place ^ k) * part, 0)
    return block


def shaped(array, dtype):
    return jax.ShapeDtypeStruct(array.shape, dtype)


def copying_sum(kernel, collective, dtype, p, hidden, gain, wanted):
    layers, own, other = zip(*wanted)
    outs = [shaped(p, dtype), shaped(p, bf16)] + [shaped(a, bf16) for a in own]
    boxes = [pltpu.VMEM((2, a.shape[0] // Copies.parts, a.shape[1]), bf16) for a in own]
    first, low, *chosen = summed(
        functools.partial(copying, kernel, layers),
        collective,
        outs,
        p,
        hidden,
        gain[None],
        *own,
        *other,
        extra=[*boxes, *[pltpu.SemaphoreType.DMA((2 * len(layers),))] * 2],
        far=(2 * len(layers), len(layers)),
        room=26,
    )
    return first, low, chosen


def back_sum(collective, p, d_out, values, gain, plan, xs, ys, beside=(), ready=(), soon=False):
    count = lax.axis_size(CTX)
    length = p.shape[0]
    outs = [shaped(p, f32), shaped(p, bf16), jax.ShapeDtypeStruct((8, p.shape[1]), f32)]
    outs += [shaped(q, bf16) for q in beside]
    widths = [sum(part[3] for part in parts) for _, _, parts in plan]
    sums = []
    for stream in range(4 if soon else 2):
        total = sum(w for (_, at, _), w in zip(plan, widths) if at == stream)
        shape = (count // 2, xs[0].shape[1] // count, total)
        sums += [jax.ShapeDtypeStruct(shape, bf16)] * 2
    outs += sums[:4]
    extra = [pltpu.VMEM(x.shape, bf16) for x in xs]
    extra += [pltpu.VMEM((length, w), bf16) for w in widths] * 2
    copies = len(xs) + sum(len(parts) for _, _, parts in plan)
    extra += [pltpu.SemaphoreType.DMA((copies,))] * 2
    outs += [jax.ShapeDtypeStruct(a.shape[1:], bf16) for a in ready[::2]]
    if soon:
        outs += [jax.ShapeDtypeStruct(sums[4].shape[1:], bf16)] * 2
        extra += [pltpu.VMEM(a.shape, bf16) for a in sums[4:]]
    if ready:
        extra += halving_scratch(ready)
    if soon:
        extra += halving_scratch(sums[4:])

    def bound(n, chunks, lag, *refs):
        back_kernel(n, chunks, lag, plan, len(xs), len(ys), bool(beside), len(ready), soon, *refs)

    operands = (p, *beside, d_out, values, gain[None], *xs, *ys, *ready)
    more = sum(q.shape[1] for q in beside)
    room = 50 if ready else 38
    out, low, gg, *sums = summed(
        bound, collective, outs, *operands, extra=extra, more=more, room=room
    )
    return out, low, jnp.sum(gg, axis=0), *sums


def back_sum_scatter(collective, p, beside, d_out, values, gain, streams):
    outs = [shaped(p, f32), shaped(p, bf16), jax.ShapeDtypeStruct((8, p.shape[1]), f32)]
    outs += [shaped(beside, bf16)]
    outs += [jax.ShapeDtypeStruct(a.shape[1:], bf16) for a in streams[::2]]
    operands = (p, beside, d_out, values, gain[None], *streams)
    more = beside.shape[1]
    out, low, gg, whole, *totals = summed(
        scatter_kernel, collective, outs, *operands, extra=halving_scratch(streams), more=more, room=36
    )
    return out, low, jnp.sum(gg, axis=0), whole, totals


def dot(left, right, dims=((1,), (0,))):
    return lax.dot_general(left, right, (dims, ((), ())), preferred_element_type=f32)


NT = ((1,), (1,))
TN = ((0,), (0,))


def in_three(values):
    high = values.astype(bf16)
    rest = values - high.astype(f32)
    mid = rest.astype(bf16)
    return high, mid, (rest - mid.astype(f32)).astype(bf16)


def running_sum(values, reverse):
    length = values.shape[0]
    row = lax.broadcasted_iota(jnp.int32, (length, length), 0)
    col = lax.broadcasted_iota(jnp.int32, (length, length), 1)
    kept = jnp.where(row <= col if reverse else row >= col, 1.0, 0.0).astype(bf16)
    return sum(dot(kept, part) for part in in_three(values))


def lanes(shape):
    return lax.broadcasted_iota(jnp.int32, shape, 1)


def column(values, head):
    return jnp.sum(jnp.where(lanes(values.shape) == head, values, 0.0), axis=1, keepdims=True)


def in_pair(values, pair):
    low, high = column(values, 2 * pair), column(values, 2 * pair + 1)
    return jnp.where(lanes(values.shape) < HP, low, high)


def from_pair(values, pair):
    lane = lanes(values.shape)
    low = jnp.sum(jnp.where(lane < HP, values, 0.0), axis=1, keepdims=True)
    high = jnp.sum(jnp.where(lane < HP, 0.0, values), axis=1, keepdims=True)
    return jnp.where(lane == 2 * pair, low, 0.0) + jnp.where(lane == 2 * pair + 1, high, 0.0)


def pair_ds(pair, start=0):
    return pl.ds(pl.multiple_of(start + pair * 2 * HP, 2 * HP), 2 * HP)


def steps_of(step_raw, vec_ref, tok_ref, cum, cum_rows, step, enter, fade):
    shifted = step_raw + vec_ref[0:1, :]
    step[...] = jnp.maximum(shifted, 0.0) + jnp.log1p(jnp.exp(-jnp.abs(shifted)))
    cum[...] = running_sum(-step[...] * vec_ref[1:2, :], False)
    total = cum[...]
    cum_rows[...] = total.T
    enter[...] = jnp.exp(total) * tok_ref[:, 1:2]
    fade[...] = jnp.exp(total[-1:, :] - total) * tok_ref[:, 2:3]
    return shifted


def masks_of(tok_ref, key_ref):
    kept = (tok_ref[:, 3:4] >= key_ref[1:2, :]) & (tok_ref[:, 0:1] == key_ref[0:1, :])
    return jnp.where(kept, 0.0, -1e30)


def ctx_barrier(count, place):
    bar = pltpu.get_barrier_semaphore()

    def greet(k, _):
        pl.semaphore_signal(
            bar, inc=1, device_id={CTX: lax.rem(place + k, count)}, device_id_type=MESH
        )
        return 0

    lax.fori_loop(1, count, greet, 0)
    pl.semaphore_wait(bar, count - 1)


def ctx_copy(source, target, send, recv, peer):
    return pltpu.make_async_remote_copy(
        source, target, send, recv, device_id={CTX: peer}, device_id_type=MESH
    )


def mix_forward_kernel(
    count,
    widths,
    heads,
    proj_ref,
    vec_ref,
    skip_ref,
    tok_ref,
    key_ref,
    both_ref,
    mixed_ref,
    state_ref,
    keyval_ref,
    decay_ref,
    cum,
    cum_rows,
    step,
    enter,
    fade,
    mask,
    crossed,
    keyvals,
    fresh,
    decays,
    total_state,
    kv_send,
    kv_recv,
    st_send,
    st_recv,
    dc_send,
    dc_recv,
):
    place = lax.axis_index(CTX)
    length = proj_ref.shape[0]
    inner = (proj_ref.shape[1] - widths[3]) // 2
    pairs = heads // 2
    states = (widths[2] - widths[1]) // 2
    ctx_barrier(count, place)

    keyvals[0] = proj_ref[:, widths[0] : widths[1]].astype(bf16)

    def kv_copy(k):
        peer = lax.rem(place + k, count)
        return ctx_copy(keyvals.at[0], keyvals.at[k], kv_send.at[k], kv_recv.at[k], peer)

    def st_copy(k):
        peer = lax.rem(place + k, count)
        return ctx_copy(fresh.at[0], fresh.at[k], st_send.at[k], st_recv.at[k], peer)

    def dc_copy(k):
        peer = lax.rem(place + k, count)
        return ctx_copy(decays.at[0], decays.at[k], dc_send.at[k], dc_recv.at[k], peer)

    def kv_start(k, _):
        kv_copy(k).start()
        return 0

    lax.fori_loop(1, count, kv_start, 0)
    steps_of(
        proj_ref[:, widths[2] : widths[2] + 128], vec_ref, tok_ref, cum, cum_rows, step, enter, fade
    )
    last = cum_rows[: decays.shape[1], length - 1 :]
    decays[0] = jnp.broadcast_to(jnp.exp(last) * tok_ref[0:1, 4:5], decays.shape[1:])
    b_low = proj_ref[:, widths[1] : widths[1] + states].astype(bf16)
    c_low = proj_ref[:, widths[1] + states : widths[2]].astype(bf16)

    def make_fresh(pair, _):
        x = proj_ref[:, pair_ds(pair, widths[3] + inner)]
        x = x.astype(bf16).astype(f32)
        faded = (x * in_pair(fade[...] * step[...], pair)).astype(bf16)
        fresh[0, pair_ds(pair), :] = dot(faded, b_low, TN).astype(bf16)
        return 0

    lax.fori_loop(0, pairs, make_fresh, 0)

    def st_start(k, _):
        dc_copy(k).start()

        @pl.when(place + k < count)
        def _():
            st_copy(k).start()

        return 0

    lax.fori_loop(1, count, st_start, 0)
    mask[...] = masks_of(tok_ref, key_ref)
    crossed[...] = dot(c_low, b_low, NT) * states ** (-0.5)

    def inside(pair, _):
        x = proj_ref[:, pair_ds(pair, widths[3] + inner)]
        x = x.astype(bf16).astype(f32)
        xdt = (x * in_pair(step[...], pair)).astype(bf16)
        parts = []
        for side in range(2):
            head = 2 * pair + side
            spread = column(cum[...], head) - cum_rows[pl.ds(head, 1), :]
            weight = jnp.exp(spread + mask[:, :length])
            parts.append(dot((weight * crossed[...]).astype(bf16), xdt))
        mixed_ref[:, pair_ds(pair)] = jnp.where(lanes(parts[0].shape) < HP, *parts)
        return 0

    lax.fori_loop(0, pairs, inside, 0)

    def kv_wait(k, _):
        kv_copy(k).wait_recv()
        return 0

    lax.fori_loop(1, count, kv_wait, 0)
    keyval_ref[...] = keyvals[...].reshape(keyval_ref.shape)
    for head in range(widths[0] // HD):
        query = proj_ref[:, head * HD : (head + 1) * HD].astype(bf16)
        scores = dot(query, keyval_ref[:, :HD], NT) * HD ** (-0.5) + mask[...]
        expo = jnp.exp(scores - jnp.max(scores, axis=1, keepdims=True))
        soft = expo * (1.0 / jnp.sum(expo, axis=1, keepdims=True))
        both_ref[:, head * HD : (head + 1) * HD] = dot(
            soft.astype(bf16), keyval_ref[:, HD:]
        ).astype(bf16)

    def dc_wait(k, _):
        dc_copy(k).wait_recv()

        @pl.when(k <= place)
        def _():
            st_copy(k).wait_recv()

        return 0

    lax.fori_loop(1, count, dc_wait, 0)
    total_state[...] = jnp.zeros_like(total_state)
    head_width = inner // heads

    def combine(index, _):
        slot = place - index

        def one_head(head, _):
            rows = pl.ds(pl.multiple_of(head * head_width, head_width), head_width)
            total_state[rows, :] = total_state[rows, :] * decays[slot, pl.ds(head, 1), :] + fresh[
                slot, rows, :
            ].astype(f32)
            return 0

        lax.fori_loop(0, heads, one_head, 0)
        return 0

    lax.fori_loop(0, place, combine, 0)
    state_ref[...] = total_state[...].astype(bf16)
    decay_ref[...] = decays[...]

    def finish(pair, _):
        carried = dot(c_low, state_ref[pair_ds(pair), :], NT)
        mixed = mixed_ref[:, pair_ds(pair)] + carried * in_pair(enter[...], pair)
        mixed_ref[:, pair_ds(pair)] = mixed
        x = proj_ref[:, pair_ds(pair, widths[3] + inner)]
        x = x.astype(bf16).astype(f32)
        gate = proj_ref[:, pair_ds(pair, widths[3])]
        y = mixed + x * skip_ref[0:1, pair_ds(pair)]
        both_ref[:, pair_ds(pair, widths[0])] = (
            y * gate / (1.0 + jnp.exp(-gate))
        ).astype(bf16)
        return 0

    lax.fori_loop(0, pairs, finish, 0)

    def drain(k, _):
        kv_copy(k).wait_send()
        dc_copy(k).wait_send()

        @pl.when(place + k < count)
        def _():
            st_copy(k).wait_send()

        return 0

    lax.fori_loop(1, count, drain, 0)


def mix_backward_kernel(
    count,
    widths,
    heads,
    proj_ref,
    vec_ref,
    skip_ref,
    tok_ref,
    key_ref,
    mixed_ref,
    state_ref,
    keyval_ref,
    decay_ref,
    d_both_ref,
    d_proj_ref,
    d_vec_ref,
    cum,
    cum_rows,
    step,
    enter,
    fade,
    mask,
    crossed,
    d_crossed,
    d_y,
    d_carried,
    d_x,
    d_keyval,
    d_b,
    d_c,
    d_cum,
    d_step,
    d_coeff,
    d_skip,
    d_states,
    total_state,
    kv_out,
    kv_in,
    kv_send,
    kv_recv,
    st_send,
    st_recv,
):
    place = lax.axis_index(CTX)
    length = proj_ref.shape[0]
    inner = (proj_ref.shape[1] - widths[3]) // 2
    pairs = heads // 2
    head_width = inner // heads
    states = (widths[2] - widths[1]) // 2
    ctx_barrier(count, place)

    def back(k):
        return lax.rem(place + count - k, count)

    def kv_copy(k):
        return ctx_copy(kv_out.at[k], kv_in.at[k], kv_send.at[k], kv_recv.at[k], back(k))

    def st_copy(k):
        return ctx_copy(d_states.at[0], d_states.at[k], st_send.at[k], st_recv.at[k], back(k))

    shifted = steps_of(
        proj_ref[:, widths[2] : widths[2] + 128], vec_ref, tok_ref, cum, cum_rows, step, enter, fade
    )
    b_low = proj_ref[:, widths[1] : widths[1] + states].astype(bf16)
    c_low = proj_ref[:, widths[1] + states : widths[2]].astype(bf16)
    d_cum[...] = jnp.zeros_like(d_cum)
    d_step[...] = jnp.zeros_like(d_step)
    d_coeff[...] = jnp.zeros_like(d_coeff)
    d_skip[...] = jnp.zeros_like(d_skip)

    def x_of(pair):
        x = proj_ref[:, pair_ds(pair, widths[3] + inner)]
        return x.astype(bf16).astype(f32)

    def outer(pair, _):
        gate = proj_ref[:, pair_ds(pair, widths[3])]
        d_gated = d_both_ref[:, pair_ds(pair, widths[0])]
        x, mixed, skip = x_of(pair), mixed_ref[:, pair_ds(pair)], skip_ref[0:1, pair_ds(pair)]
        sig = 1.0 / (1.0 + jnp.exp(-gate))
        dy = d_gated * gate * sig
        d_gate = d_gated * (mixed + x * skip) * sig * (1.0 + gate * (1.0 - sig))
        d_proj_ref[:, pair_ds(pair, widths[3])] = d_gate.astype(bf16)
        low = dy.astype(bf16)
        d_y[:, pair_ds(pair)] = low
        d_x[:, pair_ds(pair)] = dy * skip
        d_skip[...] += from_pair(dy * x, pair)
        d_cum[...] += from_pair(low.astype(f32) * mixed, pair)
        carried = (low.astype(f32) * in_pair(enter[...], pair)).astype(bf16)
        d_carried[:, pair_ds(pair)] = carried
        d_states[0, pair_ds(pair), :] = dot(carried, c_low, TN).astype(bf16)
        return 0

    lax.fori_loop(0, pairs, outer, 0)

    def st_start(k, _):
        @pl.when(k <= place)
        def _():
            st_copy(k).start()

        return 0

    lax.fori_loop(1, count, st_start, 0)
    mask[...] = masks_of(tok_ref, key_ref)
    for head in range(widths[0] // HD):
        cols = slice(head * HD, (head + 1) * HD)
        query = proj_ref[:, cols].astype(bf16)
        scores = dot(query, keyval_ref[:, :HD], NT) * HD ** (-0.5) + mask[...]
        expo = jnp.exp(scores - jnp.max(scores, axis=1, keepdims=True))
        soft = expo * (1.0 / jnp.sum(expo, axis=1, keepdims=True))
        grad = d_both_ref[:, cols].astype(bf16)
        d_soft = dot(grad, keyval_ref[:, HD:], NT)
        d_scores = soft * (d_soft - jnp.sum(soft * d_soft, axis=1, keepdims=True))
        d_raw = (d_scores * HD ** (-0.5)).astype(bf16)
        d_proj_ref[:, cols] = dot(d_raw, keyval_ref[:, :HD]).astype(bf16)
        d_keys, d_values = dot(d_raw, query, TN), dot(soft.astype(bf16), grad, TN)
        if head == 0:
            d_keyval[:, :HD] = d_keys
            d_keyval[:, HD:] = d_values
        else:
            d_keyval[:, :HD] += d_keys
            d_keyval[:, HD:] += d_values
    kv_out[...] = d_keyval[...].astype(bf16).reshape(kv_out.shape)

    def kv_start(k, _):
        kv_copy(k).start()
        return 0

    lax.fori_loop(1, count, kv_start, 0)
    crossed[...] = dot(c_low, b_low, NT) * states ** (-0.5)
    d_crossed[...] = jnp.zeros_like(d_crossed)

    def inside(pair, _):
        x = x_of(pair)
        steps = in_pair(step[...], pair)
        xdt = (x * steps).astype(bf16)
        low = d_y[:, pair_ds(pair)]
        lane = lanes(low.shape)
        parts = []
        for side in range(2):
            head = 2 * pair + side
            spread = column(cum[...], head) - cum_rows[pl.ds(head, 1), :]
            weight = jnp.exp(spread + mask[:, :length])
            parts.append(dot((weight * crossed[...]).astype(bf16), low, TN))
            mine = (lane >= HP) if side else (lane < HP)
            alone = jnp.where(mine, low.astype(f32), 0.0).astype(bf16)
            d_crossed[...] += dot(alone, xdt, NT) * weight
        d_xdt = jnp.where(lane < HP, *parts)
        d_x[:, pair_ds(pair)] += d_xdt * steps
        d_step[...] += from_pair(d_xdt * x, pair)
        d_cum[...] -= from_pair(d_xdt * xdt.astype(f32), pair)
        return 0

    lax.fori_loop(0, pairs, inside, 0)
    low_crossed = (d_crossed[...] * states ** (-0.5)).astype(bf16)
    d_c[...] = dot(low_crossed, b_low) + dot(d_carried[...], state_ref[...])
    d_b[...] = dot(low_crossed, c_low, TN)

    def st_wait(k, _):
        @pl.when(place + k < count)
        def _():
            st_copy(k).wait_recv()

        return 0

    lax.fori_loop(1, count, st_wait, 0)
    total_state[...] = jnp.zeros_like(total_state)

    def combine(index, _):
        slot = count - 1 - place - index
        source = lax.rem(count - slot, count)

        def one_head(head, _):
            rows = pl.ds(pl.multiple_of(head * head_width, head_width), head_width)
            total_state[rows, :] = total_state[rows, :] * decay_ref[
                source, pl.ds(head, 1), :
            ] + d_states[slot, rows, :].astype(f32)
            return 0

        lax.fori_loop(0, heads, one_head, 0)
        return 0

    lax.fori_loop(0, count - 1 - place, combine, 0)
    d_vec_ref[...] = jnp.zeros_like(d_vec_ref)

    def from_later(pair, _):
        rows = pair_ds(pair)
        later = total_state[rows, :]
        low = later.astype(bf16)
        x = x_of(pair)
        coeffs = in_pair(fade[...] * step[...], pair)
        back_x = dot(b_low, low, NT)
        d_proj_ref[:, pair_ds(pair, widths[3] + inner)] = (
            d_x[:, rows] + back_x * coeffs
        ).astype(bf16)
        d_coeff[...] += from_pair(back_x * x, pair)
        d_b[...] += dot((x * coeffs).astype(bf16), low)
        product = later * state_ref[rows, :].astype(f32)
        row = lax.broadcasted_iota(jnp.int32, product.shape, 0)
        lane = lanes((1, 128))
        for side in range(2):
            mine = (row >= HP) if side else (row < HP)
            part = jnp.sum(jnp.where(mine, product, 0.0), axis=0, keepdims=True)
            part = jnp.sum(part, axis=1, keepdims=True)
            d_vec_ref[3:4, :] += jnp.where(lane == 2 * pair + side, part, 0.0)
        return 0

    lax.fori_loop(0, pairs, from_later, 0)
    fading = fade[...]
    d_keep = d_coeff[...] * fading * step[...]
    block_decay = jnp.exp(cum[length - 1 :, :]) * tok_ref[0:1, 4:5]
    d_last = jnp.sum(d_keep, axis=0, keepdims=True) + block_decay * d_vec_ref[3:4, :]
    d_log = running_sum(d_cum[...] - d_keep, True) + d_last
    d_size = d_step[...] + d_coeff[...] * fading - vec_ref[1:2, :] * d_log
    d_raw_step = d_size / (1.0 + jnp.exp(-shifted))
    d_proj_ref[:, widths[2] : widths[3]] = jnp.where(
        lanes(d_raw_step.shape) < heads, d_raw_step, 0.0
    ).astype(bf16)
    d_vec_ref[0:1, :] = jnp.sum(d_raw_step, axis=0, keepdims=True)
    d_vec_ref[1:2, :] = -jnp.sum(step[...] * d_log, axis=0, keepdims=True)
    d_vec_ref[2:3, :] = jnp.sum(d_skip[...], axis=0, keepdims=True)
    d_proj_ref[:, widths[1] : widths[1] + states] = d_b[...].astype(bf16)
    d_proj_ref[:, widths[1] + states : widths[2]] = d_c[...].astype(bf16)

    def kv_wait(k, _):
        kv_copy(k).wait_recv()
        d_keyval[:length, :] += kv_in[k].astype(f32)
        return 0

    lax.fori_loop(1, count, kv_wait, 0)
    d_proj_ref[:, widths[0] : widths[1]] = d_keyval[:length, :].astype(bf16)

    def drain(k, _):
        kv_copy(k).wait_send()

        @pl.when(k <= place)
        def _():
            st_copy(k).wait_send()

        return 0

    lax.fori_loop(1, count, drain, 0)


def mixer_call(kernel, collective, outs, scratch, sems, widths, heads, operands, room):
    count = lax.axis_size(CTX)
    whole = pl.BlockSpec(memory_space=pltpu.VMEM)
    return pl.pallas_call(
        functools.partial(kernel, count, widths, heads),
        out_shape=outs,
        in_specs=[whole] * len(operands),
        out_specs=[whole] * len(outs),
        scratch_shapes=[pltpu.VMEM(*s) for s in scratch]
        + [pltpu.SemaphoreType.DMA((count,))] * sems,
        compiler_params=pltpu.CompilerParams(
            collective_id=collective,
            has_side_effects=True,
            vmem_limit_bytes=(room + 2 * count) << 20,
        ),
        cost_estimate=pl.CostEstimate(flops=0, bytes_accessed=20 << 20, transcendentals=0),
        name="mixer"+str(collective),
    )(*operands)


def mix_forward(weights, proj, layout):
    count = lax.axis_size(CTX)
    widths, heads = weights.widths, weights.heads
    length, inner = proj.shape[0], (proj.shape[1] - widths[3]) // 2
    states = (widths[2] - widths[1]) // 2
    kv = widths[1] - widths[0]
    shape = jax.ShapeDtypeStruct
    head_rows = -(-heads // 8) * 8
    outs = [
        shape((length, widths[0] + inner), bf16),
        shape((length, inner), f32),
        shape((inner, states), bf16),
        shape((count * length, kv), bf16),
        shape((count, head_rows, states), f32),
    ]
    per_head = ((length, 128), f32)
    scratch = [
        per_head,
        ((128, length), f32),
        per_head,
        per_head,
        per_head,
        ((length, count * length), f32),
        ((length, length), f32),
        ((count, length, kv), bf16),
        ((count, inner, states), bf16),
        ((count, head_rows, states), f32),
        ((inner, states), f32),
    ]
    operands = (proj, weights.head_rows, weights.skip_row, *layout)
    return mixer_call(mix_forward_kernel, 5, outs, scratch, 6, widths, heads, operands, 18)


def mix_backward(weights, saved, d_both, layout):
    count = lax.axis_size(CTX)
    widths, heads = weights.widths, weights.heads
    proj = saved.proj
    length, inner = proj.shape[0], (proj.shape[1] - widths[3]) // 2
    states = (widths[2] - widths[1]) // 2
    kv = widths[1] - widths[0]
    shape = jax.ShapeDtypeStruct
    outs = [shape(proj.shape, bf16), shape((8, 128), f32)]
    per_head = ((length, 128), f32)
    square = ((length, length), f32)
    scratch = [
        per_head,
        ((128, length), f32),
        per_head,
        per_head,
        per_head,
        ((length, count * length), f32),
        square,
        square,
        ((length, inner), bf16),
        ((length, inner), bf16),
        ((length, inner), f32),
        ((count * length, kv), f32),
        ((length, states), f32),
        ((length, states), f32),
        per_head,
        per_head,
        per_head,
        per_head,
        ((count, inner, states), bf16),
        ((inner, states), f32),
        ((count, length, kv), bf16),
        ((count, length, kv), bf16),
    ]
    operands = (
        proj,
        weights.head_rows,
        weights.skip_row,
        *layout,
        saved.mixed,
        saved.state_in,
        saved.keyval_all,
        saved.decays,
        d_both,
    )
    return mixer_call(mix_backward_kernel, 6, outs, scratch, 4, widths, heads, operands, 24)


def finish_kernel(
    count,
    places,
    widths,
    *refs,
):
    unsummed, arrays, refs = refs[:8], refs[8:18], refs[18:]
    (
        rows0,
        rows1,
        grad0,
        grad1,
        tiny0,
        tiny1,
        wide0,
        wide1,
        columns0,
        columns1,
        *refs,
    ) = refs
    (
        query_out,
        zx_out,
        up_out,
        down_out,
        out_out,
        rows_out,
        grad_out,
        shared_out,
        tiny_out,
        *refs,
    ) = refs
    arrays, refs = (*refs[:4], *arrays), refs[4:]
    boxes, refs = refs[: len(widths)], refs[len(widths) :]
    (
        rows_box,
        grad_box,
        tiny_box,
        tiny_sum,
        tiny_all,
        wide_boxes,
        columns_boxes,
        blocks,
        blocks_box,
        shared,
        shared_box,
        send,
        recv,
        ctx_send,
        ctx_recv,
    ) = refs
    section, place = lax.axis_index(SECTION), lax.axis_index(CTX)
    bar = pltpu.get_barrier_semaphore()
    pl.semaphore_signal(bar, inc=1, device_id={SECTION: 1 - section}, device_id_type=MESH)
    for k in range(1, count):
        peer = flipped(place, k, count)
        pl.semaphore_signal(bar, inc=1, device_id={CTX: peer}, device_id_type=MESH)
    pl.semaphore_wait(bar, count)
    half = wide0.shape[1] // 2
    own_half = pl.ds(pl.multiple_of(section * half, half), half)
    other_half = pl.ds(pl.multiple_of((1 - section) * half, half), half)

    def over(i, source, target):
        return pltpu.make_async_remote_copy(
            source,
            target,
            send.at[i],
            recv.at[i],
            device_id={SECTION: 1 - section},
            device_id_type=MESH,
        )

    def across(i, k, source, target):
        return pltpu.make_async_remote_copy(
            source,
            target,
            ctx_send.at[i],
            ctx_recv.at[i],
            device_id={CTX: flipped(place, k, count)},
            device_id_type=MESH,
        )

    def part(layer, i):
        array, start, width = places[layer][i]
        return arrays[array].at[:, start : start + width]

    def by_section(act, first, second):
        @pl.when(section == 1)
        def _():
            act(first)

        @pl.when(section == 0)
        def _():
            act(second)

    block = blocks.shape[2]
    wides, columns = (wide0, wide1), (columns0, columns1)
    early = [over(l, wides[l].at[:, other_half], wide_boxes.at[l]) for l in range(2)]
    early += [over(2 + l, columns[l], columns_boxes.at[l]) for l in range(2)]
    for copy in early:
        copy.start()
    for i in range(4):
        arrays[i][...] = (unsummed[2 * i][...].astype(f32) + unsummed[2 * i + 1][...].astype(f32)).astype(bf16)
    pairs = [(tiny0, tiny1, tiny_box)]
    pairs += [(part(0, i), part(1, i), box) for i, box in enumerate(boxes)]
    pairs += [(rows0, rows1, rows_box), (grad0, grad1, grad_box)]
    copies = [
        (over(4 + i, first, box), over(4 + i, second, box))
        for i, (first, second, box) in enumerate(pairs)
    ]

    def each(act, which):
        for first, second in which:
            by_section(act, first, second)

    each(lambda copy: copy.start(), copies)
    for copy in early:
        copy.wait_recv()
    dims = (((0,), (0,)), ((), ()))

    def block_copy(l, k):
        return across(2 * k + l, k, blocks.at[l, k], blocks_box.at[l, k])

    for l in range(2):
        total = lax.dot_general(
            columns[l][...], wides[l][:, own_half], dims, preferred_element_type=f32
        ) + lax.dot_general(columns_boxes[l], wide_boxes[l], dims, preferred_element_type=f32)
        for k in range(count):
            blocks[l, k] = total[k * block : (k + 1) * block, :].astype(bf16)
        for k in range(1, count):
            block_copy(l, k).start()
    each(lambda copy: copy.wait_recv(), copies[:1])

    def first_tiny(mine):
        tiny_sum[...] = mine[...] + tiny_box[...]

    by_section(first_tiny, tiny1, tiny0)
    for k in range(1, count):
        across(2 * count + k, k, tiny_sum, tiny_all.at[k]).start()

    def place_pieces(low_core, take):
        query, zx_a, zx_b, up_a, up_b, down_a, down_b, out_a, out_b = (
            functools.partial(take, i) for i in range(9)
        )
        width = query_out.shape[1] // 2
        query_out[:, pl.ds(pl.multiple_of(low_core * width, width), width)] = query()
        edge = zx_out.shape[2] // 2
        zx_out[low_core, :, :edge] = zx_a().astype(f32)
        zx_out[low_core, :, edge:] = zx_b().astype(f32)
        edge = up_out.shape[2] // 2
        up_out[low_core, :, :edge] = up_a().astype(f32)
        up_out[low_core, :, edge:] = up_b().astype(f32)
        for target, pieces in ((down_out, (down_a, down_b)), (out_out, (out_a, out_b))):
            for i, piece in enumerate(pieces):
                height = target.shape[0] // 4
                start = low_core * 2 * height + i * height
                target[pl.ds(pl.multiple_of(start, height), height), :] = piece().T

    def own(layer):
        def take(i):
            return part(layer, i)[...]

        place_pieces(section, take)

    by_section(own, 1, 0)
    each(lambda copy: copy.wait_recv(), copies[1:])
    place_pieces(1 - section, lambda i: boxes[i][...])

    def rows_done(mine):
        rows_out[section] = mine[0][...]
        grad_out[section] = mine[1][...]

    by_section(rows_done, (rows1, grad1), (rows0, grad0))
    rows_out[1 - section] = rows_box[...]
    grad_out[1 - section] = grad_box[...]
    for l in range(2):
        rows = blocks[l, 0].astype(f32)
        for k in range(1, count):
            block_copy(l, k).wait_recv()
            rows += blocks_box[l, k].astype(f32)
        shared[l] = rows.astype(bf16)
    shared_copy = over(len(pairs) + 4, shared.at[1 - section], shared_box)
    shared_copy.start()
    everything = tiny_sum[...]
    for k in range(1, count):
        across(2 * count + k, k, tiny_sum, tiny_all.at[k]).wait_recv()
        everything += tiny_all[k]
    tiny_out[...] = everything

    shared_out[:, own_half] = shared[section]
    shared_copy.wait_recv()
    shared_out[:, other_half] = shared_box[...]
    for copy in early:
        copy.wait_send()
    each(lambda copy: copy.wait_send(), copies)
    shared_copy.wait_send()
    for k in range(1, count):
        for l in range(2):
            block_copy(l, k).wait_send()
        across(2 * count + k, k, tiny_sum, tiny_all.at[k]).wait_send()


def finish(first, second, rows, d_rows, tinies, wides, columns):
    count = lax.axis_size(CTX)
    pairs = [*first.ffn, *first.out]
    arrays = (*first.proj, *second.ffn, *second.down, *second.mix, *second.out)
    up, down = second.ffn[0].shape[1], second.down[0].shape[1]
    out = first.out[0][0].shape[1]
    step = 128
    most = second.mix[1].shape[1] - step
    query = first.proj[0].shape[1] - most

    places = (
        (
            (4, 0, query),
            (4, query, most),
            (5, 0, most),
            (0, 0, up),
            (1, 0, up),
            (0, up, down),
            (1, up, down),
            (2, 0, out),
            (3, 0, out),
        ),
        (
            (10, 0, query),
            (10, query, most),
            (11, 0, most),
            (6, 0, up),
            (7, 0, up),
            (8, 0, down),
            (9, 0, down),
            (12, 0, out),
            (13, 0, out),
        ),
    )
    length = first.proj[0].shape[0]
    widths = [piece[2] for piece in places[0]]
    half, block = wides[0].shape[1] // 2, columns[0].shape[1] // count
    shape = jax.ShapeDtypeStruct
    outs = [
        shape((length, 2 * query), bf16),
        shape((2, length, 2 * most), f32),
        shape((2, length, 2 * up), f32),
        shape((4 * down, length), bf16),
        shape((4 * out, length), bf16),
        shape((2,) + rows[0].shape, bf16),
        shape((2,) + d_rows[0].shape, f32),
        shape((block, 2 * half), bf16),
        shape(tinies[0].shape, f32),
    ]
    tokens = columns[0].shape[0]
    scratch = [pltpu.VMEM(kept.shape, bf16) for kept, _ in pairs]
    scratch += [pltpu.VMEM((length, w), bf16) for w in widths]
    scratch += [
        pltpu.VMEM(rows[0].shape, bf16),
        pltpu.VMEM(d_rows[0].shape, f32),
        pltpu.VMEM(tinies[0].shape, f32),
        pltpu.VMEM(tinies[0].shape, f32),
        pltpu.VMEM((count,) + tinies[0].shape, f32),
        pltpu.VMEM((2, tokens, half), bf16),
        pltpu.VMEM((2, tokens, count * block), bf16),
        pltpu.VMEM((2, count, block, half), bf16),
        pltpu.VMEM((2, count, block, half), bf16),
        pltpu.VMEM((2, block, half), bf16),
        pltpu.VMEM((block, half), bf16),
    ]
    over = len(widths) + 8
    scratch += [pltpu.SemaphoreType.DMA((n,)) for n in (over, over, 3 * count, 3 * count)]
    whole = pl.BlockSpec(memory_space=pltpu.VMEM)
    operands = (*sum(pairs, ()), *arrays, *rows, *d_rows, *tinies, *wides, *columns)
    return pl.pallas_call(
        functools.partial(finish_kernel, count, places, widths),
        out_shape=outs,
        in_specs=[whole] * len(operands),
        out_specs=[whole] * len(outs),
        scratch_shapes=scratch,
        compiler_params=pltpu.CompilerParams(
            collective_id=11, has_side_effects=True, vmem_limit_bytes=56 << 20
        ),
        cost_estimate=pl.CostEstimate(flops=0, bytes_accessed=20 << 20, transcendentals=0),
        name="finish",
    )(*operands)


def norm_apply(values, gain):
    return values * lax.rsqrt(jnp.mean(values * values, axis=-1, keepdims=True) + eps) * gain


def matmul(left, right):
    return jnp.dot(left, right, preferred_element_type=f32)


def matmul_nt(left, right):
    return lax.dot_general(left, right, (((1,), (1,)), ((), ())), preferred_element_type=f32)


def matmul_tn(left, right):
    return lax.dot_general(left, right, (((0,), (0,)), ((), ())), preferred_element_type=f32)


def swap(values):
    return lax.ppermute(values, SECTION, [(0, 1), (1, 0)])


def block_layout(doc_lengths, length):
    count, place = lax.axis_size(CTX), lax.axis_index(CTX)
    start = place * length
    bounds = jnp.cumsum(doc_lengths)[:-1]

    def segment_of(positions):
        return jnp.sum((positions[:, None] >= bounds[None, :]).astype(jnp.int32), axis=1)

    order = lax.rem(place + count - jnp.arange(count, dtype=jnp.int32), count)
    inside = jnp.arange(length, dtype=jnp.int32)
    keys = (order[:, None] * length + inside[None, :]).reshape(-1)
    positions = start + inside
    segments = segment_of(positions)
    before = jnp.where(place > 0, segment_of(start[None] - 1)[0], -1)
    goes_on = jnp.broadcast_to(segments[-1] == before, segments.shape)
    columns = [segments, segments == before, segments == segments[-1], positions, goes_on]
    tokens = jnp.stack([c.astype(f32) for c in columns], axis=1)
    return jnp.pad(tokens, ((0, 0), (0, 3))), jnp.stack(
        [segment_of(keys).astype(f32), keys.astype(f32)]
    )


def layer_forward(weights, normed, layout):
    proj = matmul(normed, weights.proj)
    both, mixed, state_in, keyval_all, decays = mix_forward(weights, proj, layout)
    saved = types.SimpleNamespace(
        normed=normed,
        proj=proj,
        both=both,
        mixed=mixed,
        state_in=state_in,
        keyval_all=keyval_all,
        decays=decays,
    )
    return matmul(both, weights.out), saved


def ffn_forward(weights, ffn_in):
    gate_up = matmul(ffn_in, weights.gate_up)
    width = gate_up.shape[1] // 2
    gate_pre, upward = gate_up[:, :width], gate_up[:, width:]
    product = (jax.nn.silu(gate_pre) * upward).astype(bf16)
    return matmul(product, weights.down), gate_pre, upward, product


def ctx_bits():
    return [1 << i for i in reversed(range((lax.axis_size(CTX) - 1).bit_length()))]


def flip(values, bit):
    return lax.ppermute(values, CTX, [(i, i ^ bit) for i in range(lax.axis_size(CTX))])


def own_half(values):
    half = values.shape[1] // 2
    section = lax.axis_index(SECTION)
    return (
        lax.dynamic_slice_in_dim(values, section * half, half, 1),
        lax.dynamic_slice_in_dim(values, (1 - section) * half, half, 1),
    )


def both_batches(kept, sent):
    return jnp.concatenate([kept, swap(sent)], axis=0)


def ctx_orders():
    bits = ctx_bits()
    return bits, bits[::-1]


def relative_order(bits):
    order = [0]
    for bit in reversed(bits):
        order = order + [k ^ bit for k in order]
    return order


def weight_sums(columns, *rows):
    kept, sent = zip(*(own_half(r) for r in rows))
    halves = both_batches(jnp.concatenate(kept, axis=1), jnp.concatenate(sent, axis=1))
    return matmul_tn(both_batches(columns, columns), halves).astype(bf16)


def shared_columns(normed):
    place, count = lax.axis_index(CTX), lax.axis_size(CTX)
    shards = lax.axis_size(SHARD)
    block = normed.shape[1] // (count * shards)
    return jnp.concatenate(
        [
            lax.dynamic_slice_in_dim(
                normed, ((place ^ k) * shards + lax.axis_index(SHARD)) * block, block, 1
            )
            for k in range(count)
        ],
        axis=1,
    )


def streams_of(total):
    place, count = lax.axis_index(CTX), lax.axis_size(CTX)
    block, half = total.shape[0] // count, total.shape[1] // 2
    streams = []
    for stream, bits in enumerate(ctx_orders()):
        parts = [
            lax.dynamic_slice(total, ((place ^ k) * block, stream * half), (block, half))
            for k in relative_order(bits)
        ]
        streams += [jnp.stack(parts[: count // 2]), jnp.stack(parts[count // 2 :])]
    return streams


def weight_scatter(streams):
    totals = []
    for i, bits in enumerate(ctx_orders()):
        kept, sent = (a.reshape(-1, a.shape[-1]) for a in streams[2 * i : 2 * i + 2])
        totals.append(scatter_relative(kept, sent, bits))
    return totals


def scatter_relative(kept, sent, bits):
    for i, bit in enumerate(bits):
        got = flip(sent, bit)
        if i + 1 < len(bits):
            rows = kept.shape[0] // 2
            sent = (kept[rows:].astype(f32) + got[rows:].astype(f32)).astype(bf16)
            kept = (kept[:rows].astype(f32) + got[:rows].astype(f32)).astype(bf16)
    return kept, got


def after(first, *later):
    first, later = lax.optimization_barrier((first, later))
    return first, later


def layer_backward(weights, saved, d_out, d_low, values_in, layout, last, before):
    grads = types.SimpleNamespace()
    d_product = matmul_nt(d_low, weights.down)
    gate_pre, upward = saved.gate_pre, saved.upward
    gate_sig = jax.nn.sigmoid(gate_pre)
    d_gate = d_product * upward * gate_sig * (1.0 + gate_pre * (1.0 - gate_sig))
    d_upward = d_product * gate_pre * gate_sig
    d_gate_up = jnp.concatenate([d_gate, d_upward], axis=1).astype(bf16)
    d_ffn_in = matmul_nt(d_gate_up, weights.gate_up)
    width = d_product.shape[1]
    up, down = width // 2, width // 4
    plan = tuple(
        (x, stream, ((x, stream * part, 2 * part + stream * part, part),))
        for stream in range(2)
        for x, part in ((0, up), (1, down))
    )
    if not last:
        plan = tuple(
            (x, 2 * x + stream, parts)
            for x, stream, parts in sorted(plan, key=lambda entry: -entry[0])
        )
    d_middle, d_mixed, grads.gain_ffn, *sums = back_sum(
        10 if last else 3,
        d_ffn_in,
        d_out,
        saved.middle,
        weights.gain_ffn,
        plan,
        (saved.ffn_in, d_low),
        (d_gate_up, saved.product),
        (),
        before.sums_mix if last else (),
        not last,
    )
    if last:
        sums, before.mix = sums[:4], sums[4:]
        grads.ffn = weight_scatter(sums)
    else:
        sums_ffn, grads.down = sums[:4], sums[4:]
    d_both = matmul_nt(d_mixed, weights.out)
    if not last:
        (d_both,), (before.tail,) = after((d_both,), before.tail)
    if last:
        sums_out = weight_sums(d_mixed, saved.both)
        (sums_out,), (d_both,) = after((streams_of(sums_out),), d_both)
        grads.out = weight_scatter(sums_out)
    d_proj, d_vec = mix_backward(weights, saved, d_both, layout)
    heads, widths = weights.heads, weights.widths
    grads.step_bias, grads.decay, grads.skip = (d_vec[i, :heads] for i in range(3))
    d_normed = matmul_nt(d_proj, weights.proj)
    placed = [
        jnp.where(weights.kv_owner == owner, d_proj[:, start : start + HD], 0)
        for start in (widths[0], widths[0] + HD)
        for owner in range(KVH)
    ]
    d_shared = jnp.concatenate([d_proj[:, widths[1] : widths[2]], *placed], axis=1)
    normed = saved.normed
    if last:
        d_step, d_zx = d_proj[:, widths[2] : widths[3]], d_proj[:, widths[3] :]
        sums_proj = weight_sums(
            normed, d_proj[:, : widths[0]], d_zx, jnp.concatenate([d_step, d_step], axis=1)
        )
        streams = streams_of(sums_proj)
        (streams,), (d_normed,) = after((streams,), d_normed)
        d_hidden, d_hidden_low, grads.gain_in, d_shared, grads.proj = back_sum_scatter(
            7, d_normed, d_shared, d_middle, values_in, weights.gain_in, streams
        )
    else:
        query, inner = widths[0] // 2, (d_proj.shape[1] - widths[3]) // 2
        step, zx = widths[3] - widths[2], widths[3]
        both, most = saved.both.shape[1] // 4, inner // 2
        plan = (
            (1, 2, ((1, 0, 2 * both, both),)),
            (1, 3, ((1, both, 3 * both, both),)),
            (0, 0, ((0, 0, query, query), (0, zx, zx + inner, most))),
            (0, 1, ((0, zx + most, zx + inner + most, most), (0, widths[2], widths[2], step))),
        )
        d_hidden, d_hidden_low, grads.gain_in, d_shared, *sums = back_sum(
            4,
            d_normed,
            d_middle,
            values_in,
            weights.gain_in,
            plan,
            (normed, d_mixed),
            (d_proj, saved.both),
            (d_shared,),
            sums_ffn,
            True,
        )
        sums, grads.ffn, grads.out = sums[:4], sums[4:6], sums[6:]
        grads.sums_mix = sums
    grads.wide = d_shared
    return d_hidden, d_hidden_low, grads


def body(
    inputs,
    cotangent,
    doc_lengths,
    norm_in,
    w_query,
    w_keyval,
    w_attn_out,
    w_mixer_in,
    w_state_io,
    w_step,
    step_bias,
    decay_rate,
    skip_gain,
    w_mixer_out,
    norm_ffn,
    w_gate_up,
    w_down,
):
    section = lax.axis_index(SECTION)
    leading = section == 0
    shard = lax.axis_index(SHARD)
    width = w_query.shape[1]
    query_width = w_query.shape[2]
    head_count = w_step.shape[2]
    kv_owner = shard * (query_width // HD) // (QH // KVH)
    rows_in = lax.dynamic_index_in_dim(inputs, section, 0, False)
    own_keyval = lax.dynamic_slice_in_dim(w_keyval[0], kv_owner * HD, HD, 2).reshape(width, 2 * HD)
    io_end = query_width + 2 * HD + w_state_io.shape[2]
    widths = (query_width, query_width + 2 * HD, io_end, io_end - (-head_count // 128) * 128)
    proj = jnp.concatenate(
        [
            w_query[0],
            own_keyval,
            w_state_io[0],
            jnp.pad(w_step[0], ((0, 0), (0, -head_count % 128))),
            w_mixer_in[0].reshape(width, -1),
        ],
        axis=1,
    )
    vectors = jnp.concatenate([norm_in[0], norm_ffn[0], step_bias[0], decay_rate[0], skip_gain[0]])
    block_in = line_gather(rows_in)
    (block_in,), (proj,) = after((block_in,), proj)
    own = (
        proj,
        jnp.concatenate([w_attn_out[0], w_mixer_out[0]], axis=0),
        w_gate_up[0].reshape(width, -1),
        w_down[0],
        vectors,
    )
    other = tuple(swap(array) for array in own)

    def layer_weights(layer):
        weights = types.SimpleNamespace()
        chosen = [jnp.where(section == layer, a, b) for a, b in zip(own, other)]
        weights.proj, weights.out, weights.gate_up, weights.down, vectors = chosen
        heads = vectors[2 * width :]
        weights.gain_in = vectors[:width]
        weights.gain_ffn = vectors[width : 2 * width]
        skip = heads[2 * head_count :]
        rows = heads[: 2 * head_count].reshape(2, head_count)
        weights.head_rows = jnp.pad(rows, ((0, 6), (0, -head_count % 128)))
        weights.skip_row = jnp.repeat(skip, HP)[None]
        weights.heads = head_count
        weights.widths = widths
        weights.kv_owner = kv_owner
        return weights

    layers = [layer_weights(0), layer_weights(1)]
    rows_cot = lax.dynamic_index_in_dim(cotangent, section, 0, False)
    length = block_in.shape[0]
    part = rows_in.shape[0]
    layout = block_layout(lax.dynamic_index_in_dim(doc_lengths, section, 0, False), length)

    def own_rows(values):
        return lax.dynamic_slice_in_dim(values, shard * part, part, 0)

    hidden = block_in
    normed = norm_apply(hidden.astype(f32), layers[0].gain_in).astype(bf16)
    hiddens, outs, saves = [], [], []
    for layer in range(2):
        weights = layers[layer]
        hiddens.append(hidden)
        if layer == 1:
            (normed,), (rows_cot,) = after((normed,), rows_cot)
            block_cot = lax.all_gather(rows_cot, SHARD, axis=0, tiled=True)
        partial, saved = layer_forward(weights, normed, layout)
        first, second = layers
        wanted = [(1, own[i], other[i]) for i in (0, 1)]
        if layer == 1:
            wanted = [(0, own[i], other[i]) for i in (2, 3)]
        saved.middle, saved.ffn_in, chosen = copying_sum(
            middle_kernel, 1 + 8 * layer, f32, partial, hidden, weights.gain_ffn, wanted
        )
        if layer == 0:
            second.proj, second.out = chosen
        else:
            first.gate_up, first.down = chosen
        partial, saved.gate_pre, saved.upward, saved.product = ffn_forward(
            weights, saved.ffn_in
        )
        saves.append(saved)
        if layer == 0:
            wanted = [(1, own[i], other[i]) for i in (2, 3)]
            out_low, normed, chosen = copying_sum(
                layer_end_kernel, 2, bf16, partial, saved.middle, second.gain_in, wanted
            )
            second.gate_up, second.down = chosen
            outs.append(own_rows(out_low))
            hidden = out_low
        else:
            held = types.SimpleNamespace(tail=partial.astype(bf16))

    d_out = d_low = block_cot
    d_hiddens, grads = [None, None], [None, None]
    for layer in (1, 0):
        d_hidden, d_low, grads[layer] = layer_backward(
            layers[layer], saves[layer], d_out, d_low, hiddens[layer], layout, layer == 0, grads[1] if layer == 0 else held
        )
        d_hiddens[layer] = d_hidden
        d_out = d_low

    total = lax.psum_scatter(held.tail, SHARD, scatter_dimension=0, tiled=True)
    outs.append((own_rows(saves[1].middle) + total.astype(f32)).astype(bf16))
    first, second = grads
    tinies = []
    for g in grads:
        vector = jnp.concatenate([g.gain_in, g.gain_ffn, g.step_bias, g.decay, g.skip])
        size = -(-vector.shape[0] // 1024) * 8
        tinies.append(jnp.pad(vector, (0, size * 128 - vector.shape[0])).reshape(size, 128))
    query, zx, up, down, out, out_rows, grad_rows, shared, tiny = finish(
        first,
        second,
        outs,
        [own_rows(d) for d in d_hiddens],
        tinies,
        [first.wide, second.wide],
        [shared_columns(saved.normed) for saved in saves],
    )
    tiny = tiny.reshape(-1)
    place = lax.axis_index(CTX) * lax.axis_size(SHARD) + shard
    slot = width // (lax.axis_size(CTX) * lax.axis_size(SHARD))
    grad_in = lax.dynamic_slice_in_dim(tiny, place * slot, slot, 0)
    grad_ffn = lax.dynamic_slice_in_dim(tiny, width + place * slot, slot, 0)
    heads = tiny[2 * width :]
    step = jnp.where(
        leading,
        first.proj[1][:, zx.shape[2] // 2 :],
        second.mix[1][:, zx.shape[2] // 2 : zx.shape[2] // 2 + 128],
    )
    io_width = w_state_io.shape[2]
    return (
        out_rows[None],
        grad_rows[None],
        grad_in[None],
        query.astype(f32)[None],
        shared[:, io_width:].astype(f32).reshape(-1, 2, KVH * HD)[None],
        out[:query_width].astype(f32)[None],
        jnp.swapaxes(zx, 0, 1)[None],
        shared[:, :io_width].astype(f32)[None],
        step[:, :head_count].astype(f32)[None],
        heads[:head_count][None],
        heads[head_count : 2 * head_count][None],
        heads[2 * head_count : 3 * head_count][None],
        out[query_width:].astype(f32)[None],
        grad_ffn[None],
        jnp.swapaxes(up, 0, 1)[None],
        down.astype(f32)[None],
    )


def solution(mesh):
    return jax.shard_map(
        body,
        mesh=mesh,
        in_specs=(
            P(None, (CTX, SHARD), None),
            P(None, (CTX, SHARD), None),
            P(),
            P(SECTION, None),
            P(SECTION, None, SHARD),
            P(SECTION, None, None, None),
            P(SECTION, SHARD, None),
            P(SECTION, None, None, SHARD),
            P(SECTION, None, None),
            P(SECTION, None, SHARD),
            P(SECTION, SHARD),
            P(SECTION, SHARD),
            P(SECTION, SHARD),
            P(SECTION, SHARD, None),
            P(SECTION, None),
            P(SECTION, None, None, SHARD),
            P(SECTION, SHARD, None),
        ),
        out_specs=(
            P(SECTION, None, (CTX, SHARD), None),
            P(SECTION, None, (CTX, SHARD), None),
            P(SECTION, (CTX, SHARD)),
            P(SECTION, CTX, SHARD),
            P(SECTION, (CTX, SHARD), None, None),
            P(SECTION, SHARD, CTX),
            P(SECTION, CTX, None, SHARD),
            P(SECTION, (CTX, SHARD), None),
            P(SECTION, CTX, SHARD),
            P(SECTION, SHARD),
            P(SECTION, SHARD),
            P(SECTION, SHARD),
            P(SECTION, SHARD, CTX),
            P(SECTION, (CTX, SHARD)),
            P(SECTION, CTX, None, SHARD),
            P(SECTION, SHARD, CTX),
        ),
        check_vma=False,
    )
```

```python
import functools
import types

import jax
import jax.numpy as jnp
from jax import lax
from jax.experimental import pallas as pl
from jax.experimental.pallas import tpu as pltpu
from jax.sharding import PartitionSpec as P

SECTION, CTX, SHARD = "section", "ctx", "shard"
QH = 8
KVH = 2
HD = 128
HP = 64
CHUNKS = 16
LAG = 3

MESH = pl.DeviceIdType.MESH
eps = 1e-05
bf16 = jnp.bfloat16
f32 = jnp.float32


def line_sum(n, chunks, lag, p_rows, done, sr, sl, rr, rl, srs, sls, rrs, rls, tot, fill=None):
    z = lax.axis_index(SHARD)
    hasr, hasl = z < n - 1, z > 0
    bar = pltpu.get_barrier_semaphore()
    more = 0
    if fill is not None:
        more = fill.greet(bar)

    @pl.when(hasr)
    def _():
        pl.semaphore_signal(bar, inc=1, device_id={SHARD: z + 1}, device_id_type=MESH)

    @pl.when(hasl)
    def _():
        pl.semaphore_signal(bar, inc=1, device_id={SHARD: z - 1}, device_id_type=MESH)

    @pl.when(hasl & hasr)
    def _():
        pl.semaphore_wait(bar, 2 + more)

    @pl.when(jnp.logical_not(hasl & hasr))
    def _():
        pl.semaphore_wait(bar, 1 + more)

    def right(j):
        return pltpu.make_async_remote_copy(
            sr.at[j], rr.at[j], srs.at[j], rrs.at[j], device_id={SHARD: z + 1}, device_id_type=MESH
        )

    def left(j):
        return pltpu.make_async_remote_copy(
            sl.at[j], rl.at[j], sls.at[j], rls.at[j], device_id={SHARD: z - 1}, device_id_type=MESH
        )

    steps = chunks + lag * (n - 1)
    if fill is not None:
        fill.start()

    def one(i, _):
        def go(j, copy, came, goes, inbox, outbox):
            live = (j >= 0) & (j < chunks)

            @pl.when(live & came & goes)
            def _():
                copy(j).wait_recv()
                outbox[j] = (p_rows(j) + inbox[j].astype(f32)).astype(bf16)
                copy(j).start()

            @pl.when(live & jnp.logical_not(came))
            def _():
                outbox[j] = p_rows(j).astype(bf16)
                copy(j).start()

            @pl.when(live & jnp.logical_not(goes))
            def _():
                copy(j).wait_recv()

        go(i - lag * z, right, hasl, hasr, rr, sr)
        go(i - lag * (n - 1 - z), left, hasr, hasl, rl, sl)
        jd = i - lag * jnp.maximum(z, n - 1 - z)

        @pl.when((jd >= 0) & (jd < chunks))
        def _():
            tot[...] = p_rows(jd)

            @pl.when(hasl)
            def _():
                tot[...] += rr[jd].astype(f32)

            @pl.when(hasr)
            def _():
                tot[...] += rl[jd].astype(f32)

            done(jd, tot[...])

        if fill is not None:
            fill.step(i, steps)
        return 0

    lax.fori_loop(0, steps, one, 0)
    if fill is not None:
        fill.finish()

    def drain(j, _):
        @pl.when(hasr)
        def _():
            right(j).wait_send()

        @pl.when(hasl)
        def _():
            left(j).wait_send()

        return 0

    lax.fori_loop(0, chunks, drain, 0)


def row_slice(j, rows):
    return pl.ds(pl.multiple_of(j * rows, rows), rows)


def middle_kernel(n, chunks, lag, p_ref, h_ref, gain_ref, mid_ref, low_ref, *scratch, fill=None):
    rows = p_ref.shape[0] // chunks

    def p_rows(j):
        return p_ref[row_slice(j, rows), :]

    def done(j, total):
        v = h_ref[row_slice(j, rows), :].astype(f32) + total
        r = lax.rsqrt(jnp.mean(v * v, axis=-1, keepdims=True) + eps)
        mid_ref[row_slice(j, rows), :] = v
        low_ref[row_slice(j, rows), :] = (v * r * gain_ref[...]).astype(bf16)

    line_sum(n, chunks, lag, p_rows, done, *scratch, fill=fill)


class Copies:
    parts = 16

    def __init__(self, layers, own, other, out, boxes, came, went):
        self.layers, self.own, self.other, self.out = layers, own, other, out
        self.boxes, self.came, self.went = boxes, came, went

    def greet(self, bar):
        return 0

    def start(self):
        pass

    def rows(self, a, j):
        size = self.boxes[a].shape[1]
        return pl.ds(pl.multiple_of(j * size, size), size)

    def fetch(self, a, j, act):
        section, slot = lax.axis_index(SECTION), lax.rem(j, 2)
        for mine, source in ((True, self.own[a]), (False, self.other[a])):

            @pl.when((section == self.layers[a]) == mine)
            def _():
                part = source.at[self.rows(a, j), :]
                act(
                    pltpu.make_async_copy(
                        part, self.boxes[a].at[slot], self.came.at[2 * a + slot]
                    )
                )

    def store(self, a, j):
        slot = lax.rem(j, 2)
        part = self.out[a].at[self.rows(a, j), :]
        return pltpu.make_async_copy(self.boxes[a].at[slot], part, self.went.at[2 * a + slot])

    def step(self, i, steps):
        @pl.when((i >= 1) & (i <= self.parts))
        def _():
            for a in range(len(self.layers)):
                self.fetch(a, i - 1, lambda copy: copy.wait())
                self.store(a, i - 1).start()

        @pl.when((i >= 2) & (i < self.parts))
        def _():
            for a in range(len(self.layers)):
                self.store(a, i - 2).wait()

        @pl.when(i < self.parts)
        def _():
            for a in range(len(self.layers)):
                self.fetch(a, i, lambda copy: copy.start())

    def finish(self):
        for a in range(len(self.layers)):
            for j in (self.parts - 2, self.parts - 1):
                self.store(a, j).wait()


def copying(kernel, layers, n, chunks, lag, p_ref, h_ref, gain_ref, *refs):
    count = len(layers)
    own, other, refs = refs[:count], refs[count : 2 * count], refs[2 * count :]
    first_ref, low_ref, refs = refs[0], refs[1], refs[2:]
    out, refs = refs[:count], refs[count:]
    copies = Copies(layers, own, other, out, refs[9 : 9 + count], *refs[9 + count :])
    kernel(n, chunks, lag, p_ref, h_ref, gain_ref, first_ref, low_ref, *refs[:9], fill=copies)


def layer_end_kernel(n, chunks, lag, p_ref, h_ref, gain_ref, out_ref, low_ref, *scratch, fill=None):
    rows = p_ref.shape[0] // chunks

    def p_rows(j):
        return p_ref[row_slice(j, rows), :]

    def done(j, total):
        out = (h_ref[row_slice(j, rows), :] + total).astype(bf16)
        out_ref[row_slice(j, rows), :] = out
        v = out.astype(f32)
        r = lax.rsqrt(jnp.mean(v * v, axis=-1, keepdims=True) + eps)
        low_ref[row_slice(j, rows), :] = (v * r * gain_ref[...]).astype(bf16)

    line_sum(n, chunks, lag, p_rows, done, *scratch, fill=fill)


def flipped(place, k, count):
    total, bit = 0, 1
    while bit < count:
        total = total + (place // bit + k // bit) % 2 * bit
        bit *= 2
    return total


def mirrored(k, count):
    total, bit = 0, 1
    while bit < count:
        total = total + k // bit % 2 * (count // (2 * bit))
        bit *= 2
    return total


class Fill:
    first = 6

    def __init__(self, plan, xs, ys, outs, scratch):
        self.plan, self.xs, self.ys, self.outs = plan, xs, ys, outs
        count = len(plan)
        self.other_x, rest = scratch[: len(xs)], scratch[len(xs) :]
        self.own_y, self.other_y = rest[:count], rest[count : 2 * count]
        self.send, self.recv = rest[2 * count :]

    def greet(self, bar):
        other = 1 - lax.axis_index(SECTION)
        pl.semaphore_signal(bar, inc=1, device_id={SECTION: other}, device_id_type=MESH)
        return 1

    def copies(self):
        section = lax.axis_index(SECTION)
        copies = []

        def add(source, target):
            i = len(copies)
            copies.append(
                pltpu.make_async_remote_copy(
                    source,
                    target,
                    self.send.at[i],
                    self.recv.at[i],
                    device_id={SECTION: 1 - section},
                    device_id_type=MESH,
                )
            )

        for x, target in zip(self.xs, self.other_x):
            add(x, target)
        for (_, _, parts), target in zip(self.plan, self.other_y):
            at = 0
            for y, low, high, width in parts:
                start = pl.multiple_of(low + (high - low) * (1 - section), 128)
                add(self.ys[y].at[:, pl.ds(start, width)], target.at[:, at : at + width])
                at += width
        return copies

    def start(self):
        for copy in self.copies():
            copy.start()
        section = lax.axis_index(SECTION)
        for (_, _, parts), own in zip(self.plan, self.own_y):
            at = 0
            for y, low, high, width in parts:
                start = pl.multiple_of(low + (high - low) * section, 128)
                own[:, at : at + width] = self.ys[y][:, pl.ds(start, width)]
                at += width

    def each(self, steps):
        return -(-lax.axis_size(CTX) * len(self.plan) // (steps - self.first))

    def step(self, i, steps):
        place, count = lax.axis_index(CTX), lax.axis_size(CTX)

        @pl.when(i == self.first)
        def _():
            for copy in self.copies():
                copy.wait_recv()

        each = self.each(steps)
        begin = (i - self.first) * each

        def piece(t, _):
            at = [0] * 4
            for f, (x, stream, _) in enumerate(self.plan):
                k = t - f * count
                width = self.own_y[f].shape[1]
                where = slice(at[stream], at[stream] + width)
                at[stream] += width
                kept, sent = self.outs[2 * stream : 2 * stream + 2]
                turned = stream % 2

                @pl.when((k >= 0) & (k < count))
                def _():
                    block = kept.shape[1]
                    source = flipped(place, mirrored(k, count) if turned else k, count)
                    cols = pl.ds(pl.multiple_of(source * block, block), block)
                    dims = (((0,), (0,)), ((), ()))
                    total = lax.dot_general(
                        self.xs[x][:, cols], self.own_y[f][...], dims, preferred_element_type=f32
                    ) + lax.dot_general(
                        self.other_x[x][:, cols],
                        self.other_y[f][...],
                        dims,
                        preferred_element_type=f32,
                    )
                    low = total.astype(bf16)

                    @pl.when(k < count // 2)
                    def _():
                        kept[k, :, where] = low

                    @pl.when(k >= count // 2)
                    def _():
                        sent[k - count // 2, :, where] = low

            return 0

        @pl.when(i >= self.first)
        def _():
            lax.fori_loop(begin, begin + each, piece, 0)

    def finish(self):
        for copy in self.copies():
            copy.wait_send()


class Halving:
    cuts = 2

    def __init__(self, streams, outs, scratch, turns, begin=None, greets=True):
        self.turns, self.begin, self.greets = turns, begin, greets
        self.place, self.count = lax.axis_index(CTX), lax.axis_size(CTX)
        self.streams, self.outs = streams, outs
        self.orders = ctx_orders()
        self.levels = len(self.orders[0])
        self.inbox = [scratch[k * self.levels : (k + 1) * self.levels] for k in range(2)]
        rest = scratch[2 * self.levels :]
        self.sums = [rest[k * (self.levels - 1) : (k + 1) * (self.levels - 1)] for k in range(2)]
        self.send, self.recv = rest[2 * (self.levels - 1) :]

    def greet(self, bar):
        if not self.greets:
            return 0
        for bit in self.orders[0]:
            peer = flipped(self.place, bit, self.count)
            pl.semaphore_signal(bar, inc=1, device_id={CTX: peer}, device_id_type=MESH)
        return self.levels

    def rows(self, cut):
        size = self.outs[0].shape[0] // self.cuts
        return pl.ds(cut * size, size)

    def copy(self, level, stream, cut):
        rows = self.rows(cut)
        if level == 0:
            source = self.streams[2 * stream + 1].at[:, rows, :]
        else:
            blocks = self.count >> (level + 1)
            source = self.sums[stream][level - 1].at[pl.ds(blocks, blocks), rows, :]
        i = (level * 2 + stream) * self.cuts + cut
        return pltpu.make_async_remote_copy(
            source,
            self.inbox[stream][level].at[:, rows, :],
            self.send.at[i],
            self.recv.at[i],
            device_id={CTX: flipped(self.place, self.orders[stream][level], self.count)},
            device_id_type=MESH,
        )

    def advance(self, level, cut):
        rows, blocks = self.rows(cut), self.count >> (level + 1)
        for stream in range(2):
            self.copy(level, stream, cut).wait_recv()
            kept = self.streams[2 * stream] if level == 0 else self.sums[stream][level - 1]
            for k in range(blocks):
                total = kept[k, rows, :].astype(f32) + self.inbox[stream][level][k, rows, :].astype(
                    f32
                )
                if level + 1 < self.levels:
                    self.sums[stream][level][k, rows, :] = total.astype(bf16)
                else:
                    self.outs[stream][rows, :] = total.astype(bf16)
            if level + 1 < self.levels:
                self.copy(level + 1, stream, cut).start()

    def start(self):
        if self.begin is None:
            self.first_copies()

    def first_copies(self):
        for cut in range(self.cuts):
            for stream in range(2):
                self.copy(0, stream, cut).start()

    def step(self, i, steps):
        if self.begin is not None:

            @pl.when(i == self.begin)
            def _():
                self.first_copies()

        for cut, turn in enumerate(self.turns):

            @pl.when(i == turn)
            def _():
                self.advance(0, cut)

    def finish(self):
        for cut in range(len(self.turns), self.cuts):
            self.advance(0, cut)
        for level in range(1, self.levels):
            for cut in range(self.cuts):
                self.advance(level, cut)
        for level in range(self.levels):
            for stream in range(2):
                for cut in range(self.cuts):
                    self.copy(level, stream, cut).wait_send()


def halving_scratch(streams):
    blocks, rows, width = streams[0].shape
    levels = len(ctx_bits())
    inbox = [pltpu.VMEM((blocks >> k, rows, width), bf16) for k in range(levels)]
    copies = levels * 2 * Halving.cuts
    return [*inbox * 2, *inbox[: levels - 1] * 2, *[pltpu.SemaphoreType.DMA((copies,))] * 2]


class Together:
    def __init__(self, *jobs):
        self.jobs = jobs

    def greet(self, bar):
        return sum(job.greet(bar) for job in self.jobs)

    def start(self):
        for job in self.jobs:
            job.start()

    def step(self, i, steps):
        for job in self.jobs:
            job.step(i, steps)

    def finish(self):
        for job in self.jobs:
            job.finish()


def scatter_kernel(n, chunks, lag, p_ref, q_ref, d_ref, v_ref, gain_ref, *refs):
    streams, outs, totals, scratch = refs[:4], refs[4:8], refs[8:10], refs[10:]
    job = Halving(streams, totals, scratch[9:], (7, 14))
    back_rows(n, chunks, lag, p_ref, d_ref, v_ref, gain_ref, *outs[:3], scratch[:9], job, q_ref, outs[3])


def back_kernel(n, chunks, lag, plan, x_count, y_count, beside, ready, soon, p_ref, *refs):
    q_ref = q_out = None
    if beside:
        q_ref, refs = refs[0], refs[1:]
    (d_ref, v_ref, gain_ref), refs = refs[:3], refs[3:]
    xs, refs = refs[:x_count], refs[x_count:]
    ys, refs = refs[:y_count], refs[y_count:]
    streams, refs = refs[:ready], refs[ready:]
    out_ref, low_ref, gg_ref = refs[:3]
    refs = refs[3:]
    if beside:
        q_out, refs = refs[0], refs[1:]
    sums, refs = refs[:4], refs[4:]
    totals, refs = refs[: ready // 2], refs[ready // 2 :]
    soon_totals, refs = refs[: 2 * soon], refs[2 * soon :]
    scratch, rest = refs[:9], refs[9:]
    cut = len(xs) + 2 * len(plan) + 2
    own, rest = rest[:cut], rest[cut:]
    here, rest = rest[: 4 * soon], rest[4 * soon :]
    fill = Fill(plan, xs, ys, (*sums, *here), own)
    jobs = [fill]
    boxes = 4 * len(ctx_bits())
    if ready:
        turns = (9, 17) if beside else (9,)
        jobs.append(Halving(streams, totals, rest[:boxes], turns))
        rest = rest[boxes:]
    if soon:
        begin = Fill.first + -(-2 * lax.axis_size(CTX) // fill.each(chunks + lag * (n - 1)))
        jobs.append(Halving(here, soon_totals, rest, (), begin, not ready))
    fill = Together(*jobs)
    outs = out_ref, low_ref, gg_ref
    back_rows(n, chunks, lag, p_ref, d_ref, v_ref, gain_ref, *outs, scratch, fill, q_ref, q_out)


def back_rows(
    n,
    chunks,
    lag,
    p_ref,
    d_ref,
    v_ref,
    gain_ref,
    out_ref,
    low_ref,
    gg_ref,
    scratch,
    fill,
    q_ref=None,
    q_out=None,
):
    rows, width = p_ref.shape[0] // chunks, p_ref.shape[1]
    gg_ref[...] = jnp.zeros_like(gg_ref)

    def p_rows(j):
        part = row_slice(j, rows)
        if q_ref is None:
            return p_ref[part, :]
        return jnp.concatenate([p_ref[part, :], q_ref[part, :].astype(f32)], axis=1)

    def done(j, total):
        if q_ref is not None:
            q_out[row_slice(j, rows), :] = total[:, width:].astype(bf16)
            total = total[:, :width]
        v = v_ref[row_slice(j, rows), :].astype(f32)
        r = lax.rsqrt(jnp.mean(v * v, axis=-1, keepdims=True) + eps)
        vr = v * r
        dg = total * gain_ref[...]
        inner = jnp.mean(dg * vr, axis=-1, keepdims=True)
        gg_ref[...] += jnp.sum((total * vr).reshape(rows // 8, 8, vr.shape[1]), axis=0)
        out = d_ref[row_slice(j, rows), :].astype(f32) + r * (dg - vr * inner)
        out_ref[row_slice(j, rows), :] = out
        low_ref[row_slice(j, rows), :] = out.astype(bf16)

    line_sum(n, chunks, lag, p_rows, done, *scratch, fill=fill)


def summed(kernel, collective, outs, *operands, extra=(), more=0, far=(0, 0), room=50):
    n = lax.axis_size(SHARD)
    length, width = operands[0].shape[0], operands[0].shape[1] + more
    box = pltpu.VMEM((CHUNKS, length // CHUNKS, width), bf16)
    distant = pl.BlockSpec(memory_space=pl.ANY)
    whole = pl.BlockSpec(memory_space=pltpu.VMEM)
    return pl.pallas_call(
        functools.partial(kernel, n, CHUNKS, LAG),
        out_shape=outs,
        in_specs=[whole] * (len(operands) - far[0]) + [distant] * far[0],
        out_specs=[whole] * (len(outs) - far[1]) + [distant] * far[1],
        scratch_shapes=[box] * 4
        + [pltpu.SemaphoreType.DMA((CHUNKS,))] * 4
        + [pltpu.VMEM((length // CHUNKS, width), f32), *extra],
        compiler_params=pltpu.CompilerParams(
            collective_id=collective, has_side_effects=True, vmem_limit_bytes=room << 20
        ),
        cost_estimate=pl.CostEstimate(flops=0, bytes_accessed=20 << 20, transcendentals=0),
        name="line_sum"+str(collective),
    )(*operands)


def line_gather(rows):
    count, place = lax.axis_size(SHARD), lax.axis_index(SHARD)
    part = rows.shape[0]
    block = jnp.zeros((count * part, rows.shape[1]), rows.dtype)
    block = lax.dynamic_update_slice_in_dim(block, rows, place * part, 0)
    for k in reversed(range(1, count)):
        got = lax.ppermute(rows, SHARD, [(i, i ^ k) for i in range(count)])
        block = lax.dynamic_update_slice_in_dim(block, got, (place ^ k) * part, 0)
    return block


def shaped(array, dtype):
    return jax.ShapeDtypeStruct(array.shape, dtype)


def copying_sum(kernel, collective, dtype, p, hidden, gain, wanted):
    layers, own, other = zip(*wanted)
    outs = [shaped(p, dtype), shaped(p, bf16)] + [shaped(a, bf16) for a in own]
    boxes = [pltpu.VMEM((2, a.shape[0] // Copies.parts, a.shape[1]), bf16) for a in own]
    first, low, *chosen = summed(
        functools.partial(copying, kernel, layers),
        collective,
        outs,
        p,
        hidden,
        gain[None],
        *own,
        *other,
        extra=[*boxes, *[pltpu.SemaphoreType.DMA((2 * len(layers),))] * 2],
        far=(2 * len(layers), len(layers)),
        room=26,
    )
    return first, low, chosen


def back_sum(collective, p, d_out, values, gain, plan, xs, ys, beside=(), ready=(), soon=False):
    count = lax.axis_size(CTX)
    length = p.shape[0]
    outs = [shaped(p, f32), shaped(p, bf16), jax.ShapeDtypeStruct((8, p.shape[1]), f32)]
    outs += [shaped(q, bf16) for q in beside]
    widths = [sum(part[3] for part in parts) for _, _, parts in plan]
    sums = []
    for stream in range(4 if soon else 2):
        total = sum(w for (_, at, _), w in zip(plan, widths) if at == stream)
        shape = (count // 2, xs[0].shape[1] // count, total)
        sums += [jax.ShapeDtypeStruct(shape, bf16)] * 2
    outs += sums[:4]
    extra = [pltpu.VMEM(x.shape, bf16) for x in xs]
    extra += [pltpu.VMEM((length, w), bf16) for w in widths] * 2
    copies = len(xs) + sum(len(parts) for _, _, parts in plan)
    extra += [pltpu.SemaphoreType.DMA((copies,))] * 2
    outs += [jax.ShapeDtypeStruct(a.shape[1:], bf16) for a in ready[::2]]
    if soon:
        outs += [jax.ShapeDtypeStruct(sums[4].shape[1:], bf16)] * 2
        extra += [pltpu.VMEM(a.shape, bf16) for a in sums[4:]]
    if ready:
        extra += halving_scratch(ready)
    if soon:
        extra += halving_scratch(sums[4:])

    def bound(n, chunks, lag, *refs):
        back_kernel(n, chunks, lag, plan, len(xs), len(ys), bool(beside), len(ready), soon, *refs)

    operands = (p, *beside, d_out, values, gain[None], *xs, *ys, *ready)
    more = sum(q.shape[1] for q in beside)
    room = 50 if ready else 38
    out, low, gg, *sums = summed(
        bound, collective, outs, *operands, extra=extra, more=more, room=room
    )
    return out, low, jnp.sum(gg, axis=0), *sums


def back_sum_scatter(collective, p, beside, d_out, values, gain, streams):
    outs = [shaped(p, f32), shaped(p, bf16), jax.ShapeDtypeStruct((8, p.shape[1]), f32)]
    outs += [shaped(beside, bf16)]
    outs += [jax.ShapeDtypeStruct(a.shape[1:], bf16) for a in streams[::2]]
    operands = (p, beside, d_out, values, gain[None], *streams)
    more = beside.shape[1]
    out, low, gg, whole, *totals = summed(
        scatter_kernel, collective, outs, *operands, extra=halving_scratch(streams), more=more, room=36
    )
    return out, low, jnp.sum(gg, axis=0), whole, totals


def dot(left, right, dims=((1,), (0,))):
    return lax.dot_general(left, right, (dims, ((), ())), preferred_element_type=f32)


NT = ((1,), (1,))
TN = ((0,), (0,))


def in_three(values):
    high = values.astype(bf16)
    rest = values - high.astype(f32)
    mid = rest.astype(bf16)
    return high, mid, (rest - mid.astype(f32)).astype(bf16)


def running_sum(values, reverse):
    length = values.shape[0]
    row = lax.broadcasted_iota(jnp.int32, (length, length), 0)
    col = lax.broadcasted_iota(jnp.int32, (length, length), 1)
    kept = jnp.where(row <= col if reverse else row >= col, 1.0, 0.0).astype(bf16)
    return sum(dot(kept, part) for part in in_three(values))


def lanes(shape):
    return lax.broadcasted_iota(jnp.int32, shape, 1)


def column(values, head):
    return jnp.sum(jnp.where(lanes(values.shape) == head, values, 0.0), axis=1, keepdims=True)


def in_pair(values, pair):
    low, high = column(values, 2 * pair), column(values, 2 * pair + 1)
    return jnp.where(lanes(values.shape) < HP, low, high)


def from_pair(values, pair):
    lane = lanes(values.shape)
    low = jnp.sum(jnp.where(lane < HP, values, 0.0), axis=1, keepdims=True)
    high = jnp.sum(jnp.where(lane < HP, 0.0, values), axis=1, keepdims=True)
    return jnp.where(lane == 2 * pair, low, 0.0) + jnp.where(lane == 2 * pair + 1, high, 0.0)


def pair_ds(pair, start=0):
    return pl.ds(pl.multiple_of(start + pair * 2 * HP, 2 * HP), 2 * HP)


def steps_of(step_raw, vec_ref, tok_ref, cum, cum_rows, step, enter, fade):
    shifted = step_raw + vec_ref[0:1, :]
    step[...] = jnp.maximum(shifted, 0.0) + jnp.log1p(jnp.exp(-jnp.abs(shifted)))
    cum[...] = running_sum(-step[...] * vec_ref[1:2, :], False)
    total = cum[...]
    cum_rows[...] = total.T
    enter[...] = jnp.exp(total) * tok_ref[:, 1:2]
    fade[...] = jnp.exp(total[-1:, :] - total) * tok_ref[:, 2:3]
    return shifted


def masks_of(tok_ref, key_ref):
    kept = (tok_ref[:, 3:4] >= key_ref[1:2, :]) & (tok_ref[:, 0:1] == key_ref[0:1, :])
    return jnp.where(kept, 0.0, -1e30)


def ctx_barrier(count, place):
    bar = pltpu.get_barrier_semaphore()

    def greet(k, _):
        pl.semaphore_signal(
            bar, inc=1, device_id={CTX: lax.rem(place + k, count)}, device_id_type=MESH
        )
        return 0

    lax.fori_loop(1, count, greet, 0)
    pl.semaphore_wait(bar, count - 1)


def ctx_copy(source, target, send, recv, peer):
    return pltpu.make_async_remote_copy(
        source, target, send, recv, device_id={CTX: peer}, device_id_type=MESH
    )


def mix_forward_kernel(
    count,
    widths,
    heads,
    proj_ref,
    vec_ref,
    skip_ref,
    tok_ref,
    key_ref,
    both_ref,
    mixed_ref,
    state_ref,
    keyval_ref,
    decay_ref,
    cum,
    cum_rows,
    step,
    enter,
    fade,
    mask,
    crossed,
    keyvals,
    fresh,
    decays,
    total_state,
    kv_send,
    kv_recv,
    st_send,
    st_recv,
    dc_send,
    dc_recv,
):
    place = lax.axis_index(CTX)
    length = proj_ref.shape[0]
    inner = (proj_ref.shape[1] - widths[3]) // 2
    pairs = heads // 2
    states = (widths[2] - widths[1]) // 2
    ctx_barrier(count, place)

    keyvals[0] = proj_ref[:, widths[0] : widths[1]].astype(bf16)

    def kv_copy(k):
        peer = lax.rem(place + k, count)
        return ctx_copy(keyvals.at[0], keyvals.at[k], kv_send.at[k], kv_recv.at[k], peer)

    def st_copy(k):
        peer = lax.rem(place + k, count)
        return ctx_copy(fresh.at[0], fresh.at[k], st_send.at[k], st_recv.at[k], peer)

    def dc_copy(k):
        peer = lax.rem(place + k, count)
        return ctx_copy(decays.at[0], decays.at[k], dc_send.at[k], dc_recv.at[k], peer)

    def kv_start(k, _):
        kv_copy(k).start()
        return 0

    lax.fori_loop(1, count, kv_start, 0)
    steps_of(
        proj_ref[:, widths[2] : widths[2] + 128], vec_ref, tok_ref, cum, cum_rows, step, enter, fade
    )
    last = cum_rows[: decays.shape[1], length - 1 :]
    decays[0] = jnp.broadcast_to(jnp.exp(last) * tok_ref[0:1, 4:5], decays.shape[1:])
    b_low = proj_ref[:, widths[1] : widths[1] + states].astype(bf16)
    c_low = proj_ref[:, widths[1] + states : widths[2]].astype(bf16)

    def make_fresh(pair, _):
        x = proj_ref[:, pair_ds(pair, widths[3] + inner)]
        x = x.astype(bf16).astype(f32)
        faded = (x * in_pair(fade[...] * step[...], pair)).astype(bf16)
        fresh[0, pair_ds(pair), :] = dot(faded, b_low, TN).astype(bf16)
        return 0

    lax.fori_loop(0, pairs, make_fresh, 0)

    def st_start(k, _):
        dc_copy(k).start()

        @pl.when(place + k < count)
        def _():
            st_copy(k).start()

        return 0

    lax.fori_loop(1, count, st_start, 0)
    mask[...] = masks_of(tok_ref, key_ref)
    crossed[...] = dot(c_low, b_low, NT) * states ** (-0.5)

    def inside(pair, _):
        x = proj_ref[:, pair_ds(pair, widths[3] + inner)]
        x = x.astype(bf16).astype(f32)
        xdt = (x * in_pair(step[...], pair)).astype(bf16)
        parts = []
        for side in range(2):
            head = 2 * pair + side
            spread = column(cum[...], head) - cum_rows[pl.ds(head, 1), :]
            weight = jnp.exp(spread + mask[:, :length])
            parts.append(dot((weight * crossed[...]).astype(bf16), xdt))
        mixed_ref[:, pair_ds(pair)] = jnp.where(lanes(parts[0].shape) < HP, *parts)
        return 0

    lax.fori_loop(0, pairs, inside, 0)

    def kv_wait(k, _):
        kv_copy(k).wait_recv()
        return 0

    lax.fori_loop(1, count, kv_wait, 0)
    keyval_ref[...] = keyvals[...].reshape(keyval_ref.shape)
    for head in range(widths[0] // HD):
        query = proj_ref[:, head * HD : (head + 1) * HD].astype(bf16)
        scores = dot(query, keyval_ref[:, :HD], NT) * HD ** (-0.5) + mask[...]
        expo = jnp.exp(scores - jnp.max(scores, axis=1, keepdims=True))
        soft = expo * (1.0 / jnp.sum(expo, axis=1, keepdims=True))
        both_ref[:, head * HD : (head + 1) * HD] = dot(
            soft.astype(bf16), keyval_ref[:, HD:]
        ).astype(bf16)

    def dc_wait(k, _):
        dc_copy(k).wait_recv()

        @pl.when(k <= place)
        def _():
            st_copy(k).wait_recv()

        return 0

    lax.fori_loop(1, count, dc_wait, 0)
    total_state[...] = jnp.zeros_like(total_state)
    head_width = inner // heads

    def combine(index, _):
        slot = place - index

        def one_head(head, _):
            rows = pl.ds(pl.multiple_of(head * head_width, head_width), head_width)
            total_state[rows, :] = total_state[rows, :] * decays[slot, pl.ds(head, 1), :] + fresh[
                slot, rows, :
            ].astype(f32)
            return 0

        lax.fori_loop(0, heads, one_head, 0)
        return 0

    lax.fori_loop(0, place, combine, 0)
    state_ref[...] = total_state[...].astype(bf16)
    decay_ref[...] = decays[...]

    def finish(pair, _):
        carried = dot(c_low, state_ref[pair_ds(pair), :], NT)
        mixed = mixed_ref[:, pair_ds(pair)] + carried * in_pair(enter[...], pair)
        mixed_ref[:, pair_ds(pair)] = mixed
        x = proj_ref[:, pair_ds(pair, widths[3] + inner)]
        x = x.astype(bf16).astype(f32)
        gate = proj_ref[:, pair_ds(pair, widths[3])]
        y = mixed + x * skip_ref[0:1, pair_ds(pair)]
        both_ref[:, pair_ds(pair, widths[0])] = (
            y * gate / (1.0 + jnp.exp(-gate))
        ).astype(bf16)
        return 0

    lax.fori_loop(0, pairs, finish, 0)

    def drain(k, _):
        kv_copy(k).wait_send()
        dc_copy(k).wait_send()

        @pl.when(place + k < count)
        def _():
            st_copy(k).wait_send()

        return 0

    lax.fori_loop(1, count, drain, 0)


def mix_backward_kernel(
    count,
    widths,
    heads,
    proj_ref,
    vec_ref,
    skip_ref,
    tok_ref,
    key_ref,
    mixed_ref,
    state_ref,
    keyval_ref,
    decay_ref,
    d_both_ref,
    d_proj_ref,
    d_vec_ref,
    cum,
    cum_rows,
    step,
    enter,
    fade,
    mask,
    crossed,
    d_crossed,
    d_y,
    d_carried,
    d_x,
    d_keyval,
    d_b,
    d_c,
    d_cum,
    d_step,
    d_coeff,
    d_skip,
    d_states,
    total_state,
    kv_out,
    kv_in,
    kv_send,
    kv_recv,
    st_send,
    st_recv,
):
    place = lax.axis_index(CTX)
    length = proj_ref.shape[0]
    inner = (proj_ref.shape[1] - widths[3]) // 2
    pairs = heads // 2
    head_width = inner // heads
    states = (widths[2] - widths[1]) // 2
    ctx_barrier(count, place)

    def back(k):
        return lax.rem(place + count - k, count)

    def kv_copy(k):
        return ctx_copy(kv_out.at[k], kv_in.at[k], kv_send.at[k], kv_recv.at[k], back(k))

    def st_copy(k):
        return ctx_copy(d_states.at[0], d_states.at[k], st_send.at[k], st_recv.at[k], back(k))

    shifted = steps_of(
        proj_ref[:, widths[2] : widths[2] + 128], vec_ref, tok_ref, cum, cum_rows, step, enter, fade
    )
    b_low = proj_ref[:, widths[1] : widths[1] + states].astype(bf16)
    c_low = proj_ref[:, widths[1] + states : widths[2]].astype(bf16)
    d_cum[...] = jnp.zeros_like(d_cum)
    d_step[...] = jnp.zeros_like(d_step)
    d_coeff[...] = jnp.zeros_like(d_coeff)
    d_skip[...] = jnp.zeros_like(d_skip)

    def x_of(pair):
        x = proj_ref[:, pair_ds(pair, widths[3] + inner)]
        return x.astype(bf16).astype(f32)

    def outer(pair, _):
        gate = proj_ref[:, pair_ds(pair, widths[3])]
        d_gated = d_both_ref[:, pair_ds(pair, widths[0])]
        x, mixed, skip = x_of(pair), mixed_ref[:, pair_ds(pair)], skip_ref[0:1, pair_ds(pair)]
        sig = 1.0 / (1.0 + jnp.exp(-gate))
        dy = d_gated * gate * sig
        d_gate = d_gated * (mixed + x * skip) * sig * (1.0 + gate * (1.0 - sig))
        d_proj_ref[:, pair_ds(pair, widths[3])] = d_gate.astype(bf16)
        low = dy.astype(bf16)
        d_y[:, pair_ds(pair)] = low
        d_x[:, pair_ds(pair)] = dy * skip
        d_skip[...] += from_pair(dy * x, pair)
        d_cum[...] += from_pair(low.astype(f32) * mixed, pair)
        carried = (low.astype(f32) * in_pair(enter[...], pair)).astype(bf16)
        d_carried[:, pair_ds(pair)] = carried
        d_states[0, pair_ds(pair), :] = dot(carried, c_low, TN).astype(bf16)
        return 0

    lax.fori_loop(0, pairs, outer, 0)

    def st_start(k, _):
        @pl.when(k <= place)
        def _():
            st_copy(k).start()

        return 0

    lax.fori_loop(1, count, st_start, 0)
    mask[...] = masks_of(tok_ref, key_ref)
    for head in range(widths[0] // HD):
        cols = slice(head * HD, (head + 1) * HD)
        query = proj_ref[:, cols].astype(bf16)
        scores = dot(query, keyval_ref[:, :HD], NT) * HD ** (-0.5) + mask[...]
        expo = jnp.exp(scores - jnp.max(scores, axis=1, keepdims=True))
        soft = expo * (1.0 / jnp.sum(expo, axis=1, keepdims=True))
        grad = d_both_ref[:, cols].astype(bf16)
        d_soft = dot(grad, keyval_ref[:, HD:], NT)
        d_scores = soft * (d_soft - jnp.sum(soft * d_soft, axis=1, keepdims=True))
        d_raw = (d_scores * HD ** (-0.5)).astype(bf16)
        d_proj_ref[:, cols] = dot(d_raw, keyval_ref[:, :HD]).astype(bf16)
        d_keys, d_values = dot(d_raw, query, TN), dot(soft.astype(bf16), grad, TN)
        if head == 0:
            d_keyval[:, :HD] = d_keys
            d_keyval[:, HD:] = d_values
        else:
            d_keyval[:, :HD] += d_keys
            d_keyval[:, HD:] += d_values
    kv_out[...] = d_keyval[...].astype(bf16).reshape(kv_out.shape)

    def kv_start(k, _):
        kv_copy(k).start()
        return 0

    lax.fori_loop(1, count, kv_start, 0)
    crossed[...] = dot(c_low, b_low, NT) * states ** (-0.5)
    d_crossed[...] = jnp.zeros_like(d_crossed)

    def inside(pair, _):
        x = x_of(pair)
        steps = in_pair(step[...], pair)
        xdt = (x * steps).astype(bf16)
        low = d_y[:, pair_ds(pair)]
        lane = lanes(low.shape)
        parts = []
        for side in range(2):
            head = 2 * pair + side
            spread = column(cum[...], head) - cum_rows[pl.ds(head, 1), :]
            weight = jnp.exp(spread + mask[:, :length])
            parts.append(dot((weight * crossed[...]).astype(bf16), low, TN))
            mine = (lane >= HP) if side else (lane < HP)
            alone = jnp.where(mine, low.astype(f32), 0.0).astype(bf16)
            d_crossed[...] += dot(alone, xdt, NT) * weight
        d_xdt = jnp.where(lane < HP, *parts)
        d_x[:, pair_ds(pair)] += d_xdt * steps
        d_step[...] += from_pair(d_xdt * x, pair)
        d_cum[...] -= from_pair(d_xdt * xdt.astype(f32), pair)
        return 0

    lax.fori_loop(0, pairs, inside, 0)
    low_crossed = (d_crossed[...] * states ** (-0.5)).astype(bf16)
    d_c[...] = dot(low_crossed, b_low) + dot(d_carried[...], state_ref[...])
    d_b[...] = dot(low_crossed, c_low, TN)

    def st_wait(k, _):
        @pl.when(place + k < count)
        def _():
            st_copy(k).wait_recv()

        return 0

    lax.fori_loop(1, count, st_wait, 0)
    total_state[...] = jnp.zeros_like(total_state)

    def combine(index, _):
        slot = count - 1 - place - index
        source = lax.rem(count - slot, count)

        def one_head(head, _):
            rows = pl.ds(pl.multiple_of(head * head_width, head_width), head_width)
            total_state[rows, :] = total_state[rows, :] * decay_ref[
                source, pl.ds(head, 1), :
            ] + d_states[slot, rows, :].astype(f32)
            return 0

        lax.fori_loop(0, heads, one_head, 0)
        return 0

    lax.fori_loop(0, count - 1 - place, combine, 0)
    d_vec_ref[...] = jnp.zeros_like(d_vec_ref)

    def from_later(pair, _):
        rows = pair_ds(pair)
        later = total_state[rows, :]
        low = later.astype(bf16)
        x = x_of(pair)
        coeffs = in_pair(fade[...] * step[...], pair)
        back_x = dot(b_low, low, NT)
        d_proj_ref[:, pair_ds(pair, widths[3] + inner)] = (
            d_x[:, rows] + back_x * coeffs
        ).astype(bf16)
        d_coeff[...] += from_pair(back_x * x, pair)
        d_b[...] += dot((x * coeffs).astype(bf16), low)
        product = later * state_ref[rows, :].astype(f32)
        row = lax.broadcasted_iota(jnp.int32, product.shape, 0)
        lane = lanes((1, 128))
        for side in range(2):
            mine = (row >= HP) if side else (row < HP)
            part = jnp.sum(jnp.where(mine, product, 0.0), axis=0, keepdims=True)
            part = jnp.sum(part, axis=1, keepdims=True)
            d_vec_ref[3:4, :] += jnp.where(lane == 2 * pair + side, part, 0.0)
        return 0

    lax.fori_loop(0, pairs, from_later, 0)
    fading = fade[...]
    d_keep = d_coeff[...] * fading * step[...]
    block_decay = jnp.exp(cum[length - 1 :, :]) * tok_ref[0:1, 4:5]
    d_last = jnp.sum(d_keep, axis=0, keepdims=True) + block_decay * d_vec_ref[3:4, :]
    d_log = running_sum(d_cum[...] - d_keep, True) + d_last
    d_size = d_step[...] + d_coeff[...] * fading - vec_ref[1:2, :] * d_log
    d_raw_step = d_size / (1.0 + jnp.exp(-shifted))
    d_proj_ref[:, widths[2] : widths[3]] = jnp.where(
        lanes(d_raw_step.shape) < heads, d_raw_step, 0.0
    ).astype(bf16)
    d_vec_ref[0:1, :] = jnp.sum(d_raw_step, axis=0, keepdims=True)
    d_vec_ref[1:2, :] = -jnp.sum(step[...] * d_log, axis=0, keepdims=True)
    d_vec_ref[2:3, :] = jnp.sum(d_skip[...], axis=0, keepdims=True)
    d_proj_ref[:, widths[1] : widths[1] + states] = d_b[...].astype(bf16)
    d_proj_ref[:, widths[1] + states : widths[2]] = d_c[...].astype(bf16)

    def kv_wait(k, _):
        kv_copy(k).wait_recv()
        d_keyval[:length, :] += kv_in[k].astype(f32)
        return 0

    lax.fori_loop(1, count, kv_wait, 0)
    d_proj_ref[:, widths[0] : widths[1]] = d_keyval[:length, :].astype(bf16)

    def drain(k, _):
        kv_copy(k).wait_send()

        @pl.when(k <= place)
        def _():
            st_copy(k).wait_send()

        return 0

    lax.fori_loop(1, count, drain, 0)


def mixer_call(kernel, collective, outs, scratch, sems, widths, heads, operands, room):
    count = lax.axis_size(CTX)
    whole = pl.BlockSpec(memory_space=pltpu.VMEM)
    return pl.pallas_call(
        functools.partial(kernel, count, widths, heads),
        out_shape=outs,
        in_specs=[whole] * len(operands),
        out_specs=[whole] * len(outs),
        scratch_shapes=[pltpu.VMEM(*s) for s in scratch]
        + [pltpu.SemaphoreType.DMA((count,))] * sems,
        compiler_params=pltpu.CompilerParams(
            collective_id=collective,
            has_side_effects=True,
            vmem_limit_bytes=(room + 2 * count) << 20,
        ),
        cost_estimate=pl.CostEstimate(flops=0, bytes_accessed=20 << 20, transcendentals=0),
        name="mixer"+str(collective),
    )(*operands)


def mix_forward(weights, proj, layout):
    count = lax.axis_size(CTX)
    widths, heads = weights.widths, weights.heads
    length, inner = proj.shape[0], (proj.shape[1] - widths[3]) // 2
    states = (widths[2] - widths[1]) // 2
    kv = widths[1] - widths[0]
    shape = jax.ShapeDtypeStruct
    head_rows = -(-heads // 8) * 8
    outs = [
        shape((length, widths[0] + inner), bf16),
        shape((length, inner), f32),
        shape((inner, states), bf16),
        shape((count * length, kv), bf16),
        shape((count, head_rows, states), f32),
    ]
    per_head = ((length, 128), f32)
    scratch = [
        per_head,
        ((128, length), f32),
        per_head,
        per_head,
        per_head,
        ((length, count * length), f32),
        ((length, length), f32),
        ((count, length, kv), bf16),
        ((count, inner, states), bf16),
        ((count, head_rows, states), f32),
        ((inner, states), f32),
    ]
    operands = (proj, weights.head_rows, weights.skip_row, *layout)
    return mixer_call(mix_forward_kernel, 5, outs, scratch, 6, widths, heads, operands, 18)


def mix_backward(weights, saved, d_both, layout):
    count = lax.axis_size(CTX)
    widths, heads = weights.widths, weights.heads
    proj = saved.proj
    length, inner = proj.shape[0], (proj.shape[1] - widths[3]) // 2
    states = (widths[2] - widths[1]) // 2
    kv = widths[1] - widths[0]
    shape = jax.ShapeDtypeStruct
    outs = [shape(proj.shape, bf16), shape((8, 128), f32)]
    per_head = ((length, 128), f32)
    square = ((length, length), f32)
    scratch = [
        per_head,
        ((128, length), f32),
        per_head,
        per_head,
        per_head,
        ((length, count * length), f32),
        square,
        square,
        ((length, inner), bf16),
        ((length, inner), bf16),
        ((length, inner), f32),
        ((count * length, kv), f32),
        ((length, states), f32),
        ((length, states), f32),
        per_head,
        per_head,
        per_head,
        per_head,
        ((count, inner, states), bf16),
        ((inner, states), f32),
        ((count, length, kv), bf16),
        ((count, length, kv), bf16),
    ]
    operands = (
        proj,
        weights.head_rows,
        weights.skip_row,
        *layout,
        saved.mixed,
        saved.state_in,
        saved.keyval_all,
        saved.decays,
        d_both,
    )
    return mixer_call(mix_backward_kernel, 6, outs, scratch, 4, widths, heads, operands, 24)


def finish_kernel(
    count,
    places,
    widths,
    *refs,
):
    unsummed, arrays, refs = refs[:8], refs[8:18], refs[18:]
    (
        rows0,
        rows1,
        grad0,
        grad1,
        tiny0,
        tiny1,
        wide0,
        wide1,
        columns0,
        columns1,
        *refs,
    ) = refs
    (
        query_out,
        zx_out,
        up_out,
        down_out,
        out_out,
        rows_out,
        grad_out,
        shared_out,
        tiny_out,
        *refs,
    ) = refs
    arrays, refs = (*refs[:4], *arrays), refs[4:]
    boxes, refs = refs[: len(widths)], refs[len(widths) :]
    (
        rows_box,
        grad_box,
        tiny_box,
        tiny_sum,
        tiny_all,
        wide_boxes,
        columns_boxes,
        blocks,
        blocks_box,
        shared,
        shared_box,
        send,
        recv,
        ctx_send,
        ctx_recv,
    ) = refs
    section, place = lax.axis_index(SECTION), lax.axis_index(CTX)
    bar = pltpu.get_barrier_semaphore()
    pl.semaphore_signal(bar, inc=1, device_id={SECTION: 1 - section}, device_id_type=MESH)
    for k in range(1, count):
        peer = flipped(place, k, count)
        pl.semaphore_signal(bar, inc=1, device_id={CTX: peer}, device_id_type=MESH)
    pl.semaphore_wait(bar, count)
    half = wide0.shape[1] // 2
    own_half = pl.ds(pl.multiple_of(section * half, half), half)
    other_half = pl.ds(pl.multiple_of((1 - section) * half, half), half)

    def over(i, source, target):
        return pltpu.make_async_remote_copy(
            source,
            target,
            send.at[i],
            recv.at[i],
            device_id={SECTION: 1 - section},
            device_id_type=MESH,
        )

    def across(i, k, source, target):
        return pltpu.make_async_remote_copy(
            source,
            target,
            ctx_send.at[i],
            ctx_recv.at[i],
            device_id={CTX: flipped(place, k, count)},
            device_id_type=MESH,
        )

    def part(layer, i):
        array, start, width = places[layer][i]
        return arrays[array].at[:, start : start + width]

    def by_section(act, first, second):
        @pl.when(section == 1)
        def _():
            act(first)

        @pl.when(section == 0)
        def _():
            act(second)

    block = blocks.shape[2]
    wides, columns = (wide0, wide1), (columns0, columns1)
    early = [over(l, wides[l].at[:, other_half], wide_boxes.at[l]) for l in range(2)]
    early += [over(2 + l, columns[l], columns_boxes.at[l]) for l in range(2)]
    for copy in early:
        copy.start()
    for i in range(4):
        arrays[i][...] = (unsummed[2 * i][...].astype(f32) + unsummed[2 * i + 1][...].astype(f32)).astype(bf16)
    pairs = [(tiny0, tiny1, tiny_box)]
    pairs += [(part(0, i), part(1, i), box) for i, box in enumerate(boxes)]
    pairs += [(rows0, rows1, rows_box), (grad0, grad1, grad_box)]
    copies = [
        (over(4 + i, first, box), over(4 + i, second, box))
        for i, (first, second, box) in enumerate(pairs)
    ]

    def each(act, which):
        for first, second in which:
            by_section(act, first, second)

    each(lambda copy: copy.start(), copies)
    for copy in early:
        copy.wait_recv()
    dims = (((0,), (0,)), ((), ()))

    def block_copy(l, k):
        return across(2 * k + l, k, blocks.at[l, k], blocks_box.at[l, k])

    for l in range(2):
        total = lax.dot_general(
            columns[l][...], wides[l][:, own_half], dims, preferred_element_type=f32
        ) + lax.dot_general(columns_boxes[l], wide_boxes[l], dims, preferred_element_type=f32)
        for k in range(count):
            blocks[l, k] = total[k * block : (k + 1) * block, :].astype(bf16)
        for k in range(1, count):
            block_copy(l, k).start()
    each(lambda copy: copy.wait_recv(), copies[:1])

    def first_tiny(mine):
        tiny_sum[...] = mine[...] + tiny_box[...]

    by_section(first_tiny, tiny1, tiny0)
    for k in range(1, count):
        across(2 * count + k, k, tiny_sum, tiny_all.at[k]).start()

    def place_pieces(low_core, take):
        query, zx_a, zx_b, up_a, up_b, down_a, down_b, out_a, out_b = (
            functools.partial(take, i) for i in range(9)
        )
        width = query_out.shape[1] // 2
        query_out[:, pl.ds(pl.multiple_of(low_core * width, width), width)] = query()
        edge = zx_out.shape[2] // 2
        zx_out[low_core, :, :edge] = zx_a().astype(f32)
        zx_out[low_core, :, edge:] = zx_b().astype(f32)
        edge = up_out.shape[2] // 2
        up_out[low_core, :, :edge] = up_a().astype(f32)
        up_out[low_core, :, edge:] = up_b().astype(f32)
        for target, pieces in ((down_out, (down_a, down_b)), (out_out, (out_a, out_b))):
            for i, piece in enumerate(pieces):
                height = target.shape[0] // 4
                start = low_core * 2 * height + i * height
                target[pl.ds(pl.multiple_of(start, height), height), :] = piece().T

    def own(layer):
        def take(i):
            return part(layer, i)[...]

        place_pieces(section, take)

    by_section(own, 1, 0)
    each(lambda copy: copy.wait_recv(), copies[1:])
    place_pieces(1 - section, lambda i: boxes[i][...])

    def rows_done(mine):
        rows_out[section] = mine[0][...]
        grad_out[section] = mine[1][...]

    by_section(rows_done, (rows1, grad1), (rows0, grad0))
    rows_out[1 - section] = rows_box[...]
    grad_out[1 - section] = grad_box[...]
    for l in range(2):
        rows = blocks[l, 0].astype(f32)
        for k in range(1, count):
            block_copy(l, k).wait_recv()
            rows += blocks_box[l, k].astype(f32)
        shared[l] = rows.astype(bf16)
    shared_copy = over(len(pairs) + 4, shared.at[1 - section], shared_box)
    shared_copy.start()
    everything = tiny_sum[...]
    for k in range(1, count):
        across(2 * count + k, k, tiny_sum, tiny_all.at[k]).wait_recv()
        everything += tiny_all[k]
    tiny_out[...] = everything

    shared_out[:, own_half] = shared[section]
    shared_copy.wait_recv()
    shared_out[:, other_half] = shared_box[...]
    for copy in early:
        copy.wait_send()
    each(lambda copy: copy.wait_send(), copies)
    shared_copy.wait_send()
    for k in range(1, count):
        for l in range(2):
            block_copy(l, k).wait_send()
        across(2 * count + k, k, tiny_sum, tiny_all.at[k]).wait_send()


def finish(first, second, rows, d_rows, tinies, wides, columns):
    count = lax.axis_size(CTX)
    pairs = [*first.ffn, *first.out]
    arrays = (*first.proj, *second.ffn, *second.down, *second.mix, *second.out)
    up, down = second.ffn[0].shape[1], second.down[0].shape[1]
    out = first.out[0][0].shape[1]
    step = 128
    most = second.mix[1].shape[1] - step
    query = first.proj[0].shape[1] - most

    places = (
        (
            (4, 0, query),
            (4, query, most),
            (5, 0, most),
            (0, 0, up),
            (1, 0, up),
            (0, up, down),
            (1, up, down),
            (2, 0, out),
            (3, 0, out),
        ),
        (
            (10, 0, query),
            (10, query, most),
            (11, 0, most),
            (6, 0, up),
            (7, 0, up),
            (8, 0, down),
            (9, 0, down),
            (12, 0, out),
            (13, 0, out),
        ),
    )
    length = first.proj[0].shape[0]
    widths = [piece[2] for piece in places[0]]
    half, block = wides[0].shape[1] // 2, columns[0].shape[1] // count
    shape = jax.ShapeDtypeStruct
    outs = [
        shape((length, 2 * query), bf16),
        shape((2, length, 2 * most), f32),
        shape((2, length, 2 * up), f32),
        shape((4 * down, length), bf16),
        shape((4 * out, length), bf16),
        shape((2,) + rows[0].shape, bf16),
        shape((2,) + d_rows[0].shape, f32),
        shape((block, 2 * half), bf16),
        shape(tinies[0].shape, f32),
    ]
    tokens = columns[0].shape[0]
    scratch = [pltpu.VMEM(kept.shape, bf16) for kept, _ in pairs]
    scratch += [pltpu.VMEM((length, w), bf16) for w in widths]
    scratch += [
        pltpu.VMEM(rows[0].shape, bf16),
        pltpu.VMEM(d_rows[0].shape, f32),
        pltpu.VMEM(tinies[0].shape, f32),
        pltpu.VMEM(tinies[0].shape, f32),
        pltpu.VMEM((count,) + tinies[0].shape, f32),
        pltpu.VMEM((2, tokens, half), bf16),
        pltpu.VMEM((2, tokens, count * block), bf16),
        pltpu.VMEM((2, count, block, half), bf16),
        pltpu.VMEM((2, count, block, half), bf16),
        pltpu.VMEM((2, block, half), bf16),
        pltpu.VMEM((block, half), bf16),
    ]
    over = len(widths) + 8
    scratch += [pltpu.SemaphoreType.DMA((n,)) for n in (over, over, 3 * count, 3 * count)]
    whole = pl.BlockSpec(memory_space=pltpu.VMEM)
    operands = (*sum(pairs, ()), *arrays, *rows, *d_rows, *tinies, *wides, *columns)
    return pl.pallas_call(
        functools.partial(finish_kernel, count, places, widths),
        out_shape=outs,
        in_specs=[whole] * len(operands),
        out_specs=[whole] * len(outs),
        scratch_shapes=scratch,
        compiler_params=pltpu.CompilerParams(
            collective_id=11, has_side_effects=True, vmem_limit_bytes=56 << 20
        ),
        cost_estimate=pl.CostEstimate(flops=0, bytes_accessed=20 << 20, transcendentals=0),
        name="finish",
    )(*operands)


def norm_apply(values, gain):
    return values * lax.rsqrt(jnp.mean(values * values, axis=-1, keepdims=True) + eps) * gain


def matmul(left, right):
    return jnp.dot(left, right, preferred_element_type=f32)


def matmul_nt(left, right):
    return lax.dot_general(left, right, (((1,), (1,)), ((), ())), preferred_element_type=f32)


def matmul_tn(left, right):
    return lax.dot_general(left, right, (((0,), (0,)), ((), ())), preferred_element_type=f32)


def swap(values):
    return lax.ppermute(values, SECTION, [(0, 1), (1, 0)])


def block_layout(doc_lengths, length):
    count, place = lax.axis_size(CTX), lax.axis_index(CTX)
    start = place * length
    bounds = jnp.cumsum(doc_lengths)[:-1]

    def segment_of(positions):
        return jnp.sum((positions[:, None] >= bounds[None, :]).astype(jnp.int32), axis=1)

    order = lax.rem(place + count - jnp.arange(count, dtype=jnp.int32), count)
    inside = jnp.arange(length, dtype=jnp.int32)
    keys = (order[:, None] * length + inside[None, :]).reshape(-1)
    positions = start + inside
    segments = segment_of(positions)
    before = jnp.where(place > 0, segment_of(start[None] - 1)[0], -1)
    goes_on = jnp.broadcast_to(segments[-1] == before, segments.shape)
    columns = [segments, segments == before, segments == segments[-1], positions, goes_on]
    tokens = jnp.stack([c.astype(f32) for c in columns], axis=1)
    return jnp.pad(tokens, ((0, 0), (0, 3))), jnp.stack(
        [segment_of(keys).astype(f32), keys.astype(f32)]
    )


def layer_forward(weights, normed, layout):
    proj = matmul(normed, weights.proj)
    both, mixed, state_in, keyval_all, decays = mix_forward(weights, proj, layout)
    saved = types.SimpleNamespace(
        normed=normed,
        proj=proj,
        both=both,
        mixed=mixed,
        state_in=state_in,
        keyval_all=keyval_all,
        decays=decays,
    )
    return matmul(both, weights.out), saved


def ffn_forward(weights, ffn_in):
    gate_up = matmul(ffn_in, weights.gate_up)
    width = gate_up.shape[1] // 2
    gate_pre, upward = gate_up[:, :width], gate_up[:, width:]
    product = (jax.nn.silu(gate_pre) * upward).astype(bf16)
    return matmul(product, weights.down), gate_pre.astype(bf16), upward.astype(bf16), product


def ctx_bits():
    return [1 << i for i in reversed(range((lax.axis_size(CTX) - 1).bit_length()))]


def flip(values, bit):
    return lax.ppermute(values, CTX, [(i, i ^ bit) for i in range(lax.axis_size(CTX))])


def own_half(values):
    half = values.shape[1] // 2
    section = lax.axis_index(SECTION)
    return (
        lax.dynamic_slice_in_dim(values, section * half, half, 1),
        lax.dynamic_slice_in_dim(values, (1 - section) * half, half, 1),
    )


def both_batches(kept, sent):
    return jnp.concatenate([kept, swap(sent)], axis=0)


def ctx_orders():
    bits = ctx_bits()
    return bits, bits[::-1]


def relative_order(bits):
    order = [0]
    for bit in reversed(bits):
        order = order + [k ^ bit for k in order]
    return order


def weight_sums(columns, *rows):
    kept, sent = zip(*(own_half(r) for r in rows))
    halves = both_batches(jnp.concatenate(kept, axis=1), jnp.concatenate(sent, axis=1))
    return matmul_tn(both_batches(columns, columns), halves).astype(bf16)


def shared_columns(normed):
    place, count = lax.axis_index(CTX), lax.axis_size(CTX)
    shards = lax.axis_size(SHARD)
    block = normed.shape[1] // (count * shards)
    return jnp.concatenate(
        [
            lax.dynamic_slice_in_dim(
                normed, ((place ^ k) * shards + lax.axis_index(SHARD)) * block, block, 1
            )
            for k in range(count)
        ],
        axis=1,
    )


def streams_of(total):
    place, count = lax.axis_index(CTX), lax.axis_size(CTX)
    block, half = total.shape[0] // count, total.shape[1] // 2
    streams = []
    for stream, bits in enumerate(ctx_orders()):
        parts = [
            lax.dynamic_slice(total, ((place ^ k) * block, stream * half), (block, half))
            for k in relative_order(bits)
        ]
        streams += [jnp.stack(parts[: count // 2]), jnp.stack(parts[count // 2 :])]
    return streams


def weight_scatter(streams):
    totals = []
    for i, bits in enumerate(ctx_orders()):
        kept, sent = (a.reshape(-1, a.shape[-1]) for a in streams[2 * i : 2 * i + 2])
        totals.append(scatter_relative(kept, sent, bits))
    return totals


def scatter_relative(kept, sent, bits):
    for i, bit in enumerate(bits):
        got = flip(sent, bit)
        if i + 1 < len(bits):
            rows = kept.shape[0] // 2
            sent = (kept[rows:].astype(f32) + got[rows:].astype(f32)).astype(bf16)
            kept = (kept[:rows].astype(f32) + got[:rows].astype(f32)).astype(bf16)
    return kept, got


def after(first, *later):
    first, later = lax.optimization_barrier((first, later))
    return first, later


def layer_backward(weights, saved, d_out, d_low, values_in, layout, last, before):
    grads = types.SimpleNamespace()
    d_product = matmul_nt(d_low, weights.down)
    gate_pre, upward = saved.gate_pre.astype(f32), saved.upward.astype(f32)
    gate_sig = jax.nn.sigmoid(gate_pre)
    d_gate = d_product * upward * gate_sig * (1.0 + gate_pre * (1.0 - gate_sig))
    d_upward = d_product * gate_pre * gate_sig
    d_gate_up = jnp.concatenate([d_gate, d_upward], axis=1).astype(bf16)
    d_ffn_in = matmul_nt(d_gate_up, weights.gate_up)
    width = d_product.shape[1]
    up, down = width // 2, width // 4
    plan = tuple(
        (x, stream, ((x, stream * part, 2 * part + stream * part, part),))
        for stream in range(2)
        for x, part in ((0, up), (1, down))
    )
    if not last:
        plan = tuple(
            (x, 2 * x + stream, parts)
            for x, stream, parts in sorted(plan, key=lambda entry: -entry[0])
        )
    d_middle, d_mixed, grads.gain_ffn, *sums = back_sum(
        10 if last else 3,
        d_ffn_in,
        d_out,
        saved.middle,
        weights.gain_ffn,
        plan,
        (saved.ffn_in, d_low),
        (d_gate_up, saved.product),
        (),
        before.sums_mix if last else (),
        not last,
    )
    if last:
        sums, before.mix = sums[:4], sums[4:]
        grads.ffn = weight_scatter(sums)
    else:
        sums_ffn, grads.down = sums[:4], sums[4:]
    d_both = matmul_nt(d_mixed, weights.out)
    if not last:
        (d_both,), (before.tail,) = after((d_both,), before.tail)
    if last:
        sums_out = weight_sums(d_mixed, saved.both)
        (sums_out,), (d_both,) = after((streams_of(sums_out),), d_both)
        grads.out = weight_scatter(sums_out)
    d_proj, d_vec = mix_backward(weights, saved, d_both, layout)
    heads, widths = weights.heads, weights.widths
    grads.step_bias, grads.decay, grads.skip = (d_vec[i, :heads] for i in range(3))
    d_normed = matmul_nt(d_proj, weights.proj)
    placed = [
        jnp.where(weights.kv_owner == owner, d_proj[:, start : start + HD], 0)
        for start in (widths[0], widths[0] + HD)
        for owner in range(KVH)
    ]
    d_shared = jnp.concatenate([d_proj[:, widths[1] : widths[2]], *placed], axis=1)
    normed = saved.normed
    if last:
        d_step, d_zx = d_proj[:, widths[2] : widths[3]], d_proj[:, widths[3] :]
        sums_proj = weight_sums(
            normed, d_proj[:, : widths[0]], d_zx, jnp.concatenate([d_step, d_step], axis=1)
        )
        streams = streams_of(sums_proj)
        (streams,), (d_normed,) = after((streams,), d_normed)
        d_hidden, d_hidden_low, grads.gain_in, d_shared, grads.proj = back_sum_scatter(
            7, d_normed, d_shared, d_middle, values_in, weights.gain_in, streams
        )
    else:
        query, inner = widths[0] // 2, (d_proj.shape[1] - widths[3]) // 2
        step, zx = widths[3] - widths[2], widths[3]
        both, most = saved.both.shape[1] // 4, inner // 2
        plan = (
            (1, 2, ((1, 0, 2 * both, both),)),
            (1, 3, ((1, both, 3 * both, both),)),
            (0, 0, ((0, 0, query, query), (0, zx, zx + inner, most))),
            (0, 1, ((0, zx + most, zx + inner + most, most), (0, widths[2], widths[2], step))),
        )
        d_hidden, d_hidden_low, grads.gain_in, d_shared, *sums = back_sum(
            4,
            d_normed,
            d_middle,
            values_in,
            weights.gain_in,
            plan,
            (normed, d_mixed),
            (d_proj, saved.both),
            (d_shared,),
            sums_ffn,
            True,
        )
        sums, grads.ffn, grads.out = sums[:4], sums[4:6], sums[6:]
        grads.sums_mix = sums
    grads.wide = d_shared
    return d_hidden, d_hidden_low, grads


def body(
    inputs,
    cotangent,
    doc_lengths,
    norm_in,
    w_query,
    w_keyval,
    w_attn_out,
    w_mixer_in,
    w_state_io,
    w_step,
    step_bias,
    decay_rate,
    skip_gain,
    w_mixer_out,
    norm_ffn,
    w_gate_up,
    w_down,
):
    section = lax.axis_index(SECTION)
    leading = section == 0
    shard = lax.axis_index(SHARD)
    width = w_query.shape[1]
    query_width = w_query.shape[2]
    head_count = w_step.shape[2]
    kv_owner = shard * (query_width // HD) // (QH // KVH)
    rows_in = lax.dynamic_index_in_dim(inputs, section, 0, False)
    own_keyval = lax.dynamic_slice_in_dim(w_keyval[0], kv_owner * HD, HD, 2).reshape(width, 2 * HD)
    io_end = query_width + 2 * HD + w_state_io.shape[2]
    widths = (query_width, query_width + 2 * HD, io_end, io_end - (-head_count // 128) * 128)
    proj = jnp.concatenate(
        [
            w_query[0],
            own_keyval,
            w_state_io[0],
            jnp.pad(w_step[0], ((0, 0), (0, -head_count % 128))),
            w_mixer_in[0].reshape(width, -1),
        ],
        axis=1,
    )
    vectors = jnp.concatenate([norm_in[0], norm_ffn[0], step_bias[0], decay_rate[0], skip_gain[0]])
    block_in = line_gather(rows_in)
    (block_in,), (proj,) = after((block_in,), proj)
    own = (
        proj,
        jnp.concatenate([w_attn_out[0], w_mixer_out[0]], axis=0),
        w_gate_up[0].reshape(width, -1),
        w_down[0],
        vectors,
    )
    other = tuple(swap(array) for array in own)

    def layer_weights(layer):
        weights = types.SimpleNamespace()
        chosen = [jnp.where(section == layer, a, b) for a, b in zip(own, other)]
        weights.proj, weights.out, weights.gate_up, weights.down, vectors = chosen
        heads = vectors[2 * width :]
        weights.gain_in = vectors[:width]
        weights.gain_ffn = vectors[width : 2 * width]
        skip = heads[2 * head_count :]
        rows = heads[: 2 * head_count].reshape(2, head_count)
        weights.head_rows = jnp.pad(rows, ((0, 6), (0, -head_count % 128)))
        weights.skip_row = jnp.repeat(skip, HP)[None]
        weights.heads = head_count
        weights.widths = widths
        weights.kv_owner = kv_owner
        return weights

    layers = [layer_weights(0), layer_weights(1)]
    rows_cot = lax.dynamic_index_in_dim(cotangent, section, 0, False)
    length = block_in.shape[0]
    part = rows_in.shape[0]
    layout = block_layout(lax.dynamic_index_in_dim(doc_lengths, section, 0, False), length)

    def own_rows(values):
        return lax.dynamic_slice_in_dim(values, shard * part, part, 0)

    hidden = block_in
    normed = norm_apply(hidden.astype(f32), layers[0].gain_in).astype(bf16)
    hiddens, outs, saves = [], [], []
    for layer in range(2):
        weights = layers[layer]
        hiddens.append(hidden)
        if layer == 1:
            (normed,), (rows_cot,) = after((normed,), rows_cot)
            block_cot = lax.all_gather(rows_cot, SHARD, axis=0, tiled=True)
        partial, saved = layer_forward(weights, normed, layout)
        first, second = layers
        wanted = [(1, own[i], other[i]) for i in (0, 1)]
        if layer == 1:
            wanted = [(0, own[i], other[i]) for i in (2, 3)]
        saved.middle, saved.ffn_in, chosen = copying_sum(
            middle_kernel, 1 + 8 * layer, f32, partial, hidden, weights.gain_ffn, wanted
        )
        if layer == 0:
            second.proj, second.out = chosen
        else:
            first.gate_up, first.down = chosen
        partial, saved.gate_pre, saved.upward, saved.product = ffn_forward(
            weights, saved.ffn_in
        )
        saves.append(saved)
        if layer == 0:
            wanted = [(1, own[i], other[i]) for i in (2, 3)]
            out_low, normed, chosen = copying_sum(
                layer_end_kernel, 2, bf16, partial, saved.middle, second.gain_in, wanted
            )
            second.gate_up, second.down = chosen
            outs.append(own_rows(out_low))
            hidden = out_low
        else:
            held = types.SimpleNamespace(tail=partial.astype(bf16))

    d_out = d_low = block_cot
    d_hiddens, grads = [None, None], [None, None]
    for layer in (1, 0):
        d_hidden, d_low, grads[layer] = layer_backward(
            layers[layer], saves[layer], d_out, d_low, hiddens[layer], layout, layer == 0, grads[1] if layer == 0 else held
        )
        d_hiddens[layer] = d_hidden
        d_out = d_low

    total = lax.psum_scatter(held.tail, SHARD, scatter_dimension=0, tiled=True)
    outs.append((own_rows(saves[1].middle) + total.astype(f32)).astype(bf16))
    first, second = grads
    tinies = []
    for g in grads:
        vector = jnp.concatenate([g.gain_in, g.gain_ffn, g.step_bias, g.decay, g.skip])
        size = -(-vector.shape[0] // 1024) * 8
        tinies.append(jnp.pad(vector, (0, size * 128 - vector.shape[0])).reshape(size, 128))
    query, zx, up, down, out, out_rows, grad_rows, shared, tiny = finish(
        first,
        second,
        outs,
        [own_rows(d) for d in d_hiddens],
        tinies,
        [first.wide, second.wide],
        [shared_columns(saved.normed) for saved in saves],
    )
    tiny = tiny.reshape(-1)
    place = lax.axis_index(CTX) * lax.axis_size(SHARD) + shard
    slot = width // (lax.axis_size(CTX) * lax.axis_size(SHARD))
    grad_in = lax.dynamic_slice_in_dim(tiny, place * slot, slot, 0)
    grad_ffn = lax.dynamic_slice_in_dim(tiny, width + place * slot, slot, 0)
    heads = tiny[2 * width :]
    step = jnp.where(
        leading,
        first.proj[1][:, zx.shape[2] // 2 :],
        second.mix[1][:, zx.shape[2] // 2 : zx.shape[2] // 2 + 128],
    )
    io_width = w_state_io.shape[2]
    return (
        out_rows[None],
        grad_rows[None],
        grad_in[None],
        query.astype(f32)[None],
        shared[:, io_width:].astype(f32).reshape(-1, 2, KVH * HD)[None],
        out[:query_width].astype(f32)[None],
        jnp.swapaxes(zx, 0, 1)[None],
        shared[:, :io_width].astype(f32)[None],
        step[:, :head_count].astype(f32)[None],
        heads[:head_count][None],
        heads[head_count : 2 * head_count][None],
        heads[2 * head_count : 3 * head_count][None],
        out[query_width:].astype(f32)[None],
        grad_ffn[None],
        jnp.swapaxes(up, 0, 1)[None],
        down.astype(f32)[None],
    )


def solution(mesh):
    return jax.shard_map(
        body,
        mesh=mesh,
        in_specs=(
            P(None, (CTX, SHARD), None),
            P(None, (CTX, SHARD), None),
            P(),
            P(SECTION, None),
            P(SECTION, None, SHARD),
            P(SECTION, None, None, None),
            P(SECTION, SHARD, None),
            P(SECTION, None, None, SHARD),
            P(SECTION, None, None),
            P(SECTION, None, SHARD),
            P(SECTION, SHARD),
            P(SECTION, SHARD),
            P(SECTION, SHARD),
            P(SECTION, SHARD, None),
            P(SECTION, None),
            P(SECTION, None, None, SHARD),
            P(SECTION, SHARD, None),
        ),
        out_specs=(
            P(SECTION, None, (CTX, SHARD), None),
            P(SECTION, None, (CTX, SHARD), None),
            P(SECTION, (CTX, SHARD)),
            P(SECTION, CTX, SHARD),
            P(SECTION, (CTX, SHARD), None, None),
            P(SECTION, SHARD, CTX),
            P(SECTION, CTX, None, SHARD),
            P(SECTION, (CTX, SHARD), None),
            P(SECTION, CTX, SHARD),
            P(SECTION, SHARD),
            P(SECTION, SHARD),
            P(SECTION, SHARD),
            P(SECTION, SHARD, CTX),
            P(SECTION, (CTX, SHARD)),
            P(SECTION, CTX, None, SHARD),
            P(SECTION, SHARD, CTX),
        ),
        check_vma=False,
    )
```
